32 devices in a mesh: dp: 16 (over z, y, x), mp: 2 (over core).
Axes of the slice: x: 2, y: 2, z: 4, core: 2. Of those that a mesh axis runs over, the one named last changes fastest.
Arguments:
- tokens: bfloat16 [128, 256, 1152], P('dp'), may hold values from -6 to 6
- condition: bfloat16 [128, 1152], P('dp'), may hold values from -6 to 6
- counts: int32 [16], P('dp'), may hold values from 1 to 8, as said below
- w_qkv: bfloat16 [1152, 3, 1152], P(None, None, 'mp'), may hold values from -0.1875 to 0.1875
- b_qv: bfloat16 [2, 1152], P(None, 'mp'), may hold values from -3 to 3
- w_proj: bfloat16 [1152, 1152], P('mp'), may hold values from -0.75 to 0.75
- b_proj: bfloat16 [1152], replicated, may hold values from -3 to 3
- w_up: bfloat16 [1152, 4608], P(None, 'mp'), may hold values from -0.1875 to 0.1875
- b_up: bfloat16 [4608], P('mp'), may hold values from -3 to 3
- w_down: bfloat16 [4608, 1152], P('mp'), may hold values from -0.09375 to 0.09375
- b_down: bfloat16 [1152], replicated, may hold values from -3 to 3
- w_mod: bfloat16 [1152, 6912], P(None, 'mp'), may hold values from -0.1875 to 0.1875
- b_mod: bfloat16 [6912], P('mp'), may hold values from -3 to 3
- cotangent: bfloat16 [128, 256, 1152], P('dp'), may hold values from -6 to 6
Outputs:
- output: bfloat16 [128, 256, 1152], P('dp')
- grad_tokens: float32 [128, 256, 1152], P('dp')
- grad_condition: float32 [128, 1152], P('dp')
- grad_w_qkv: float32 [1152, 3, 1152], P(None, None, 'mp')
- grad_b_qv: float32 [2, 1152], P(None, 'mp')
- grad_w_proj: float32 [1152, 1152], P('mp')
- grad_b_proj: float32 [1152], replicated
- grad_w_up: float32 [1152, 4608], P(None, 'mp')
- grad_b_up: float32 [4608], P('mp')
- grad_w_down: float32 [4608, 1152], P('mp')
- grad_b_down: float32 [1152], replicated
- grad_w_mod: float32 [1152, 6912], P(None, 'mp')
- grad_b_mod: float32 [6912], P('mp')
The draws below stay inside these ranges and needn't reach their ends.
Inputs may be any that keep to these rules, and one draw needn't show every extreme that they name: counts[g] of group g's 8 slots are live, its first ones; some group has all 8 live in every draw.
All inputs are finite; a program needn't handle non-finite values.
Results may differ from the reference program's by a relative error of at most 0.02.
Values may be sent and summed in bfloat16 or wider, within the bound.
No kernel may reach another device: no remote copies, remote signals or barrier semaphores. Data moves between devices by JAX's collectives and lax.ppermute only.
A program may use at most 256 MiB of HBM per device.

```python
import jax
import jax.numpy as jnp
from jax import lax

D = 1152
HEADS = 16
HEAD_DIM = 72
FF = 4608
SEQ = 256
CAP = 8
GROUPS = 16
IMAGES = 128
N_MP = 2


def draw_counts(key, part):
    key_count, key_pick = jax.random.split(key)
    values = jax.random.randint(key_count, (GROUPS,), 1, CAP + 1)
    chosen = jax.random.randint(key_pick, (), 0, GROUPS)
    return jnp.where(jnp.arange(GROUPS) == chosen, CAP, values).astype(jnp.int32)


def shard_levels(rng, extent, cuts, smallest, largest):
    loudness = 1.0
    for position, shards_of in cuts:
        heights = jax.random.uniform(jax.random.fold_in(jax.random.fold_in(rng, 6), position), (shards_of,), jnp.float32, smallest / len(cuts), largest / len(cuts))
        loudness = loudness * jnp.repeat(jnp.exp(heights), extent[position] // shards_of).reshape((-1,) + (1,) * (len(extent) - 1 - position))
    return loudness


def normal_values(rng, dims, scale, bound, shards=(), kind=jnp.bfloat16):
    array = jax.random.normal(rng, dims, jnp.float32) * scale
    if len(shards) > 0:
        array = shard_levels(rng, dims, shards, -0.22, 0.18) * array
    return jnp.clip(array, min=-bound, max=bound).astype(kind)


def setup_inputs(seed: int = 0) -> dict:
    splits = jax.random.split(jax.random.key(seed), 15)
    tokens = normal_values(splits[0], (IMAGES, SEQ, D), 1.0, 6.0, ((0, 16),))
    condition = normal_values(splits[1], (IMAGES, D), 1.0, 6.0, ((0, 16),))
    counts = draw_counts(jax.random.fold_in(splits[14], 71), 0)
    w_qkv = normal_values(splits[3], (D, 3, D), D ** -0.5, 0.1875, ((2, 2),))
    b_qv = normal_values(splits[4], (2, D), 0.5, 3.0, ((1, 2),))
    w_proj = normal_values(splits[5], (D, D), (D // 16) ** -0.5, 0.75, ((0, 2),))
    b_proj = normal_values(splits[6], (D,), 0.5, 3.0)
    w_up = normal_values(splits[7], (D, FF), D ** -0.5, 0.1875, ((1, 2),))
    b_up = normal_values(splits[8], (FF,), 0.5, 3.0, ((0, 2),))
    w_down = normal_values(splits[9], (FF, D), FF ** -0.5, 0.09375, ((0, 2),))
    b_down = normal_values(splits[10], (D,), 0.5, 3.0)
    w_mod = normal_values(splits[11], (D, 6 * D), D ** -0.5, 0.1875, ((1, 2),))
    b_mod = normal_values(splits[12], (6 * D,), 0.5, 3.0, ((0, 2),))
    cotangent = normal_values(splits[13], (IMAGES, SEQ, D), 1.0, 6.0, ((0, 16),))
    return dict(tokens=tokens, condition=condition, counts=counts, w_qkv=w_qkv, b_qv=b_qv, w_proj=w_proj, b_proj=b_proj, w_up=w_up, b_up=b_up, w_down=w_down, b_down=b_down, w_mod=w_mod, b_mod=b_mod, cotangent=cotangent)


@jax.custom_vjp
def low(v):
    return lax.optimization_barrier(v.astype(jnp.bfloat16)).astype(jnp.float32)

@jax.custom_vjp
def low_back(v):
    return v

def low_keep(v):
    return (low(v), None)

def low_pass(kept, grad):
    return (grad,)

def back_keep(v):
    return (v, None)

def back_low(kept, grad):
    return (low(grad),)
low.defvjp(low_keep, low_pass)
low_back.defvjp(back_keep, back_low)
highest = lax.Precision.HIGHEST
epsilon = 1e-06

def matmul(left, right):
    return jnp.matmul(left, right, precision=highest)

def layer_norm(values):
    center = values - lax.optimization_barrier(jnp.mean(values, axis=-1, keepdims=True))
    return center * lax.rsqrt(lax.optimization_barrier(jnp.mean(center * center, axis=-1, keepdims=True)) + epsilon)

def modulate(values, shift_part, scale_part):
    return layer_norm(values) * (1.0 + scale_part) + shift_part

def gelu_tanh(values):
    return 0.5 * values * (1.0 + jnp.tanh(0.7978845608028654 * (values + 0.044715 * values * values * values)))

def group_forward(params, tokens, condition, live_mask):
    w_qkv, b_qv, w_proj, b_proj, w_up, b_up, w_down, b_down, w_mod, b_mod = params
    scaled = low(jax.nn.silu(condition))
    modulation = low_back(matmul(scaled, w_mod) + b_mod)
    spans = [modulation[:, None, part_idx * D:(part_idx + 1) * D] for part_idx in range(6)]
    shift_attn, scale_attn, gate_attn, shift_mlp, scale_mlp, gate_mlp = spans
    normed = low(modulate(tokens, shift_attn, scale_attn))
    head_cols = D // N_MP
    head_count = HEADS // N_MP
    ff_cols = FF // N_MP
    shape_four = (CAP, SEQ, head_count, HEAD_DIM)
    attn_total = jnp.zeros_like(tokens)
    for group_idx in range(N_MP):
        lower = group_idx * head_cols
        upper = lower + head_cols
        inner = low_back(normed)
        query_rows = low(low_back(matmul(inner, w_qkv[:, 0, lower:upper]) + b_qv[0, lower:upper]))
        key_rows = low(low_back(matmul(inner, w_qkv[:, 1, lower:upper])))
        value_rows = low(low_back(matmul(inner, w_qkv[:, 2, lower:upper]) + b_qv[1, lower:upper]))
        scores = jnp.einsum('bqhd,bkhd->bhqk', query_rows.reshape(shape_four), key_rows.reshape(shape_four), precision=highest)
        scores = low_back(scores * HEAD_DIM ** (-0.5))
        prob_b = low(jax.nn.softmax(scores, axis=-1))
        mixed_out = jnp.einsum('bhqk,bkhd->bqhd', prob_b, value_rows.reshape(shape_four), precision=highest)
        mixed_out = low(low_back(mixed_out.reshape(CAP, SEQ, head_cols)))
        attn_total = attn_total + low(matmul(mixed_out, w_proj[lower:upper]))
    attn_out = low_back(attn_total + b_proj)
    residual = tokens + gate_attn * attn_out
    normed_mlp = low(modulate(residual, shift_mlp, scale_mlp))
    mlp_total = jnp.zeros_like(tokens)
    for group_idx in range(N_MP):
        lower = group_idx * ff_cols
        upper = lower + ff_cols
        inner = low_back(normed_mlp)
        hidden = low_back(matmul(inner, w_up[:, lower:upper]) + b_up[lower:upper])
        mlp_total = mlp_total + low(matmul(low(gelu_tanh(hidden)), w_down[lower:upper]))
    mlp_out = low_back(mlp_total + b_down)
    return (residual + gate_mlp * mlp_out) * live_mask[:, None, None]

def reference(tokens, condition, counts, w_qkv, b_qv, w_proj, b_proj, w_up, b_up, w_down, b_down, w_mod, b_mod, cotangent):
    live_mask = (jnp.arange(CAP, dtype=jnp.int32)[None, :] < counts[:, None]).astype(jnp.float32)
    params = tuple((array_in.astype(jnp.float32) for array_in in (w_qkv, b_qv, w_proj, b_proj, w_up, b_up, w_down, b_down, w_mod, b_mod)))
    token_f = tokens.astype(jnp.float32).reshape(GROUPS, CAP, SEQ, D)
    cond_f = condition.astype(jnp.float32).reshape(GROUPS, CAP, D)

    def whole_batch(weights, token_in, cond_in):

        def one_group(inputs):
            return group_forward(weights, inputs[0], inputs[1], inputs[2])
        return lax.map(jax.checkpoint(one_group), (token_in, cond_in, live_mask))
    output, pullback = jax.vjp(whole_batch, params, token_f, cond_f)
    grad_params, grad_tokens, grad_cond = pullback(cotangent.astype(jnp.float32).reshape(GROUPS, CAP, SEQ, D))
    g_qkv, g_bqv, g_proj, g_bproj, g_up, g_bup, g_down, g_bdown, g_mod, g_bmod = grad_params
    return (output.astype(jnp.bfloat16).reshape(IMAGES, SEQ, D), grad_tokens.reshape(IMAGES, SEQ, D), grad_cond.reshape(IMAGES, D), g_qkv, g_bqv, g_proj, g_bproj, g_up, g_bup, g_down, g_bdown, g_mod, g_bmod)
```

```python
import functools

import jax
import jax.numpy as jnp
from jax import lax
from jax.experimental import pallas as pl
from jax.experimental.pallas import tpu as pltpu
from jax.sharding import PartitionSpec as P

HEAD_DIM = 72


epsilon = 1e-06

f32 = jnp.float32
bf16 = jnp.bfloat16


def dot_nn(left, right):
    return lax.dot_general(left, right, (((1,), (0,)), ((), ())), preferred_element_type=f32)


def dot_nt(left, right):
    return lax.dot_general(left, right, (((1,), (1,)), ((), ())), preferred_element_type=f32)


def dot_tn(left, right):
    return lax.dot_general(left, right, (((0,), (0,)), ((), ())), preferred_element_type=f32)


def normalize(values):
    center = values - jnp.mean(values, axis=-1, keepdims=True)
    recip = lax.rsqrt(jnp.mean(center * center, axis=-1, keepdims=True) + epsilon)
    return center * recip, recip


def norm_pullback(grad_normed, unit, recip, scale_row):
    scaled_grad = grad_normed * (1.0 + scale_row)
    mean_grad = jnp.mean(scaled_grad, axis=-1, keepdims=True)
    mean_unit = jnp.mean(scaled_grad * unit, axis=-1, keepdims=True)
    return recip * (scaled_grad - mean_grad - unit * mean_unit)


def column(rows):
    return rows[...].T[:, 0:1]


def token_sum(values):
    return jnp.sum(values, axis=0, keepdims=True)


def entry_kernel(own_images, sc, tok, cot, mod, normed, grad_mlp, sums):
    image = sc[0] * own_images + pl.program_id(0)
    live = jnp.where(image < sc[1], 1.0, 0.0).astype(f32)
    unit, _ = normalize(tok[0].astype(f32))
    normed[0] = (unit * (1.0 + mod[0, 1:2, :]) + mod[0, 0:1, :]).astype(bf16)
    grad = (mod[0, 5:6, :] * (cot[0].astype(f32) * live)).astype(bf16)
    grad_mlp[0] = grad
    sums[0] = token_sum(grad.astype(f32))


def attention_kernel(parts, sc, tok, normed, mod, b_proj, *refs):
    w_qkv, w_proj, bias = refs[:parts], refs[parts : 2 * parts], refs[2 * parts : 3 * parts]
    qkv, prob, mixed, attn_out, residual, normed_mlp = refs[3 * parts :]
    cols = w_proj[0].shape[0]
    pairs = cols // (2 * HEAD_DIM)
    span = 2 * HEAD_DIM
    factor = HEAD_DIM ** (-0.5)
    rows = normed[0]
    total = b_proj[...]
    for part in range(parts):
        base = part * 3 * cols
        shift = column(bias[part])
        for proj in range(3):
            lo = proj * cols
            value = dot_nt(w_qkv[part][lo : lo + cols, :], rows) + shift[lo : lo + cols, :]
            qkv[0, base + lo : base + lo + cols, :] = value.astype(bf16)

        def pair_step(pair, carry, base=base, part=part):
            at = pl.multiple_of(base + pair * span, 16)
            query = qkv[0, pl.ds(at, span), :].astype(f32)
            key = qkv[0, pl.ds(at + cols, span), :].astype(f32)
            value = qkv[0, pl.ds(at + 2 * cols, span), :].astype(f32)
            outs = []
            for one in range(2):
                rows_of = slice(one * HEAD_DIM, (one + 1) * HEAD_DIM)
                scores = dot_tn(key[rows_of].astype(bf16), query[rows_of].astype(bf16)) * factor
                raised = jnp.exp(scores - jnp.max(scores, axis=0, keepdims=True))
                share = 1.0 / jnp.sum(raised, axis=0, keepdims=True)
                prob_b = (raised * share).astype(bf16)
                prob[0, part * 2 * pairs + 2 * pair + one] = prob_b
                outs.append(dot_nn(value[rows_of].astype(bf16), prob_b))
            to = pl.multiple_of(part * cols + pair * span, 16)
            mixed[0, pl.ds(to, span), :] = jnp.concatenate(outs, axis=0).astype(bf16)
            return carry

        lax.fori_loop(0, pairs, pair_step, 0, unroll=True)
        total = total + dot_tn(mixed[0, part * cols : (part + 1) * cols, :], w_proj[part][...])
    attn_out[0] = total
    summed = tok[0].astype(f32) + mod[0, 2:3, :] * total
    residual[0] = summed
    unit, _ = normalize(summed)
    normed_mlp[0] = (unit * (1.0 + mod[0, 4:5, :]) + mod[0, 3:4, :]).astype(bf16)


def mlp_kernel(per, sc, rows, grad_mlp, w_up, w_down, bias, act_in, back_in, act, back, grads, sums):
    step = pl.program_id(0)
    here = w_down.shape[0] // per
    hidden = lax.dot_general(
        w_up[...], rows[...], (((0,), (1,)), ((), ())), preferred_element_type=f32
    ) + column(bias)
    square = hidden * hidden
    bend = jnp.tanh(0.7978845608028654 * hidden * (1.0 + 0.044715 * square))
    half = 0.5 * (1.0 + bend)
    act_b = (hidden * half).astype(bf16)
    slope = half + 0.5 * hidden * (1.0 - bend * bend) * (
        0.7978845608028654 * (1.0 + 3.0 * 0.044715 * square)
    )
    back_b = (dot_nt(w_down[...], grad_mlp[...]) * slope).astype(bf16)
    act[0] = act_b
    back[0] = back_b
    sums[...] = dot_nt(jnp.ones((8, rows.shape[0]), bf16), back_b)
    grad_down = dot_nn(act_b, grad_mlp[...]).astype(bf16)
    grad_up = dot_nn(back_b, rows[...]).astype(bf16)
    for piece in range(here):
        at = jnp.bitwise_xor(step * here + piece, sc[2])
        lo = piece * per
        grads[at, 0:per, :] = grad_down[lo : lo + per]
        grads[at, per : 2 * per, :] = grad_up[lo : lo + per]


def norm_back_kernel(
    images, own_images, sc, back, w_up0, w_up1, residual, cot, mod, attn_out,
    grad_residual, grad_attn, sums, total
):
    step, steps = pl.program_id(0), pl.num_programs(0)
    seq = residual.shape[1]

    def term(w_up):
        return lax.dot_general(
            back[0], w_up[...], (((0,), (1,)), ((), ())), preferred_element_type=f32
        )

    @pl.when(step == 0)
    def _():
        total[...] = term(w_up0)

    @pl.when(jnp.logical_and(step > 0, step < steps // 2))
    def _():
        total[...] += term(w_up0)

    @pl.when(step >= steps // 2)
    def _():
        total[...] += term(w_up1)

    @pl.when(step == steps - 1)
    def _():
        for one in range(images):
            live = jnp.where(sc[0] * own_images + one < sc[1], 1.0, 0.0).astype(f32)
            grad_normed = total[one * seq : (one + 1) * seq, :]
            unit, recip = normalize(residual[one])
            sums[one, 0:1, :] = token_sum(grad_normed)
            sums[one, 1:2, :] = token_sum(grad_normed * unit)
            grad_res = cot[one].astype(f32) * live + norm_pullback(
                grad_normed, unit, recip, mod[one, 4:5, :]
            )
            grad_residual[one] = grad_res
            sums[one, 2:3, :] = token_sum(grad_res * attn_out[one])
            grad_att = (mod[one, 2:3, :] * grad_res).astype(bf16)
            grad_attn[one] = grad_att
            sums[one, 3:4, :] = token_sum(grad_att.astype(f32))


def back_kernel(parts, sc, grad_attn, qkv, prob, *refs):
    w_proj = refs[:parts]
    grad_qkv, grad_mixed = refs[parts:]
    cols = w_proj[0].shape[0]
    pairs = cols // (2 * HEAD_DIM)
    span = 2 * HEAD_DIM
    factor = HEAD_DIM ** (-0.5)
    grad_att = grad_attn[0]
    for part in range(parts):
        base = part * 3 * cols
        grad_mixed[part * cols : (part + 1) * cols, :] = dot_nt(w_proj[part][...], grad_att).astype(bf16)

        def pair_step(pair, carry, base=base, part=part):
            at = pl.multiple_of(base + pair * span, 16)
            query = qkv[0, pl.ds(at, span), :].astype(f32)
            key = qkv[0, pl.ds(at + cols, span), :].astype(f32)
            value = qkv[0, pl.ds(at + 2 * cols, span), :].astype(f32)
            grads = grad_mixed[pl.ds(pl.multiple_of(part * cols + pair * span, 16), span), :].astype(f32)
            to_query, to_key, to_value = [], [], []
            for one in range(2):
                rows_of = slice(one * HEAD_DIM, (one + 1) * HEAD_DIM)
                prob_b = prob[0, part * 2 * pairs + 2 * pair + one]
                prob_f = prob_b.astype(f32)
                grad_b = grads[rows_of].astype(bf16)
                grad_prob = dot_tn(value[rows_of].astype(bf16), grad_b)
                delta = jnp.sum(prob_f * grad_prob, axis=0, keepdims=True)
                grad_scores = (prob_f * (grad_prob - delta)).astype(bf16)
                to_query.append(dot_nn(key[rows_of].astype(bf16), grad_scores) * factor)
                to_key.append(dot_nt(query[rows_of].astype(bf16), grad_scores) * factor)
                to_value.append(dot_nt(grad_b, prob_b))
            grad_qkv[0, pl.ds(at, span), :] = jnp.concatenate(to_query, axis=0).astype(bf16)
            grad_qkv[0, pl.ds(at + cols, span), :] = jnp.concatenate(to_key, axis=0).astype(bf16)
            grad_qkv[0, pl.ds(at + 2 * cols, span), :] = jnp.concatenate(to_value, axis=0).astype(bf16)
            return carry

        lax.fori_loop(0, pairs, pair_step, 0, unroll=True)


def attn_grad_kernel(pieces, per, sc, *refs):
    grad_qkv, mixed, normed, grad_attn = refs[:pieces], refs[pieces], refs[pieces + 1], refs[pieces + 2]
    grads, sums = refs[pieces + 3 :]
    step = pl.program_id(0)
    here = mixed.shape[1] // per
    images = mixed.shape[0]
    each = images // pieces

    def spread(total):
        total = total.astype(bf16)
        for piece in range(here):
            at = jnp.bitwise_xor(step * here + piece, sc[2])
            grads[at] = total[piece * per : (piece + 1) * per]

    @pl.when(step < 3)
    def _():
        ones = jnp.ones((8, mixed.shape[2]), bf16)
        total = count = None
        for image in range(images):
            left = grad_qkv[image // each][image % each]
            term, one = dot_nn(left, normed[image]), dot_nt(ones, left)
            total = term if image == 0 else total + term
            count = one if image == 0 else count + one
        sums[0] = count
        spread(total)

    @pl.when(step == 3)
    def _():
        total = dot_nn(mixed[0], grad_attn[0])
        for image in range(1, images):
            total = total + dot_nn(mixed[image], grad_attn[image])
        spread(total)


def first_back_kernel(pieces, images, sc, *refs):
    grad_qkv = refs[:pieces]
    w_qkv0, w_qkv1, tok, mod, grad_residual = refs[pieces : pieces + 5]
    grad_tokens, sums = refs[pieces + 5 :]
    step, steps = pl.program_id(0), pl.num_programs(0)
    each = images // pieces

    def add(w_qkv, fresh):
        for one in range(images):
            term = dot_tn(grad_qkv[one // each][one % each], w_qkv[...])
            if fresh:
                grad_tokens[one] = term
            else:
                grad_tokens[one] += term

    @pl.when(step == 0)
    def _():
        add(w_qkv0, True)

    @pl.when(jnp.logical_and(step > 0, step < steps // 2))
    def _():
        add(w_qkv0, False)

    @pl.when(step >= steps // 2)
    def _():
        add(w_qkv1, False)

    @pl.when(step == steps - 1)
    def _():
        for one in range(images):
            grad_normed = grad_tokens[one]
            unit, recip = normalize(tok[one].astype(f32))
            sums[one, 0:1, :] = token_sum(grad_normed)
            sums[one, 1:2, :] = token_sum(grad_normed * unit)
            grad_tokens[one] = grad_residual[one] + norm_pullback(
                grad_normed, unit, recip, mod[one, 1:2, :]
            )


def output_kernel(images, own_images, sc, act, w_down0, w_down1, residual, cot, mod, b_down, output, sums, total):
    step, steps = pl.program_id(0), pl.num_programs(0)
    seq = residual.shape[1]

    @pl.when(step == 0)
    def _():
        total[...] = dot_tn(act[0], w_down0[...])

    @pl.when(jnp.logical_and(step > 0, step < steps // 2))
    def _():
        total[...] += dot_tn(act[0], w_down0[...])

    @pl.when(step >= steps // 2)
    def _():
        total[...] += dot_tn(act[0], w_down1[...])

    @pl.when(step == steps - 1)
    def _():
        for one in range(images):
            live = jnp.where(sc[0] * own_images + one < sc[1], 1.0, 0.0).astype(f32)
            mlp_out = total[one * seq : (one + 1) * seq, :] + b_down[...]
            sums[one] = token_sum((cot[one].astype(f32) * live) * mlp_out)
            output[one] = ((residual[one] + mod[one, 5:6, :] * mlp_out) * live).astype(bf16)


def final_piece(sc, halves, piece, store):
    rel = jnp.bitwise_xor(piece, sc[2])
    for low, high, bit, lo, hi in halves:
        index = ((rel >> (bit + 1)) << bit) | (rel & ((1 << bit) - 1))
        side = (rel >> bit) & 1

        @pl.when(side == 0)
        def _(low=low, index=index, lo=lo, hi=hi):
            store(low[index].astype(f32), lo, hi)

        @pl.when(side == 1)
        def _(high=high, index=index, lo=lo, hi=hi):
            store(high[index].astype(f32), lo, hi)


def final_mlp_kernel(cuts, per, sc, *refs):
    count = 2 * len(cuts)
    arrays, (_, _, down, up, turned) = refs[:count], refs[count:]
    here = down.shape[0] // per
    halves = [(arrays[2 * k], arrays[2 * k + 1]) + cut for k, cut in enumerate(cuts)]
    for piece in range(here):

        def store(value, lo, hi, piece=piece):
            down[piece * per : (piece + 1) * per, lo:hi] = value[0:per]
            turned[piece * per : (piece + 1) * per, lo:hi] = value[per : 2 * per]

        final_piece(sc, halves, pl.program_id(0) * here + piece, store)
    up[...] = turned[...].T


def final_attn_kernel(cuts, per, sc, *refs):
    count = 2 * len(cuts)
    arrays, (qkv, proj) = refs[:count], refs[count:]
    here = proj.shape[0] // per
    halves = [(arrays[2 * k], arrays[2 * k + 1]) + cut for k, cut in enumerate(cuts)]
    for target, wanted in ((qkv, True), (proj, False)):

        @pl.when((pl.program_id(0) < 3) == wanted)
        def _(target=target):
            for piece in range(here):

                def store(value, lo, hi, piece=piece):
                    target[piece * per : (piece + 1) * per, lo:hi] = value

                final_piece(sc, halves, pl.program_id(0) * here + piece, store)


VMEM_LIMIT = 60 << 20


def run_kernel(body, sc, args, in_specs, out_specs, out_shape, grid, flops, scratch=(), alias=None):
    size = sum(a.size * a.dtype.itemsize for a in args) + sum(
        s.size * s.dtype.itemsize for s in out_shape
    )
    return pl.pallas_call(
        body,
        out_shape=out_shape,
        grid_spec=pltpu.PrefetchScalarGridSpec(
            num_scalar_prefetch=1,
            grid=grid,
            in_specs=in_specs,
            out_specs=out_specs,
            scratch_shapes=list(scratch),
        ),
        compiler_params=pltpu.CompilerParams(vmem_limit_bytes=VMEM_LIMIT),
        cost_estimate=pl.CostEstimate(flops=int(flops), bytes_accessed=int(size), transcendentals=0),
        input_output_aliases=alias or {},
    )(sc, *args)


def whole_block(array):
    zeros = (0,) * array.ndim
    return pl.BlockSpec(array.shape, lambda *_: zeros, pipeline_mode=pl.Buffered(1))


def shape_of(dims, kind):
    return jax.ShapeDtypeStruct(dims, kind)


SWAP = [(0, 1), (1, 0)]


def swap_cores(value):
    return lax.ppermute(value, "mp", SWAP)


def bit_pairs(bit):
    return [(index, index ^ (1 << bit)) for index in range(16)]


MLP_WAYS = ((0, 640, (0, 1, 2, 3)), (640, 1152, (1, 0, 2, 3)))
ATTN_WAYS = ((0, 512, (0, 1, 2, 3)), (512, 896, (1, 0, 2, 3)), (896, 1152, (2, 3, 0, 1)))


def cut(array, bits, bit, side, cols=None):
    lo = [0] * array.ndim
    hi = list(array.shape)
    place = bits.index(bit)
    lo[place], hi[place] = side, side + 1
    if cols is not None:
        lo[-1], hi[-1] = cols
    out = lax.slice(array, lo, hi)
    return out.reshape(out.shape[:place] + out.shape[place + 1 :])


class Flow:
    def __init__(self, ways, own, other):
        self.ways = ways
        self.shape = (2, 2, 2, 2) + other.shape[1:]
        self.own, self.other = own, other
        self.stage = 0
        self.halves = None

    def set_own(self, own):
        self.own = own

    def pending(self):
        if self.stage == 0:
            return [self.other]
        if self.stage == 1:
            return [self.own, self.came]
        return [self.keeps, self.comes]

    def step(self, fence):
        if self.stage == 0:
            (other,) = fence([self.other])
            self.came = swap_cores(other)
        elif self.stage <= 5:
            first, second = fence(self.pending())
            if self.stage == 1:
                first = [first.reshape(self.shape)] * len(self.ways)
                second = [second.reshape(self.shape)] * len(self.ways)
            sends, keeps = [], []
            for (lo, hi, order), one, two in zip(self.ways, first, second):
                if self.stage == 5:
                    keeps.append(one + two)
                    sends.append(one + two)
                    continue
                bits = [bit for bit in (3, 2, 1, 0) if bit not in order[: self.stage - 1]]
                bit = order[self.stage - 1]
                cols = (lo, hi) if self.stage == 1 else None
                sends.append(cut(one, bits, bit, 1, cols) + cut(two, bits, bit, 1, cols))
                keeps.append(cut(one, bits, bit, 0, cols) + cut(two, bits, bit, 0, cols))
            if self.stage == 5:
                self.sets = [[] for _ in self.ways]
                (keeps,) = fence([keeps])
                self.send(keeps, keeps)
            else:
                sends, keeps = fence([sends, keeps])
                self.send(sends, keeps)
        else:
            haves, comes = fence(self.pending())
            joined = []
            for (lo, hi, order), bits, have, got in zip(self.ways, self.sets, haves, comes):
                bit = order[8 - self.stage + 1]
                if self.stage == 9:
                    continue
                place = sum(1 for other in bits if other > bit)
                joined.append(jnp.stack([have, got], axis=place))
                bits.insert(place, bit)
            if self.stage == 9:
                self.halves = [
                    part.reshape((8,) + part.shape[-2:]) for pair in zip(haves, comes) for part in pair
                ]
            else:
                (joined,) = fence([joined])
                self.send(joined, joined)
        self.stage += 1

    def send(self, sends, keeps):
        self.keeps = keeps
        which = self.stage - 1 if self.stage <= 4 else 8 - self.stage
        self.comes = [
            lax.ppermute(value, "dp", bit_pairs(order[which]))
            for value, (_, _, order) in zip(sends, self.ways)
        ]


class Order:
    def __init__(self, sc):
        self.sc = sc

    def fence(self, values):
        self.sc, values = lax.optimization_barrier((self.sc, values))
        return values

    def after(self, value):
        self.sc, _ = lax.optimization_barrier((self.sc, value))

    def tick(self, *flows):
        for flow in flows:
            if flow.halves is None:
                flow.step(self.fence)


CHUNKS = 3


def fast_device(
    tokens, condition, counts, w_qkv, b_qv, w_proj, b_proj, w_up, b_up, w_down, b_down, w_mod, b_mod,
    cotangent,
):
    slots, seq, dim = tokens.shape
    images = slots // 2
    count = images * seq
    cols = w_qkv.shape[2]
    ff = w_up.shape[1]
    own_cols = w_mod.shape[1]
    heads = cols // HEAD_DIM
    core = lax.axis_index("mp")
    order = Order(jnp.stack([core, counts[0], lax.axis_index("dp")]).astype(jnp.int32))

    qkv_rows = jnp.transpose(w_qkv, (1, 2, 0)).reshape(3 * cols, dim)
    wq = [qkv_rows, swap_cores(qkv_rows)]
    wp = [w_proj, swap_cores(w_proj)]
    wu = [w_up, swap_cores(w_up)]
    wd = [w_down, swap_cores(w_down)]

    cond_f = condition.astype(f32)
    scaled = jax.nn.silu(cond_f).astype(bf16)
    own_mod = jnp.dot(scaled, w_mod, preferred_element_type=f32) + b_mod.astype(f32)
    own_bias = jnp.concatenate([b_qv.reshape(-1), b_up]).astype(f32)[None]
    gathered = lax.all_gather(jnp.concatenate([own_mod, own_bias]), "mp", axis=0, tiled=False)
    modulation = jnp.concatenate([gathered[0, :slots], gathered[1, :slots]], axis=1).reshape(slots, 6, dim)
    zero_bias = jnp.zeros((cols,), f32)
    qkv_bias, up_bias = [], []
    for part in range(2):
        row = lax.dynamic_index_in_dim(gathered[:, slots], core ^ part, 0, keepdims=False)
        qkv_row = jnp.concatenate([row[:cols], zero_bias, row[cols : 2 * cols]])
        qkv_bias.append(jnp.broadcast_to(qkv_row, (8, 3 * cols)))
        up_bias.append(jnp.broadcast_to(row[2 * cols :], (8, ff)))
    proj_bias = b_proj.astype(f32)[None]
    down_bias = b_down.astype(f32)[None]

    local = lambda i, s: (s[0] * images + i, 0, 0)
    mine = lambda i, s: (i, 0, 0)
    tok_spec = pl.BlockSpec((1, seq, dim), local)
    own_spec = pl.BlockSpec((1, seq, dim), mine)
    mod_spec = pl.BlockSpec((1, 6, dim), local)
    group = lambda i, s: (s[0], 0, 0)
    once = pl.Buffered(1)
    all_tok_spec = pl.BlockSpec((images, seq, dim), group, pipeline_mode=once)
    all_mod_spec = pl.BlockSpec((images, 6, dim), group, pipeline_mode=once)

    normed, grad_mlp, down_sums = run_kernel(
        functools.partial(entry_kernel, images),
        order.sc,
        [tokens, cotangent, modulation],
        [tok_spec, tok_spec, mod_spec],
        [own_spec, own_spec, pl.BlockSpec((1, 1, dim), mine)],
        [shape_of((images, seq, dim), bf16)] * 2 + [shape_of((images, 1, dim), f32)],
        (images,),
        count * dim * 20,
    )
    order.after(down_sums)
    qkv_spec = pl.BlockSpec((1, 6 * cols, seq), mine)
    prob_spec = pl.BlockSpec((1, 2 * heads, seq, seq), lambda i, s: (i, 0, 0, 0))
    mixed_spec = pl.BlockSpec((1, 2 * cols, seq), mine)
    attn_args = wq + wp + qkv_bias
    qkv, prob, mixed, attn_out, residual, normed_mlp = run_kernel(
        functools.partial(attention_kernel, 2),
        order.sc,
        [tokens, normed, modulation, proj_bias] + attn_args,
        [tok_spec, own_spec, mod_spec, whole_block(proj_bias)] + [whole_block(a) for a in attn_args],
        [qkv_spec, prob_spec, mixed_spec, own_spec, own_spec, own_spec],
        [
            shape_of((images, 6 * cols, seq), bf16),
            shape_of((images, 2 * heads, seq, seq), bf16),
            shape_of((images, 2 * cols, seq), bf16),
            shape_of((images, seq, dim), f32),
            shape_of((images, seq, dim), f32),
            shape_of((images, seq, dim), bf16),
        ],
        (images,),
        2 * count * dim * 8 * cols + 8 * count * seq * dim,
    )

    rows_flat = normed_mlp.reshape(count, dim)
    grad_flat = grad_mlp.reshape(count, dim)
    width = ff // CHUNKS
    per = width // 16
    steps = 2
    block = width // steps
    anywhere = pl.BlockSpec(memory_space=pl.ANY)
    act = back = None
    up_sums = [[None] * CHUNKS, [None] * CHUNKS]

    def mlp_part(chunk, part):
        nonlocal act, back
        first = act is None
        if first:
            act = back = jnp.zeros((8, 128), bf16)
        at = chunk * steps
        spread = pl.BlockSpec((1, block, count), lambda s, c: (part, at + s, 0))
        act, back, grads, sums = run_kernel(
            functools.partial(mlp_kernel, per),
            order.sc,
            [rows_flat, grad_flat, wu[part], wd[part], up_bias[part], act, back],
            [
                whole_block(rows_flat),
                whole_block(grad_flat),
                pl.BlockSpec((dim, block), lambda s, c: (0, at + s)),
                pl.BlockSpec((block, dim), lambda s, c: (at + s, 0)),
                pl.BlockSpec((8, block), lambda s, c: (0, at + s)),
                anywhere,
                anywhere,
            ],
            [
                spread,
                spread,
                pl.BlockSpec((16, 2 * per, dim), lambda s, c: (0, 0, 0)),
                pl.BlockSpec((8, block), lambda s, c: (0, s)),
            ],
            [shape_of((2, ff, count), bf16)] * 2
            + [shape_of((16, 2 * per, dim), bf16), shape_of((8, width), f32)],
            (steps,),
            8 * count * dim * width,
            alias=None if first else {6: 0, 7: 1},
        )
        up_sums[part][chunk] = sums[0]
        order.after(sums)
        return grads

    other = mlp_part(0, 1)
    first = Flow(MLP_WAYS, None, other)
    order.tick(first)
    first.set_own(mlp_part(0, 0))
    order.tick(first)
    second = Flow(MLP_WAYS, None, mlp_part(1, 1))
    order.tick(second)
    second.set_own(mlp_part(1, 0))
    order.tick(first, second)
    third = Flow(MLP_WAYS, None, mlp_part(2, 1))
    order.tick(first, third)
    third.set_own(mlp_part(2, 0))
    order.tick(first, second, third)

    reach = 768
    per_part = ff // reach
    every = lambda s, c: (0, 0, 0)
    own_whole = pl.BlockSpec((images, seq, dim), every, pipeline_mode=once)
    grad_residual, grad_attn, mid_sums = run_kernel(
        functools.partial(norm_back_kernel, images, images),
        order.sc,
        [back] + wu + [residual, cotangent, modulation, attn_out],
        [
            pl.BlockSpec((1, reach, count), lambda s, c: (s // per_part, s % per_part, 0)),
            pl.BlockSpec((dim, reach), lambda s, c: (0, jnp.minimum(s, per_part - 1))),
            pl.BlockSpec((dim, reach), lambda s, c: (0, jnp.maximum(s - per_part, 0))),
            own_whole,
            all_tok_spec,
            all_mod_spec,
            own_whole,
        ],
        [own_whole, own_whole, pl.BlockSpec((images, 4, dim), every)],
        [
            shape_of((images, seq, dim), f32),
            shape_of((images, seq, dim), bf16),
            shape_of((images, 4, dim), f32),
        ],
        (2 * per_part,),
        2 * count * dim * 2 * ff,
        scratch=[pltpu.VMEM((count, dim), f32)],
    )
    order.after(mid_sums)
    order.tick(first, second, third)
    pieces = 2
    each = images // pieces
    grad_qkv = []
    for piece in range(pieces):
        there = lambda i, s, piece=piece: (piece * each + i, 0, 0)
        (grad_piece,) = run_kernel(
            functools.partial(back_kernel, 2),
            order.sc,
            [grad_attn, qkv, prob] + wp,
            [
                pl.BlockSpec((1, seq, dim), there),
                pl.BlockSpec((1, 6 * cols, seq), there),
                pl.BlockSpec((1, 2 * heads, seq, seq), lambda i, s, piece=piece: (piece * each + i, 0, 0, 0)),
            ]
            + [whole_block(a) for a in wp],
            [qkv_spec],
            [shape_of((each, 6 * cols, seq), bf16)],
            (each,),
            (2 * count * dim * 2 * cols + 10 * count * seq * dim) // pieces,
            scratch=[pltpu.VMEM((2 * cols, seq), bf16)],
        )
        grad_qkv.append(grad_piece)
        order.after(grad_piece)
        order.tick(first, second, third)

    attn_per = 4 * cols // 16
    qv_sums = [None, None]

    def attn_part(part):
        grads, sums = run_kernel(
            functools.partial(attn_grad_kernel, pieces, attn_per),
            order.sc,
            grad_qkv + [mixed, normed, grad_attn],
            [
                pl.BlockSpec((each, cols, seq), lambda s, c: (0, 3 * part + jnp.minimum(s, 2), 0))
                for _ in range(pieces)
            ]
            + [pl.BlockSpec((images, cols, seq), lambda s, c: (0, part, 0))]
            + [whole_block(normed), whole_block(grad_attn)],
            [
                pl.BlockSpec((16, attn_per, dim), every),
                pl.BlockSpec((1, 8, cols), lambda s, c: (jnp.minimum(s, 2), 0, 0)),
            ],
            [shape_of((16, attn_per, dim), bf16), shape_of((3, 8, cols), f32)],
            (4,),
            2 * count * dim * 4 * cols,
        )
        qv_sums[part] = sums[:, 0]
        order.after(sums)
        return grads

    last = Flow(ATTN_WAYS, None, attn_part(1))
    order.tick(last, first, second, third)
    last.set_own(attn_part(0))
    order.tick(last, first, second, third)

    per_part = 3
    rows = cols
    grad_tokens, low_sums = run_kernel(
        functools.partial(first_back_kernel, pieces, images),
        order.sc,
        grad_qkv + wq + [tokens, modulation, grad_residual],
        [pl.BlockSpec((each, rows, seq), lambda s, c: (0, s, 0)) for _ in range(pieces)]
        + [
            pl.BlockSpec((rows, dim), lambda s, c: (jnp.minimum(s, 2), 0)),
            pl.BlockSpec((rows, dim), lambda s, c: (jnp.maximum(s - 3, 0), 0)),
            all_tok_spec,
            all_mod_spec,
            own_whole,
        ],
        [own_whole, pl.BlockSpec((images, 2, dim), every)],
        [shape_of((images, seq, dim), f32), shape_of((images, 2, dim), f32)],
        (6,),
        2 * count * dim * 6 * cols,
    )
    order.after(low_sums)
    order.tick(last, first, second, third)
    per_part = ff // reach
    output, gate_sums = run_kernel(
        functools.partial(output_kernel, images, images),
        order.sc,
        [act] + wd + [residual, cotangent, modulation, down_bias],
        [
            pl.BlockSpec((1, reach, count), lambda s, c: (s // per_part, s % per_part, 0)),
            pl.BlockSpec((reach, dim), lambda s, c: (jnp.minimum(s, per_part - 1), 0)),
            pl.BlockSpec((reach, dim), lambda s, c: (jnp.maximum(s - per_part, 0), 0)),
            own_whole,
            all_tok_spec,
            all_mod_spec,
            whole_block(down_bias),
        ],
        [own_whole, pl.BlockSpec((images, 1, dim), every)],
        [shape_of((images, seq, dim), bf16), shape_of((images, 1, dim), f32)],
        (2 * per_part,),
        2 * count * dim * 2 * ff,
        scratch=[pltpu.VMEM((count, dim), f32)],
    )
    order.after(gate_sums)
    order.tick(last, first, second, third)
    output = lax.all_gather(output, "mp", axis=0, tiled=True)
    grad_tokens = lax.all_gather(grad_tokens, "mp", axis=0, tiled=True)

    grad_modulation = jnp.concatenate([low_sums, mid_sums[:, 2:3], mid_sums[:, 0:2], gate_sums], axis=1)
    grad_modulation = grad_modulation.reshape(images, 6 * dim).astype(bf16)
    bias_sums = [
        jnp.concatenate([qv_sums[part][0], qv_sums[part][2]] + up_sums[part]) for part in range(2)
    ]
    shared = jnp.concatenate([jnp.sum(mid_sums[:, 3], axis=0), jnp.sum(down_sums[:, 0], axis=0)])
    shared = jnp.pad(shared, (0, own_cols - 2 * dim))
    packed = jnp.concatenate(
        [grad_modulation.astype(f32).reshape(2 * images, own_cols), jnp.stack(bias_sums + [shared])]
    )
    both = lax.all_gather(packed, "mp", axis=0, tiled=False)
    group_mod = both[:, : 2 * images].reshape(2, images, 2, own_cols)
    group_mod = lax.dynamic_index_in_dim(group_mod, core, 2, keepdims=False).reshape(slots, own_cols)
    group_mod = group_mod.astype(bf16)
    own_bias_sum = lax.dynamic_index_in_dim(both[:, 2 * images], core, 0) + lax.dynamic_index_in_dim(
        both[:, 2 * images + 1], 1 - core, 0
    )
    shared_sum = both[0, -1:] + both[1, -1:]
    part_scaled = outer_cols(group_mod, w_mod).astype(bf16)
    grad_scaled = part_scaled.astype(f32) + swap_cores(part_scaled).astype(f32)
    _, silu_back = jax.vjp(jax.nn.silu, cond_f)
    grad_condition = silu_back(grad_scaled)[0]
    wide_scaled = jnp.pad(scaled.reshape(-1), (0, 3 * own_cols - slots * dim)).reshape(3, own_cols)
    packed_rows = jnp.concatenate(
        [group_mod, own_bias_sum.astype(bf16), shared_sum.astype(bf16), wide_scaled]
    )
    all_rows = lax.all_gather(packed_rows, "dp", axis=0, tiled=False)
    all_mod = all_rows[:, :slots].reshape(-1, own_cols)
    all_scaled = all_rows[:, slots + 2 :].reshape(16, -1)[:, : slots * dim].reshape(-1, dim)
    grad_w_mod = inner_rows(all_scaled, all_mod)
    grad_b_mod = jnp.sum(all_mod.astype(f32), axis=0)
    bias_total = jnp.sum(all_rows[:, slots : slots + 2].astype(f32), axis=0)
    grad_b_qv = bias_total[0, : 2 * cols].reshape(2, cols)
    grad_b_up = bias_total[0, 2 * cols :]
    grad_b_proj = bias_total[1, :dim]
    grad_b_down = bias_total[1, dim : 2 * dim]

    while first.halves is None or second.halves is None or third.halves is None:
        order.tick(last, *[flow for flow in (first, second, third) if flow.halves is None])

    def cuts(ways):
        return tuple((way[0], lo, hi) for lo, hi, way in ways)

    grad_w_down = grad_w_up = jnp.zeros((8, 128), f32)
    for chunk, flow in enumerate((first, second, third)):
        args = flow.halves
        spot = len(args) + 1
        grad_w_down, grad_w_up = run_kernel(
            functools.partial(final_mlp_kernel, cuts(MLP_WAYS), per),
            order.sc,
            list(args) + [grad_w_down, grad_w_up],
            [whole_block(a) for a in args] + [anywhere, anywhere],
            [
                pl.BlockSpec((block, dim), lambda s, c, chunk=chunk: (chunk * steps + s, 0)),
                pl.BlockSpec((dim, block), lambda s, c, chunk=chunk: (0, chunk * steps + s)),
            ],
            [shape_of((ff, dim), f32), shape_of((dim, ff), f32)],
            (steps,),
            width * dim,
            scratch=[pltpu.VMEM((block, dim), f32)],
            alias=None if chunk == 0 else {spot: 0, spot + 1: 1},
        )
        if last.halves is None:
            order.after(grad_w_down[0, :1])
            order.tick(last)
    while last.halves is None:
        order.tick(last)
    args = last.halves
    grad_qkv_rows, grad_w_proj = run_kernel(
        functools.partial(final_attn_kernel, cuts(ATTN_WAYS), attn_per),
        order.sc,
        list(args),
        [whole_block(a) for a in args],
        [
            pl.BlockSpec((cols, dim), lambda s, c: (jnp.minimum(s, 2), 0)),
            pl.BlockSpec((cols, dim), lambda s, c: (0, 0)),
        ],
        [shape_of((3 * cols, dim), f32), shape_of((cols, dim), f32)],
        (4,),
        cols * dim,
    )
    grad_w_qkv = jnp.transpose(grad_qkv_rows.reshape(3, cols, dim), (2, 0, 1))
    return (
        output,
        grad_tokens,
        grad_condition,
        grad_w_qkv,
        grad_b_qv,
        grad_w_proj,
        grad_b_proj,
        grad_w_up,
        grad_b_up,
        grad_w_down,
        grad_b_down,
        grad_w_mod,
        grad_b_mod,
    )


def layer_norm(values):
    center = values - jnp.mean(values, axis=-1, keepdims=True)
    return center * lax.rsqrt(jnp.mean(center * center, axis=-1, keepdims=True) + epsilon)


def modulate(values, shift_part, scale_part):
    return layer_norm(values) * (1.0 + scale_part) + shift_part


def gelu_tanh(values):
    return (
        0.5
        * values
        * (1.0 + jnp.tanh(0.7978845608028654 * (values + 0.044715 * values * values * values)))
    )


def inner_rows(left, right):
    return lax.dot_general(
        left, right, (((0,), (0,)), ((), ())), preferred_element_type=jnp.float32
    )


def outer_cols(left, right):
    return lax.dot_general(
        left, right, (((1,), (1,)), ((), ())), preferred_element_type=jnp.float32
    )


def attention_forward(query_rows, key_rows, value_rows):
    factor = HEAD_DIM ** (-0.5)
    scores = (
        jnp.einsum("bqhd,bkhd->bhqk", query_rows, key_rows, preferred_element_type=jnp.float32)
        * factor
    )
    row_max = jnp.max(scores, axis=-1, keepdims=True)
    row_total = jnp.sum(jnp.exp(scores - row_max), axis=-1, keepdims=True)
    logsum = row_max + jnp.log(row_total)
    prob_b = jnp.exp(scores - logsum).astype(jnp.bfloat16)
    mixed_out = jnp.einsum(
        "bhqk,bkhd->bqhd", prob_b, value_rows, preferred_element_type=jnp.float32
    )
    return (mixed_out, logsum)


def attention_backward(query_rows, key_rows, value_rows, logsum, grad_mixed):
    factor = HEAD_DIM ** (-0.5)
    scores = (
        jnp.einsum("bqhd,bkhd->bhqk", query_rows, key_rows, preferred_element_type=jnp.float32)
        * factor
    )
    prob_f = jnp.exp(scores - logsum)
    prob_b = prob_f.astype(jnp.bfloat16)
    grad_prob = jnp.einsum(
        "bqhd,bkhd->bhqk", grad_mixed, value_rows, preferred_element_type=jnp.float32
    )
    row_delta = jnp.sum(prob_f * grad_prob, axis=-1, keepdims=True)
    grad_scores = (prob_f * (grad_prob - row_delta)).astype(jnp.bfloat16)
    grad_query = (
        jnp.einsum("bhqk,bkhd->bqhd", grad_scores, key_rows, preferred_element_type=jnp.float32)
        * factor
    )
    grad_key = (
        jnp.einsum("bhqk,bqhd->bkhd", grad_scores, query_rows, preferred_element_type=jnp.float32)
        * factor
    )
    grad_value = jnp.einsum(
        "bhqk,bqhd->bkhd", prob_b, grad_mixed, preferred_element_type=jnp.float32
    )
    return (
        grad_query.astype(jnp.bfloat16),
        grad_key.astype(jnp.bfloat16),
        grad_value.astype(jnp.bfloat16),
    )


def forward(tokens_f, spans, weights, repeat):
    w_qkv, b_qv, w_proj, b_proj, w_up, b_up, w_down, b_down = weights
    shift_attn, scale_attn, gate_attn, shift_mlp, scale_mlp, gate_mlp = spans
    slot_count, seq_len, model_dim = tokens_f.shape
    row_count = slot_count * seq_len
    head_cols = w_qkv.shape[2]
    head_count = head_cols // HEAD_DIM
    shape_four = (slot_count, seq_len, head_count, HEAD_DIM)
    normed = (
        modulate(tokens_f, shift_attn, scale_attn)
        .astype(jnp.bfloat16)
        .reshape(row_count, model_dim)
    )
    projected = jnp.dot(
        normed, w_qkv.reshape(model_dim, 3 * head_cols), preferred_element_type=jnp.float32
    )
    qkv_bias = jnp.stack([b_qv[0], jnp.zeros_like(b_qv[0]), b_qv[1]]).astype(jnp.float32)
    projected = (projected.reshape(row_count, 3, head_cols) + qkv_bias).astype(jnp.bfloat16)
    query_rows = projected[:, 0].reshape(shape_four)
    key_rows = projected[:, 1].reshape(shape_four)
    value_rows = projected[:, 2].reshape(shape_four)
    mixed_out, logsum = attention_forward(query_rows, key_rows, value_rows)
    mixed_b = mixed_out.astype(jnp.bfloat16).reshape(row_count, head_cols)
    partial_value = jnp.dot(mixed_b, w_proj, preferred_element_type=jnp.float32)
    if repeat:
        summed = lax.psum(partial_value.astype(jnp.bfloat16), "mp").astype(jnp.float32)
    else:
        summed = lax.psum(partial_value.astype(jnp.bfloat16), "mp").astype(jnp.float32)
    attn_out = (summed + b_proj.astype(jnp.float32)).reshape(slot_count, seq_len, model_dim)
    residual = tokens_f + gate_attn * attn_out
    normed_mlp = (
        modulate(residual, shift_mlp, scale_mlp).astype(jnp.bfloat16).reshape(row_count, model_dim)
    )
    hidden = jnp.dot(normed_mlp, w_up, preferred_element_type=jnp.float32) + b_up.astype(
        jnp.float32
    )
    act_bf = gelu_tanh(hidden).astype(jnp.bfloat16)
    partial_mlp = jnp.dot(act_bf, w_down, preferred_element_type=jnp.float32)
    if repeat:
        summed_mlp = lax.psum(partial_mlp.astype(jnp.bfloat16), "mp").astype(jnp.float32)
    else:
        summed_mlp = lax.psum(partial_mlp.astype(jnp.bfloat16), "mp").astype(jnp.float32)
    mlp_out = (summed_mlp + b_down.astype(jnp.float32)).reshape(slot_count, seq_len, model_dim)
    output = residual + gate_mlp * mlp_out
    return {
        "normed": normed,
        "query_rows": query_rows,
        "key_rows": key_rows,
        "value_rows": value_rows,
        "logsum": logsum,
        "mixed_b": mixed_b,
        "attn_out": attn_out,
        "residual": residual,
        "normed_mlp": normed_mlp,
        "hidden": hidden,
        "act_bf": act_bf,
        "mlp_out": mlp_out,
        "output": output,
    }


def image_pass(tokens_f, grad_out, spans, weights):
    w_qkv, b_qv, w_proj, b_proj, w_up, b_up, w_down, b_down = weights
    shift_attn, scale_attn, gate_attn, shift_mlp, scale_mlp, gate_mlp = spans
    slot_count, seq_len, model_dim = tokens_f.shape
    row_count = slot_count * seq_len
    head_cols = w_qkv.shape[2]
    head_count = head_cols // HEAD_DIM
    kept_fwd = forward(tokens_f, spans, weights, False)
    out_one = kept_fwd["output"]
    stored = forward(tokens_f, spans, weights, True)
    grad_gate_mlp = jnp.sum(grad_out * stored["mlp_out"], axis=1)
    grad_mlp = (gate_mlp * grad_out).astype(jnp.bfloat16).reshape(row_count, model_dim)
    grad_b_down = jnp.sum(grad_mlp.astype(jnp.float32), axis=0)
    grad_w_down = inner_rows(stored["act_bf"], grad_mlp)
    grad_act = outer_cols(grad_mlp, w_down)
    gelu_value, gelu_back = jax.vjp(gelu_tanh, stored["hidden"])
    grad_hidden = gelu_back(grad_act)[0].astype(jnp.bfloat16)
    grad_b_up = jnp.sum(grad_hidden.astype(jnp.float32), axis=0)
    grad_w_up = inner_rows(stored["normed_mlp"], grad_hidden)
    part_normed_mlp = outer_cols(grad_hidden, w_up)
    grad_normed_mlp = (
        lax.psum(part_normed_mlp.astype(jnp.bfloat16), "mp")
        .astype(jnp.float32)
        .reshape(slot_count, seq_len, model_dim)
    )
    norm_value, norm_back = jax.vjp(modulate, stored["residual"], shift_mlp, scale_mlp)
    grad_resid_norm, grad_shift_mlp, grad_scale_mlp = norm_back(grad_normed_mlp)
    grad_residual = grad_out + grad_resid_norm
    grad_gate_attn = jnp.sum(grad_residual * stored["attn_out"], axis=1)
    grad_attn = (gate_attn * grad_residual).astype(jnp.bfloat16).reshape(row_count, model_dim)
    grad_b_proj = jnp.sum(grad_attn.astype(jnp.float32), axis=0)
    grad_w_proj = inner_rows(stored["mixed_b"], grad_attn)
    grad_mixed = (
        outer_cols(grad_attn, w_proj)
        .astype(jnp.bfloat16)
        .reshape(slot_count, seq_len, head_count, HEAD_DIM)
    )
    grad_query, grad_key, grad_value = attention_backward(
        stored["query_rows"], stored["key_rows"], stored["value_rows"], stored["logsum"], grad_mixed
    )
    grad_qkv = jnp.stack(
        [
            grad_query.reshape(row_count, head_cols),
            grad_key.reshape(row_count, head_cols),
            grad_value.reshape(row_count, head_cols),
        ],
        axis=1,
    )
    grad_b_qv = jnp.stack(
        [
            jnp.sum(grad_qkv[:, 0].astype(jnp.float32), axis=0),
            jnp.sum(grad_qkv[:, 2].astype(jnp.float32), axis=0),
        ]
    )
    grad_w_qkv = inner_rows(stored["normed"], grad_qkv)
    part_normed = outer_cols(
        grad_qkv.reshape(row_count, 3 * head_cols), w_qkv.reshape(model_dim, 3 * head_cols)
    )
    grad_normed = (
        lax.psum(part_normed.astype(jnp.bfloat16), "mp")
        .astype(jnp.float32)
        .reshape(slot_count, seq_len, model_dim)
    )
    first_value, first_back = jax.vjp(modulate, tokens_f, shift_attn, scale_attn)
    grad_tok_norm, grad_shift_attn, grad_scale_attn = first_back(grad_normed)
    grad_tok_one = grad_residual + grad_tok_norm
    grad_mod_one = jnp.concatenate(
        [
            grad_shift_attn[:, 0],
            grad_scale_attn[:, 0],
            grad_gate_attn,
            grad_shift_mlp[:, 0],
            grad_scale_mlp[:, 0],
            grad_gate_mlp,
        ],
        axis=1,
    )
    grad_terms = (
        grad_w_qkv,
        grad_b_qv,
        grad_w_proj,
        grad_b_proj,
        grad_w_up,
        grad_b_up,
        grad_w_down,
        grad_b_down,
    )
    return (out_one, grad_tok_one, grad_mod_one, grad_terms)


def run_layer(tokens, condition, cotangent, live_count, turns, weights, w_mod, b_mod):
    slot_count, seq_len, model_dim = tokens.shape
    cond_f = condition.astype(jnp.float32)
    scaled = jax.nn.silu(cond_f).astype(jnp.bfloat16)
    own_mod = jnp.dot(scaled, w_mod, preferred_element_type=jnp.float32) + b_mod.astype(jnp.float32)
    modulation = lax.all_gather(own_mod, "mp", axis=1, tiled=True)
    tokens_f = tokens.astype(jnp.float32)
    cot_f = cotangent.astype(jnp.float32)

    def image_step(slot_idx, carry):
        out_buf, grad_buf, mod_buf, grad_sums = carry
        live_flag = (slot_idx < live_count).astype(jnp.float32)
        tok_one = lax.dynamic_slice_in_dim(tokens_f, slot_idx, 1, 0)
        cot_one = lax.dynamic_slice_in_dim(cot_f, slot_idx, 1, 0) * live_flag
        mod_row = lax.dynamic_slice_in_dim(modulation, slot_idx, 1, 0)
        spans = [
            mod_row[:, None, part_idx * model_dim : (part_idx + 1) * model_dim]
            for part_idx in range(6)
        ]
        out_one, grad_tok_one, grad_mod_one, grad_terms = image_pass(
            tok_one, cot_one, spans, weights
        )
        out_one = (out_one * live_flag).astype(jnp.bfloat16)
        out_buf = lax.dynamic_update_slice_in_dim(out_buf, out_one, slot_idx, 0)
        grad_buf = lax.dynamic_update_slice_in_dim(grad_buf, grad_tok_one, slot_idx, 0)
        mod_buf = lax.dynamic_update_slice_in_dim(mod_buf, grad_mod_one, slot_idx, 0)
        grad_sums = tuple((total_a + term_b for total_a, term_b in zip(grad_sums, grad_terms)))
        return (out_buf, grad_buf, mod_buf, grad_sums)

    start_sums = tuple((jnp.zeros(weight_in.shape, jnp.float32) for weight_in in weights))
    start_state = (
        jnp.zeros(tokens.shape, jnp.bfloat16),
        jnp.zeros(tokens.shape, jnp.float32),
        jnp.zeros((slot_count, 6 * model_dim), jnp.float32),
        start_sums,
    )
    out_buf, grad_buf, mod_buf, grad_sums = lax.fori_loop(0, turns, image_step, start_state)
    grad_modulation = mod_buf.astype(jnp.bfloat16)
    own_cols = w_mod.shape[1]
    grad_own = lax.dynamic_slice_in_dim(
        grad_modulation, lax.axis_index("mp") * own_cols, own_cols, 1
    )
    part_scaled = outer_cols(grad_own, w_mod)
    grad_scaled = lax.psum(part_scaled.astype(jnp.bfloat16), "mp").astype(jnp.float32)
    silu_value, silu_back = jax.vjp(jax.nn.silu, cond_f)
    grad_condition = silu_back(grad_scaled)[0]
    return (out_buf, grad_buf, grad_condition, grad_sums, scaled, grad_own)


def on_device(
    tokens,
    condition,
    counts,
    w_qkv,
    b_qv,
    w_proj,
    b_proj,
    w_up,
    b_up,
    w_down,
    b_down,
    w_mod,
    b_mod,
    cotangent,
):
    slot_count, seq_len, model_dim = tokens.shape
    weights = (w_qkv, b_qv, w_proj, b_proj, w_up, b_up, w_down, b_down)
    own_count = counts[0]
    output, grad_tokens, grad_condition, grad_sums, scaled, grad_own = run_layer(
        tokens, condition, cotangent, own_count, slot_count, weights, w_mod, b_mod
    )
    (
        grad_w_qkv,
        grad_b_qv,
        grad_w_proj,
        grad_b_proj,
        grad_w_up,
        grad_b_up,
        grad_w_down,
        grad_b_down,
    ) = grad_sums
    grad_w_mod = inner_rows(scaled, grad_own)
    grad_b_mod = jnp.sum(grad_own.astype(jnp.float32), axis=0)
    (
        grad_w_qkv,
        grad_b_qv,
        grad_w_proj,
        grad_b_proj,
        grad_w_up,
        grad_b_up,
        grad_w_down,
        grad_b_down,
        grad_w_mod,
        grad_b_mod,
    ) = (
        lax.psum(grad_w_qkv.astype(jnp.bfloat16), "dp").astype(jnp.float32),
        lax.psum(grad_b_qv.astype(jnp.bfloat16), "dp").astype(jnp.float32),
        lax.psum(grad_w_proj.astype(jnp.bfloat16), "dp").astype(jnp.float32),
        lax.psum(grad_b_proj.astype(jnp.bfloat16), "dp").astype(jnp.float32),
        lax.psum(grad_w_up.astype(jnp.bfloat16), "dp").astype(jnp.float32),
        lax.psum(grad_b_up.astype(jnp.bfloat16), "dp").astype(jnp.float32),
        lax.psum(grad_w_down.astype(jnp.bfloat16), "dp").astype(jnp.float32),
        lax.psum(grad_b_down.astype(jnp.bfloat16), "dp").astype(jnp.float32),
        lax.psum(grad_w_mod.astype(jnp.bfloat16), "dp").astype(jnp.float32),
        lax.psum(grad_b_mod.astype(jnp.bfloat16), "dp").astype(jnp.float32),
    )
    return (
        output,
        grad_tokens,
        grad_condition,
        grad_w_qkv,
        grad_b_qv,
        grad_w_proj,
        grad_b_proj,
        grad_w_up,
        grad_b_up,
        grad_w_down,
        grad_b_down,
        grad_w_mod,
        grad_b_mod,
    )


def solution(mesh):
    placed = (
        P("dp", None, None),
        P("dp", None),
        P("dp"),
        P(None, None, "mp"),
        P(None, "mp"),
        P("mp", None),
        P(),
        P(None, "mp"),
        P("mp"),
        P("mp", None),
        P(),
        P(None, "mp"),
        P("mp"),
        P("dp", None, None),
    )
    fast = mesh.shape["dp"] == 16 and mesh.shape["mp"] == 2
    return jax.shard_map(
        fast_device if fast else on_device,
        mesh=mesh,
        in_specs=placed,
        out_specs=(
            P("dp", None, None),
            P("dp", None, None),
            P("dp", None),
            P(None, None, "mp"),
            P(None, "mp"),
            P("mp", None),
            P(),
            P(None, "mp"),
            P("mp"),
            P("mp", None),
            P(),
            P(None, "mp"),
            P("mp"),
        ),
        check_vma=False,
    )
```

```python
import functools

import jax
import jax.numpy as jnp
from jax import lax
from jax.experimental import pallas as pl
from jax.experimental.pallas import tpu as pltpu
from jax.sharding import PartitionSpec as P

HEAD_DIM = 72


epsilon = 1e-06

f32 = jnp.float32
bf16 = jnp.bfloat16


def dot_nn(left, right):
    return lax.dot_general(left, right, (((1,), (0,)), ((), ())), preferred_element_type=f32)


def dot_nt(left, right):
    return lax.dot_general(left, right, (((1,), (1,)), ((), ())), preferred_element_type=f32)


def dot_tn(left, right):
    return lax.dot_general(left, right, (((0,), (0,)), ((), ())), preferred_element_type=f32)


def normalize(values):
    center = values - jnp.mean(values, axis=-1, keepdims=True)
    recip = lax.rsqrt(jnp.mean(center * center, axis=-1, keepdims=True) + epsilon)
    return center * recip, recip


def norm_pullback(grad_normed, unit, recip, scale_row):
    scaled_grad = grad_normed * (1.0 + scale_row)
    mean_grad = jnp.mean(scaled_grad, axis=-1, keepdims=True)
    mean_unit = jnp.mean(scaled_grad * unit, axis=-1, keepdims=True)
    return recip * (scaled_grad - mean_grad - unit * mean_unit)


def column(row):
    return jnp.broadcast_to(row[...].astype(f32), (8, row.shape[1])).T[:, 0:1]


def token_sum(values):
    return jnp.sum(values, axis=0, keepdims=True)


def attention_kernel(parts, own_images, sc, tok, cot, mod, b_proj, *refs):
    w_qkv, w_proj, bias = refs[:parts], refs[parts : 2 * parts], refs[2 * parts : 3 * parts]
    qkv, prob, mixed, attn_out, residual, normed_mlp, normed, grad_mlp, down_sums = refs[3 * parts :]
    image = sc[0] * own_images + pl.program_id(0)
    live = jnp.where(image < sc[1], 1.0, 0.0).astype(f32)
    unit, _ = normalize(tok[0].astype(f32))
    normed[0] = (unit * (1.0 + mod[0, 1:2, :]) + mod[0, 0:1, :]).astype(bf16)
    grad = (mod[0, 5:6, :] * (cot[0].astype(f32) * live)).astype(bf16)
    grad_mlp[0] = grad
    down_sums[0] = token_sum(grad.astype(f32))
    cols = w_proj[0].shape[0]
    pairs = cols // (2 * HEAD_DIM)
    span = 2 * HEAD_DIM
    factor = HEAD_DIM ** (-0.5)
    rows = normed[0]
    total = b_proj[...]
    for part in range(parts):
        base = part * 3 * cols
        shift = bias[part][...].astype(f32).T
        for proj in range(3):
            lo = proj * cols
            value = dot_nt(w_qkv[part][lo : lo + cols, :], rows)
            if proj != 1:
                value = value + shift[:, proj // 2 : proj // 2 + 1]
            qkv[0, base + lo : base + lo + cols, :] = value.astype(bf16)

        def pair_step(pair, carry, base=base, part=part):
            at = pl.multiple_of(base + pair * span, 16)
            query = qkv[0, pl.ds(at, span), :].astype(f32)
            key = qkv[0, pl.ds(at + cols, span), :].astype(f32)
            value = qkv[0, pl.ds(at + 2 * cols, span), :].astype(f32)
            outs = []
            for one in range(2):
                rows_of = slice(one * HEAD_DIM, (one + 1) * HEAD_DIM)
                scores = dot_tn(key[rows_of].astype(bf16), query[rows_of].astype(bf16)) * factor
                raised = jnp.exp(scores - jnp.max(scores, axis=0, keepdims=True))
                share = 1.0 / jnp.sum(raised, axis=0, keepdims=True)
                prob_b = (raised * share).astype(bf16)
                prob[0, part * 2 * pairs + 2 * pair + one] = prob_b
                outs.append(dot_nn(value[rows_of].astype(bf16), prob_b))
            to = pl.multiple_of(part * cols + pair * span, 16)
            mixed[0, pl.ds(to, span), :] = jnp.concatenate(outs, axis=0).astype(bf16)
            return carry

        lax.fori_loop(0, pairs, pair_step, 0, unroll=True)
        total = total + dot_tn(mixed[0, part * cols : (part + 1) * cols, :], w_proj[part][...])
    attn_out[0] = total
    summed = tok[0].astype(f32) + mod[0, 2:3, :] * total
    residual[0] = summed
    unit, _ = normalize(summed)
    normed_mlp[0] = (unit * (1.0 + mod[0, 4:5, :]) + mod[0, 3:4, :]).astype(bf16)


def mlp_kernel(
    per, steps, sc, rows, grad_mlp, w_up0, w_up1, w_down0, w_down1, bias0, bias1, act_in, back_in,
    act, back, grad_own, grad_other, sums
):
    part, step = pl.program_id(0), pl.program_id(1)

    @pl.when(part == 0)
    def _():
        mlp_block(per, step, sc, rows, grad_mlp, w_up0, w_down0, bias0, act, back, grad_own, sums)

    @pl.when(part == 1)
    def _():
        mlp_block(per, step, sc, rows, grad_mlp, w_up1, w_down1, bias1, act, back, grad_other, sums)


def mlp_block(per, step, sc, rows, grad_mlp, w_up, w_down, bias, act, back, grads, sums):
    here = w_down.shape[0] // per
    hidden = lax.dot_general(
        w_up[...], rows[...], (((0,), (1,)), ((), ())), preferred_element_type=f32
    ) + column(bias)
    square = hidden * hidden
    bend = jnp.tanh(0.7978845608028654 * hidden * (1.0 + 0.044715 * square))
    half = 0.5 * (1.0 + bend)
    act_b = (hidden * half).astype(bf16)
    slope = half + 0.5 * hidden * (1.0 - bend * bend) * (
        0.7978845608028654 * (1.0 + 3.0 * 0.044715 * square)
    )
    back_b = (dot_nt(w_down[...], grad_mlp[...]) * slope).astype(bf16)
    act[0] = act_b
    back[0] = back_b
    sums[0] = dot_nt(jnp.ones((8, rows.shape[0]), bf16), back_b)
    grad_down = dot_nn(act_b, grad_mlp[...]).astype(bf16)
    grad_up = dot_nn(back_b, rows[...]).astype(bf16)
    for piece in range(here):
        at = jnp.bitwise_xor(step * here + piece, sc[2])
        lo = piece * per
        grads[at, 0:per, :] = grad_down[lo : lo + per]
        grads[at, per : 2 * per, :] = grad_up[lo : lo + per]


def grow(total, part_steps, left, rights, dims):
    step = pl.program_id(0)

    def term(right):
        return lax.dot_general(left, right[...], (dims, ((), ())), preferred_element_type=f32)

    @pl.when(step == 0)
    def _():
        total[...] = term(rights[0])

    @pl.when(jnp.logical_and(step > 0, step < part_steps))
    def _():
        total[...] += term(rights[0])

    @pl.when(jnp.logical_and(step >= part_steps, step < 2 * part_steps))
    def _():
        total[...] += term(rights[1])


def norm_back_kernel(
    part_steps, own_images, sc, back, w_up0, w_up1, residual, cot, mod, attn_out,
    grad_residual, grad_attn, sums, total
):
    grow(total, part_steps, back[0], (w_up0, w_up1), ((0,), (1,)))
    one = pl.program_id(0) - 2 * part_steps
    seq = residual.shape[1]

    @pl.when(one >= 0)
    def _():
        live = jnp.where(sc[0] * own_images + one < sc[1], 1.0, 0.0).astype(f32)
        grad_normed = total[pl.ds(pl.multiple_of(one * seq, seq), seq), :]
        unit, recip = normalize(residual[0])
        sums[0, 0:1, :] = token_sum(grad_normed)
        sums[0, 1:2, :] = token_sum(grad_normed * unit)
        grad_res = cot[0].astype(f32) * live + norm_pullback(grad_normed, unit, recip, mod[0, 4:5, :])
        grad_residual[0] = grad_res
        sums[0, 2:3, :] = token_sum(grad_res * attn_out[0])
        grad_att = (mod[0, 2:3, :] * grad_res).astype(bf16)
        grad_attn[0] = grad_att
        sums[0, 3:4, :] = token_sum(grad_att.astype(f32))


def back_kernel(parts, sc, grad_attn, qkv, prob, *refs):
    w_proj = refs[:parts]
    grad_qkv, grad_mixed = refs[parts:]
    cols = w_proj[0].shape[0]
    pairs = cols // (2 * HEAD_DIM)
    span = 2 * HEAD_DIM
    factor = HEAD_DIM ** (-0.5)
    grad_att = grad_attn[0]
    for part in range(parts):
        base = part * 3 * cols
        grad_mixed[part * cols : (part + 1) * cols, :] = dot_nt(w_proj[part][...], grad_att).astype(bf16)

        def pair_step(pair, carry, base=base, part=part):
            at = pl.multiple_of(base + pair * span, 16)
            query = qkv[0, pl.ds(at, span), :].astype(f32)
            key = qkv[0, pl.ds(at + cols, span), :].astype(f32)
            value = qkv[0, pl.ds(at + 2 * cols, span), :].astype(f32)
            grads = grad_mixed[pl.ds(pl.multiple_of(part * cols + pair * span, 16), span), :].astype(f32)
            to_query, to_key, to_value = [], [], []
            for one in range(2):
                rows_of = slice(one * HEAD_DIM, (one + 1) * HEAD_DIM)
                prob_b = prob[0, part * 2 * pairs + 2 * pair + one]
                prob_f = prob_b.astype(f32)
                grad_b = grads[rows_of].astype(bf16)
                grad_prob = dot_tn(value[rows_of].astype(bf16), grad_b)
                delta = jnp.sum(prob_f * grad_prob, axis=0, keepdims=True)
                grad_scores = (prob_f * (grad_prob - delta)).astype(bf16)
                to_query.append(dot_nn(key[rows_of].astype(bf16), grad_scores) * factor)
                to_key.append(dot_nt(query[rows_of].astype(bf16), grad_scores) * factor)
                to_value.append(dot_nt(grad_b, prob_b))
            grad_qkv[0, pl.ds(at, span), :] = jnp.concatenate(to_query, axis=0).astype(bf16)
            grad_qkv[0, pl.ds(at + cols, span), :] = jnp.concatenate(to_key, axis=0).astype(bf16)
            grad_qkv[0, pl.ds(at + 2 * cols, span), :] = jnp.concatenate(to_value, axis=0).astype(bf16)
            return carry

        lax.fori_loop(0, pairs, pair_step, 0, unroll=True)


def attn_grad_kernel(pieces, per, sc, *refs):
    grad_qkv, mixed, normed, grad_attn = refs[:pieces], refs[pieces], refs[pieces + 1], refs[pieces + 2]
    grads, sums = refs[pieces + 3 :]
    step = pl.program_id(0)
    here = mixed.shape[1] // per
    images = mixed.shape[0]
    each = images // pieces

    def spread(total):
        total = total.astype(bf16)
        for piece in range(here):
            at = jnp.bitwise_xor(step * here + piece, sc[2])
            grads[at] = total[piece * per : (piece + 1) * per]

    @pl.when(step < 3)
    def _():
        ones = jnp.ones((8, mixed.shape[2]), bf16)
        total = count = None
        for image in range(images):
            left = grad_qkv[image // each][image % each]
            term, one = dot_nn(left, normed[image]), dot_nt(ones, left)
            total = term if image == 0 else total + term
            count = one if image == 0 else count + one
        sums[0] = count
        spread(total)

    @pl.when(step == 3)
    def _():
        total = dot_nn(mixed[0], grad_attn[0])
        for image in range(1, images):
            total = total + dot_nn(mixed[image], grad_attn[image])
        spread(total)


def first_back_kernel(pieces, images, sc, *refs):
    grad_qkv = refs[:pieces]
    w_qkv0, w_qkv1, tok, mod, grad_residual = refs[pieces : pieces + 5]
    grad_tokens, grad_own, sums, total = refs[pieces + 5 :]
    step = pl.program_id(0)
    each = images // pieces
    seq = tok.shape[1]

    def add(w_qkv, fresh):
        for one in range(images):
            term = dot_tn(grad_qkv[one // each][one % each], w_qkv[...])
            if fresh:
                total[one * seq : (one + 1) * seq, :] = term
            else:
                total[one * seq : (one + 1) * seq, :] += term

    @pl.when(step == 0)
    def _():
        add(w_qkv0, True)

    @pl.when(jnp.logical_and(step > 0, step < 3))
    def _():
        add(w_qkv0, False)

    @pl.when(jnp.logical_and(step >= 3, step < 6))
    def _():
        add(w_qkv1, False)

    @pl.when(step >= 6)
    def _():
        grad_normed = total[pl.ds(pl.multiple_of((step - 6) * seq, seq), seq), :]
        unit, recip = normalize(tok[0].astype(f32))
        sums[0, 0:1, :] = token_sum(grad_normed)
        sums[0, 1:2, :] = token_sum(grad_normed * unit)
        grad = grad_residual[0] + norm_pullback(grad_normed, unit, recip, mod[0, 1:2, :])
        grad_tokens[0] = grad
        grad_own[0] = grad


def output_kernel(
    part_steps, own_images, sc, act, w_down0, w_down1, residual, cot, mod, b_down, output, own, sums, total
):
    grow(total, part_steps, act[0], (w_down0, w_down1), ((0,), (0,)))
    one = pl.program_id(0) - 2 * part_steps
    seq = residual.shape[1]

    @pl.when(one >= 0)
    def _():
        live = jnp.where(sc[0] * own_images + one < sc[1], 1.0, 0.0).astype(f32)
        mlp_out = total[pl.ds(pl.multiple_of(one * seq, seq), seq), :] + b_down[...]
        sums[0] = token_sum((cot[0].astype(f32) * live) * mlp_out)
        rows = ((residual[0] + mod[0, 5:6, :] * mlp_out) * live).astype(bf16)
        output[0] = rows
        own[0] = rows


def final_piece(sc, halves, piece, store):
    rel = jnp.bitwise_xor(piece, sc[2])
    for low, high, bit, lo, hi in halves:
        index = ((rel >> (bit + 1)) << bit) | (rel & ((1 << bit) - 1))
        side = (rel >> bit) & 1

        @pl.when(side == 0)
        def _(low=low, index=index, lo=lo, hi=hi):
            store(low[index].astype(f32), lo, hi)

        @pl.when(side == 1)
        def _(high=high, index=index, lo=lo, hi=hi):
            store(high[index].astype(f32), lo, hi)


def final_mlp_kernel(cuts, per, sc, *refs):
    count = 2 * len(cuts)
    arrays, (_, _, down, up, mark, turned) = refs[:count], refs[count:]
    here = down.shape[0] // per
    halves = [(arrays[2 * k], arrays[2 * k + 1]) + cut for k, cut in enumerate(cuts)]
    for piece in range(here):

        def store(value, lo, hi, piece=piece):
            down[piece * per : (piece + 1) * per, lo:hi] = value[0:per]
            turned[piece * per : (piece + 1) * per, lo:hi] = value[per : 2 * per]

        final_piece(sc, halves, pl.program_id(0) * here + piece, store)
    up[...] = turned[...].T
    mark[...] = jnp.zeros_like(mark)


def final_attn_kernel(cuts, per, sc, *refs):
    count = 2 * len(cuts)
    arrays, (qkv, proj) = refs[:count], refs[count:]
    here = proj.shape[0] // per
    halves = [(arrays[2 * k], arrays[2 * k + 1]) + cut for k, cut in enumerate(cuts)]
    for target, wanted in ((qkv, True), (proj, False)):

        @pl.when((pl.program_id(0) < 3) == wanted)
        def _(target=target):
            for piece in range(here):

                def store(value, lo, hi, piece=piece):
                    target[piece * per : (piece + 1) * per, lo:hi] = value

                final_piece(sc, halves, pl.program_id(0) * here + piece, store)


def run_kernel(
    body, sc, args, in_specs, out_specs, out_shape, grid, micros, scratch=(), alias=None, room=60
):
    size = sum(a.size * a.dtype.itemsize for a in args) + sum(
        s.size * s.dtype.itemsize for s in out_shape
    )
    return pl.pallas_call(
        body,
        out_shape=out_shape,
        grid_spec=pltpu.PrefetchScalarGridSpec(
            num_scalar_prefetch=1,
            grid=grid,
            in_specs=in_specs,
            out_specs=out_specs,
            scratch_shapes=list(scratch),
        ),
        compiler_params=pltpu.CompilerParams(vmem_limit_bytes=room << 20),
        cost_estimate=pl.CostEstimate(
            flops=int(micros * 1.15e9), bytes_accessed=int(size), transcendentals=0
        ),
        input_output_aliases=alias or {},
    )(sc, *args)


def whole_block(array):
    zeros = (0,) * array.ndim
    return pl.BlockSpec(array.shape, lambda *_: zeros, pipeline_mode=pl.Buffered(1))


def shape_of(dims, kind):
    return jax.ShapeDtypeStruct(dims, kind)


SWAP = [(0, 1), (1, 0)]


def swap_cores(value):
    return lax.ppermute(value, "mp", SWAP)


def bit_pairs(bit):
    return [(index, index ^ (1 << bit)) for index in range(16)]


MLP_WAYS = ((0, 640, (0, 1, 2, 3)), (640, 1152, (1, 0, 2, 3)))
ATTN_WAYS = ((0, 512, (0, 1, 2, 3)), (512, 896, (1, 0, 2, 3)), (896, 1152, (2, 3, 0, 1)))


def cut(array, bits, bit, side, cols=None):
    lo = [0] * array.ndim
    hi = list(array.shape)
    place = bits.index(bit)
    lo[place], hi[place] = side, side + 1
    if cols is not None:
        lo[-1], hi[-1] = cols
    out = lax.slice(array, lo, hi)
    return out.reshape(out.shape[:place] + out.shape[place + 1 :])


def left_bits(done):
    return [bit for bit in (3, 2, 1, 0) if bit not in done]


def exchange(values, bits):
    return [lax.ppermute(value, "dp", bit_pairs(bit)) for value, bit in zip(values, bits)]


def reduce_flow(ways, get_own, other):
    shape = (2, 2, 2, 2) + other.shape[1:]
    (other,) = yield [other]
    came = swap_cores(other)
    yield None
    own, came = yield [get_own(), came]
    firsts, seconds = [own.reshape(shape)] * len(ways), [came.reshape(shape)] * len(ways)
    routes = [way for _, _, way in ways]
    for stage in range(4):
        sends, keeps = [], []
        for (lo, hi, _), route, one, two in zip(ways, routes, firsts, seconds):
            bits = left_bits(route[:stage])
            cols = (lo, hi) if stage == 0 else None
            for side, into in ((1, sends), (0, keeps)):
                into.append(
                    cut(one, bits, route[stage], side, cols) + cut(two, bits, route[stage], side, cols)
                )
        if stage == 2 and routes[0][2:] == routes[1][2:]:
            sends = [jnp.concatenate(sends[:2], axis=-1)] + sends[2:]
            keeps = [jnp.concatenate(keeps[:2], axis=-1)] + keeps[2:]
            routes = [routes[0]] + routes[2:]
            ways = [(0, 0, way) for way in routes]
        sends, keeps = yield [sends, keeps]
        comes = exchange(sends, [route[stage] for route in routes])
        yield None
        firsts, seconds = yield [keeps, comes]
    return [one + two for one, two in zip(firsts, seconds)]


def gather_flow(ways, have):
    routes = [ways[0][2]] + [way for _, _, way in ways[2:]]
    middle = ways[0][1]
    known = [[] for _ in routes]
    (have,) = yield [have]
    comes = exchange(have, [route[3] for route in routes])
    yield None
    for stage in (2, 1, 0):
        have, comes = yield [have, comes]
        joined = []
        for route, bits, one, two in zip(routes, known, have, comes):
            bit = route[stage + 1]
            place = sum(1 for other in bits if other > bit)
            joined.append(jnp.stack([one, two], axis=place))
            bits.insert(place, bit)
        if stage == 1:
            joined = [joined[0][..., :middle], joined[0][..., middle:]] + joined[1:]
            routes = [way for _, _, way in ways]
            known = [list(known[0]), list(known[0])] + known[1:]
        (have,) = yield [joined]
        comes = exchange(have, [route[stage] for route in routes])
        yield None
    have, comes = yield [have, comes]
    return [part.reshape((8,) + part.shape[-2:]) for pair in zip(have, comes) for part in pair]


def sum_flow(ways, get_own, other):
    have = yield from reduce_flow(ways, get_own, other)
    return (yield from gather_flow(ways, have))


class Order:
    def __init__(self, sc):
        self.sc = sc
        self.results = {}

    def fence(self, values):
        self.sc, values = lax.optimization_barrier((self.sc, values))
        return values

    def after(self, value):
        self.sc, _ = lax.optimization_barrier((self.sc, value))

    def tick(self, *flows):
        replies = {flow: None for flow in flows if flow not in self.results}
        while replies:
            wants = {}
            for flow, reply in replies.items():
                try:
                    want = flow.send(reply)
                except StopIteration as stop:
                    self.results[flow] = stop.value
                    continue
                if want is not None:
                    wants[flow] = want
            replies = dict(zip(wants, self.fence(list(wants.values())))) if wants else {}

    def finish(self, flow):
        while flow not in self.results:
            self.tick(flow)
        return self.results[flow]


CHUNKS = 3


def fill_other(both, came, core):
    size = came.shape[0]
    return lax.dynamic_update_slice_in_dim(both, came, (1 - core) * size, 0)


def fast_device(
    tokens, condition, counts, w_qkv, b_qv, w_proj, b_proj, w_up, b_up, w_down, b_down, w_mod, b_mod,
    cotangent,
):
    slots, seq, dim = tokens.shape
    images = slots // 2
    count = images * seq
    cols = w_qkv.shape[2]
    ff = w_up.shape[1]
    own_cols = w_mod.shape[1]
    heads = cols // HEAD_DIM
    core = lax.axis_index("mp")
    order = Order(jnp.stack([core, counts[0], lax.axis_index("dp")]).astype(jnp.int32))

    qkv_rows = jnp.transpose(w_qkv, (1, 2, 0)).reshape(3 * cols, dim)
    wq = [qkv_rows, swap_cores(qkv_rows)]
    wp = [w_proj, swap_cores(w_proj)]
    qkv_bias = [b_qv, swap_cores(b_qv)]

    cond_f = condition.astype(f32)
    scaled = jax.nn.silu(cond_f).astype(bf16)
    own_mod = jnp.dot(scaled, w_mod, preferred_element_type=f32) + b_mod.astype(f32)
    other_mod = swap_cores(own_mod)
    sides = [jnp.where(core == side, own_mod, other_mod) for side in range(2)]
    modulation = jnp.concatenate(sides, axis=1).reshape(slots, 6, dim)
    proj_bias = b_proj.astype(f32)[None]
    down_bias = b_down.astype(f32)[None]

    late_up, late_down, late_bias = lax.optimization_barrier((wq[1], w_up, w_down, b_up, modulation))[1:4]
    wu = [w_up, swap_cores(late_up)]
    wd = [w_down, swap_cores(late_down)]
    up_bias = [b_up[None], swap_cores(late_bias[None])]

    local = lambda i, s: (s[0] * images + i, 0, 0)
    mine = lambda i, s: (i, 0, 0)
    tok_spec = pl.BlockSpec((1, seq, dim), local)
    own_spec = pl.BlockSpec((1, seq, dim), mine)
    mod_spec = pl.BlockSpec((1, 6, dim), local)
    row_spec = pl.BlockSpec((1, 1, dim), mine)
    qkv_spec = pl.BlockSpec((1, 6 * cols, seq), mine)
    prob_spec = pl.BlockSpec((1, 2 * heads, seq, seq), lambda i, s: (i, 0, 0, 0))
    mixed_spec = pl.BlockSpec((1, 2 * cols, seq), mine)
    token_f = shape_of((images, seq, dim), f32)
    token_b = shape_of((images, seq, dim), bf16)
    attn_args = wq + wp + qkv_bias
    qkv, prob, mixed, attn_out, residual, normed_mlp, normed, grad_mlp, down_sums = run_kernel(
        functools.partial(attention_kernel, 2, images),
        order.sc,
        [tokens, cotangent, modulation, proj_bias] + attn_args,
        [tok_spec, tok_spec, mod_spec, whole_block(proj_bias)] + [whole_block(a) for a in attn_args],
        [qkv_spec, prob_spec, mixed_spec] + [own_spec] * 5 + [row_spec],
        [
            shape_of((images, 6 * cols, seq), bf16),
            shape_of((images, 2 * heads, seq, seq), bf16),
            shape_of((images, 2 * cols, seq), bf16),
            token_f,
            token_f,
            token_b,
            token_b,
            token_b,
            shape_of((images, 1, dim), f32),
        ],
        (images,),
        45,
        room=44,
    )
    order.after(down_sums)

    rows_flat = normed_mlp.reshape(count, dim)
    grad_flat = grad_mlp.reshape(count, dim)
    width = ff // CHUNKS
    per = width // 16
    steps = 2
    block = width // steps
    anywhere = pl.BlockSpec(memory_space=pl.ANY)
    act = back = jnp.zeros((8, 128), bf16)
    flows, up_sums = [], []
    for chunk in range(CHUNKS):
        at = chunk * steps

        def pick(which, at=at):
            rest = (steps - 1) * (1 - which)
            return lambda p, s, c: at + jnp.where(p == which, s, rest)

        def up_map(which):
            return lambda p, s, c: (0, pick(which)(p, s, c))

        def down_map(which):
            return lambda p, s, c: (pick(which)(p, s, c), 0)

        spread = pl.BlockSpec((1, block, count), lambda p, s, c, at=at: (p, at + s, 0))
        act, back, grad_own, grad_other, sums = run_kernel(
            functools.partial(mlp_kernel, per, steps),
            order.sc,
            [rows_flat, grad_flat] + wu + wd + up_bias + [act, back],
            [whole_block(rows_flat), whole_block(grad_flat)]
            + [pl.BlockSpec((dim, block), up_map(which)) for which in range(2)]
            + [pl.BlockSpec((block, dim), down_map(which)) for which in range(2)]
            + [pl.BlockSpec((1, block), up_map(which)) for which in range(2)]
            + [anywhere, anywhere],
            [spread, spread]
            + [pl.BlockSpec((16, 2 * per, dim), lambda p, s, c: (0, 0, 0))] * 2
            + [pl.BlockSpec((1, 8, block), lambda p, s, c: (p, 0, s))],
            [shape_of((2, ff, count), bf16)] * 2
            + [shape_of((16, 2 * per, dim), bf16)] * 2
            + [shape_of((2, 8, width), f32)],
            (2, steps),
            28,
            alias=None if chunk == 0 else {9: 0, 10: 1},
            room=48,
        )
        up_sums.append(sums)
        order.after(sums)
        flows.append(sum_flow(MLP_WAYS, lambda grad_own=grad_own: grad_own, grad_other))
        order.tick(*flows)

    reach = 768
    turns = ff // reach
    every = lambda s, c: (0, 0, 0)
    tail = lambda first: lambda s, c: (jnp.maximum(s - first, 0), 0, 0)
    tail_local = lambda first: lambda s, c: (c[0] * images + jnp.maximum(s - first, 0), 0, 0)

    def image_spec(first, where=tail):
        return pl.BlockSpec((1, seq, dim), where(first))

    def rows_of(part, size):
        if part == 0:
            return lambda s, c: jnp.minimum(s, size - 1)
        return lambda s, c: jnp.clip(s - size, 0, size - 1)

    span_spec = pl.BlockSpec(
        (1, reach, count),
        lambda s, c: (jnp.minimum(s // turns, 1), jnp.where(s < 2 * turns, s % turns, turns - 1), 0),
    )
    grad_residual, grad_attn, mid_sums = run_kernel(
        functools.partial(norm_back_kernel, turns, images),
        order.sc,
        [back] + wu + [residual, cotangent, modulation, attn_out],
        [
            span_spec,
            pl.BlockSpec((dim, reach), lambda s, c: (0, rows_of(0, turns)(s, c))),
            pl.BlockSpec((dim, reach), lambda s, c: (0, rows_of(1, turns)(s, c))),
            image_spec(2 * turns),
            image_spec(2 * turns, tail_local),
            pl.BlockSpec((1, 6, dim), tail_local(2 * turns)),
            image_spec(2 * turns),
        ],
        [image_spec(2 * turns)] * 2 + [pl.BlockSpec((1, 4, dim), tail(2 * turns))],
        [token_f, token_b, shape_of((images, 4, dim), f32)],
        (2 * turns + images,),
        24,
        scratch=[pltpu.VMEM((count, dim), f32)],
        room=44,
    )
    order.after(mid_sums)
    order.tick(*flows)
    pieces = 2
    each = images // pieces
    grad_qkv = []
    for piece in range(pieces):
        there = lambda i, s, piece=piece: (piece * each + i, 0, 0)
        (grad_piece,) = run_kernel(
            functools.partial(back_kernel, 2),
            order.sc,
            [grad_attn, qkv, prob] + wp,
            [
                pl.BlockSpec((1, seq, dim), there),
                pl.BlockSpec((1, 6 * cols, seq), there),
                pl.BlockSpec((1, 2 * heads, seq, seq), lambda i, s, piece=piece: (piece * each + i, 0, 0, 0)),
            ]
            + [whole_block(a) for a in wp],
            [qkv_spec],
            [shape_of((each, 6 * cols, seq), bf16)],
            (each,),
            20,
            scratch=[pltpu.VMEM((2 * cols, seq), bf16)],
            room=40,
        )
        grad_qkv.append(grad_piece)
        order.after(grad_piece)
        order.tick(*flows)

    attn_per = 4 * cols // 16
    qv_sums = [None, None]

    def attn_part(part):
        grads, sums = run_kernel(
            functools.partial(attn_grad_kernel, pieces, attn_per),
            order.sc,
            grad_qkv + [mixed, normed, grad_attn],
            [
                pl.BlockSpec((each, cols, seq), lambda s, c: (0, 3 * part + jnp.minimum(s, 2), 0))
                for _ in range(pieces)
            ]
            + [pl.BlockSpec((images, cols, seq), lambda s, c: (0, part, 0))]
            + [whole_block(normed), whole_block(grad_attn)],
            [
                pl.BlockSpec((16, attn_per, dim), every),
                pl.BlockSpec((1, 8, cols), lambda s, c: (jnp.minimum(s, 2), 0, 0)),
            ],
            [shape_of((16, attn_per, dim), bf16), shape_of((3, 8, cols), f32)],
            (4,),
            14,
            room=40,
        )
        qv_sums[part] = sums
        order.after(sums)
        return grads

    grad_other = attn_part(1)
    made = []
    last = sum_flow(ATTN_WAYS, lambda: made[0], grad_other)
    order.tick(last, *flows)
    made.append(attn_part(0))
    order.tick(last, *flows)

    first_spec = lambda part: pl.BlockSpec((cols, dim), lambda s, c: (rows_of(part, 3)(s, c), 0))
    grad_tokens, grad_own_tokens, low_sums = run_kernel(
        functools.partial(first_back_kernel, pieces, images),
        order.sc,
        grad_qkv + wq + [tokens, modulation, grad_residual],
        [pl.BlockSpec((each, cols, seq), lambda s, c: (0, jnp.minimum(s, 5), 0)) for _ in range(pieces)]
        + [first_spec(0), first_spec(1)]
        + [image_spec(6, tail_local), pl.BlockSpec((1, 6, dim), tail_local(6)), image_spec(6)],
        [image_spec(6, tail_local), image_spec(6), pl.BlockSpec((1, 2, dim), tail(6))],
        [shape_of((slots, seq, dim), f32), token_f, shape_of((images, 2, dim), f32)],
        (6 + images,),
        20,
        scratch=[pltpu.VMEM((count, dim), f32)],
        room=40,
    )
    order.after(low_sums)
    order.tick(last, *flows)
    other_tokens = swap_cores(grad_own_tokens)
    down_spec = lambda part: pl.BlockSpec((reach, dim), lambda s, c: (rows_of(part, turns)(s, c), 0))
    output, own_output, gate_sums = run_kernel(
        functools.partial(output_kernel, turns, images),
        order.sc,
        [act] + wd + [residual, cotangent, modulation, down_bias],
        [
            span_spec,
            down_spec(0),
            down_spec(1),
            image_spec(2 * turns),
            image_spec(2 * turns, tail_local),
            pl.BlockSpec((1, 6, dim), tail_local(2 * turns)),
            whole_block(down_bias),
        ],
        [image_spec(2 * turns, tail_local), image_spec(2 * turns), pl.BlockSpec((1, 1, dim), tail(2 * turns))],
        [shape_of((slots, seq, dim), bf16), token_b, shape_of((images, 1, dim), f32)],
        (2 * turns + images,),
        22,
        scratch=[pltpu.VMEM((count, dim), f32)],
        room=40,
    )
    order.after(gate_sums)
    order.tick(last, *flows)
    other_output = swap_cores(own_output)

    grad_modulation = jnp.concatenate([low_sums, mid_sums[:, 2:3], mid_sums[:, 0:2], gate_sums], axis=1)
    grad_modulation = grad_modulation.reshape(images, 6 * dim).astype(bf16)
    bias_sums = [
        jnp.concatenate(
            [qv_sums[part][0, 0:1], qv_sums[part][2, 0:1]] + [sums[part, 0:1] for sums in up_sums], axis=1
        )
        for part in range(2)
    ]
    shared = jnp.concatenate(
        [
            jnp.sum(mid_sums[:, 3], axis=0, keepdims=True),
            jnp.sum(down_sums[:, 0], axis=0, keepdims=True),
            jnp.zeros((1, own_cols - 2 * dim), f32),
        ],
        axis=1,
    )
    halves = grad_modulation.reshape(images, 2, own_cols)
    kept = lax.dynamic_index_in_dim(halves, core, 1, keepdims=False)
    given = lax.dynamic_index_in_dim(halves, 1 - core, 1, keepdims=False)
    got = swap_cores(jnp.concatenate([given.astype(f32), bias_sums[1], shared]))
    came = got[:images].astype(bf16)
    group_mod = jnp.where(
        core == 0, jnp.concatenate([kept, came]), jnp.concatenate([came, kept])
    )
    own_bias_sum = bias_sums[0] + got[images : images + 1]
    shared_sum = shared + got[images + 1 :]
    part_scaled = outer_cols(group_mod, w_mod).astype(bf16)
    grad_scaled = part_scaled.astype(f32) + swap_cores(part_scaled).astype(f32)
    _, silu_back = jax.vjp(jax.nn.silu, cond_f)
    grad_condition = silu_back(grad_scaled)[0]
    wide_scaled = jnp.pad(scaled.reshape(-1), (0, 3 * own_cols - slots * dim)).reshape(3, own_cols)
    packed_rows = jnp.concatenate(
        [group_mod, own_bias_sum.astype(bf16), shared_sum.astype(bf16), wide_scaled]
    )
    all_rows = lax.all_gather(packed_rows, "dp", axis=0, tiled=False)
    order.tick(last, *flows)
    output = fill_other(output, order.fence(other_output), core)
    order.after(output[0, 0, :1])

    def cuts(ways):
        return tuple((way[0], lo, hi) for lo, hi, way in ways)

    grad_w_down = grad_w_up = jnp.zeros((8, 128), f32)
    for chunk, flow in enumerate(flows):
        args = order.finish(flow)
        spot = len(args) + 1
        grad_w_down, grad_w_up, mark = run_kernel(
            functools.partial(final_mlp_kernel, cuts(MLP_WAYS), per),
            order.sc,
            list(args) + [grad_w_down, grad_w_up],
            [whole_block(a) for a in args] + [anywhere, anywhere],
            [
                pl.BlockSpec((block, dim), lambda s, c, chunk=chunk: (chunk * steps + s, 0)),
                pl.BlockSpec((dim, block), lambda s, c, chunk=chunk: (0, chunk * steps + s)),
                pl.BlockSpec((8, 128), lambda s, c: (0, 0)),
            ],
            [shape_of((ff, dim), f32), shape_of((dim, ff), f32), shape_of((8, 128), f32)],
            (steps,),
            6,
            scratch=[pltpu.VMEM((block, dim), f32)],
            alias=None if chunk == 0 else {spot: 0, spot + 1: 1},
            room=32,
        )
        order.after(mark)
        order.tick(last)
    grad_tokens = fill_other(grad_tokens, order.fence(other_tokens), core)
    all_rows = order.fence(all_rows)
    all_mod = all_rows[:, :slots].reshape(-1, own_cols)
    all_scaled = all_rows[:, slots + 2 :].reshape(16, -1)[:, : slots * dim].reshape(-1, dim)
    grad_w_mod = inner_rows(all_scaled, all_mod)
    grad_b_mod = jnp.sum(all_mod.astype(f32), axis=0)
    bias_total = jnp.sum(all_rows[:, slots : slots + 2].astype(f32), axis=0)
    grad_b_qv = bias_total[0, : 2 * cols].reshape(2, cols)
    grad_b_up = bias_total[0, 2 * cols :]
    grad_b_proj = bias_total[1, :dim]
    grad_b_down = bias_total[1, dim : 2 * dim]
    order.after((grad_tokens[0, 0, :1], grad_w_mod[0, :1], grad_b_mod[:1], bias_total[0, :1]))
    args = order.finish(last)
    grad_qkv_rows, grad_w_proj = run_kernel(
        functools.partial(final_attn_kernel, cuts(ATTN_WAYS), attn_per),
        order.sc,
        list(args),
        [whole_block(a) for a in args],
        [
            pl.BlockSpec((cols, dim), lambda s, c: (jnp.minimum(s, 2), 0)),
            pl.BlockSpec((cols, dim), lambda s, c: (0, 0)),
        ],
        [shape_of((3 * cols, dim), f32), shape_of((cols, dim), f32)],
        (4,),
        9,
        room=32,
    )
    grad_w_qkv = jnp.transpose(grad_qkv_rows.reshape(3, cols, dim), (2, 0, 1))
    return (
        output,
        grad_tokens,
        grad_condition,
        grad_w_qkv,
        grad_b_qv,
        grad_w_proj,
        grad_b_proj,
        grad_w_up,
        grad_b_up,
        grad_w_down,
        grad_b_down,
        grad_w_mod,
        grad_b_mod,
    )


def layer_norm(values):
    center = values - jnp.mean(values, axis=-1, keepdims=True)
    return center * lax.rsqrt(jnp.mean(center * center, axis=-1, keepdims=True) + epsilon)


def modulate(values, shift_part, scale_part):
    return layer_norm(values) * (1.0 + scale_part) + shift_part


def gelu_tanh(values):
    return (
        0.5
        * values
        * (1.0 + jnp.tanh(0.7978845608028654 * (values + 0.044715 * values * values * values)))
    )


def inner_rows(left, right):
    return lax.dot_general(
        left, right, (((0,), (0,)), ((), ())), preferred_element_type=jnp.float32
    )


def outer_cols(left, right):
    return lax.dot_general(
        left, right, (((1,), (1,)), ((), ())), preferred_element_type=jnp.float32
    )


def attention_forward(query_rows, key_rows, value_rows):
    factor = HEAD_DIM ** (-0.5)
    scores = (
        jnp.einsum("bqhd,bkhd->bhqk", query_rows, key_rows, preferred_element_type=jnp.float32)
        * factor
    )
    row_max = jnp.max(scores, axis=-1, keepdims=True)
    row_total = jnp.sum(jnp.exp(scores - row_max), axis=-1, keepdims=True)
    logsum = row_max + jnp.log(row_total)
    prob_b = jnp.exp(scores - logsum).astype(jnp.bfloat16)
    mixed_out = jnp.einsum(
        "bhqk,bkhd->bqhd", prob_b, value_rows, preferred_element_type=jnp.float32
    )
    return (mixed_out, logsum)


def attention_backward(query_rows, key_rows, value_rows, logsum, grad_mixed):
    factor = HEAD_DIM ** (-0.5)
    scores = (
        jnp.einsum("bqhd,bkhd->bhqk", query_rows, key_rows, preferred_element_type=jnp.float32)
        * factor
    )
    prob_f = jnp.exp(scores - logsum)
    prob_b = prob_f.astype(jnp.bfloat16)
    grad_prob = jnp.einsum(
        "bqhd,bkhd->bhqk", grad_mixed, value_rows, preferred_element_type=jnp.float32
    )
    row_delta = jnp.sum(prob_f * grad_prob, axis=-1, keepdims=True)
    grad_scores = (prob_f * (grad_prob - row_delta)).astype(jnp.bfloat16)
    grad_query = (
        jnp.einsum("bhqk,bkhd->bqhd", grad_scores, key_rows, preferred_element_type=jnp.float32)
        * factor
    )
    grad_key = (
        jnp.einsum("bhqk,bqhd->bkhd", grad_scores, query_rows, preferred_element_type=jnp.float32)
        * factor
    )
    grad_value = jnp.einsum(
        "bhqk,bqhd->bkhd", prob_b, grad_mixed, preferred_element_type=jnp.float32
    )
    return (
        grad_query.astype(jnp.bfloat16),
        grad_key.astype(jnp.bfloat16),
        grad_value.astype(jnp.bfloat16),
    )


def forward(tokens_f, spans, weights, repeat):
    w_qkv, b_qv, w_proj, b_proj, w_up, b_up, w_down, b_down = weights
    shift_attn, scale_attn, gate_attn, shift_mlp, scale_mlp, gate_mlp = spans
    slot_count, seq_len, model_dim = tokens_f.shape
    row_count = slot_count * seq_len
    head_cols = w_qkv.shape[2]
    head_count = head_cols // HEAD_DIM
    shape_four = (slot_count, seq_len, head_count, HEAD_DIM)
    normed = (
        modulate(tokens_f, shift_attn, scale_attn)
        .astype(jnp.bfloat16)
        .reshape(row_count, model_dim)
    )
    projected = jnp.dot(
        normed, w_qkv.reshape(model_dim, 3 * head_cols), preferred_element_type=jnp.float32
    )
    qkv_bias = jnp.stack([b_qv[0], jnp.zeros_like(b_qv[0]), b_qv[1]]).astype(jnp.float32)
    projected = (projected.reshape(row_count, 3, head_cols) + qkv_bias).astype(jnp.bfloat16)
    query_rows = projected[:, 0].reshape(shape_four)
    key_rows = projected[:, 1].reshape(shape_four)
    value_rows = projected[:, 2].reshape(shape_four)
    mixed_out, logsum = attention_forward(query_rows, key_rows, value_rows)
    mixed_b = mixed_out.astype(jnp.bfloat16).reshape(row_count, head_cols)
    partial_value = jnp.dot(mixed_b, w_proj, preferred_element_type=jnp.float32)
    if repeat:
        summed = lax.psum(partial_value.astype(jnp.bfloat16), "mp").astype(jnp.float32)
    else:
        summed = lax.psum(partial_value.astype(jnp.bfloat16), "mp").astype(jnp.float32)
    attn_out = (summed + b_proj.astype(jnp.float32)).reshape(slot_count, seq_len, model_dim)
    residual = tokens_f + gate_attn * attn_out
    normed_mlp = (
        modulate(residual, shift_mlp, scale_mlp).astype(jnp.bfloat16).reshape(row_count, model_dim)
    )
    hidden = jnp.dot(normed_mlp, w_up, preferred_element_type=jnp.float32) + b_up.astype(
        jnp.float32
    )
    act_bf = gelu_tanh(hidden).astype(jnp.bfloat16)
    partial_mlp = jnp.dot(act_bf, w_down, preferred_element_type=jnp.float32)
    if repeat:
        summed_mlp = lax.psum(partial_mlp.astype(jnp.bfloat16), "mp").astype(jnp.float32)
    else:
        summed_mlp = lax.psum(partial_mlp.astype(jnp.bfloat16), "mp").astype(jnp.float32)
    mlp_out = (summed_mlp + b_down.astype(jnp.float32)).reshape(slot_count, seq_len, model_dim)
    output = residual + gate_mlp * mlp_out
    return {
        "normed": normed,
        "query_rows": query_rows,
        "key_rows": key_rows,
        "value_rows": value_rows,
        "logsum": logsum,
        "mixed_b": mixed_b,
        "attn_out": attn_out,
        "residual": residual,
        "normed_mlp": normed_mlp,
        "hidden": hidden,
        "act_bf": act_bf,
        "mlp_out": mlp_out,
        "output": output,
    }


def image_pass(tokens_f, grad_out, spans, weights):
    w_qkv, b_qv, w_proj, b_proj, w_up, b_up, w_down, b_down = weights
    shift_attn, scale_attn, gate_attn, shift_mlp, scale_mlp, gate_mlp = spans
    slot_count, seq_len, model_dim = tokens_f.shape
    row_count = slot_count * seq_len
    head_cols = w_qkv.shape[2]
    head_count = head_cols // HEAD_DIM
    kept_fwd = forward(tokens_f, spans, weights, False)
    out_one = kept_fwd["output"]
    stored = forward(tokens_f, spans, weights, True)
    grad_gate_mlp = jnp.sum(grad_out * stored["mlp_out"], axis=1)
    grad_mlp = (gate_mlp * grad_out).astype(jnp.bfloat16).reshape(row_count, model_dim)
    grad_b_down = jnp.sum(grad_mlp.astype(jnp.float32), axis=0)
    grad_w_down = inner_rows(stored["act_bf"], grad_mlp)
    grad_act = outer_cols(grad_mlp, w_down)
    gelu_value, gelu_back = jax.vjp(gelu_tanh, stored["hidden"])
    grad_hidden = gelu_back(grad_act)[0].astype(jnp.bfloat16)
    grad_b_up = jnp.sum(grad_hidden.astype(jnp.float32), axis=0)
    grad_w_up = inner_rows(stored["normed_mlp"], grad_hidden)
    part_normed_mlp = outer_cols(grad_hidden, w_up)
    grad_normed_mlp = (
        lax.psum(part_normed_mlp.astype(jnp.bfloat16), "mp")
        .astype(jnp.float32)
        .reshape(slot_count, seq_len, model_dim)
    )
    norm_value, norm_back = jax.vjp(modulate, stored["residual"], shift_mlp, scale_mlp)
    grad_resid_norm, grad_shift_mlp, grad_scale_mlp = norm_back(grad_normed_mlp)
    grad_residual = grad_out + grad_resid_norm
    grad_gate_attn = jnp.sum(grad_residual * stored["attn_out"], axis=1)
    grad_attn = (gate_attn * grad_residual).astype(jnp.bfloat16).reshape(row_count, model_dim)
    grad_b_proj = jnp.sum(grad_attn.astype(jnp.float32), axis=0)
    grad_w_proj = inner_rows(stored["mixed_b"], grad_attn)
    grad_mixed = (
        outer_cols(grad_attn, w_proj)
        .astype(jnp.bfloat16)
        .reshape(slot_count, seq_len, head_count, HEAD_DIM)
    )
    grad_query, grad_key, grad_value = attention_backward(
        stored["query_rows"], stored["key_rows"], stored["value_rows"], stored["logsum"], grad_mixed
    )
    grad_qkv = jnp.stack(
        [
            grad_query.reshape(row_count, head_cols),
            grad_key.reshape(row_count, head_cols),
            grad_value.reshape(row_count, head_cols),
        ],
        axis=1,
    )
    grad_b_qv = jnp.stack(
        [
            jnp.sum(grad_qkv[:, 0].astype(jnp.float32), axis=0),
            jnp.sum(grad_qkv[:, 2].astype(jnp.float32), axis=0),
        ]
    )
    grad_w_qkv = inner_rows(stored["normed"], grad_qkv)
    part_normed = outer_cols(
        grad_qkv.reshape(row_count, 3 * head_cols), w_qkv.reshape(model_dim, 3 * head_cols)
    )
    grad_normed = (
        lax.psum(part_normed.astype(jnp.bfloat16), "mp")
        .astype(jnp.float32)
        .reshape(slot_count, seq_len, model_dim)
    )
    first_value, first_back = jax.vjp(modulate, tokens_f, shift_attn, scale_attn)
    grad_tok_norm, grad_shift_attn, grad_scale_attn = first_back(grad_normed)
    grad_tok_one = grad_residual + grad_tok_norm
    grad_mod_one = jnp.concatenate(
        [
            grad_shift_attn[:, 0],
            grad_scale_attn[:, 0],
            grad_gate_attn,
            grad_shift_mlp[:, 0],
            grad_scale_mlp[:, 0],
            grad_gate_mlp,
        ],
        axis=1,
    )
    grad_terms = (
        grad_w_qkv,
        grad_b_qv,
        grad_w_proj,
        grad_b_proj,
        grad_w_up,
        grad_b_up,
        grad_w_down,
        grad_b_down,
    )
    return (out_one, grad_tok_one, grad_mod_one, grad_terms)


def run_layer(tokens, condition, cotangent, live_count, turns, weights, w_mod, b_mod):
    slot_count, seq_len, model_dim = tokens.shape
    cond_f = condition.astype(jnp.float32)
    scaled = jax.nn.silu(cond_f).astype(jnp.bfloat16)
    own_mod = jnp.dot(scaled, w_mod, preferred_element_type=jnp.float32) + b_mod.astype(jnp.float32)
    modulation = lax.all_gather(own_mod, "mp", axis=1, tiled=True)
    tokens_f = tokens.astype(jnp.float32)
    cot_f = cotangent.astype(jnp.float32)

    def image_step(slot_idx, carry):
        out_buf, grad_buf, mod_buf, grad_sums = carry
        live_flag = (slot_idx < live_count).astype(jnp.float32)
        tok_one = lax.dynamic_slice_in_dim(tokens_f, slot_idx, 1, 0)
        cot_one = lax.dynamic_slice_in_dim(cot_f, slot_idx, 1, 0) * live_flag
        mod_row = lax.dynamic_slice_in_dim(modulation, slot_idx, 1, 0)
        spans = [
            mod_row[:, None, part_idx * model_dim : (part_idx + 1) * model_dim]
            for part_idx in range(6)
        ]
        out_one, grad_tok_one, grad_mod_one, grad_terms = image_pass(
            tok_one, cot_one, spans, weights
        )
        out_one = (out_one * live_flag).astype(jnp.bfloat16)
        out_buf = lax.dynamic_update_slice_in_dim(out_buf, out_one, slot_idx, 0)
        grad_buf = lax.dynamic_update_slice_in_dim(grad_buf, grad_tok_one, slot_idx, 0)
        mod_buf = lax.dynamic_update_slice_in_dim(mod_buf, grad_mod_one, slot_idx, 0)
        grad_sums = tuple((total_a + term_b for total_a, term_b in zip(grad_sums, grad_terms)))
        return (out_buf, grad_buf, mod_buf, grad_sums)

    start_sums = tuple((jnp.zeros(weight_in.shape, jnp.float32) for weight_in in weights))
    start_state = (
        jnp.zeros(tokens.shape, jnp.bfloat16),
        jnp.zeros(tokens.shape, jnp.float32),
        jnp.zeros((slot_count, 6 * model_dim), jnp.float32),
        start_sums,
    )
    out_buf, grad_buf, mod_buf, grad_sums = lax.fori_loop(0, turns, image_step, start_state)
    grad_modulation = mod_buf.astype(jnp.bfloat16)
    own_cols = w_mod.shape[1]
    grad_own = lax.dynamic_slice_in_dim(
        grad_modulation, lax.axis_index("mp") * own_cols, own_cols, 1
    )
    part_scaled = outer_cols(grad_own, w_mod)
    grad_scaled = lax.psum(part_scaled.astype(jnp.bfloat16), "mp").astype(jnp.float32)
    silu_value, silu_back = jax.vjp(jax.nn.silu, cond_f)
    grad_condition = silu_back(grad_scaled)[0]
    return (out_buf, grad_buf, grad_condition, grad_sums, scaled, grad_own)


def on_device(
    tokens,
    condition,
    counts,
    w_qkv,
    b_qv,
    w_proj,
    b_proj,
    w_up,
    b_up,
    w_down,
    b_down,
    w_mod,
    b_mod,
    cotangent,
):
    slot_count, seq_len, model_dim = tokens.shape
    weights = (w_qkv, b_qv, w_proj, b_proj, w_up, b_up, w_down, b_down)
    own_count = counts[0]
    output, grad_tokens, grad_condition, grad_sums, scaled, grad_own = run_layer(
        tokens, condition, cotangent, own_count, slot_count, weights, w_mod, b_mod
    )
    (
        grad_w_qkv,
        grad_b_qv,
        grad_w_proj,
        grad_b_proj,
        grad_w_up,
        grad_b_up,
        grad_w_down,
        grad_b_down,
    ) = grad_sums
    grad_w_mod = inner_rows(scaled, grad_own)
    grad_b_mod = jnp.sum(grad_own.astype(jnp.float32), axis=0)
    (
        grad_w_qkv,
        grad_b_qv,
        grad_w_proj,
        grad_b_proj,
        grad_w_up,
        grad_b_up,
        grad_w_down,
        grad_b_down,
        grad_w_mod,
        grad_b_mod,
    ) = (
        lax.psum(grad_w_qkv.astype(jnp.bfloat16), "dp").astype(jnp.float32),
        lax.psum(grad_b_qv.astype(jnp.bfloat16), "dp").astype(jnp.float32),
        lax.psum(grad_w_proj.astype(jnp.bfloat16), "dp").astype(jnp.float32),
        lax.psum(grad_b_proj.astype(jnp.bfloat16), "dp").astype(jnp.float32),
        lax.psum(grad_w_up.astype(jnp.bfloat16), "dp").astype(jnp.float32),
        lax.psum(grad_b_up.astype(jnp.bfloat16), "dp").astype(jnp.float32),
        lax.psum(grad_w_down.astype(jnp.bfloat16), "dp").astype(jnp.float32),
        lax.psum(grad_b_down.astype(jnp.bfloat16), "dp").astype(jnp.float32),
        lax.psum(grad_w_mod.astype(jnp.bfloat16), "dp").astype(jnp.float32),
        lax.psum(grad_b_mod.astype(jnp.bfloat16), "dp").astype(jnp.float32),
    )
    return (
        output,
        grad_tokens,
        grad_condition,
        grad_w_qkv,
        grad_b_qv,
        grad_w_proj,
        grad_b_proj,
        grad_w_up,
        grad_b_up,
        grad_w_down,
        grad_b_down,
        grad_w_mod,
        grad_b_mod,
    )


def solution(mesh):
    placed = (
        P("dp", None, None),
        P("dp", None),
        P("dp"),
        P(None, None, "mp"),
        P(None, "mp"),
        P("mp", None),
        P(),
        P(None, "mp"),
        P("mp"),
        P("mp", None),
        P(),
        P(None, "mp"),
        P("mp"),
        P("dp", None, None),
    )
    fast = mesh.shape["dp"] == 16 and mesh.shape["mp"] == 2
    return jax.shard_map(
        fast_device if fast else on_device,
        mesh=mesh,
        in_specs=placed,
        out_specs=(
            P("dp", None, None),
            P("dp", None, None),
            P("dp", None),
            P(None, None, "mp"),
            P(None, "mp"),
            P("mp", None),
            P(),
            P(None, "mp"),
            P("mp"),
            P("mp", None),
            P(),
            P(None, "mp"),
            P("mp"),
        ),
        check_vma=False,
    )
```

```python
import functools

import jax
import jax.numpy as jnp
from jax import lax
from jax.experimental import pallas as pl
from jax.experimental.pallas import tpu as pltpu
from jax.sharding import PartitionSpec as P

HEAD_DIM = 72


epsilon = 1e-06

f32 = jnp.float32
bf16 = jnp.bfloat16


def dot_nn(left, right):
    return lax.dot_general(left, right, (((1,), (0,)), ((), ())), preferred_element_type=f32)


def dot_nt(left, right):
    return lax.dot_general(left, right, (((1,), (1,)), ((), ())), preferred_element_type=f32)


def dot_tn(left, right):
    return lax.dot_general(left, right, (((0,), (0,)), ((), ())), preferred_element_type=f32)


def normalize(values):
    center = values - jnp.mean(values, axis=-1, keepdims=True)
    recip = lax.rsqrt(jnp.mean(center * center, axis=-1, keepdims=True) + epsilon)
    return center * recip, recip


def norm_pullback(grad_normed, unit, recip, scale_row):
    scaled_grad = grad_normed * (1.0 + scale_row)
    mean_grad = jnp.mean(scaled_grad, axis=-1, keepdims=True)
    mean_unit = jnp.mean(scaled_grad * unit, axis=-1, keepdims=True)
    return recip * (scaled_grad - mean_grad - unit * mean_unit)


def column(row):
    return jnp.broadcast_to(row[...].astype(f32), (8, row.shape[1])).T[:, 0:1]


def token_sum(values):
    return jnp.sum(values, axis=0, keepdims=True)


def attention_kernel(parts, own_images, sc, tok, cot, mod, b_proj, *refs):
    w_qkv, w_proj, bias = refs[:parts], refs[parts : 2 * parts], refs[2 * parts : 3 * parts]
    qkv, prob, mixed, attn_out, residual, normed_mlp, normed, grad_mlp, down_sums = refs[3 * parts :]
    image = sc[0] * own_images + pl.program_id(0)
    live = jnp.where(image < sc[1], 1.0, 0.0).astype(f32)
    unit, _ = normalize(tok[0].astype(f32))
    normed[0] = (unit * (1.0 + mod[0, 1:2, :]) + mod[0, 0:1, :]).astype(bf16)
    grad = (mod[0, 5:6, :] * (cot[0].astype(f32) * live)).astype(bf16)
    grad_mlp[0] = grad
    down_sums[0] = token_sum(grad.astype(f32))
    cols = w_proj[0].shape[0]
    pairs = cols // (2 * HEAD_DIM)
    span = 2 * HEAD_DIM
    factor = HEAD_DIM ** (-0.5)
    rows = normed[0]
    total = b_proj[...]
    for part in range(parts):
        base = part * 3 * cols
        shift = bias[part][...].astype(f32).T
        for proj in range(3):
            lo = proj * cols
            value = dot_nt(w_qkv[part][lo : lo + cols, :], rows)
            if proj != 1:
                value = value + shift[:, proj // 2 : proj // 2 + 1]
            qkv[0, base + lo : base + lo + cols, :] = value.astype(bf16)

        def pair_step(pair, carry, base=base, part=part):
            at = pl.multiple_of(base + pair * span, 16)
            query = qkv[0, pl.ds(at, span), :].astype(f32)
            key = qkv[0, pl.ds(at + cols, span), :].astype(f32)
            value = qkv[0, pl.ds(at + 2 * cols, span), :].astype(f32)
            outs = []
            for one in range(2):
                rows_of = slice(one * HEAD_DIM, (one + 1) * HEAD_DIM)
                scores = dot_tn(key[rows_of].astype(bf16), query[rows_of].astype(bf16)) * factor
                raised = jnp.exp(scores - jnp.max(scores, axis=0, keepdims=True))
                share = 1.0 / jnp.sum(raised, axis=0, keepdims=True)
                prob_b = (raised * share).astype(bf16)
                prob[0, part * 2 * pairs + 2 * pair + one] = prob_b
                outs.append(dot_nn(value[rows_of].astype(bf16), prob_b))
            to = pl.multiple_of(part * cols + pair * span, 16)
            mixed[0, pl.ds(to, span), :] = jnp.concatenate(outs, axis=0).astype(bf16)
            return carry

        lax.fori_loop(0, pairs, pair_step, 0, unroll=True)
        total = total + dot_tn(mixed[0, part * cols : (part + 1) * cols, :], w_proj[part][...])
    attn_out[0] = total
    summed = tok[0].astype(f32) + mod[0, 2:3, :] * total
    residual[0] = summed
    unit, _ = normalize(summed)
    normed_mlp[0] = (unit * (1.0 + mod[0, 4:5, :]) + mod[0, 3:4, :]).astype(bf16)


def mlp_kernel(
    per, natural, sc, rows, grad_mlp, w_up0, w_up1, w_down0, w_down1, bias0, bias1, act_in, back_in,
    act, back, grad_own, grad_other, sums
):
    part, step = pl.program_id(0), pl.program_id(1)

    @pl.when(part == 0)
    def _():
        mlp_block(per, natural, step, sc, rows, grad_mlp, w_up0, w_down0, bias0, act, back, grad_own, sums)

    @pl.when(part == 1)
    def _():
        mlp_block(per, natural, step, sc, rows, grad_mlp, w_up1, w_down1, bias1, act, back, grad_other, sums)


def mlp_block(per, natural, step, sc, rows, grad_mlp, w_up, w_down, bias, act, back, grads, sums):
    here = w_down.shape[0] // per
    hidden = lax.dot_general(
        w_up[...], rows[...], (((0,), (1,)), ((), ())), preferred_element_type=f32
    ) + column(bias)
    square = hidden * hidden
    bend = jnp.tanh(0.7978845608028654 * hidden * (1.0 + 0.044715 * square))
    half = 0.5 * (1.0 + bend)
    act_b = (hidden * half).astype(bf16)
    slope = half + 0.5 * hidden * (1.0 - bend * bend) * (
        0.7978845608028654 * (1.0 + 3.0 * 0.044715 * square)
    )
    back_b = (dot_nt(w_down[...], grad_mlp[...]) * slope).astype(bf16)
    act[0] = act_b
    back[0] = back_b
    sums[0] = dot_nt(jnp.ones((8, rows.shape[0]), bf16), back_b)
    grad_down = dot_nn(act_b, grad_mlp[...]).astype(bf16)
    grad_up = dot_nn(back_b, rows[...]).astype(bf16)
    for piece in range(here):
        at = step * here + piece
        if not natural:
            at = jnp.bitwise_xor(at, sc[2])
        lo = piece * per
        grads[at, 0:per, :] = grad_down[lo : lo + per]
        grads[at, per : 2 * per, :] = grad_up[lo : lo + per]


def grow(total, part_steps, left, rights, dims):
    step = pl.program_id(0)

    def term(right):
        return lax.dot_general(left, right[...], (dims, ((), ())), preferred_element_type=f32)

    @pl.when(step == 0)
    def _():
        total[...] = term(rights[0])

    @pl.when(jnp.logical_and(step > 0, step < part_steps))
    def _():
        total[...] += term(rights[0])

    @pl.when(jnp.logical_and(step >= part_steps, step < 2 * part_steps))
    def _():
        total[...] += term(rights[1])


def norm_back_kernel(
    part_steps, own_images, sc, back, w_up0, w_up1, residual, cot, mod, attn_out,
    grad_residual, grad_attn, sums, total
):
    grow(total, part_steps, back[0], (w_up0, w_up1), ((0,), (1,)))
    one = pl.program_id(0) - 2 * part_steps
    seq = residual.shape[1]

    @pl.when(one >= 0)
    def _():
        live = jnp.where(sc[0] * own_images + one < sc[1], 1.0, 0.0).astype(f32)
        grad_normed = total[pl.ds(pl.multiple_of(one * seq, seq), seq), :]
        unit, recip = normalize(residual[0])
        sums[0, 0:1, :] = token_sum(grad_normed)
        sums[0, 1:2, :] = token_sum(grad_normed * unit)
        grad_res = cot[0].astype(f32) * live + norm_pullback(grad_normed, unit, recip, mod[0, 4:5, :])
        grad_residual[0] = grad_res
        sums[0, 2:3, :] = token_sum(grad_res * attn_out[0])
        grad_att = (mod[0, 2:3, :] * grad_res).astype(bf16)
        grad_attn[0] = grad_att
        sums[0, 3:4, :] = token_sum(grad_att.astype(f32))


def back_kernel(parts, sc, grad_attn, qkv, prob, *refs):
    w_proj = refs[:parts]
    grad_qkv, grad_mixed = refs[parts:]
    cols = w_proj[0].shape[0]
    pairs = cols // (2 * HEAD_DIM)
    span = 2 * HEAD_DIM
    factor = HEAD_DIM ** (-0.5)
    grad_att = grad_attn[0]
    for part in range(parts):
        base = part * 3 * cols
        grad_mixed[part * cols : (part + 1) * cols, :] = dot_nt(w_proj[part][...], grad_att).astype(bf16)

        def pair_step(pair, carry, base=base, part=part):
            at = pl.multiple_of(base + pair * span, 16)
            query = qkv[0, pl.ds(at, span), :].astype(f32)
            key = qkv[0, pl.ds(at + cols, span), :].astype(f32)
            value = qkv[0, pl.ds(at + 2 * cols, span), :].astype(f32)
            grads = grad_mixed[pl.ds(pl.multiple_of(part * cols + pair * span, 16), span), :].astype(f32)
            to_query, to_key, to_value = [], [], []
            for one in range(2):
                rows_of = slice(one * HEAD_DIM, (one + 1) * HEAD_DIM)
                prob_b = prob[0, part * 2 * pairs + 2 * pair + one]
                prob_f = prob_b.astype(f32)
                grad_b = grads[rows_of].astype(bf16)
                grad_prob = dot_tn(value[rows_of].astype(bf16), grad_b)
                delta = jnp.sum(prob_f * grad_prob, axis=0, keepdims=True)
                grad_scores = (prob_f * (grad_prob - delta)).astype(bf16)
                to_query.append(dot_nn(key[rows_of].astype(bf16), grad_scores) * factor)
                to_key.append(dot_nt(query[rows_of].astype(bf16), grad_scores) * factor)
                to_value.append(dot_nt(grad_b, prob_b))
            grad_qkv[0, pl.ds(at, span), :] = jnp.concatenate(to_query, axis=0).astype(bf16)
            grad_qkv[0, pl.ds(at + cols, span), :] = jnp.concatenate(to_key, axis=0).astype(bf16)
            grad_qkv[0, pl.ds(at + 2 * cols, span), :] = jnp.concatenate(to_value, axis=0).astype(bf16)
            return carry

        lax.fori_loop(0, pairs, pair_step, 0, unroll=True)


def attn_grad_kernel(pieces, per, sc, *refs):
    grad_qkv, mixed, normed, grad_attn = refs[:pieces], refs[pieces], refs[pieces + 1], refs[pieces + 2]
    grads, sums = refs[pieces + 3 :]
    step = pl.program_id(0)
    here = mixed.shape[1] // per
    images = mixed.shape[0]
    each = images // pieces

    def spread(total):
        total = total.astype(bf16)
        for piece in range(here):
            at = jnp.bitwise_xor(step * here + piece, sc[2])
            grads[at] = total[piece * per : (piece + 1) * per]

    @pl.when(step < 3)
    def _():
        ones = jnp.ones((8, mixed.shape[2]), bf16)
        total = count = None
        for image in range(images):
            left = grad_qkv[image // each][image % each]
            term, one = dot_nn(left, normed[image]), dot_nt(ones, left)
            total = term if image == 0 else total + term
            count = one if image == 0 else count + one
        sums[0] = count
        spread(total)

    @pl.when(step == 3)
    def _():
        total = dot_nn(mixed[0], grad_attn[0])
        for image in range(1, images):
            total = total + dot_nn(mixed[image], grad_attn[image])
        spread(total)


def first_back_kernel(pieces, images, sc, *refs):
    grad_qkv = refs[:pieces]
    w_qkv0, w_qkv1, tok, mod, grad_residual = refs[pieces : pieces + 5]
    grad_tokens, grad_own, sums, total = refs[pieces + 5 :]
    step = pl.program_id(0)
    each = images // pieces
    seq = tok.shape[1]

    def add(w_qkv, fresh):
        for one in range(images):
            term = dot_tn(grad_qkv[one // each][one % each], w_qkv[...])
            if fresh:
                total[one * seq : (one + 1) * seq, :] = term
            else:
                total[one * seq : (one + 1) * seq, :] += term

    @pl.when(step == 0)
    def _():
        add(w_qkv0, True)

    @pl.when(jnp.logical_and(step > 0, step < 3))
    def _():
        add(w_qkv0, False)

    @pl.when(jnp.logical_and(step >= 3, step < 6))
    def _():
        add(w_qkv1, False)

    @pl.when(step >= 6)
    def _():
        grad_normed = total[pl.ds(pl.multiple_of((step - 6) * seq, seq), seq), :]
        unit, recip = normalize(tok[0].astype(f32))
        sums[0, 0:1, :] = token_sum(grad_normed)
        sums[0, 1:2, :] = token_sum(grad_normed * unit)
        grad = grad_residual[0] + norm_pullback(grad_normed, unit, recip, mod[0, 1:2, :])
        grad_tokens[0] = grad
        grad_own[0] = grad


def output_kernel(
    part_steps, own_images, sc, act, w_down0, w_down1, residual, cot, mod, b_down, output, own, sums, total
):
    grow(total, part_steps, act[0], (w_down0, w_down1), ((0,), (0,)))
    one = pl.program_id(0) - 2 * part_steps
    seq = residual.shape[1]

    @pl.when(one >= 0)
    def _():
        live = jnp.where(sc[0] * own_images + one < sc[1], 1.0, 0.0).astype(f32)
        mlp_out = total[pl.ds(pl.multiple_of(one * seq, seq), seq), :] + b_down[...]
        sums[0] = token_sum((cot[0].astype(f32) * live) * mlp_out)
        rows = ((residual[0] + mod[0, 5:6, :] * mlp_out) * live).astype(bf16)
        output[0] = rows
        own[0] = rows


def final_piece(sc, halves, piece, store):
    rel = jnp.bitwise_xor(piece, sc[2])
    for low, high, bit, lo, hi in halves:
        index = ((rel >> (bit + 1)) << bit) | (rel & ((1 << bit) - 1))
        side = (rel >> bit) & 1

        @pl.when(side == 0)
        def _(low=low, index=index, lo=lo, hi=hi):
            store(low[index].astype(f32), lo, hi)

        @pl.when(side == 1)
        def _(high=high, index=index, lo=lo, hi=hi):
            store(high[index].astype(f32), lo, hi)


def final_mlp_kernel(cuts, per, sc, *refs):
    count = 2 * len(cuts)
    arrays, (_, _, down, up, mark, turned) = refs[:count], refs[count:]
    here = down.shape[0] // per
    halves = [(arrays[2 * k], arrays[2 * k + 1]) + cut for k, cut in enumerate(cuts)]
    for piece in range(here):

        def store(value, lo, hi, piece=piece):
            down[piece * per : (piece + 1) * per, lo:hi] = value[0:per]
            turned[piece * per : (piece + 1) * per, lo:hi] = value[per : 2 * per]

        final_piece(sc, halves, pl.program_id(0) * here + piece, store)
    up[...] = turned[...].T
    mark[...] = jnp.zeros_like(mark)


def final_plain_kernel(per, sc, summed, down_in, up_in, down, up, mark, turned):
    for piece in range(summed.shape[0]):
        lo = piece * per
        down[lo : lo + per, :] = summed[piece, 0:per, :].astype(f32)
        turned[lo : lo + per, :] = summed[piece, per : 2 * per, :].astype(f32)
    up[...] = turned[...].T
    mark[...] = jnp.zeros_like(mark)


def final_attn_kernel(cuts, per, sc, *refs):
    count = 2 * len(cuts)
    arrays, (qkv, proj) = refs[:count], refs[count:]
    here = proj.shape[0] // per
    halves = [(arrays[2 * k], arrays[2 * k + 1]) + cut for k, cut in enumerate(cuts)]
    for target, wanted in ((qkv, True), (proj, False)):

        @pl.when((pl.program_id(0) < 3) == wanted)
        def _(target=target):
            for piece in range(here):

                def store(value, lo, hi, piece=piece):
                    target[piece * per : (piece + 1) * per, lo:hi] = value

                final_piece(sc, halves, pl.program_id(0) * here + piece, store)


def run_kernel(
    body, sc, args, in_specs, out_specs, out_shape, grid, micros, scratch=(), alias=None, room=60
):
    size = sum(a.size * a.dtype.itemsize for a in args) + sum(
        s.size * s.dtype.itemsize for s in out_shape
    )
    return pl.pallas_call(
        body,
        out_shape=out_shape,
        grid_spec=pltpu.PrefetchScalarGridSpec(
            num_scalar_prefetch=1,
            grid=grid,
            in_specs=in_specs,
            out_specs=out_specs,
            scratch_shapes=list(scratch),
        ),
        compiler_params=pltpu.CompilerParams(vmem_limit_bytes=room << 20),
        cost_estimate=pl.CostEstimate(
            flops=int(micros * 1.15e9), bytes_accessed=int(min(size, micros * 1e6)), transcendentals=0
        ),
        input_output_aliases=alias or {},
    )(sc, *args)


def whole_block(array):
    zeros = (0,) * array.ndim
    return pl.BlockSpec(array.shape, lambda *_: zeros, pipeline_mode=pl.Buffered(1))


def shape_of(dims, kind):
    return jax.ShapeDtypeStruct(dims, kind)


SWAP = [(0, 1), (1, 0)]


def swap_cores(value):
    return lax.ppermute(value, "mp", SWAP)


def bit_pairs(bit):
    return [(index, index ^ (1 << bit)) for index in range(16)]


MLP_WAYS = ((0, 640, (0, 1, 2, 3)), (640, 1152, (1, 0, 2, 3)))
ATTN_WAYS = ((0, 512, (0, 1, 2, 3)), (512, 896, (1, 0, 2, 3)), (896, 1152, (2, 3, 0, 1)))


def cut(array, bits, bit, side, cols=None):
    lo = [0] * array.ndim
    hi = list(array.shape)
    place = bits.index(bit)
    lo[place], hi[place] = side, side + 1
    if cols is not None:
        lo[-1], hi[-1] = cols
    out = lax.slice(array, lo, hi)
    return out.reshape(out.shape[:place] + out.shape[place + 1 :])


def left_bits(done):
    return [bit for bit in (3, 2, 1, 0) if bit not in done]


def exchange(values, bits):
    return [lax.ppermute(value, "dp", bit_pairs(bit)) for value, bit in zip(values, bits)]


def reduce_flow(ways, get_own, other):
    shape = (2, 2, 2, 2) + other.shape[1:]
    (other,) = yield [other]
    came = swap_cores(other)
    yield None
    own, came = yield [get_own(), came]
    firsts, seconds = [own.reshape(shape)] * len(ways), [came.reshape(shape)] * len(ways)
    routes = [way for _, _, way in ways]
    for stage in range(4):
        sends, keeps = [], []
        for (lo, hi, _), route, one, two in zip(ways, routes, firsts, seconds):
            bits = left_bits(route[:stage])
            cols = (lo, hi) if stage == 0 else None
            for side, into in ((1, sends), (0, keeps)):
                into.append(
                    cut(one, bits, route[stage], side, cols) + cut(two, bits, route[stage], side, cols)
                )
        if stage == 2 and routes[0][2:] == routes[1][2:]:
            sends = [jnp.concatenate(sends[:2], axis=-1)] + sends[2:]
            keeps = [jnp.concatenate(keeps[:2], axis=-1)] + keeps[2:]
            routes = [routes[0]] + routes[2:]
            ways = [(0, 0, way) for way in routes]
        sends, keeps = yield [sends, keeps]
        comes = exchange(sends, [route[stage] for route in routes])
        yield None
        firsts, seconds = yield [keeps, comes]
    return [one + two for one, two in zip(firsts, seconds)]


def gather_flow(ways, have):
    routes = [ways[0][2]] + [way for _, _, way in ways[2:]]
    middle = ways[0][1]
    known = [[] for _ in routes]
    (have,) = yield [have]
    comes = exchange(have, [route[3] for route in routes])
    yield None
    for stage in (2, 1, 0):
        have, comes = yield [have, comes]
        joined = []
        for route, bits, one, two in zip(routes, known, have, comes):
            bit = route[stage + 1]
            place = sum(1 for other in bits if other > bit)
            joined.append(jnp.stack([one, two], axis=place))
            bits.insert(place, bit)
        if stage == 1:
            joined = [joined[0][..., :middle], joined[0][..., middle:]] + joined[1:]
            routes = [way for _, _, way in ways]
            known = [list(known[0]), list(known[0])] + known[1:]
        (have,) = yield [joined]
        comes = exchange(have, [route[stage] for route in routes])
        yield None
    have, comes = yield [have, comes]
    return [part.reshape((8,) + part.shape[-2:]) for pair in zip(have, comes) for part in pair]


def sum_flow(ways, get_own, other):
    have = yield from reduce_flow(ways, get_own, other)
    return (yield from gather_flow(ways, have))


def core_flow(own, other):
    (other,) = yield [other]
    came = swap_cores(other)
    yield None
    own, came = yield [own, came]
    (total,) = yield [own + came]
    return total


def rows_flow(rows):
    for bit in range(4):
        (rows,) = yield [rows]
        came = lax.ppermute(rows, "dp", bit_pairs(bit))
        yield None
        rows, came = yield [rows, came]
        rows = jnp.concatenate([rows, came])
    return rows


class Order:
    def __init__(self, sc):
        self.sc = sc
        self.results = {}

    def fence(self, values):
        self.sc, values = lax.optimization_barrier((self.sc, values))
        return values

    def after(self, value):
        self.sc, _ = lax.optimization_barrier((self.sc, value))

    def tick(self, *flows):
        replies = {flow: None for flow in flows if flow not in self.results}
        while replies:
            wants = {}
            for flow, reply in replies.items():
                try:
                    want = flow.send(reply)
                except StopIteration as stop:
                    self.results[flow] = stop.value
                    continue
                if want is not None:
                    wants[flow] = want
            replies = dict(zip(wants, self.fence(list(wants.values())))) if wants else {}

    def finish(self, flow):
        while flow not in self.results:
            self.tick(flow)
        return self.results[flow]


CHUNKS = 3
PLAIN = 2


def fill_other(both, came, core):
    size = came.shape[0]
    return lax.dynamic_update_slice_in_dim(both, came, (1 - core) * size, 0)


def fast_device(
    tokens, condition, counts, w_qkv, b_qv, w_proj, b_proj, w_up, b_up, w_down, b_down, w_mod, b_mod,
    cotangent,
):
    slots, seq, dim = tokens.shape
    images = slots // 2
    count = images * seq
    cols = w_qkv.shape[2]
    ff = w_up.shape[1]
    own_cols = w_mod.shape[1]
    heads = cols // HEAD_DIM
    core = lax.axis_index("mp")
    order = Order(jnp.stack([core, counts[0], lax.axis_index("dp")]).astype(jnp.int32))

    qkv_rows = jnp.transpose(w_qkv, (1, 2, 0)).reshape(3 * cols, dim)
    wq = [qkv_rows, swap_cores(qkv_rows)]
    wp = [w_proj, swap_cores(w_proj)]
    qkv_bias = [b_qv, swap_cores(b_qv)]

    cond_f = condition.astype(f32)
    scaled = jax.nn.silu(cond_f).astype(bf16)
    own_mod = jnp.dot(scaled, w_mod, preferred_element_type=f32) + b_mod.astype(f32)
    other_mod = swap_cores(own_mod)
    sides = [jnp.where(core == side, own_mod, other_mod) for side in range(2)]
    modulation = jnp.concatenate(sides, axis=1).reshape(slots, 6, dim)
    proj_bias = b_proj.astype(f32)[None]
    down_bias = b_down.astype(f32)[None]

    late_up, late_down, late_bias = lax.optimization_barrier((wq[1], w_up, w_down, b_up, modulation))[1:4]
    wu = [w_up, swap_cores(late_up)]
    wd = [w_down, swap_cores(late_down)]
    up_bias = [b_up[None], swap_cores(late_bias[None])]

    local = lambda i, s: (s[0] * images + i, 0, 0)
    mine = lambda i, s: (i, 0, 0)
    tok_spec = pl.BlockSpec((1, seq, dim), local)
    own_spec = pl.BlockSpec((1, seq, dim), mine)
    mod_spec = pl.BlockSpec((1, 6, dim), local)
    row_spec = pl.BlockSpec((1, 1, dim), mine)
    qkv_spec = pl.BlockSpec((1, 6 * cols, seq), mine)
    prob_spec = pl.BlockSpec((1, 2 * heads, seq, seq), lambda i, s: (i, 0, 0, 0))
    mixed_spec = pl.BlockSpec((1, 2 * cols, seq), mine)
    token_f = shape_of((images, seq, dim), f32)
    token_b = shape_of((images, seq, dim), bf16)
    attn_args = wq + wp + qkv_bias
    qkv, prob, mixed, attn_out, residual, normed_mlp, normed, grad_mlp, down_sums = run_kernel(
        functools.partial(attention_kernel, 2, images),
        order.sc,
        [tokens, cotangent, modulation, proj_bias] + attn_args,
        [tok_spec, tok_spec, mod_spec, whole_block(proj_bias)] + [whole_block(a) for a in attn_args],
        [qkv_spec, prob_spec, mixed_spec] + [own_spec] * 5 + [row_spec],
        [
            shape_of((images, 6 * cols, seq), bf16),
            shape_of((images, 2 * heads, seq, seq), bf16),
            shape_of((images, 2 * cols, seq), bf16),
            token_f,
            token_f,
            token_b,
            token_b,
            token_b,
            shape_of((images, 1, dim), f32),
        ],
        (images,),
        45,
        room=44,
    )
    order.after(down_sums)

    rows_flat = normed_mlp.reshape(count, dim)
    grad_flat = grad_mlp.reshape(count, dim)
    width = ff // CHUNKS
    per = width // 16
    steps = 2
    block = width // steps
    anywhere = pl.BlockSpec(memory_space=pl.ANY)
    act = back = jnp.zeros((8, 128), bf16)
    plain, flows, up_sums = [], [], []
    for chunk in range(CHUNKS):
        at = chunk * steps

        def pick(which, at=at):
            rest = (steps - 1) * (1 - which)
            return lambda p, s, c: at + jnp.where(p == which, s, rest)

        def up_map(which):
            return lambda p, s, c: (0, pick(which)(p, s, c))

        def down_map(which):
            return lambda p, s, c: (pick(which)(p, s, c), 0)

        spread = pl.BlockSpec((1, block, count), lambda p, s, c, at=at: (p, at + s, 0))
        act, back, grad_own, grad_other, sums = run_kernel(
            functools.partial(mlp_kernel, per, chunk < PLAIN),
            order.sc,
            [rows_flat, grad_flat] + wu + wd + up_bias + [act, back],
            [whole_block(rows_flat), whole_block(grad_flat)]
            + [pl.BlockSpec((dim, block), up_map(which)) for which in range(2)]
            + [pl.BlockSpec((block, dim), down_map(which)) for which in range(2)]
            + [pl.BlockSpec((1, block), up_map(which)) for which in range(2)]
            + [anywhere, anywhere],
            [spread, spread]
            + [pl.BlockSpec((16, 2 * per, dim), lambda p, s, c: (0, 0, 0))] * 2
            + [pl.BlockSpec((1, 8, block), lambda p, s, c: (p, 0, s))],
            [shape_of((2, ff, count), bf16)] * 2
            + [shape_of((16, 2 * per, dim), bf16)] * 2
            + [shape_of((2, 8, width), f32)],
            (2, steps),
            28,
            alias=None if chunk == 0 else {9: 0, 10: 1},
            room=48,
        )
        up_sums.append(sums)
        order.after(sums)
        if chunk < PLAIN:
            flow = core_flow(grad_own, grad_other)
            plain.append(flow)
        else:
            flow = sum_flow(MLP_WAYS, lambda grad_own=grad_own: grad_own, grad_other)
            flows.append(flow)
        order.tick(*plain, *flows)

    plain_sums = lax.psum([order.results[flow] for flow in plain], "dp")

    reach = 768
    turns = ff // reach
    every = lambda s, c: (0, 0, 0)
    tail = lambda first: lambda s, c: (jnp.maximum(s - first, 0), 0, 0)
    tail_local = lambda first: lambda s, c: (c[0] * images + jnp.maximum(s - first, 0), 0, 0)

    def image_spec(first, where=tail):
        return pl.BlockSpec((1, seq, dim), where(first))

    def rows_of(part, size):
        if part == 0:
            return lambda s, c: jnp.minimum(s, size - 1)
        return lambda s, c: jnp.clip(s - size, 0, size - 1)

    span_spec = pl.BlockSpec(
        (1, reach, count),
        lambda s, c: (jnp.minimum(s // turns, 1), jnp.where(s < 2 * turns, s % turns, turns - 1), 0),
    )
    grad_residual, grad_attn, mid_sums = run_kernel(
        functools.partial(norm_back_kernel, turns, images),
        order.sc,
        [back] + wu + [residual, cotangent, modulation, attn_out],
        [
            span_spec,
            pl.BlockSpec((dim, reach), lambda s, c: (0, rows_of(0, turns)(s, c))),
            pl.BlockSpec((dim, reach), lambda s, c: (0, rows_of(1, turns)(s, c))),
            image_spec(2 * turns),
            image_spec(2 * turns, tail_local),
            pl.BlockSpec((1, 6, dim), tail_local(2 * turns)),
            image_spec(2 * turns),
        ],
        [image_spec(2 * turns)] * 2 + [pl.BlockSpec((1, 4, dim), tail(2 * turns))],
        [token_f, token_b, shape_of((images, 4, dim), f32)],
        (2 * turns + images,),
        60,
        scratch=[pltpu.VMEM((count, dim), f32)],
        room=44,
    )
    order.after(mid_sums)
    order.tick(*flows)
    pieces = 2
    each = images // pieces
    grad_qkv = []
    for piece in range(pieces):
        there = lambda i, s, piece=piece: (piece * each + i, 0, 0)
        (grad_piece,) = run_kernel(
            functools.partial(back_kernel, 2),
            order.sc,
            [grad_attn, qkv, prob] + wp,
            [
                pl.BlockSpec((1, seq, dim), there),
                pl.BlockSpec((1, 6 * cols, seq), there),
                pl.BlockSpec((1, 2 * heads, seq, seq), lambda i, s, piece=piece: (piece * each + i, 0, 0, 0)),
            ]
            + [whole_block(a) for a in wp],
            [qkv_spec],
            [shape_of((each, 6 * cols, seq), bf16)],
            (each,),
            60,
            scratch=[pltpu.VMEM((2 * cols, seq), bf16)],
            room=40,
        )
        grad_qkv.append(grad_piece)
        order.after(grad_piece)
        order.tick(*flows)

    attn_per = 4 * cols // 16
    qv_sums = [None, None]

    def attn_part(part):
        grads, sums = run_kernel(
            functools.partial(attn_grad_kernel, pieces, attn_per),
            order.sc,
            grad_qkv + [mixed, normed, grad_attn],
            [
                pl.BlockSpec((each, cols, seq), lambda s, c: (0, 3 * part + jnp.minimum(s, 2), 0))
                for _ in range(pieces)
            ]
            + [pl.BlockSpec((images, cols, seq), lambda s, c: (0, part, 0))]
            + [whole_block(normed), whole_block(grad_attn)],
            [
                pl.BlockSpec((16, attn_per, dim), every),
                pl.BlockSpec((1, 8, cols), lambda s, c: (jnp.minimum(s, 2), 0, 0)),
            ],
            [shape_of((16, attn_per, dim), bf16), shape_of((3, 8, cols), f32)],
            (4,),
            60,
            room=40,
        )
        qv_sums[part] = sums
        order.after(sums)
        return grads

    grad_other = attn_part(1)
    made = []
    last = sum_flow(ATTN_WAYS, lambda: made[0], grad_other)
    order.tick(last, *flows)
    made.append(attn_part(0))
    order.tick(last, *flows)

    first_spec = lambda part: pl.BlockSpec((cols, dim), lambda s, c: (rows_of(part, 3)(s, c), 0))
    grad_tokens, grad_own_tokens, low_sums = run_kernel(
        functools.partial(first_back_kernel, pieces, images),
        order.sc,
        grad_qkv + wq + [tokens, modulation, grad_residual],
        [pl.BlockSpec((each, cols, seq), lambda s, c: (0, jnp.minimum(s, 5), 0)) for _ in range(pieces)]
        + [first_spec(0), first_spec(1)]
        + [image_spec(6, tail_local), pl.BlockSpec((1, 6, dim), tail_local(6)), image_spec(6)],
        [image_spec(6, tail_local), image_spec(6), pl.BlockSpec((1, 2, dim), tail(6))],
        [shape_of((slots, seq, dim), f32), token_f, shape_of((images, 2, dim), f32)],
        (6 + images,),
        60,
        scratch=[pltpu.VMEM((count, dim), f32)],
        room=40,
    )
    order.after(low_sums)
    order.tick(last, *flows)
    other_tokens = swap_cores(grad_own_tokens)
    down_spec = lambda part: pl.BlockSpec((reach, dim), lambda s, c: (rows_of(part, turns)(s, c), 0))
    output, own_output, gate_sums = run_kernel(
        functools.partial(output_kernel, turns, images),
        order.sc,
        [act] + wd + [residual, cotangent, modulation, down_bias],
        [
            span_spec,
            down_spec(0),
            down_spec(1),
            image_spec(2 * turns),
            image_spec(2 * turns, tail_local),
            pl.BlockSpec((1, 6, dim), tail_local(2 * turns)),
            whole_block(down_bias),
        ],
        [image_spec(2 * turns, tail_local), image_spec(2 * turns), pl.BlockSpec((1, 1, dim), tail(2 * turns))],
        [shape_of((slots, seq, dim), bf16), token_b, shape_of((images, 1, dim), f32)],
        (2 * turns + images,),
        60,
        scratch=[pltpu.VMEM((count, dim), f32)],
        room=40,
    )
    order.after(gate_sums)
    order.tick(last, *flows)
    other_output = swap_cores(own_output)

    grad_modulation = jnp.concatenate([low_sums, mid_sums[:, 2:3], mid_sums[:, 0:2], gate_sums], axis=1)
    grad_modulation = grad_modulation.reshape(images, 6 * dim).astype(bf16)
    bias_sums = [
        jnp.concatenate(
            [qv_sums[part][0, 0:1], qv_sums[part][2, 0:1]] + [sums[part, 0:1] for sums in up_sums], axis=1
        )
        for part in range(2)
    ]
    shared = jnp.concatenate(
        [
            jnp.sum(mid_sums[:, 3], axis=0, keepdims=True),
            jnp.sum(down_sums[:, 0], axis=0, keepdims=True),
            jnp.zeros((1, own_cols - 2 * dim), f32),
        ],
        axis=1,
    )
    halves = grad_modulation.reshape(images, 2, own_cols)
    kept = lax.dynamic_index_in_dim(halves, core, 1, keepdims=False)
    given = lax.dynamic_index_in_dim(halves, 1 - core, 1, keepdims=False)
    got = swap_cores(jnp.concatenate([given.astype(f32), bias_sums[1], shared]))
    came = got[:images].astype(bf16)
    group_mod = jnp.where(
        core == 0, jnp.concatenate([kept, came]), jnp.concatenate([came, kept])
    )
    own_bias_sum = bias_sums[0] + got[images : images + 1]
    shared_sum = shared + got[images + 1 :]
    part_scaled = outer_cols(group_mod, w_mod).astype(bf16)
    grad_scaled = part_scaled.astype(f32) + swap_cores(part_scaled).astype(f32)
    _, silu_back = jax.vjp(jax.nn.silu, cond_f)
    grad_condition = silu_back(grad_scaled)[0]
    wide_scaled = jnp.pad(scaled.reshape(-1), (0, 3 * own_cols - slots * dim)).reshape(3, own_cols)
    packed_rows = jnp.concatenate(
        [group_mod, own_bias_sum.astype(bf16), shared_sum.astype(bf16), wide_scaled]
    )
    small = rows_flow(packed_rows)
    order.tick(last, *flows, small)
    output = fill_other(output, order.fence(other_output), core)
    order.after(output[0, 0, :1])

    def cuts(ways):
        return tuple((way[0], lo, hi) for lo, hi, way in ways)

    order.tick(last, *flows, small)
    grad_tokens = fill_other(grad_tokens, order.fence(other_tokens), core)
    order.after(grad_tokens[0, 0, :1])
    order.tick(last, *flows, small)
    all_rows = order.finish(small).reshape(16, slots + 5, own_cols)
    all_mod = all_rows[:, :slots].reshape(-1, own_cols)
    all_scaled = all_rows[:, slots + 2 :].reshape(16, -1)[:, : slots * dim].reshape(-1, dim)
    grad_w_mod = inner_rows(all_scaled, all_mod)
    grad_b_mod = jnp.sum(all_mod.astype(f32), axis=0)
    bias_total = jnp.sum(all_rows[:, slots : slots + 2].astype(f32), axis=0)
    grad_b_qv = bias_total[0, : 2 * cols].reshape(2, cols)
    grad_b_up = bias_total[0, 2 * cols :]
    grad_b_proj = bias_total[1, :dim]
    grad_b_down = bias_total[1, dim : 2 * dim]
    order.after((grad_w_mod[0, :1], grad_b_mod[:1], bias_total[0, :1]))
    order.tick(last, *flows)
    grad_w_down = grad_w_up = jnp.zeros((8, 128), f32)

    def final_mlp(chunk, body, args):
        nonlocal grad_w_down, grad_w_up
        spot = len(args) + 1
        grad_w_down, grad_w_up, mark = run_kernel(
            body,
            order.sc,
            list(args) + [grad_w_down, grad_w_up],
            [
                whole_block(a) if a.shape[0] == 8 else pl.BlockSpec((16 // steps,) + a.shape[1:], lambda s, c: (s, 0, 0))
                for a in args
            ]
            + [anywhere, anywhere],
            [
                pl.BlockSpec((block, dim), lambda s, c: (chunk * steps + s, 0)),
                pl.BlockSpec((dim, block), lambda s, c: (0, chunk * steps + s)),
                pl.BlockSpec((8, 128), lambda s, c: (0, 0)),
            ],
            [shape_of((ff, dim), f32), shape_of((dim, ff), f32), shape_of((8, 128), f32)],
            (steps,),
            2,
            scratch=[pltpu.VMEM((block, dim), f32)],
            alias=None if spot == len(args) + 1 and grad_w_down.shape[0] == 8 else {spot: 0, spot + 1: 1},
            room=32,
        )
        order.after(mark)

    for chunk, flow in enumerate(flows):
        body = functools.partial(final_mlp_kernel, cuts(MLP_WAYS), per)
        final_mlp(PLAIN + chunk, body, order.finish(flow))
        order.tick(last)
    args = order.finish(last)
    grad_qkv_rows, grad_w_proj = run_kernel(
        functools.partial(final_attn_kernel, cuts(ATTN_WAYS), attn_per),
        order.sc,
        list(args),
        [whole_block(a) for a in args],
        [
            pl.BlockSpec((cols, dim), lambda s, c: (jnp.minimum(s, 2), 0)),
            pl.BlockSpec((cols, dim), lambda s, c: (0, 0)),
        ],
        [shape_of((3 * cols, dim), f32), shape_of((cols, dim), f32)],
        (4,),
        2,
        room=32,
    )
    grad_w_qkv = jnp.transpose(grad_qkv_rows.reshape(3, cols, dim), (2, 0, 1))
    order.after(grad_w_proj[0, :1])
    for chunk, summed in enumerate(plain_sums):
        final_mlp(chunk, functools.partial(final_plain_kernel, per), [summed])
    return (
        output,
        grad_tokens,
        grad_condition,
        grad_w_qkv,
        grad_b_qv,
        grad_w_proj,
        grad_b_proj,
        grad_w_up,
        grad_b_up,
        grad_w_down,
        grad_b_down,
        grad_w_mod,
        grad_b_mod,
    )


def layer_norm(values):
    center = values - jnp.mean(values, axis=-1, keepdims=True)
    return center * lax.rsqrt(jnp.mean(center * center, axis=-1, keepdims=True) + epsilon)


def modulate(values, shift_part, scale_part):
    return layer_norm(values) * (1.0 + scale_part) + shift_part


def gelu_tanh(values):
    return (
        0.5
        * values
        * (1.0 + jnp.tanh(0.7978845608028654 * (values + 0.044715 * values * values * values)))
    )


def inner_rows(left, right):
    return lax.dot_general(
        left, right, (((0,), (0,)), ((), ())), preferred_element_type=jnp.float32
    )


def outer_cols(left, right):
    return lax.dot_general(
        left, right, (((1,), (1,)), ((), ())), preferred_element_type=jnp.float32
    )


def attention_forward(query_rows, key_rows, value_rows):
    factor = HEAD_DIM ** (-0.5)
    scores = (
        jnp.einsum("bqhd,bkhd->bhqk", query_rows, key_rows, preferred_element_type=jnp.float32)
        * factor
    )
    row_max = jnp.max(scores, axis=-1, keepdims=True)
    row_total = jnp.sum(jnp.exp(scores - row_max), axis=-1, keepdims=True)
    logsum = row_max + jnp.log(row_total)
    prob_b = jnp.exp(scores - logsum).astype(jnp.bfloat16)
    mixed_out = jnp.einsum(
        "bhqk,bkhd->bqhd", prob_b, value_rows, preferred_element_type=jnp.float32
    )
    return (mixed_out, logsum)


def attention_backward(query_rows, key_rows, value_rows, logsum, grad_mixed):
    factor = HEAD_DIM ** (-0.5)
    scores = (
        jnp.einsum("bqhd,bkhd->bhqk", query_rows, key_rows, preferred_element_type=jnp.float32)
        * factor
    )
    prob_f = jnp.exp(scores - logsum)
    prob_b = prob_f.astype(jnp.bfloat16)
    grad_prob = jnp.einsum(
        "bqhd,bkhd->bhqk", grad_mixed, value_rows, preferred_element_type=jnp.float32
    )
    row_delta = jnp.sum(prob_f * grad_prob, axis=-1, keepdims=True)
    grad_scores = (prob_f * (grad_prob - row_delta)).astype(jnp.bfloat16)
    grad_query = (
        jnp.einsum("bhqk,bkhd->bqhd", grad_scores, key_rows, preferred_element_type=jnp.float32)
        * factor
    )
    grad_key = (
        jnp.einsum("bhqk,bqhd->bkhd", grad_scores, query_rows, preferred_element_type=jnp.float32)
        * factor
    )
    grad_value = jnp.einsum(
        "bhqk,bqhd->bkhd", prob_b, grad_mixed, preferred_element_type=jnp.float32
    )
    return (
        grad_query.astype(jnp.bfloat16),
        grad_key.astype(jnp.bfloat16),
        grad_value.astype(jnp.bfloat16),
    )


def forward(tokens_f, spans, weights, repeat):
    w_qkv, b_qv, w_proj, b_proj, w_up, b_up, w_down, b_down = weights
    shift_attn, scale_attn, gate_attn, shift_mlp, scale_mlp, gate_mlp = spans
    slot_count, seq_len, model_dim = tokens_f.shape
    row_count = slot_count * seq_len
    head_cols = w_qkv.shape[2]
    head_count = head_cols // HEAD_DIM
    shape_four = (slot_count, seq_len, head_count, HEAD_DIM)
    normed = (
        modulate(tokens_f, shift_attn, scale_attn)
        .astype(jnp.bfloat16)
        .reshape(row_count, model_dim)
    )
    projected = jnp.dot(
        normed, w_qkv.reshape(model_dim, 3 * head_cols), preferred_element_type=jnp.float32
    )
    qkv_bias = jnp.stack([b_qv[0], jnp.zeros_like(b_qv[0]), b_qv[1]]).astype(jnp.float32)
    projected = (projected.reshape(row_count, 3, head_cols) + qkv_bias).astype(jnp.bfloat16)
    query_rows = projected[:, 0].reshape(shape_four)
    key_rows = projected[:, 1].reshape(shape_four)
    value_rows = projected[:, 2].reshape(shape_four)
    mixed_out, logsum = attention_forward(query_rows, key_rows, value_rows)
    mixed_b = mixed_out.astype(jnp.bfloat16).reshape(row_count, head_cols)
    partial_value = jnp.dot(mixed_b, w_proj, preferred_element_type=jnp.float32)
    if repeat:
        summed = lax.psum(partial_value.astype(jnp.bfloat16), "mp").astype(jnp.float32)
    else:
        summed = lax.psum(partial_value.astype(jnp.bfloat16), "mp").astype(jnp.float32)
    attn_out = (summed + b_proj.astype(jnp.float32)).reshape(slot_count, seq_len, model_dim)
    residual = tokens_f + gate_attn * attn_out
    normed_mlp = (
        modulate(residual, shift_mlp, scale_mlp).astype(jnp.bfloat16).reshape(row_count, model_dim)
    )
    hidden = jnp.dot(normed_mlp, w_up, preferred_element_type=jnp.float32) + b_up.astype(
        jnp.float32
    )
    act_bf = gelu_tanh(hidden).astype(jnp.bfloat16)
    partial_mlp = jnp.dot(act_bf, w_down, preferred_element_type=jnp.float32)
    if repeat:
        summed_mlp = lax.psum(partial_mlp.astype(jnp.bfloat16), "mp").astype(jnp.float32)
    else:
        summed_mlp = lax.psum(partial_mlp.astype(jnp.bfloat16), "mp").astype(jnp.float32)
    mlp_out = (summed_mlp + b_down.astype(jnp.float32)).reshape(slot_count, seq_len, model_dim)
    output = residual + gate_mlp * mlp_out
    return {
        "normed": normed,
        "query_rows": query_rows,
        "key_rows": key_rows,
        "value_rows": value_rows,
        "logsum": logsum,
        "mixed_b": mixed_b,
        "attn_out": attn_out,
        "residual": residual,
        "normed_mlp": normed_mlp,
        "hidden": hidden,
        "act_bf": act_bf,
        "mlp_out": mlp_out,
        "output": output,
    }


def image_pass(tokens_f, grad_out, spans, weights):
    w_qkv, b_qv, w_proj, b_proj, w_up, b_up, w_down, b_down = weights
    shift_attn, scale_attn, gate_attn, shift_mlp, scale_mlp, gate_mlp = spans
    slot_count, seq_len, model_dim = tokens_f.shape
    row_count = slot_count * seq_len
    head_cols = w_qkv.shape[2]
    head_count = head_cols // HEAD_DIM
    kept_fwd = forward(tokens_f, spans, weights, False)
    out_one = kept_fwd["output"]
    stored = forward(tokens_f, spans, weights, True)
    grad_gate_mlp = jnp.sum(grad_out * stored["mlp_out"], axis=1)
    grad_mlp = (gate_mlp * grad_out).astype(jnp.bfloat16).reshape(row_count, model_dim)
    grad_b_down = jnp.sum(grad_mlp.astype(jnp.float32), axis=0)
    grad_w_down = inner_rows(stored["act_bf"], grad_mlp)
    grad_act = outer_cols(grad_mlp, w_down)
    gelu_value, gelu_back = jax.vjp(gelu_tanh, stored["hidden"])
    grad_hidden = gelu_back(grad_act)[0].astype(jnp.bfloat16)
    grad_b_up = jnp.sum(grad_hidden.astype(jnp.float32), axis=0)
    grad_w_up = inner_rows(stored["normed_mlp"], grad_hidden)
    part_normed_mlp = outer_cols(grad_hidden, w_up)
    grad_normed_mlp = (
        lax.psum(part_normed_mlp.astype(jnp.bfloat16), "mp")
        .astype(jnp.float32)
        .reshape(slot_count, seq_len, model_dim)
    )
    norm_value, norm_back = jax.vjp(modulate, stored["residual"], shift_mlp, scale_mlp)
    grad_resid_norm, grad_shift_mlp, grad_scale_mlp = norm_back(grad_normed_mlp)
    grad_residual = grad_out + grad_resid_norm
    grad_gate_attn = jnp.sum(grad_residual * stored["attn_out"], axis=1)
    grad_attn = (gate_attn * grad_residual).astype(jnp.bfloat16).reshape(row_count, model_dim)
    grad_b_proj = jnp.sum(grad_attn.astype(jnp.float32), axis=0)
    grad_w_proj = inner_rows(stored["mixed_b"], grad_attn)
    grad_mixed = (
        outer_cols(grad_attn, w_proj)
        .astype(jnp.bfloat16)
        .reshape(slot_count, seq_len, head_count, HEAD_DIM)
    )
    grad_query, grad_key, grad_value = attention_backward(
        stored["query_rows"], stored["key_rows"], stored["value_rows"], stored["logsum"], grad_mixed
    )
    grad_qkv = jnp.stack(
        [
            grad_query.reshape(row_count, head_cols),
            grad_key.reshape(row_count, head_cols),
            grad_value.reshape(row_count, head_cols),
        ],
        axis=1,
    )
    grad_b_qv = jnp.stack(
        [
            jnp.sum(grad_qkv[:, 0].astype(jnp.float32), axis=0),
            jnp.sum(grad_qkv[:, 2].astype(jnp.float32), axis=0),
        ]
    )
    grad_w_qkv = inner_rows(stored["normed"], grad_qkv)
    part_normed = outer_cols(
        grad_qkv.reshape(row_count, 3 * head_cols), w_qkv.reshape(model_dim, 3 * head_cols)
    )
    grad_normed = (
        lax.psum(part_normed.astype(jnp.bfloat16), "mp")
        .astype(jnp.float32)
        .reshape(slot_count, seq_len, model_dim)
    )
    first_value, first_back = jax.vjp(modulate, tokens_f, shift_attn, scale_attn)
    grad_tok_norm, grad_shift_attn, grad_scale_attn = first_back(grad_normed)
    grad_tok_one = grad_residual + grad_tok_norm
    grad_mod_one = jnp.concatenate(
        [
            grad_shift_attn[:, 0],
            grad_scale_attn[:, 0],
            grad_gate_attn,
            grad_shift_mlp[:, 0],
            grad_scale_mlp[:, 0],
            grad_gate_mlp,
        ],
        axis=1,
    )
    grad_terms = (
        grad_w_qkv,
        grad_b_qv,
        grad_w_proj,
        grad_b_proj,
        grad_w_up,
        grad_b_up,
        grad_w_down,
        grad_b_down,
    )
    return (out_one, grad_tok_one, grad_mod_one, grad_terms)


def run_layer(tokens, condition, cotangent, live_count, turns, weights, w_mod, b_mod):
    slot_count, seq_len, model_dim = tokens.shape
    cond_f = condition.astype(jnp.float32)
    scaled = jax.nn.silu(cond_f).astype(jnp.bfloat16)
    own_mod = jnp.dot(scaled, w_mod, preferred_element_type=jnp.float32) + b_mod.astype(jnp.float32)
    modulation = lax.all_gather(own_mod, "mp", axis=1, tiled=True)
    tokens_f = tokens.astype(jnp.float32)
    cot_f = cotangent.astype(jnp.float32)

    def image_step(slot_idx, carry):
        out_buf, grad_buf, mod_buf, grad_sums = carry
        live_flag = (slot_idx < live_count).astype(jnp.float32)
        tok_one = lax.dynamic_slice_in_dim(tokens_f, slot_idx, 1, 0)
        cot_one = lax.dynamic_slice_in_dim(cot_f, slot_idx, 1, 0) * live_flag
        mod_row = lax.dynamic_slice_in_dim(modulation, slot_idx, 1, 0)
        spans = [
            mod_row[:, None, part_idx * model_dim : (part_idx + 1) * model_dim]
            for part_idx in range(6)
        ]
        out_one, grad_tok_one, grad_mod_one, grad_terms = image_pass(
            tok_one, cot_one, spans, weights
        )
        out_one = (out_one * live_flag).astype(jnp.bfloat16)
        out_buf = lax.dynamic_update_slice_in_dim(out_buf, out_one, slot_idx, 0)
        grad_buf = lax.dynamic_update_slice_in_dim(grad_buf, grad_tok_one, slot_idx, 0)
        mod_buf = lax.dynamic_update_slice_in_dim(mod_buf, grad_mod_one, slot_idx, 0)
        grad_sums = tuple((total_a + term_b for total_a, term_b in zip(grad_sums, grad_terms)))
        return (out_buf, grad_buf, mod_buf, grad_sums)

    start_sums = tuple((jnp.zeros(weight_in.shape, jnp.float32) for weight_in in weights))
    start_state = (
        jnp.zeros(tokens.shape, jnp.bfloat16),
        jnp.zeros(tokens.shape, jnp.float32),
        jnp.zeros((slot_count, 6 * model_dim), jnp.float32),
        start_sums,
    )
    out_buf, grad_buf, mod_buf, grad_sums = lax.fori_loop(0, turns, image_step, start_state)
    grad_modulation = mod_buf.astype(jnp.bfloat16)
    own_cols = w_mod.shape[1]
    grad_own = lax.dynamic_slice_in_dim(
        grad_modulation, lax.axis_index("mp") * own_cols, own_cols, 1
    )
    part_scaled = outer_cols(grad_own, w_mod)
    grad_scaled = lax.psum(part_scaled.astype(jnp.bfloat16), "mp").astype(jnp.float32)
    silu_value, silu_back = jax.vjp(jax.nn.silu, cond_f)
    grad_condition = silu_back(grad_scaled)[0]
    return (out_buf, grad_buf, grad_condition, grad_sums, scaled, grad_own)


def on_device(
    tokens,
    condition,
    counts,
    w_qkv,
    b_qv,
    w_proj,
    b_proj,
    w_up,
    b_up,
    w_down,
    b_down,
    w_mod,
    b_mod,
    cotangent,
):
    slot_count, seq_len, model_dim = tokens.shape
    weights = (w_qkv, b_qv, w_proj, b_proj, w_up, b_up, w_down, b_down)
    own_count = counts[0]
    output, grad_tokens, grad_condition, grad_sums, scaled, grad_own = run_layer(
        tokens, condition, cotangent, own_count, slot_count, weights, w_mod, b_mod
    )
    (
        grad_w_qkv,
        grad_b_qv,
        grad_w_proj,
        grad_b_proj,
        grad_w_up,
        grad_b_up,
        grad_w_down,
        grad_b_down,
    ) = grad_sums
    grad_w_mod = inner_rows(scaled, grad_own)
    grad_b_mod = jnp.sum(grad_own.astype(jnp.float32), axis=0)
    (
        grad_w_qkv,
        grad_b_qv,
        grad_w_proj,
        grad_b_proj,
        grad_w_up,
        grad_b_up,
        grad_w_down,
        grad_b_down,
        grad_w_mod,
        grad_b_mod,
    ) = (
        lax.psum(grad_w_qkv.astype(jnp.bfloat16), "dp").astype(jnp.float32),
        lax.psum(grad_b_qv.astype(jnp.bfloat16), "dp").astype(jnp.float32),
        lax.psum(grad_w_proj.astype(jnp.bfloat16), "dp").astype(jnp.float32),
        lax.psum(grad_b_proj.astype(jnp.bfloat16), "dp").astype(jnp.float32),
        lax.psum(grad_w_up.astype(jnp.bfloat16), "dp").astype(jnp.float32),
        lax.psum(grad_b_up.astype(jnp.bfloat16), "dp").astype(jnp.float32),
        lax.psum(grad_w_down.astype(jnp.bfloat16), "dp").astype(jnp.float32),
        lax.psum(grad_b_down.astype(jnp.bfloat16), "dp").astype(jnp.float32),
        lax.psum(grad_w_mod.astype(jnp.bfloat16), "dp").astype(jnp.float32),
        lax.psum(grad_b_mod.astype(jnp.bfloat16), "dp").astype(jnp.float32),
    )
    return (
        output,
        grad_tokens,
        grad_condition,
        grad_w_qkv,
        grad_b_qv,
        grad_w_proj,
        grad_b_proj,
        grad_w_up,
        grad_b_up,
        grad_w_down,
        grad_b_down,
        grad_w_mod,
        grad_b_mod,
    )


def solution(mesh):
    placed = (
        P("dp", None, None),
        P("dp", None),
        P("dp"),
        P(None, None, "mp"),
        P(None, "mp"),
        P("mp", None),
        P(),
        P(None, "mp"),
        P("mp"),
        P("mp", None),
        P(),
        P(None, "mp"),
        P("mp"),
        P("dp", None, None),
    )
    fast = mesh.shape["dp"] == 16 and mesh.shape["mp"] == 2
    return jax.shard_map(
        fast_device if fast else on_device,
        mesh=mesh,
        in_specs=placed,
        out_specs=(
            P("dp", None, None),
            P("dp", None, None),
            P("dp", None),
            P(None, None, "mp"),
            P(None, "mp"),
            P("mp", None),
            P(),
            P(None, "mp"),
            P("mp"),
            P("mp", None),
            P(),
            P(None, "mp"),
            P("mp"),
        ),
        check_vma=False,
    )
```

```python
import functools

import jax
import jax.numpy as jnp
from jax import lax
from jax.experimental import pallas as pl
from jax.experimental.pallas import tpu as pltpu
from jax.sharding import PartitionSpec as P

HEAD_DIM = 72


epsilon = 1e-06

f32 = jnp.float32
bf16 = jnp.bfloat16


def dot_nn(left, right):
    return lax.dot_general(left, right, (((1,), (0,)), ((), ())), preferred_element_type=f32)


def dot_nt(left, right):
    return lax.dot_general(left, right, (((1,), (1,)), ((), ())), preferred_element_type=f32)


def dot_tn(left, right):
    return lax.dot_general(left, right, (((0,), (0,)), ((), ())), preferred_element_type=f32)


def normalize(values):
    center = values - jnp.mean(values, axis=-1, keepdims=True)
    recip = lax.rsqrt(jnp.mean(center * center, axis=-1, keepdims=True) + epsilon)
    return center * recip, recip


def norm_pullback(grad_normed, unit, recip, scale_row):
    scaled_grad = grad_normed * (1.0 + scale_row)
    mean_grad = jnp.mean(scaled_grad, axis=-1, keepdims=True)
    mean_unit = jnp.mean(scaled_grad * unit, axis=-1, keepdims=True)
    return recip * (scaled_grad - mean_grad - unit * mean_unit)


def column(row):
    return jnp.broadcast_to(row[...].astype(f32), (8, row.shape[1])).T[:, 0:1]


def token_sum(values):
    return jnp.sum(values, axis=0, keepdims=True)


def attention_kernel(parts, own_images, sc, tok, cot, mod, b_proj, *refs):
    w_qkv, w_proj, bias = refs[:parts], refs[parts : 2 * parts], refs[2 * parts : 3 * parts]
    qkv, prob, mixed, attn_out, residual, normed_mlp, normed, grad_mlp, down_sums = refs[3 * parts :]
    image = sc[0] * own_images + pl.program_id(0)
    live = jnp.where(image < sc[1], 1.0, 0.0).astype(f32)
    unit, _ = normalize(tok[0].astype(f32))
    normed[0] = (unit * (1.0 + mod[0, 1:2, :]) + mod[0, 0:1, :]).astype(bf16)
    grad = (mod[0, 5:6, :] * (cot[0].astype(f32) * live)).astype(bf16)
    grad_mlp[0] = grad
    down_sums[0] = token_sum(grad.astype(f32))
    cols = w_proj[0].shape[0]
    pairs = cols // (2 * HEAD_DIM)
    span = 2 * HEAD_DIM
    factor = HEAD_DIM ** (-0.5)
    rows = normed[0]
    total = b_proj[...]
    for part in range(parts):
        base = part * 3 * cols
        shift = bias[part][...].astype(f32).T
        for proj in range(3):
            lo = proj * cols
            value = dot_nt(w_qkv[part][lo : lo + cols, :], rows)
            if proj != 1:
                value = value + shift[:, proj // 2 : proj // 2 + 1]
            qkv[0, base + lo : base + lo + cols, :] = value.astype(bf16)

        def pair_step(pair, carry, base=base, part=part):
            at = pl.multiple_of(base + pair * span, 16)
            query = qkv[0, pl.ds(at, span), :].astype(f32)
            key = qkv[0, pl.ds(at + cols, span), :].astype(f32)
            value = qkv[0, pl.ds(at + 2 * cols, span), :].astype(f32)
            outs = []
            for one in range(2):
                rows_of = slice(one * HEAD_DIM, (one + 1) * HEAD_DIM)
                scores = dot_tn(key[rows_of].astype(bf16), query[rows_of].astype(bf16)) * factor
                raised = jnp.exp(scores - jnp.max(scores, axis=0, keepdims=True))
                share = 1.0 / jnp.sum(raised, axis=0, keepdims=True)
                prob_b = (raised * share).astype(bf16)
                prob[0, part * 2 * pairs + 2 * pair + one] = prob_b
                outs.append(dot_nn(value[rows_of].astype(bf16), prob_b))
            to = pl.multiple_of(part * cols + pair * span, 16)
            mixed[0, pl.ds(to, span), :] = jnp.concatenate(outs, axis=0).astype(bf16)
            return carry

        lax.fori_loop(0, pairs, pair_step, 0, unroll=True)
        total = total + dot_tn(mixed[0, part * cols : (part + 1) * cols, :], w_proj[part][...])
    attn_out[0] = total
    summed = tok[0].astype(f32) + mod[0, 2:3, :] * total
    residual[0] = summed
    unit, _ = normalize(summed)
    normed_mlp[0] = (unit * (1.0 + mod[0, 4:5, :]) + mod[0, 3:4, :]).astype(bf16)


def mlp_kernel(per, jobs, sc, rows, grad_mlp, *refs):
    count = len(jobs)
    weights = [refs[3 * k : 3 * k + 3] for k in range(count)]
    refs = refs[3 * count :]
    came = []
    for _, summed in jobs:
        came.append(refs[0] if summed else None)
        refs = refs[1:] if summed else refs
    act, back = refs[2], refs[3]
    grads, sums = refs[4 : 4 + count], refs[4 + count :]
    job, step = pl.program_id(0), pl.program_id(1)
    for k in range(count):

        @pl.when(job == k)
        def _(k=k):
            mlp_block(
                per, jobs[k][0], step, sc, rows, grad_mlp, *weights[k], act, back, grads[k], sums[k], came[k]
            )


def mlp_block(per, natural, step, sc, rows, grad_mlp, w_up, w_down, bias, act, back, grads, sums, came):
    here = w_down.shape[0] // per
    hidden = lax.dot_general(
        w_up[...], rows[...], (((0,), (1,)), ((), ())), preferred_element_type=f32
    ) + column(bias)
    square = hidden * hidden
    bend = jnp.tanh(0.7978845608028654 * hidden * (1.0 + 0.044715 * square))
    half = 0.5 * (1.0 + bend)
    act_b = (hidden * half).astype(bf16)
    slope = half + 0.5 * hidden * (1.0 - bend * bend) * (
        0.7978845608028654 * (1.0 + 3.0 * 0.044715 * square)
    )
    back_b = (dot_nt(w_down[...], grad_mlp[...]) * slope).astype(bf16)
    act[0] = act_b
    back[0] = back_b
    sums[...] = dot_nt(jnp.ones((8, rows.shape[0]), bf16), back_b)
    for lo_row, left, right in ((0, act_b, grad_mlp), (per, back_b, rows)):
        grad = dot_nn(left, right[...])
        for piece in range(here):
            value = grad[piece * per : (piece + 1) * per]
            if natural:
                if came is not None:
                    value = value + came[piece, lo_row : lo_row + per, :].astype(f32)
                grads[piece, lo_row : lo_row + per, :] = value.astype(bf16)
            else:
                at = jnp.bitwise_xor(step * here + piece, sc[2])
                grads[at, lo_row : lo_row + per, :] = value.astype(bf16)


def grow(total, part_steps, left, rights, dims):
    step = pl.program_id(0)

    def term(right):
        return lax.dot_general(left, right[...], (dims, ((), ())), preferred_element_type=f32)

    @pl.when(step == 0)
    def _():
        total[...] = term(rights[0])

    @pl.when(jnp.logical_and(step > 0, step < part_steps))
    def _():
        total[...] += term(rights[0])

    @pl.when(jnp.logical_and(step >= part_steps, step < 2 * part_steps))
    def _():
        total[...] += term(rights[1])


def norm_back_kernel(
    part_steps, own_images, sc, back, w_up0, w_up1, residual, cot, mod, attn_out,
    grad_residual, grad_attn, sums, total
):
    grow(total, part_steps, back[0], (w_up0, w_up1), ((0,), (1,)))
    one = pl.program_id(0) - 2 * part_steps
    seq = residual.shape[1]

    @pl.when(one >= 0)
    def _():
        live = jnp.where(sc[0] * own_images + one < sc[1], 1.0, 0.0).astype(f32)
        grad_normed = total[pl.ds(pl.multiple_of(one * seq, seq), seq), :]
        unit, recip = normalize(residual[0])
        sums[0, 0:1, :] = token_sum(grad_normed)
        sums[0, 1:2, :] = token_sum(grad_normed * unit)
        grad_res = cot[0].astype(f32) * live + norm_pullback(grad_normed, unit, recip, mod[0, 4:5, :])
        grad_residual[0] = grad_res
        sums[0, 2:3, :] = token_sum(grad_res * attn_out[0])
        grad_att = (mod[0, 2:3, :] * grad_res).astype(bf16)
        grad_attn[0] = grad_att
        sums[0, 3:4, :] = token_sum(grad_att.astype(f32))


def back_kernel(parts, sc, grad_attn, qkv, prob, *refs):
    w_proj = refs[:parts]
    grad_qkv, grad_mixed = refs[parts:]
    cols = w_proj[0].shape[0]
    pairs = cols // (2 * HEAD_DIM)
    span = 2 * HEAD_DIM
    factor = HEAD_DIM ** (-0.5)
    grad_att = grad_attn[0]
    for part in range(parts):
        base = part * 3 * cols
        grad_mixed[part * cols : (part + 1) * cols, :] = dot_nt(w_proj[part][...], grad_att).astype(bf16)

        def pair_step(pair, carry, base=base, part=part):
            at = pl.multiple_of(base + pair * span, 16)
            query = qkv[0, pl.ds(at, span), :].astype(f32)
            key = qkv[0, pl.ds(at + cols, span), :].astype(f32)
            value = qkv[0, pl.ds(at + 2 * cols, span), :].astype(f32)
            grads = grad_mixed[pl.ds(pl.multiple_of(part * cols + pair * span, 16), span), :].astype(f32)
            to_query, to_key, to_value = [], [], []
            for one in range(2):
                rows_of = slice(one * HEAD_DIM, (one + 1) * HEAD_DIM)
                prob_b = prob[0, part * 2 * pairs + 2 * pair + one]
                prob_f = prob_b.astype(f32)
                grad_b = grads[rows_of].astype(bf16)
                grad_prob = dot_tn(value[rows_of].astype(bf16), grad_b)
                delta = jnp.sum(prob_f * grad_prob, axis=0, keepdims=True)
                grad_scores = (prob_f * (grad_prob - delta)).astype(bf16)
                to_query.append(dot_nn(key[rows_of].astype(bf16), grad_scores) * factor)
                to_key.append(dot_nt(query[rows_of].astype(bf16), grad_scores) * factor)
                to_value.append(dot_nt(grad_b, prob_b))
            grad_qkv[0, pl.ds(at, span), :] = jnp.concatenate(to_query, axis=0).astype(bf16)
            grad_qkv[0, pl.ds(at + cols, span), :] = jnp.concatenate(to_key, axis=0).astype(bf16)
            grad_qkv[0, pl.ds(at + 2 * cols, span), :] = jnp.concatenate(to_value, axis=0).astype(bf16)
            return carry

        lax.fori_loop(0, pairs, pair_step, 0, unroll=True)


def attn_grad_kernel(pieces, per, sc, *refs):
    grad_qkv, mixed, normed, grad_attn = refs[:pieces], refs[pieces], refs[pieces + 1], refs[pieces + 2]
    grads, sums = refs[pieces + 3 :]
    step = pl.program_id(0)
    here = mixed.shape[1] // per
    images = mixed.shape[0]
    each = images // pieces

    def spread(total):
        total = total.astype(bf16)
        for piece in range(here):
            at = jnp.bitwise_xor(step * here + piece, sc[2])
            grads[at] = total[piece * per : (piece + 1) * per]

    @pl.when(step < 3)
    def _():
        ones = jnp.ones((8, mixed.shape[2]), bf16)
        total = count = None
        for image in range(images):
            left = grad_qkv[image // each][image % each]
            term, one = dot_nn(left, normed[image]), dot_nt(ones, left)
            total = term if image == 0 else total + term
            count = one if image == 0 else count + one
        sums[0] = count
        spread(total)

    @pl.when(step == 3)
    def _():
        total = dot_nn(mixed[0], grad_attn[0])
        for image in range(1, images):
            total = total + dot_nn(mixed[image], grad_attn[image])
        spread(total)


def first_back_kernel(pieces, images, sc, *refs):
    grad_qkv = refs[:pieces]
    w_qkv0, w_qkv1, tok, mod, grad_residual = refs[pieces : pieces + 5]
    grad_tokens, grad_own, sums, total = refs[pieces + 5 :]
    step = pl.program_id(0)
    each = images // pieces
    seq = tok.shape[1]

    def add(w_qkv, fresh):
        for one in range(images):
            term = dot_tn(grad_qkv[one // each][one % each], w_qkv[...])
            if fresh:
                total[one * seq : (one + 1) * seq, :] = term
            else:
                total[one * seq : (one + 1) * seq, :] += term

    @pl.when(step == 0)
    def _():
        add(w_qkv0, True)

    @pl.when(jnp.logical_and(step > 0, step < 3))
    def _():
        add(w_qkv0, False)

    @pl.when(jnp.logical_and(step >= 3, step < 6))
    def _():
        add(w_qkv1, False)

    @pl.when(step >= 6)
    def _():
        grad_normed = total[pl.ds(pl.multiple_of((step - 6) * seq, seq), seq), :]
        unit, recip = normalize(tok[0].astype(f32))
        sums[0, 0:1, :] = token_sum(grad_normed)
        sums[0, 1:2, :] = token_sum(grad_normed * unit)
        grad = grad_residual[0] + norm_pullback(grad_normed, unit, recip, mod[0, 1:2, :])
        grad_tokens[0] = grad
        grad_own[0] = grad


def output_kernel(
    part_steps, own_images, sc, act, w_down0, w_down1, residual, cot, mod, b_down, output, own, sums, total
):
    grow(total, part_steps, act[0], (w_down0, w_down1), ((0,), (0,)))
    one = pl.program_id(0) - 2 * part_steps
    seq = residual.shape[1]

    @pl.when(one >= 0)
    def _():
        live = jnp.where(sc[0] * own_images + one < sc[1], 1.0, 0.0).astype(f32)
        mlp_out = total[pl.ds(pl.multiple_of(one * seq, seq), seq), :] + b_down[...]
        sums[0] = token_sum((cot[0].astype(f32) * live) * mlp_out)
        rows = ((residual[0] + mod[0, 5:6, :] * mlp_out) * live).astype(bf16)
        output[0] = rows
        own[0] = rows


def final_piece(sc, halves, piece, store):
    rel = jnp.bitwise_xor(piece, sc[2])
    for low, high, bit, lo, hi in halves:
        index = ((rel >> (bit + 1)) << bit) | (rel & ((1 << bit) - 1))
        side = (rel >> bit) & 1

        @pl.when(side == 0)
        def _(low=low, index=index, lo=lo, hi=hi):
            store(low[index].astype(f32), lo, hi)

        @pl.when(side == 1)
        def _(high=high, index=index, lo=lo, hi=hi):
            store(high[index].astype(f32), lo, hi)


def final_mlp_kernel(cuts, per, sc, *refs):
    count = 2 * len(cuts)
    arrays, (_, _, down, up, mark, turned) = refs[:count], refs[count:]
    here = down.shape[0] // per
    halves = [(arrays[2 * k], arrays[2 * k + 1]) + cut for k, cut in enumerate(cuts)]
    for piece in range(here):

        def store(value, lo, hi, piece=piece):
            down[piece * per : (piece + 1) * per, lo:hi] = value[0:per]
            turned[piece * per : (piece + 1) * per, lo:hi] = value[per : 2 * per]

        final_piece(sc, halves, pl.program_id(0) * here + piece, store)
    up[...] = turned[...].T
    mark[...] = jnp.zeros_like(mark)


def final_plain_kernel(per, sc, summed, down_in, up_in, down, up, mark, turned):
    for piece in range(summed.shape[0]):
        lo = piece * per
        down[lo : lo + per, :] = summed[piece, 0:per, :].astype(f32)
        turned[lo : lo + per, :] = summed[piece, per : 2 * per, :].astype(f32)
    up[...] = turned[...].T
    mark[...] = jnp.zeros_like(mark)


def final_attn_kernel(cuts, per, sc, *refs):
    count = 2 * len(cuts)
    arrays, (qkv, proj) = refs[:count], refs[count:]
    here = proj.shape[0] // per
    halves = [(arrays[2 * k], arrays[2 * k + 1]) + cut for k, cut in enumerate(cuts)]
    for target, wanted in ((qkv, True), (proj, False)):

        @pl.when((pl.program_id(0) < 3) == wanted)
        def _(target=target):
            for piece in range(here):

                def store(value, lo, hi, piece=piece):
                    target[piece * per : (piece + 1) * per, lo:hi] = value

                final_piece(sc, halves, pl.program_id(0) * here + piece, store)


def run_kernel(
    body, sc, args, in_specs, out_specs, out_shape, grid, micros, scratch=(), alias=None, room=60
):
    size = sum(a.size * a.dtype.itemsize for a in args) + sum(
        s.size * s.dtype.itemsize for s in out_shape
    )
    return pl.pallas_call(
        body,
        out_shape=out_shape,
        grid_spec=pltpu.PrefetchScalarGridSpec(
            num_scalar_prefetch=1,
            grid=grid,
            in_specs=in_specs,
            out_specs=out_specs,
            scratch_shapes=list(scratch),
        ),
        compiler_params=pltpu.CompilerParams(vmem_limit_bytes=room << 20),
        cost_estimate=pl.CostEstimate(
            flops=int(micros * 1.15e9), bytes_accessed=int(min(size, micros * 1e6)), transcendentals=0
        ),
        input_output_aliases=alias or {},
    )(sc, *args)


def whole_block(array):
    zeros = (0,) * array.ndim
    return pl.BlockSpec(array.shape, lambda *_: zeros, pipeline_mode=pl.Buffered(1))


def shape_of(dims, kind):
    return jax.ShapeDtypeStruct(dims, kind)


SWAP = [(0, 1), (1, 0)]


def swap_cores(value):
    return lax.ppermute(value, "mp", SWAP)


def bit_pairs(bit):
    return [(index, index ^ (1 << bit)) for index in range(16)]


MLP_WAYS = ((0, 640, (0, 1, 2, 3)), (640, 1152, (1, 0, 2, 3)))
ATTN_WAYS = ((0, 512, (0, 1, 2, 3)), (512, 896, (1, 0, 2, 3)), (896, 1152, (2, 3, 0, 1)))


def cut(array, bits, bit, side, cols=None):
    lo = [0] * array.ndim
    hi = list(array.shape)
    place = bits.index(bit)
    lo[place], hi[place] = side, side + 1
    if cols is not None:
        lo[-1], hi[-1] = cols
    out = lax.slice(array, lo, hi)
    return out.reshape(out.shape[:place] + out.shape[place + 1 :])


def left_bits(done):
    return [bit for bit in (3, 2, 1, 0) if bit not in done]


def exchange(values, bits):
    return [lax.ppermute(value, "dp", bit_pairs(bit)) for value, bit in zip(values, bits)]


def reduce_flow(ways, get_own, other):
    shape = (2, 2, 2, 2) + other.shape[1:]
    (other,) = yield [other]
    came = swap_cores(other)
    yield None
    own, came = yield [get_own(), came]
    firsts, seconds = [own.reshape(shape)] * len(ways), [came.reshape(shape)] * len(ways)
    routes = [way for _, _, way in ways]
    for stage in range(4):
        sends, keeps = [], []
        for (lo, hi, _), route, one, two in zip(ways, routes, firsts, seconds):
            bits = left_bits(route[:stage])
            cols = (lo, hi) if stage == 0 else None
            for side, into in ((1, sends), (0, keeps)):
                into.append(
                    cut(one, bits, route[stage], side, cols) + cut(two, bits, route[stage], side, cols)
                )
        if stage == 2 and routes[0][2:] == routes[1][2:]:
            sends = [jnp.concatenate(sends[:2], axis=-1)] + sends[2:]
            keeps = [jnp.concatenate(keeps[:2], axis=-1)] + keeps[2:]
            routes = [routes[0]] + routes[2:]
            ways = [(0, 0, way) for way in routes]
        sends, keeps = yield [sends, keeps]
        comes = exchange(sends, [route[stage] for route in routes])
        yield None
        firsts, seconds = yield [keeps, comes]
    return [one + two for one, two in zip(firsts, seconds)]


def gather_flow(ways, have):
    routes = [ways[0][2]] + [way for _, _, way in ways[2:]]
    middle = ways[0][1]
    known = [[] for _ in routes]
    (have,) = yield [have]
    comes = exchange(have, [route[3] for route in routes])
    yield None
    for stage in (2, 1, 0):
        have, comes = yield [have, comes]
        joined = []
        for route, bits, one, two in zip(routes, known, have, comes):
            bit = route[stage + 1]
            place = sum(1 for other in bits if other > bit)
            joined.append(jnp.stack([one, two], axis=place))
            bits.insert(place, bit)
        if stage == 1:
            joined = [joined[0][..., :middle], joined[0][..., middle:]] + joined[1:]
            routes = [way for _, _, way in ways]
            known = [list(known[0]), list(known[0])] + known[1:]
        (have,) = yield [joined]
        comes = exchange(have, [route[stage] for route in routes])
        yield None
    have, comes = yield [have, comes]
    return [part.reshape((8,) + part.shape[-2:]) for pair in zip(have, comes) for part in pair]


def sum_flow(ways, get_own, other):
    have = yield from reduce_flow(ways, get_own, other)
    return (yield from gather_flow(ways, have))


def swap_flow(other):
    (other,) = yield [other]
    came = swap_cores(other)
    yield None
    (came,) = yield [came]
    return came


def rows_flow(rows):
    for bit in (3, 2, 1, 0):
        (rows,) = yield [rows]
        came = lax.ppermute(rows, "dp", bit_pairs(bit))
        yield None
        rows, came = yield [rows, came]
        rows = jnp.concatenate([rows, came])
    return rows


class Order:
    def __init__(self, sc):
        self.sc = sc
        self.results = {}

    def fence(self, values):
        self.sc, values = lax.optimization_barrier((self.sc, values))
        return values

    def after(self, value):
        self.sc, _ = lax.optimization_barrier((self.sc, value))

    def tick(self, *flows):
        replies = {flow: None for flow in flows if flow not in self.results}
        while replies:
            wants = {}
            for flow, reply in replies.items():
                try:
                    want = flow.send(reply)
                except StopIteration as stop:
                    self.results[flow] = stop.value
                    continue
                if want is not None:
                    wants[flow] = want
            replies = dict(zip(wants, self.fence(list(wants.values())))) if wants else {}

    def finish(self, flow):
        while flow not in self.results:
            self.tick(flow)
        return self.results[flow]


CHUNKS = 3
PLAIN = 2


def fill_other(both, came, core):
    size = came.shape[0]
    return lax.dynamic_update_slice_in_dim(both, came, (1 - core) * size, 0)


def fast_device(
    tokens, condition, counts, w_qkv, b_qv, w_proj, b_proj, w_up, b_up, w_down, b_down, w_mod, b_mod,
    cotangent,
):
    slots, seq, dim = tokens.shape
    images = slots // 2
    count = images * seq
    cols = w_qkv.shape[2]
    ff = w_up.shape[1]
    own_cols = w_mod.shape[1]
    heads = cols // HEAD_DIM
    core = lax.axis_index("mp")
    order = Order(jnp.stack([core, counts[0], lax.axis_index("dp")]).astype(jnp.int32))

    qkv_rows = jnp.transpose(w_qkv, (1, 2, 0)).reshape(3 * cols, dim)
    wq = [qkv_rows, swap_cores(qkv_rows)]
    wp = [w_proj, swap_cores(w_proj)]
    qkv_bias = [b_qv, swap_cores(b_qv)]

    cond_f = condition.astype(f32)
    scaled = jax.nn.silu(cond_f).astype(bf16)
    own_mod = jnp.dot(scaled, w_mod, preferred_element_type=f32) + b_mod.astype(f32)
    other_mod = swap_cores(own_mod)
    sides = [jnp.where(core == side, own_mod, other_mod) for side in range(2)]
    modulation = jnp.concatenate(sides, axis=1).reshape(slots, 6, dim)
    proj_bias = b_proj.astype(f32)[None]
    down_bias = b_down.astype(f32)[None]

    late_up, late_down, late_bias = lax.optimization_barrier((wq[1], w_up, w_down, b_up, modulation))[1:4]
    wu = [w_up, swap_cores(late_up)]
    wd = [w_down, swap_cores(late_down)]
    up_bias = [b_up[None], swap_cores(late_bias[None])]

    local = lambda i, s: (s[0] * images + i, 0, 0)
    mine = lambda i, s: (i, 0, 0)
    tok_spec = pl.BlockSpec((1, seq, dim), local)
    own_spec = pl.BlockSpec((1, seq, dim), mine)
    mod_spec = pl.BlockSpec((1, 6, dim), local)
    row_spec = pl.BlockSpec((1, 1, dim), mine)
    qkv_spec = pl.BlockSpec((1, 6 * cols, seq), mine)
    prob_spec = pl.BlockSpec((1, 2 * heads, seq, seq), lambda i, s: (i, 0, 0, 0))
    mixed_spec = pl.BlockSpec((1, 2 * cols, seq), mine)
    token_f = shape_of((images, seq, dim), f32)
    token_b = shape_of((images, seq, dim), bf16)
    attn_args = wq + wp + qkv_bias
    qkv, prob, mixed, attn_out, residual, normed_mlp, normed, grad_mlp, down_sums = run_kernel(
        functools.partial(attention_kernel, 2, images),
        order.sc,
        [tokens, cotangent, modulation, proj_bias] + attn_args,
        [tok_spec, tok_spec, mod_spec, whole_block(proj_bias)] + [whole_block(a) for a in attn_args],
        [qkv_spec, prob_spec, mixed_spec] + [own_spec] * 5 + [row_spec],
        [
            shape_of((images, 6 * cols, seq), bf16),
            shape_of((images, 2 * heads, seq, seq), bf16),
            shape_of((images, 2 * cols, seq), bf16),
            token_f,
            token_f,
            token_b,
            token_b,
            token_b,
            shape_of((images, 1, dim), f32),
        ],
        (images,),
        45,
    )
    order.after(down_sums)

    rows_flat = normed_mlp.reshape(count, dim)
    grad_flat = grad_mlp.reshape(count, dim)
    width = ff // CHUNKS
    per = width // 16
    steps = 2
    block = width // steps
    anywhere = pl.BlockSpec(memory_space=pl.ANY)
    act = back = jnp.zeros((8, 128), bf16)
    up_sums = {}

    def mlp_call(jobs, came, micros):
        nonlocal act, back
        first = act.shape[0] == 8
        kinds = tuple((chunk < PLAIN, (chunk, part) in came) for chunk, part in jobs)

        def turn(k):
            return lambda p, s, c: jnp.clip((p - k) * steps + s, 0, steps - 1)

        def pick(values):
            return lambda p: sum(jnp.where(p == k, value, 0) for k, value in enumerate(values))

        parts = pick([part for _, part in jobs])
        starts = pick([chunk * steps for chunk, _ in jobs])
        spread = pl.BlockSpec((1, block, count), lambda p, s, c: (parts(p), starts(p) + s, 0))
        args, specs = [], []
        for k, (chunk, part) in enumerate(jobs):
            at = chunk * steps
            wide = lambda p, s, c, k=k, at=at: (0, at + turn(k)(p, s, c))
            tall = lambda p, s, c, k=k, at=at: (at + turn(k)(p, s, c), 0)
            args += [wu[part], wd[part], up_bias[part]]
            specs += [
                pl.BlockSpec((dim, block), wide),
                pl.BlockSpec((block, dim), tall),
                pl.BlockSpec((1, block), wide),
            ]
        grad_specs = []
        for k, (natural, _) in enumerate(kinds):
            own = lambda p, s, c, k=k: (turn(k)(p, s, c), 0, 0)
            fixed = lambda p, s, c: (0, 0, 0)
            grad_specs.append(
                pl.BlockSpec((16 // steps, 2 * per, dim), own)
                if natural
                else pl.BlockSpec((16, 2 * per, dim), fixed)
            )
        for k, job in enumerate(jobs):
            if job in came:
                args.append(came[job])
                specs.append(grad_specs[k])
        args += [act, back]
        spot = len(args) + 1
        outs = run_kernel(
            functools.partial(mlp_kernel, per, kinds),
            order.sc,
            [rows_flat, grad_flat] + args,
            [whole_block(rows_flat), whole_block(grad_flat)] + specs + [anywhere, anywhere],
            [spread, spread]
            + grad_specs
            + [pl.BlockSpec((8, block), lambda p, s, c, k=k: (0, turn(k)(p, s, c))) for k in range(len(jobs))],
            [shape_of((2, ff, count), bf16)] * 2
            + [shape_of((16, 2 * per, dim), bf16)] * len(jobs)
            + [shape_of((8, width), f32)] * len(jobs),
            (len(jobs), steps),
            micros,
            alias=None if first else {spot: 0, spot + 1: 1},
        )
        act, back = outs[:2]
        grads = outs[2 : 2 + len(jobs)]
        for job, sums in zip(jobs, outs[2 + len(jobs) :]):
            up_sums[job] = sums[0:1]
        order.after(outs[-1])
        return grads

    summed = range(PLAIN)
    swaps = [swap_flow(grad) for grad in mlp_call([(chunk, 1) for chunk in summed], {}, 26)]
    order.tick(*swaps)
    rest = [(chunk, part) for chunk in range(PLAIN, CHUNKS) for part in (1, 0)]
    grads = mlp_call(rest, {}, 26)
    flows = [
        sum_flow(MLP_WAYS, lambda own=own: own, other) for other, own in zip(grads[0::2], grads[1::2])
    ]
    order.tick(*swaps, *flows)
    came = {(chunk, 0): order.results[swap] for chunk, swap in zip(summed, swaps)}
    plain_sums = lax.psum(mlp_call([(chunk, 0) for chunk in summed], came, 26), "dp")
    order.tick(*flows)

    reach = 768
    turns = ff // reach
    every = lambda s, c: (0, 0, 0)
    tail = lambda first: lambda s, c: (jnp.maximum(s - first, 0), 0, 0)
    tail_local = lambda first: lambda s, c: (c[0] * images + jnp.maximum(s - first, 0), 0, 0)

    def image_spec(first, where=tail):
        return pl.BlockSpec((1, seq, dim), where(first))

    def rows_of(part, size):
        if part == 0:
            return lambda s, c: jnp.minimum(s, size - 1)
        return lambda s, c: jnp.clip(s - size, 0, size - 1)

    span_spec = pl.BlockSpec(
        (1, reach, count),
        lambda s, c: (jnp.minimum(s // turns, 1), jnp.where(s < 2 * turns, s % turns, turns - 1), 0),
    )
    grad_residual, grad_attn, mid_sums = run_kernel(
        functools.partial(norm_back_kernel, turns, images),
        order.sc,
        [back] + wu + [residual, cotangent, modulation, attn_out],
        [
            span_spec,
            pl.BlockSpec((dim, reach), lambda s, c: (0, rows_of(0, turns)(s, c))),
            pl.BlockSpec((dim, reach), lambda s, c: (0, rows_of(1, turns)(s, c))),
            image_spec(2 * turns),
            image_spec(2 * turns, tail_local),
            pl.BlockSpec((1, 6, dim), tail_local(2 * turns)),
            image_spec(2 * turns),
        ],
        [image_spec(2 * turns)] * 2 + [pl.BlockSpec((1, 4, dim), tail(2 * turns))],
        [token_f, token_b, shape_of((images, 4, dim), f32)],
        (2 * turns + images,),
        60,
        scratch=[pltpu.VMEM((count, dim), f32)],
    )
    order.after(mid_sums)
    order.tick(*flows)
    pieces = 2
    each = images // pieces
    grad_qkv = []
    for piece in range(pieces):
        there = lambda i, s, piece=piece: (piece * each + i, 0, 0)
        (grad_piece,) = run_kernel(
            functools.partial(back_kernel, 2),
            order.sc,
            [grad_attn, qkv, prob] + wp,
            [
                pl.BlockSpec((1, seq, dim), there),
                pl.BlockSpec((1, 6 * cols, seq), there),
                pl.BlockSpec((1, 2 * heads, seq, seq), lambda i, s, piece=piece: (piece * each + i, 0, 0, 0)),
            ]
            + [whole_block(a) for a in wp],
            [qkv_spec],
            [shape_of((each, 6 * cols, seq), bf16)],
            (each,),
            60,
            scratch=[pltpu.VMEM((2 * cols, seq), bf16)],
            )
        grad_qkv.append(grad_piece)
        order.after(grad_piece)
        order.tick(*flows)

    attn_per = 4 * cols // 16
    qv_sums = [None, None]

    def attn_part(part):
        grads, sums = run_kernel(
            functools.partial(attn_grad_kernel, pieces, attn_per),
            order.sc,
            grad_qkv + [mixed, normed, grad_attn],
            [
                pl.BlockSpec((each, cols, seq), lambda s, c: (0, 3 * part + jnp.minimum(s, 2), 0))
                for _ in range(pieces)
            ]
            + [pl.BlockSpec((images, cols, seq), lambda s, c: (0, part, 0))]
            + [whole_block(normed), whole_block(grad_attn)],
            [
                pl.BlockSpec((16, attn_per, dim), every),
                pl.BlockSpec((1, 8, cols), lambda s, c: (jnp.minimum(s, 2), 0, 0)),
            ],
            [shape_of((16, attn_per, dim), bf16), shape_of((3, 8, cols), f32)],
            (4,),
            60,
            )
        qv_sums[part] = sums
        order.after(sums)
        return grads

    grad_other = attn_part(1)
    made = []
    last = sum_flow(ATTN_WAYS, lambda: made[0], grad_other)
    order.tick(last, *flows)
    made.append(attn_part(0))
    order.tick(last, *flows)

    first_spec = lambda part: pl.BlockSpec((cols, dim), lambda s, c: (rows_of(part, 3)(s, c), 0))
    grad_tokens, grad_own_tokens, low_sums = run_kernel(
        functools.partial(first_back_kernel, pieces, images),
        order.sc,
        grad_qkv + wq + [tokens, modulation, grad_residual],
        [pl.BlockSpec((each, cols, seq), lambda s, c: (0, jnp.minimum(s, 5), 0)) for _ in range(pieces)]
        + [first_spec(0), first_spec(1)]
        + [image_spec(6, tail_local), pl.BlockSpec((1, 6, dim), tail_local(6)), image_spec(6)],
        [image_spec(6, tail_local), image_spec(6), pl.BlockSpec((1, 2, dim), tail(6))],
        [shape_of((slots, seq, dim), f32), token_f, shape_of((images, 2, dim), f32)],
        (6 + images,),
        60,
        scratch=[pltpu.VMEM((count, dim), f32)],
    )
    order.after(low_sums)
    order.tick(last, *flows)
    other_tokens = swap_cores(grad_own_tokens)
    down_spec = lambda part: pl.BlockSpec((reach, dim), lambda s, c: (rows_of(part, turns)(s, c), 0))
    output, own_output, gate_sums = run_kernel(
        functools.partial(output_kernel, turns, images),
        order.sc,
        [act] + wd + [residual, cotangent, modulation, down_bias],
        [
            span_spec,
            down_spec(0),
            down_spec(1),
            image_spec(2 * turns),
            image_spec(2 * turns, tail_local),
            pl.BlockSpec((1, 6, dim), tail_local(2 * turns)),
            whole_block(down_bias),
        ],
        [image_spec(2 * turns, tail_local), image_spec(2 * turns), pl.BlockSpec((1, 1, dim), tail(2 * turns))],
        [shape_of((slots, seq, dim), bf16), token_b, shape_of((images, 1, dim), f32)],
        (2 * turns + images,),
        60,
        scratch=[pltpu.VMEM((count, dim), f32)],
    )
    order.after(gate_sums)
    order.tick(last, *flows)
    other_output = swap_cores(own_output)

    low_sums, mid_sums, gate_sums, down_sums = order.fence((low_sums, mid_sums, gate_sums, down_sums))
    grad_modulation = jnp.concatenate([low_sums, mid_sums[:, 2:3], mid_sums[:, 0:2], gate_sums], axis=1)
    grad_modulation = grad_modulation.reshape(images, 6 * dim).astype(bf16)
    bias_sums = [
        jnp.concatenate(
            [qv_sums[part][0, 0:1], qv_sums[part][2, 0:1]]
            + [up_sums[chunk, part] for chunk in range(CHUNKS)],
            axis=1,
        )
        for part in range(2)
    ]
    shared = jnp.concatenate(
        [
            jnp.sum(mid_sums[:, 3], axis=0, keepdims=True),
            jnp.sum(down_sums[:, 0], axis=0, keepdims=True),
            jnp.zeros((1, own_cols - 2 * dim), f32),
        ],
        axis=1,
    )
    halves = grad_modulation.reshape(images, 2, own_cols)
    kept = lax.dynamic_index_in_dim(halves, core, 1, keepdims=False)
    given = lax.dynamic_index_in_dim(halves, 1 - core, 1, keepdims=False)
    got = swap_cores(jnp.concatenate([given.astype(f32), bias_sums[1], shared]))
    came = got[:images].astype(bf16)
    group_mod = jnp.where(core == 0, jnp.concatenate([kept, came]), jnp.concatenate([came, kept]))
    own_bias_sum = bias_sums[0] + got[images : images + 1]
    shared_sum = shared + got[images + 1 :]
    wide_scaled = jnp.pad(scaled.reshape(-1), (0, 3 * own_cols - slots * dim)).reshape(3, own_cols)
    packed_rows = jnp.concatenate(
        [group_mod, own_bias_sum.astype(bf16), shared_sum.astype(bf16), wide_scaled]
    )
    (packed_rows,) = order.fence([packed_rows])
    small = rows_flow(packed_rows)
    order.tick(last, small, *flows)
    (group_mod,) = order.fence([group_mod])
    part_scaled = outer_cols(group_mod, w_mod).astype(bf16)
    came_scaled = swap_cores(part_scaled)
    output = fill_other(output, order.fence(other_output), core)
    order.after((output[0, 0, :1], part_scaled[0, :1]))
    order.tick(last, small, *flows)
    grad_tokens = fill_other(grad_tokens, order.fence(other_tokens), core)
    part_scaled, came_scaled = order.fence((part_scaled, came_scaled))
    grad_scaled = part_scaled.astype(f32) + came_scaled.astype(f32)
    _, silu_back = jax.vjp(jax.nn.silu, cond_f)
    grad_condition = silu_back(grad_scaled)[0]
    order.after((grad_tokens[0, 0, :1], grad_condition[0, :1]))
    order.tick(last, small, *flows)

    def cuts(ways):
        return tuple((way[0], lo, hi) for lo, hi, way in ways)

    grad_w_down = grad_w_up = jnp.zeros((8, 128), f32)

    def final_mlp(chunk, body, args):
        nonlocal grad_w_down, grad_w_up
        first = grad_w_down.shape[0] == 8
        spot = len(args) + 1
        grad_w_down, grad_w_up, mark = run_kernel(
            body,
            order.sc,
            list(args) + [grad_w_down, grad_w_up],
            [
                whole_block(a)
                if a.shape[0] == 8
                else pl.BlockSpec((16 // steps,) + a.shape[1:], lambda s, c: (s, 0, 0))
                for a in args
            ]
            + [anywhere, anywhere],
            [
                pl.BlockSpec((block, dim), lambda s, c: (chunk * steps + s, 0)),
                pl.BlockSpec((dim, block), lambda s, c: (0, chunk * steps + s)),
                pl.BlockSpec((8, 128), lambda s, c: (0, 0)),
            ],
            [shape_of((ff, dim), f32), shape_of((dim, ff), f32), shape_of((8, 128), f32)],
            (steps,),
            4,
            scratch=[pltpu.VMEM((block, dim), f32)],
            alias=None if first else {spot: 0, spot + 1: 1},
        )
        order.after(mark)

    for chunk, flow in enumerate(flows):
        body = functools.partial(final_mlp_kernel, cuts(MLP_WAYS), per)
        final_mlp(PLAIN + chunk, body, order.finish(flow))
    order.tick(last, small)
    all_rows = order.fence(order.finish(small)).reshape(16, slots + 5, own_cols)
    all_mod = all_rows[:, :slots].reshape(-1, own_cols)
    all_scaled = all_rows[:, slots + 2 :].reshape(16, -1)[:, : slots * dim].reshape(-1, dim)
    grad_w_mod = inner_rows(all_scaled, all_mod)
    grad_b_mod = jnp.sum(all_mod.astype(f32), axis=0)
    bias_total = jnp.sum(all_rows[:, slots : slots + 2].astype(f32), axis=0)
    grad_b_qv = bias_total[0, : 2 * cols].reshape(2, cols)
    grad_b_up = bias_total[0, 2 * cols :]
    grad_b_proj = bias_total[1, :dim]
    grad_b_down = bias_total[1, dim : 2 * dim]
    order.after((grad_w_mod[0, :1], grad_b_mod[:1], bias_total[0, :1]))
    args = order.finish(last)
    grad_qkv_rows, grad_w_proj = run_kernel(
        functools.partial(final_attn_kernel, cuts(ATTN_WAYS), attn_per),
        order.sc,
        list(args),
        [whole_block(a) for a in args],
        [
            pl.BlockSpec((cols, dim), lambda s, c: (jnp.minimum(s, 2), 0)),
            pl.BlockSpec((cols, dim), lambda s, c: (0, 0)),
        ],
        [shape_of((3 * cols, dim), f32), shape_of((cols, dim), f32)],
        (4,),
        9,
    )
    grad_w_qkv = jnp.transpose(grad_qkv_rows.reshape(3, cols, dim), (2, 0, 1))
    order.after(grad_w_proj[0, :1])
    for chunk, total in enumerate(plain_sums):
        final_mlp(chunk, functools.partial(final_plain_kernel, per), [total])
    return (
        output,
        grad_tokens,
        grad_condition,
        grad_w_qkv,
        grad_b_qv,
        grad_w_proj,
        grad_b_proj,
        grad_w_up,
        grad_b_up,
        grad_w_down,
        grad_b_down,
        grad_w_mod,
        grad_b_mod,
    )


def layer_norm(values):
    center = values - jnp.mean(values, axis=-1, keepdims=True)
    return center * lax.rsqrt(jnp.mean(center * center, axis=-1, keepdims=True) + epsilon)


def modulate(values, shift_part, scale_part):
    return layer_norm(values) * (1.0 + scale_part) + shift_part


def gelu_tanh(values):
    return (
        0.5
        * values
        * (1.0 + jnp.tanh(0.7978845608028654 * (values + 0.044715 * values * values * values)))
    )


def inner_rows(left, right):
    return lax.dot_general(
        left, right, (((0,), (0,)), ((), ())), preferred_element_type=jnp.float32
    )


def outer_cols(left, right):
    return lax.dot_general(
        left, right, (((1,), (1,)), ((), ())), preferred_element_type=jnp.float32
    )


def attention_forward(query_rows, key_rows, value_rows):
    factor = HEAD_DIM ** (-0.5)
    scores = (
        jnp.einsum("bqhd,bkhd->bhqk", query_rows, key_rows, preferred_element_type=jnp.float32)
        * factor
    )
    row_max = jnp.max(scores, axis=-1, keepdims=True)
    row_total = jnp.sum(jnp.exp(scores - row_max), axis=-1, keepdims=True)
    logsum = row_max + jnp.log(row_total)
    prob_b = jnp.exp(scores - logsum).astype(jnp.bfloat16)
    mixed_out = jnp.einsum(
        "bhqk,bkhd->bqhd", prob_b, value_rows, preferred_element_type=jnp.float32
    )
    return (mixed_out, logsum)


def attention_backward(query_rows, key_rows, value_rows, logsum, grad_mixed):
    factor = HEAD_DIM ** (-0.5)
    scores = (
        jnp.einsum("bqhd,bkhd->bhqk", query_rows, key_rows, preferred_element_type=jnp.float32)
        * factor
    )
    prob_f = jnp.exp(scores - logsum)
    prob_b = prob_f.astype(jnp.bfloat16)
    grad_prob = jnp.einsum(
        "bqhd,bkhd->bhqk", grad_mixed, value_rows, preferred_element_type=jnp.float32
    )
    row_delta = jnp.sum(prob_f * grad_prob, axis=-1, keepdims=True)
    grad_scores = (prob_f * (grad_prob - row_delta)).astype(jnp.bfloat16)
    grad_query = (
        jnp.einsum("bhqk,bkhd->bqhd", grad_scores, key_rows, preferred_element_type=jnp.float32)
        * factor
    )
    grad_key = (
        jnp.einsum("bhqk,bqhd->bkhd", grad_scores, query_rows, preferred_element_type=jnp.float32)
        * factor
    )
    grad_value = jnp.einsum(
        "bhqk,bqhd->bkhd", prob_b, grad_mixed, preferred_element_type=jnp.float32
    )
    return (
        grad_query.astype(jnp.bfloat16),
        grad_key.astype(jnp.bfloat16),
        grad_value.astype(jnp.bfloat16),
    )


def forward(tokens_f, spans, weights, repeat):
    w_qkv, b_qv, w_proj, b_proj, w_up, b_up, w_down, b_down = weights
    shift_attn, scale_attn, gate_attn, shift_mlp, scale_mlp, gate_mlp = spans
    slot_count, seq_len, model_dim = tokens_f.shape
    row_count = slot_count * seq_len
    head_cols = w_qkv.shape[2]
    head_count = head_cols // HEAD_DIM
    shape_four = (slot_count, seq_len, head_count, HEAD_DIM)
    normed = (
        modulate(tokens_f, shift_attn, scale_attn)
        .astype(jnp.bfloat16)
        .reshape(row_count, model_dim)
    )
    projected = jnp.dot(
        normed, w_qkv.reshape(model_dim, 3 * head_cols), preferred_element_type=jnp.float32
    )
    qkv_bias = jnp.stack([b_qv[0], jnp.zeros_like(b_qv[0]), b_qv[1]]).astype(jnp.float32)
    projected = (projected.reshape(row_count, 3, head_cols) + qkv_bias).astype(jnp.bfloat16)
    query_rows = projected[:, 0].reshape(shape_four)
    key_rows = projected[:, 1].reshape(shape_four)
    value_rows = projected[:, 2].reshape(shape_four)
    mixed_out, logsum = attention_forward(query_rows, key_rows, value_rows)
    mixed_b = mixed_out.astype(jnp.bfloat16).reshape(row_count, head_cols)
    partial_value = jnp.dot(mixed_b, w_proj, preferred_element_type=jnp.float32)
    if repeat:
        summed = lax.psum(partial_value.astype(jnp.bfloat16), "mp").astype(jnp.float32)
    else:
        summed = lax.psum(partial_value.astype(jnp.bfloat16), "mp").astype(jnp.float32)
    attn_out = (summed + b_proj.astype(jnp.float32)).reshape(slot_count, seq_len, model_dim)
    residual = tokens_f + gate_attn * attn_out
    normed_mlp = (
        modulate(residual, shift_mlp, scale_mlp).astype(jnp.bfloat16).reshape(row_count, model_dim)
    )
    hidden = jnp.dot(normed_mlp, w_up, preferred_element_type=jnp.float32) + b_up.astype(
        jnp.float32
    )
    act_bf = gelu_tanh(hidden).astype(jnp.bfloat16)
    partial_mlp = jnp.dot(act_bf, w_down, preferred_element_type=jnp.float32)
    if repeat:
        summed_mlp = lax.psum(partial_mlp.astype(jnp.bfloat16), "mp").astype(jnp.float32)
    else:
        summed_mlp = lax.psum(partial_mlp.astype(jnp.bfloat16), "mp").astype(jnp.float32)
    mlp_out = (summed_mlp + b_down.astype(jnp.float32)).reshape(slot_count, seq_len, model_dim)
    output = residual + gate_mlp * mlp_out
    return {
        "normed": normed,
        "query_rows": query_rows,
        "key_rows": key_rows,
        "value_rows": value_rows,
        "logsum": logsum,
        "mixed_b": mixed_b,
        "attn_out": attn_out,
        "residual": residual,
        "normed_mlp": normed_mlp,
        "hidden": hidden,
        "act_bf": act_bf,
        "mlp_out": mlp_out,
        "output": output,
    }


def image_pass(tokens_f, grad_out, spans, weights):
    w_qkv, b_qv, w_proj, b_proj, w_up, b_up, w_down, b_down = weights
    shift_attn, scale_attn, gate_attn, shift_mlp, scale_mlp, gate_mlp = spans
    slot_count, seq_len, model_dim = tokens_f.shape
    row_count = slot_count * seq_len
    head_cols = w_qkv.shape[2]
    head_count = head_cols // HEAD_DIM
    kept_fwd = forward(tokens_f, spans, weights, False)
    out_one = kept_fwd["output"]
    stored = forward(tokens_f, spans, weights, True)
    grad_gate_mlp = jnp.sum(grad_out * stored["mlp_out"], axis=1)
    grad_mlp = (gate_mlp * grad_out).astype(jnp.bfloat16).reshape(row_count, model_dim)
    grad_b_down = jnp.sum(grad_mlp.astype(jnp.float32), axis=0)
    grad_w_down = inner_rows(stored["act_bf"], grad_mlp)
    grad_act = outer_cols(grad_mlp, w_down)
    gelu_value, gelu_back = jax.vjp(gelu_tanh, stored["hidden"])
    grad_hidden = gelu_back(grad_act)[0].astype(jnp.bfloat16)
    grad_b_up = jnp.sum(grad_hidden.astype(jnp.float32), axis=0)
    grad_w_up = inner_rows(stored["normed_mlp"], grad_hidden)
    part_normed_mlp = outer_cols(grad_hidden, w_up)
    grad_normed_mlp = (
        lax.psum(part_normed_mlp.astype(jnp.bfloat16), "mp")
        .astype(jnp.float32)
        .reshape(slot_count, seq_len, model_dim)
    )
    norm_value, norm_back = jax.vjp(modulate, stored["residual"], shift_mlp, scale_mlp)
    grad_resid_norm, grad_shift_mlp, grad_scale_mlp = norm_back(grad_normed_mlp)
    grad_residual = grad_out + grad_resid_norm
    grad_gate_attn = jnp.sum(grad_residual * stored["attn_out"], axis=1)
    grad_attn = (gate_attn * grad_residual).astype(jnp.bfloat16).reshape(row_count, model_dim)
    grad_b_proj = jnp.sum(grad_attn.astype(jnp.float32), axis=0)
    grad_w_proj = inner_rows(stored["mixed_b"], grad_attn)
    grad_mixed = (
        outer_cols(grad_attn, w_proj)
        .astype(jnp.bfloat16)
        .reshape(slot_count, seq_len, head_count, HEAD_DIM)
    )
    grad_query, grad_key, grad_value = attention_backward(
        stored["query_rows"], stored["key_rows"], stored["value_rows"], stored["logsum"], grad_mixed
    )
    grad_qkv = jnp.stack(
        [
            grad_query.reshape(row_count, head_cols),
            grad_key.reshape(row_count, head_cols),
            grad_value.reshape(row_count, head_cols),
        ],
        axis=1,
    )
    grad_b_qv = jnp.stack(
        [
            jnp.sum(grad_qkv[:, 0].astype(jnp.float32), axis=0),
            jnp.sum(grad_qkv[:, 2].astype(jnp.float32), axis=0),
        ]
    )
    grad_w_qkv = inner_rows(stored["normed"], grad_qkv)
    part_normed = outer_cols(
        grad_qkv.reshape(row_count, 3 * head_cols), w_qkv.reshape(model_dim, 3 * head_cols)
    )
    grad_normed = (
        lax.psum(part_normed.astype(jnp.bfloat16), "mp")
        .astype(jnp.float32)
        .reshape(slot_count, seq_len, model_dim)
    )
    first_value, first_back = jax.vjp(modulate, tokens_f, shift_attn, scale_attn)
    grad_tok_norm, grad_shift_attn, grad_scale_attn = first_back(grad_normed)
    grad_tok_one = grad_residual + grad_tok_norm
    grad_mod_one = jnp.concatenate(
        [
            grad_shift_attn[:, 0],
            grad_scale_attn[:, 0],
            grad_gate_attn,
            grad_shift_mlp[:, 0],
            grad_scale_mlp[:, 0],
            grad_gate_mlp,
        ],
        axis=1,
    )
    grad_terms = (
        grad_w_qkv,
        grad_b_qv,
        grad_w_proj,
        grad_b_proj,
        grad_w_up,
        grad_b_up,
        grad_w_down,
        grad_b_down,
    )
    return (out_one, grad_tok_one, grad_mod_one, grad_terms)


def run_layer(tokens, condition, cotangent, live_count, turns, weights, w_mod, b_mod):
    slot_count, seq_len, model_dim = tokens.shape
    cond_f = condition.astype(jnp.float32)
    scaled = jax.nn.silu(cond_f).astype(jnp.bfloat16)
    own_mod = jnp.dot(scaled, w_mod, preferred_element_type=jnp.float32) + b_mod.astype(jnp.float32)
    modulation = lax.all_gather(own_mod, "mp", axis=1, tiled=True)
    tokens_f = tokens.astype(jnp.float32)
    cot_f = cotangent.astype(jnp.float32)

    def image_step(slot_idx, carry):
        out_buf, grad_buf, mod_buf, grad_sums = carry
        live_flag = (slot_idx < live_count).astype(jnp.float32)
        tok_one = lax.dynamic_slice_in_dim(tokens_f, slot_idx, 1, 0)
        cot_one = lax.dynamic_slice_in_dim(cot_f, slot_idx, 1, 0) * live_flag
        mod_row = lax.dynamic_slice_in_dim(modulation, slot_idx, 1, 0)
        spans = [
            mod_row[:, None, part_idx * model_dim : (part_idx + 1) * model_dim]
            for part_idx in range(6)
        ]
        out_one, grad_tok_one, grad_mod_one, grad_terms = image_pass(
            tok_one, cot_one, spans, weights
        )
        out_one = (out_one * live_flag).astype(jnp.bfloat16)
        out_buf = lax.dynamic_update_slice_in_dim(out_buf, out_one, slot_idx, 0)
        grad_buf = lax.dynamic_update_slice_in_dim(grad_buf, grad_tok_one, slot_idx, 0)
        mod_buf = lax.dynamic_update_slice_in_dim(mod_buf, grad_mod_one, slot_idx, 0)
        grad_sums = tuple((total_a + term_b for total_a, term_b in zip(grad_sums, grad_terms)))
        return (out_buf, grad_buf, mod_buf, grad_sums)

    start_sums = tuple((jnp.zeros(weight_in.shape, jnp.float32) for weight_in in weights))
    start_state = (
        jnp.zeros(tokens.shape, jnp.bfloat16),
        jnp.zeros(tokens.shape, jnp.float32),
        jnp.zeros((slot_count, 6 * model_dim), jnp.float32),
        start_sums,
    )
    out_buf, grad_buf, mod_buf, grad_sums = lax.fori_loop(0, turns, image_step, start_state)
    grad_modulation = mod_buf.astype(jnp.bfloat16)
    own_cols = w_mod.shape[1]
    grad_own = lax.dynamic_slice_in_dim(
        grad_modulation, lax.axis_index("mp") * own_cols, own_cols, 1
    )
    part_scaled = outer_cols(grad_own, w_mod)
    grad_scaled = lax.psum(part_scaled.astype(jnp.bfloat16), "mp").astype(jnp.float32)
    silu_value, silu_back = jax.vjp(jax.nn.silu, cond_f)
    grad_condition = silu_back(grad_scaled)[0]
    return (out_buf, grad_buf, grad_condition, grad_sums, scaled, grad_own)


def on_device(
    tokens,
    condition,
    counts,
    w_qkv,
    b_qv,
    w_proj,
    b_proj,
    w_up,
    b_up,
    w_down,
    b_down,
    w_mod,
    b_mod,
    cotangent,
):
    slot_count, seq_len, model_dim = tokens.shape
    weights = (w_qkv, b_qv, w_proj, b_proj, w_up, b_up, w_down, b_down)
    own_count = counts[0]
    output, grad_tokens, grad_condition, grad_sums, scaled, grad_own = run_layer(
        tokens, condition, cotangent, own_count, slot_count, weights, w_mod, b_mod
    )
    (
        grad_w_qkv,
        grad_b_qv,
        grad_w_proj,
        grad_b_proj,
        grad_w_up,
        grad_b_up,
        grad_w_down,
        grad_b_down,
    ) = grad_sums
    grad_w_mod = inner_rows(scaled, grad_own)
    grad_b_mod = jnp.sum(grad_own.astype(jnp.float32), axis=0)
    (
        grad_w_qkv,
        grad_b_qv,
        grad_w_proj,
        grad_b_proj,
        grad_w_up,
        grad_b_up,
        grad_w_down,
        grad_b_down,
        grad_w_mod,
        grad_b_mod,
    ) = (
        lax.psum(grad_w_qkv.astype(jnp.bfloat16), "dp").astype(jnp.float32),
        lax.psum(grad_b_qv.astype(jnp.bfloat16), "dp").astype(jnp.float32),
        lax.psum(grad_w_proj.astype(jnp.bfloat16), "dp").astype(jnp.float32),
        lax.psum(grad_b_proj.astype(jnp.bfloat16), "dp").astype(jnp.float32),
        lax.psum(grad_w_up.astype(jnp.bfloat16), "dp").astype(jnp.float32),
        lax.psum(grad_b_up.astype(jnp.bfloat16), "dp").astype(jnp.float32),
        lax.psum(grad_w_down.astype(jnp.bfloat16), "dp").astype(jnp.float32),
        lax.psum(grad_b_down.astype(jnp.bfloat16), "dp").astype(jnp.float32),
        lax.psum(grad_w_mod.astype(jnp.bfloat16), "dp").astype(jnp.float32),
        lax.psum(grad_b_mod.astype(jnp.bfloat16), "dp").astype(jnp.float32),
    )
    return (
        output,
        grad_tokens,
        grad_condition,
        grad_w_qkv,
        grad_b_qv,
        grad_w_proj,
        grad_b_proj,
        grad_w_up,
        grad_b_up,
        grad_w_down,
        grad_b_down,
        grad_w_mod,
        grad_b_mod,
    )


def solution(mesh):
    placed = (
        P("dp", None, None),
        P("dp", None),
        P("dp"),
        P(None, None, "mp"),
        P(None, "mp"),
        P("mp", None),
        P(),
        P(None, "mp"),
        P("mp"),
        P("mp", None),
        P(),
        P(None, "mp"),
        P("mp"),
        P("dp", None, None),
    )
    fast = mesh.shape["dp"] == 16 and mesh.shape["mp"] == 2
    return jax.shard_map(
        fast_device if fast else on_device,
        mesh=mesh,
        in_specs=placed,
        out_specs=(
            P("dp", None, None),
            P("dp", None, None),
            P("dp", None),
            P(None, None, "mp"),
            P(None, "mp"),
            P("mp", None),
            P(),
            P(None, "mp"),
            P("mp"),
            P("mp", None),
            P(),
            P(None, "mp"),
            P("mp"),
        ),
        check_vma=False,
    )
```

```python
import functools

import jax
import jax.numpy as jnp
from jax import lax
from jax.experimental import pallas as pl
from jax.experimental.pallas import tpu as pltpu
from jax.sharding import PartitionSpec as P

HEAD_DIM = 72


epsilon = 1e-06

f32 = jnp.float32
bf16 = jnp.bfloat16


def dot_nn(left, right):
    return lax.dot_general(left, right, (((1,), (0,)), ((), ())), preferred_element_type=f32)


def dot_nt(left, right):
    return lax.dot_general(left, right, (((1,), (1,)), ((), ())), preferred_element_type=f32)


def dot_tn(left, right):
    return lax.dot_general(left, right, (((0,), (0,)), ((), ())), preferred_element_type=f32)


def normalize(values):
    center = values - jnp.mean(values, axis=-1, keepdims=True)
    recip = lax.rsqrt(jnp.mean(center * center, axis=-1, keepdims=True) + epsilon)
    return center * recip, recip


def norm_pullback(grad_normed, unit, recip, scale_row):
    scaled_grad = grad_normed * (1.0 + scale_row)
    mean_grad = jnp.mean(scaled_grad, axis=-1, keepdims=True)
    mean_unit = jnp.mean(scaled_grad * unit, axis=-1, keepdims=True)
    return recip * (scaled_grad - mean_grad - unit * mean_unit)


def column(row):
    return jnp.broadcast_to(row[...].astype(f32), (8, row.shape[1])).T[:, 0:1]


def token_sum(values):
    return jnp.sum(values, axis=0, keepdims=True)


def attention_kernel(parts, own_images, sc, tok, cot, mod, b_proj, *refs):
    w_qkv, w_proj, bias = refs[:parts], refs[parts : 2 * parts], refs[2 * parts : 3 * parts]
    qkv, prob, mixed, attn_out, residual, normed_mlp, normed, grad_mlp, down_sums = refs[3 * parts :]
    image = sc[0] * own_images + pl.program_id(0)
    live = jnp.where(image < sc[1], 1.0, 0.0).astype(f32)
    unit, _ = normalize(tok[0].astype(f32))
    normed[0] = (unit * (1.0 + mod[0, 1:2, :]) + mod[0, 0:1, :]).astype(bf16)
    grad = (mod[0, 5:6, :] * (cot[0].astype(f32) * live)).astype(bf16)
    grad_mlp[0] = grad
    down_sums[0] = token_sum(grad.astype(f32))
    cols = w_proj[0].shape[0]
    pairs = cols // (2 * HEAD_DIM)
    span = 2 * HEAD_DIM
    factor = HEAD_DIM ** (-0.5)
    rows = normed[0]
    total = b_proj[...]
    for part in range(parts):
        base = part * 3 * cols
        shift = bias[part][...].astype(f32).T
        for proj in range(3):
            lo = proj * cols
            value = dot_nt(w_qkv[part][lo : lo + cols, :], rows)
            if proj != 1:
                value = value + shift[:, proj // 2 : proj // 2 + 1]
            qkv[0, base + lo : base + lo + cols, :] = value.astype(bf16)

        def pair_step(pair, carry, base=base, part=part):
            at = pl.multiple_of(base + pair * span, 16)
            query = qkv[0, pl.ds(at, span), :].astype(f32)
            key = qkv[0, pl.ds(at + cols, span), :].astype(f32)
            value = qkv[0, pl.ds(at + 2 * cols, span), :].astype(f32)
            outs = []
            for one in range(2):
                rows_of = slice(one * HEAD_DIM, (one + 1) * HEAD_DIM)
                scores = dot_tn(key[rows_of].astype(bf16), query[rows_of].astype(bf16)) * factor
                raised = jnp.exp(scores - jnp.max(scores, axis=0, keepdims=True))
                share = 1.0 / jnp.sum(raised, axis=0, keepdims=True)
                prob_b = (raised * share).astype(bf16)
                prob[0, part * 2 * pairs + 2 * pair + one] = prob_b
                outs.append(dot_nn(value[rows_of].astype(bf16), prob_b))
            to = pl.multiple_of(part * cols + pair * span, 16)
            mixed[0, pl.ds(to, span), :] = jnp.concatenate(outs, axis=0).astype(bf16)
            return carry

        lax.fori_loop(0, pairs, pair_step, 0, unroll=True)
        total = total + dot_tn(mixed[0, part * cols : (part + 1) * cols, :], w_proj[part][...])
    attn_out[0] = total
    summed = tok[0].astype(f32) + mod[0, 2:3, :] * total
    residual[0] = summed
    unit, _ = normalize(summed)
    normed_mlp[0] = (unit * (1.0 + mod[0, 4:5, :]) + mod[0, 3:4, :]).astype(bf16)


def mlp_kernel(per, jobs, sc, rows, grad_mlp, *refs):
    count = len(jobs)
    weights = [refs[3 * k : 3 * k + 3] for k in range(count)]
    refs = refs[3 * count :]
    came = []
    for _, summed in jobs:
        came.append(refs[0] if summed else None)
        refs = refs[1:] if summed else refs
    act, back = refs[2], refs[3]
    grads, sums = refs[4 : 4 + count], refs[4 + count :]
    job, step = pl.program_id(0), pl.program_id(1)
    for k in range(count):

        @pl.when(job == k)
        def _(k=k):
            mlp_block(
                per, jobs[k][0], step, sc, rows, grad_mlp, *weights[k], act, back, grads[k], sums[k], came[k]
            )


def mlp_block(per, natural, step, sc, rows, grad_mlp, w_up, w_down, bias, act, back, grads, sums, came):
    here = w_down.shape[0] // per
    hidden = lax.dot_general(
        w_up[...], rows[...], (((0,), (1,)), ((), ())), preferred_element_type=f32
    ) + column(bias)
    square = hidden * hidden
    bend = jnp.tanh(0.7978845608028654 * hidden * (1.0 + 0.044715 * square))
    half = 0.5 * (1.0 + bend)
    act_b = (hidden * half).astype(bf16)
    slope = half + 0.5 * hidden * (1.0 - bend * bend) * (
        0.7978845608028654 * (1.0 + 3.0 * 0.044715 * square)
    )
    back_b = (dot_nt(w_down[...], grad_mlp[...]) * slope).astype(bf16)
    act[0] = act_b
    back[0] = back_b
    sums[...] = dot_nt(jnp.ones((8, rows.shape[0]), bf16), back_b)
    for lo_row, left, right in ((0, act_b, grad_mlp), (per, back_b, rows)):
        grad = dot_nn(left, right[...])
        for piece in range(here):
            value = grad[piece * per : (piece + 1) * per]
            if natural:
                if came is not None:
                    value = value + came[piece, lo_row : lo_row + per, :].astype(f32)
                grads[piece, lo_row : lo_row + per, :] = value.astype(bf16)
            else:
                at = jnp.bitwise_xor(step * here + piece, sc[2])
                grads[at, lo_row : lo_row + per, :] = value.astype(bf16)


def grow(total, part_steps, left, rights, dims):
    step = pl.program_id(0)

    def term(right):
        return lax.dot_general(left, right[...], (dims, ((), ())), preferred_element_type=f32)

    @pl.when(step == 0)
    def _():
        total[...] = term(rights[0])

    @pl.when(jnp.logical_and(step > 0, step < part_steps))
    def _():
        total[...] += term(rights[0])

    @pl.when(jnp.logical_and(step >= part_steps, step < 2 * part_steps))
    def _():
        total[...] += term(rights[1])


def norm_back_kernel(
    part_steps, own_images, sc, back, w_up0, w_up1, residual, cot, mod, attn_out,
    grad_residual, grad_attn, sums, total
):
    grow(total, part_steps, back[0], (w_up0, w_up1), ((0,), (1,)))
    one = pl.program_id(0) - 2 * part_steps
    seq = residual.shape[1]

    @pl.when(one >= 0)
    def _():
        live = jnp.where(sc[0] * own_images + one < sc[1], 1.0, 0.0).astype(f32)
        grad_normed = total[pl.ds(pl.multiple_of(one * seq, seq), seq), :]
        unit, recip = normalize(residual[0])
        sums[0, 0:1, :] = token_sum(grad_normed)
        sums[0, 1:2, :] = token_sum(grad_normed * unit)
        grad_res = cot[0].astype(f32) * live + norm_pullback(grad_normed, unit, recip, mod[0, 4:5, :])
        grad_residual[0] = grad_res
        sums[0, 2:3, :] = token_sum(grad_res * attn_out[0])
        grad_att = (mod[0, 2:3, :] * grad_res).astype(bf16)
        grad_attn[0] = grad_att
        sums[0, 3:4, :] = token_sum(grad_att.astype(f32))


def back_kernel(parts, sc, grad_attn, qkv, prob, *refs):
    w_proj = refs[:parts]
    grad_qkv, grad_mixed = refs[parts:]
    cols = w_proj[0].shape[0]
    pairs = cols // (2 * HEAD_DIM)
    span = 2 * HEAD_DIM
    factor = HEAD_DIM ** (-0.5)
    grad_att = grad_attn[0]
    for part in range(parts):
        base = part * 3 * cols
        grad_mixed[part * cols : (part + 1) * cols, :] = dot_nt(w_proj[part][...], grad_att).astype(bf16)

        def pair_step(pair, carry, base=base, part=part):
            at = pl.multiple_of(base + pair * span, 16)
            query = qkv[0, pl.ds(at, span), :].astype(f32)
            key = qkv[0, pl.ds(at + cols, span), :].astype(f32)
            value = qkv[0, pl.ds(at + 2 * cols, span), :].astype(f32)
            grads = grad_mixed[pl.ds(pl.multiple_of(part * cols + pair * span, 16), span), :].astype(f32)
            to_query, to_key, to_value = [], [], []
            for one in range(2):
                rows_of = slice(one * HEAD_DIM, (one + 1) * HEAD_DIM)
                prob_b = prob[0, part * 2 * pairs + 2 * pair + one]
                prob_f = prob_b.astype(f32)
                grad_b = grads[rows_of].astype(bf16)
                grad_prob = dot_tn(value[rows_of].astype(bf16), grad_b)
                delta = jnp.sum(prob_f * grad_prob, axis=0, keepdims=True)
                grad_scores = (prob_f * (grad_prob - delta)).astype(bf16)
                to_query.append(dot_nn(key[rows_of].astype(bf16), grad_scores) * factor)
                to_key.append(dot_nt(query[rows_of].astype(bf16), grad_scores) * factor)
                to_value.append(dot_nt(grad_b, prob_b))
            grad_qkv[0, pl.ds(at, span), :] = jnp.concatenate(to_query, axis=0).astype(bf16)
            grad_qkv[0, pl.ds(at + cols, span), :] = jnp.concatenate(to_key, axis=0).astype(bf16)
            grad_qkv[0, pl.ds(at + 2 * cols, span), :] = jnp.concatenate(to_value, axis=0).astype(bf16)
            return carry

        lax.fori_loop(0, pairs, pair_step, 0, unroll=True)


def attn_grad_kernel(pieces, per, sc, *refs):
    grad_qkv, mixed, normed, grad_attn = refs[:pieces], refs[pieces], refs[pieces + 1], refs[pieces + 2]
    grads, sums = refs[pieces + 3 :]
    step = pl.program_id(0)
    here = mixed.shape[1] // per
    images = mixed.shape[0]
    each = images // pieces

    def spread(total):
        total = total.astype(bf16)
        for piece in range(here):
            at = jnp.bitwise_xor(step * here + piece, sc[2])
            grads[at] = total[piece * per : (piece + 1) * per]

    @pl.when(step < 3)
    def _():
        ones = jnp.ones((8, mixed.shape[2]), bf16)
        total = count = None
        for image in range(images):
            left = grad_qkv[image // each][image % each]
            term, one = dot_nn(left, normed[image]), dot_nt(ones, left)
            total = term if image == 0 else total + term
            count = one if image == 0 else count + one
        sums[0] = count
        spread(total)

    @pl.when(step == 3)
    def _():
        total = dot_nn(mixed[0], grad_attn[0])
        for image in range(1, images):
            total = total + dot_nn(mixed[image], grad_attn[image])
        spread(total)


def first_back_kernel(pieces, images, sc, *refs):
    grad_qkv = refs[:pieces]
    w_qkv0, w_qkv1, tok, mod, grad_residual = refs[pieces : pieces + 5]
    grad_tokens, grad_own, sums, total = refs[pieces + 5 :]
    step = pl.program_id(0)
    each = images // pieces
    seq = tok.shape[1]

    def add(w_qkv, fresh):
        for one in range(images):
            term = dot_tn(grad_qkv[one // each][one % each], w_qkv[...])
            if fresh:
                total[one * seq : (one + 1) * seq, :] = term
            else:
                total[one * seq : (one + 1) * seq, :] += term

    @pl.when(step == 0)
    def _():
        add(w_qkv0, True)

    @pl.when(jnp.logical_and(step > 0, step < 3))
    def _():
        add(w_qkv0, False)

    @pl.when(jnp.logical_and(step >= 3, step < 6))
    def _():
        add(w_qkv1, False)

    @pl.when(step >= 6)
    def _():
        grad_normed = total[pl.ds(pl.multiple_of((step - 6) * seq, seq), seq), :]
        unit, recip = normalize(tok[0].astype(f32))
        sums[0, 0:1, :] = token_sum(grad_normed)
        sums[0, 1:2, :] = token_sum(grad_normed * unit)
        grad = grad_residual[0] + norm_pullback(grad_normed, unit, recip, mod[0, 1:2, :])
        grad_tokens[0] = grad
        grad_own[0] = grad


def output_kernel(
    part_steps, own_images, sc, act, w_down0, w_down1, residual, cot, mod, b_down, output, own, sums, total
):
    grow(total, part_steps, act[0], (w_down0, w_down1), ((0,), (0,)))
    one = pl.program_id(0) - 2 * part_steps
    seq = residual.shape[1]

    @pl.when(one >= 0)
    def _():
        live = jnp.where(sc[0] * own_images + one < sc[1], 1.0, 0.0).astype(f32)
        mlp_out = total[pl.ds(pl.multiple_of(one * seq, seq), seq), :] + b_down[...]
        sums[0] = token_sum((cot[0].astype(f32) * live) * mlp_out)
        rows = ((residual[0] + mod[0, 5:6, :] * mlp_out) * live).astype(bf16)
        output[0] = rows
        own[0] = rows


def final_piece(sc, halves, piece, store):
    rel = jnp.bitwise_xor(piece, sc[2])
    for low, high, bit, lo, hi in halves:
        index = ((rel >> (bit + 1)) << bit) | (rel & ((1 << bit) - 1))
        side = (rel >> bit) & 1

        @pl.when(side == 0)
        def _(low=low, index=index, lo=lo, hi=hi):
            store(low[index].astype(f32), lo, hi)

        @pl.when(side == 1)
        def _(high=high, index=index, lo=lo, hi=hi):
            store(high[index].astype(f32), lo, hi)


def final_mlp_kernel(cuts, per, sc, *refs):
    count = 2 * len(cuts)
    arrays, (_, _, down, up, mark, turned) = refs[:count], refs[count:]
    here = down.shape[0] // per
    halves = [(arrays[2 * k], arrays[2 * k + 1]) + cut for k, cut in enumerate(cuts)]
    for piece in range(here):

        def store(value, lo, hi, piece=piece):
            down[piece * per : (piece + 1) * per, lo:hi] = value[0:per]
            turned[piece * per : (piece + 1) * per, lo:hi] = value[per : 2 * per]

        final_piece(sc, halves, pl.program_id(0) * here + piece, store)
    up[...] = turned[...].T
    mark[...] = jnp.zeros_like(mark)


def final_plain_kernel(per, sc, summed, down_in, up_in, down, up, mark, turned):
    for piece in range(summed.shape[0]):
        lo = piece * per
        down[lo : lo + per, :] = summed[piece, 0:per, :].astype(f32)
        turned[lo : lo + per, :] = summed[piece, per : 2 * per, :].astype(f32)
    up[...] = turned[...].T
    mark[...] = jnp.zeros_like(mark)


def final_attn_kernel(cuts, per, sc, *refs):
    count = 2 * len(cuts)
    arrays, (qkv, proj) = refs[:count], refs[count:]
    here = proj.shape[0] // per
    halves = [(arrays[2 * k], arrays[2 * k + 1]) + cut for k, cut in enumerate(cuts)]
    for target, wanted in ((qkv, True), (proj, False)):

        @pl.when((pl.program_id(0) < 3) == wanted)
        def _(target=target):
            for piece in range(here):

                def store(value, lo, hi, piece=piece):
                    target[piece * per : (piece + 1) * per, lo:hi] = value

                final_piece(sc, halves, pl.program_id(0) * here + piece, store)


def run_kernel(
    body, sc, args, in_specs, out_specs, out_shape, grid, micros, scratch=(), alias=None, room=60
):
    size = sum(a.size * a.dtype.itemsize for a in args) + sum(
        s.size * s.dtype.itemsize for s in out_shape
    )
    return pl.pallas_call(
        body,
        out_shape=out_shape,
        grid_spec=pltpu.PrefetchScalarGridSpec(
            num_scalar_prefetch=1,
            grid=grid,
            in_specs=in_specs,
            out_specs=out_specs,
            scratch_shapes=list(scratch),
        ),
        compiler_params=pltpu.CompilerParams(vmem_limit_bytes=room << 20),
        cost_estimate=pl.CostEstimate(
            flops=int(micros * 1.15e9), bytes_accessed=int(min(size, micros * 1e6)), transcendentals=0
        ),
        input_output_aliases=alias or {},
    )(sc, *args)


def whole_block(array):
    zeros = (0,) * array.ndim
    return pl.BlockSpec(array.shape, lambda *_: zeros, pipeline_mode=pl.Buffered(1))


def shape_of(dims, kind):
    return jax.ShapeDtypeStruct(dims, kind)


SWAP = [(0, 1), (1, 0)]


def swap_cores(value):
    return lax.ppermute(value, "mp", SWAP)


def bit_pairs(bit):
    return [(index, index ^ (1 << bit)) for index in range(16)]


MLP_WAYS = ((0, 640, (0, 1, 2, 3)), (640, 1152, (1, 0, 2, 3)))
ATTN_WAYS = ((0, 512, (0, 1, 2, 3)), (512, 896, (1, 0, 2, 3)), (896, 1152, (2, 3, 0, 1)))


def cut(array, bits, bit, side, cols=None):
    lo = [0] * array.ndim
    hi = list(array.shape)
    place = bits.index(bit)
    lo[place], hi[place] = side, side + 1
    if cols is not None:
        lo[-1], hi[-1] = cols
    out = lax.slice(array, lo, hi)
    return out.reshape(out.shape[:place] + out.shape[place + 1 :])


def left_bits(done):
    return [bit for bit in (3, 2, 1, 0) if bit not in done]


def exchange(values, bits):
    return [lax.ppermute(value, "dp", bit_pairs(bit)) for value, bit in zip(values, bits)]


def reduce_flow(ways, get_own, other):
    shape = (2, 2, 2, 2) + other.shape[1:]
    (other,) = yield [other]
    came = swap_cores(other)
    yield None
    own, came = yield [get_own(), came]
    firsts, seconds = [own.reshape(shape)] * len(ways), [came.reshape(shape)] * len(ways)
    routes = [way for _, _, way in ways]
    for stage in range(4):
        sends, keeps = [], []
        for (lo, hi, _), route, one, two in zip(ways, routes, firsts, seconds):
            bits = left_bits(route[:stage])
            cols = (lo, hi) if stage == 0 else None
            for side, into in ((1, sends), (0, keeps)):
                into.append(
                    cut(one, bits, route[stage], side, cols) + cut(two, bits, route[stage], side, cols)
                )
        if stage == 2 and routes[0][2:] == routes[1][2:]:
            sends = [jnp.concatenate(sends[:2], axis=-1)] + sends[2:]
            keeps = [jnp.concatenate(keeps[:2], axis=-1)] + keeps[2:]
            routes = [routes[0]] + routes[2:]
            ways = [(0, 0, way) for way in routes]
        sends, keeps = yield [sends, keeps]
        comes = exchange(sends, [route[stage] for route in routes])
        yield None
        firsts, seconds = yield [keeps, comes]
    return [one + two for one, two in zip(firsts, seconds)]


def gather_flow(ways, have):
    routes = [ways[0][2]] + [way for _, _, way in ways[2:]]
    middle = ways[0][1]
    known = [[] for _ in routes]
    (have,) = yield [have]
    comes = exchange(have, [route[3] for route in routes])
    yield None
    for stage in (2, 1, 0):
        have, comes = yield [have, comes]
        joined = []
        for route, bits, one, two in zip(routes, known, have, comes):
            bit = route[stage + 1]
            place = sum(1 for other in bits if other > bit)
            joined.append(jnp.stack([one, two], axis=place))
            bits.insert(place, bit)
        if stage == 1:
            joined = [joined[0][..., :middle], joined[0][..., middle:]] + joined[1:]
            routes = [way for _, _, way in ways]
            known = [list(known[0]), list(known[0])] + known[1:]
        (have,) = yield [joined]
        comes = exchange(have, [route[stage] for route in routes])
        yield None
    have, comes = yield [have, comes]
    return [part.reshape((8,) + part.shape[-2:]) for pair in zip(have, comes) for part in pair]


def sum_flow(ways, get_own, other):
    have = yield from reduce_flow(ways, get_own, other)
    return (yield from gather_flow(ways, have))


def swap_flow(other):
    (other,) = yield [other]
    came = swap_cores(other)
    yield None
    (came,) = yield [came]
    return came


def rows_flow(rows):
    for bit in (3, 2, 1, 0):
        (rows,) = yield [rows]
        came = lax.ppermute(rows, "dp", bit_pairs(bit))
        yield None
        rows, came = yield [rows, came]
        rows = jnp.concatenate([rows, came])
    return rows


class Order:
    def __init__(self, sc):
        self.sc = sc
        self.results = {}

    def fence(self, values):
        self.sc, values = lax.optimization_barrier((self.sc, values))
        return values

    def after(self, value):
        self.sc, _ = lax.optimization_barrier((self.sc, value))

    def tick(self, *flows):
        replies = {flow: None for flow in flows if flow not in self.results}
        while replies:
            wants = {}
            for flow, reply in replies.items():
                try:
                    want = flow.send(reply)
                except StopIteration as stop:
                    self.results[flow] = stop.value
                    continue
                if want is not None:
                    wants[flow] = want
            replies = dict(zip(wants, self.fence(list(wants.values())))) if wants else {}

    def finish(self, flow):
        while flow not in self.results:
            self.tick(flow)
        return self.results[flow]


CHUNKS = 3


def fill_other(both, came, core):
    size = came.shape[0]
    return lax.dynamic_update_slice_in_dim(both, came, (1 - core) * size, 0)


def fast_device(
    tokens, condition, counts, w_qkv, b_qv, w_proj, b_proj, w_up, b_up, w_down, b_down, w_mod, b_mod,
    cotangent,
):
    slots, seq, dim = tokens.shape
    images = slots // 2
    count = images * seq
    cols = w_qkv.shape[2]
    ff = w_up.shape[1]
    own_cols = w_mod.shape[1]
    heads = cols // HEAD_DIM
    core = lax.axis_index("mp")
    order = Order(jnp.stack([core, counts[0], lax.axis_index("dp")]).astype(jnp.int32))

    qkv_rows = jnp.transpose(w_qkv, (1, 2, 0)).reshape(3 * cols, dim)
    wq = [qkv_rows, swap_cores(qkv_rows)]
    wp = [w_proj, swap_cores(w_proj)]
    qkv_bias = [b_qv, swap_cores(b_qv)]

    cond_f = condition.astype(f32)
    scaled = jax.nn.silu(cond_f).astype(bf16)
    own_mod = jnp.dot(scaled, w_mod, preferred_element_type=f32) + b_mod.astype(f32)
    other_mod = swap_cores(own_mod)
    sides = [jnp.where(core == side, own_mod, other_mod) for side in range(2)]
    modulation = jnp.concatenate(sides, axis=1).reshape(slots, 6, dim)
    proj_bias = b_proj.astype(f32)[None]
    down_bias = b_down.astype(f32)[None]

    late_up, late_down, late_bias = lax.optimization_barrier((wq[1], w_up, w_down, b_up, modulation))[1:4]
    wu = [w_up, swap_cores(late_up)]
    wd = [w_down, swap_cores(late_down)]
    up_bias = [b_up[None], swap_cores(late_bias[None])]

    local = lambda i, s: (s[0] * images + i, 0, 0)
    mine = lambda i, s: (i, 0, 0)
    tok_spec = pl.BlockSpec((1, seq, dim), local)
    own_spec = pl.BlockSpec((1, seq, dim), mine)
    mod_spec = pl.BlockSpec((1, 6, dim), local)
    row_spec = pl.BlockSpec((1, 1, dim), mine)
    qkv_spec = pl.BlockSpec((1, 6 * cols, seq), mine)
    prob_spec = pl.BlockSpec((1, 2 * heads, seq, seq), lambda i, s: (i, 0, 0, 0))
    mixed_spec = pl.BlockSpec((1, 2 * cols, seq), mine)
    token_f = shape_of((images, seq, dim), f32)
    token_b = shape_of((images, seq, dim), bf16)
    attn_args = wq + wp + qkv_bias
    qkv, prob, mixed, attn_out, residual, normed_mlp, normed, grad_mlp, down_sums = run_kernel(
        functools.partial(attention_kernel, 2, images),
        order.sc,
        [tokens, cotangent, modulation, proj_bias] + attn_args,
        [tok_spec, tok_spec, mod_spec, whole_block(proj_bias)] + [whole_block(a) for a in attn_args],
        [qkv_spec, prob_spec, mixed_spec] + [own_spec] * 5 + [row_spec],
        [
            shape_of((images, 6 * cols, seq), bf16),
            shape_of((images, 2 * heads, seq, seq), bf16),
            shape_of((images, 2 * cols, seq), bf16),
            token_f,
            token_f,
            token_b,
            token_b,
            token_b,
            shape_of((images, 1, dim), f32),
        ],
        (images,),
        45,
    )
    order.after(down_sums)

    rows_flat = normed_mlp.reshape(count, dim)
    grad_flat = grad_mlp.reshape(count, dim)
    width = ff // CHUNKS
    per = width // 16
    steps = 2
    block = width // steps
    anywhere = pl.BlockSpec(memory_space=pl.ANY)
    act = back = jnp.zeros((8, 128), bf16)
    up_sums = {}

    def mlp_call(jobs, came, micros):
        nonlocal act, back
        first = act.shape[0] == 8
        kinds = tuple((job[0] > 0, job in came) for job in jobs)

        def turn(k):
            return lambda p, s, c: jnp.clip((p - k) * steps + s, 0, steps - 1)

        def pick(values):
            return lambda p: sum(jnp.where(p == k, value, 0) for k, value in enumerate(values))

        parts = pick([part for _, part in jobs])
        starts = pick([chunk * steps for chunk, _ in jobs])
        spread = pl.BlockSpec((1, block, count), lambda p, s, c: (parts(p), starts(p) + s, 0))
        args, specs = [], []
        for k, (chunk, part) in enumerate(jobs):
            at = chunk * steps
            wide = lambda p, s, c, k=k, at=at: (0, at + turn(k)(p, s, c))
            tall = lambda p, s, c, k=k, at=at: (at + turn(k)(p, s, c), 0)
            args += [wu[part], wd[part], up_bias[part]]
            specs += [
                pl.BlockSpec((dim, block), wide),
                pl.BlockSpec((block, dim), tall),
                pl.BlockSpec((1, block), wide),
            ]
        grad_specs = []
        for k, (natural, _) in enumerate(kinds):
            own = lambda p, s, c, k=k: (turn(k)(p, s, c), 0, 0)
            fixed = lambda p, s, c: (0, 0, 0)
            grad_specs.append(
                pl.BlockSpec((16 // steps, 2 * per, dim), own)
                if natural
                else pl.BlockSpec((16, 2 * per, dim), fixed)
            )
        for k, job in enumerate(jobs):
            if job in came:
                args.append(came[job])
                specs.append(grad_specs[k])
        args += [act, back]
        spot = len(args) + 1
        outs = run_kernel(
            functools.partial(mlp_kernel, per, kinds),
            order.sc,
            [rows_flat, grad_flat] + args,
            [whole_block(rows_flat), whole_block(grad_flat)] + specs + [anywhere, anywhere],
            [spread, spread]
            + grad_specs
            + [pl.BlockSpec((8, block), lambda p, s, c, k=k: (0, turn(k)(p, s, c))) for k in range(len(jobs))],
            [shape_of((2, ff, count), bf16)] * 2
            + [shape_of((16, 2 * per, dim), bf16)] * len(jobs)
            + [shape_of((8, width), f32)] * len(jobs),
            (len(jobs), steps),
            micros,
            alias=None if first else {spot: 0, spot + 1: 1},
        )
        act, back = outs[:2]
        grads = outs[2 : 2 + len(jobs)]
        for job, sums in zip(jobs, outs[2 + len(jobs) :]):
            up_sums[job] = sums[0:1]
        order.after(outs[-1])
        return grads

    summed = range(1, CHUNKS)
    (grad_other,) = mlp_call([(0, 1)], {}, 13)
    made_first = []
    flows = [sum_flow(MLP_WAYS, lambda: made_first[0], grad_other)]
    order.tick(*flows)
    grads = mlp_call([(chunk, 1) for chunk in summed], {}, 26)
    swaps = [swap_flow(grad) for grad in grads]
    order.tick(*swaps)
    made_first += mlp_call([(0, 0)], {}, 13)
    order.tick(*flows, *swaps)
    came = {(chunk, 0): order.results[swap] for chunk, swap in zip(summed, swaps)}
    plain_sums = lax.psum(mlp_call([(chunk, 0) for chunk in summed], came, 26), "dp")
    order.tick(*flows)

    reach = 768
    turns = ff // reach
    every = lambda s, c: (0, 0, 0)
    tail = lambda first: lambda s, c: (jnp.maximum(s - first, 0), 0, 0)
    tail_local = lambda first: lambda s, c: (c[0] * images + jnp.maximum(s - first, 0), 0, 0)

    def image_spec(first, where=tail):
        return pl.BlockSpec((1, seq, dim), where(first))

    def rows_of(part, size):
        if part == 0:
            return lambda s, c: jnp.minimum(s, size - 1)
        return lambda s, c: jnp.clip(s - size, 0, size - 1)

    span_spec = pl.BlockSpec(
        (1, reach, count),
        lambda s, c: (jnp.minimum(s // turns, 1), jnp.where(s < 2 * turns, s % turns, turns - 1), 0),
    )
    grad_residual, grad_attn, mid_sums = run_kernel(
        functools.partial(norm_back_kernel, turns, images),
        order.sc,
        [back] + wu + [residual, cotangent, modulation, attn_out],
        [
            span_spec,
            pl.BlockSpec((dim, reach), lambda s, c: (0, rows_of(0, turns)(s, c))),
            pl.BlockSpec((dim, reach), lambda s, c: (0, rows_of(1, turns)(s, c))),
            image_spec(2 * turns),
            image_spec(2 * turns, tail_local),
            pl.BlockSpec((1, 6, dim), tail_local(2 * turns)),
            image_spec(2 * turns),
        ],
        [image_spec(2 * turns)] * 2 + [pl.BlockSpec((1, 4, dim), tail(2 * turns))],
        [token_f, token_b, shape_of((images, 4, dim), f32)],
        (2 * turns + images,),
        60,
        scratch=[pltpu.VMEM((count, dim), f32)],
    )
    order.after(mid_sums)
    order.tick(*flows)
    pieces = 2
    each = images // pieces
    grad_qkv = []
    for piece in range(pieces):
        there = lambda i, s, piece=piece: (piece * each + i, 0, 0)
        (grad_piece,) = run_kernel(
            functools.partial(back_kernel, 2),
            order.sc,
            [grad_attn, qkv, prob] + wp,
            [
                pl.BlockSpec((1, seq, dim), there),
                pl.BlockSpec((1, 6 * cols, seq), there),
                pl.BlockSpec((1, 2 * heads, seq, seq), lambda i, s, piece=piece: (piece * each + i, 0, 0, 0)),
            ]
            + [whole_block(a) for a in wp],
            [qkv_spec],
            [shape_of((each, 6 * cols, seq), bf16)],
            (each,),
            60,
            scratch=[pltpu.VMEM((2 * cols, seq), bf16)],
            )
        grad_qkv.append(grad_piece)
        order.after(grad_piece)
        order.tick(*flows)

    attn_per = 4 * cols // 16
    qv_sums = [None, None]

    def attn_part(part):
        grads, sums = run_kernel(
            functools.partial(attn_grad_kernel, pieces, attn_per),
            order.sc,
            grad_qkv + [mixed, normed, grad_attn],
            [
                pl.BlockSpec((each, cols, seq), lambda s, c: (0, 3 * part + jnp.minimum(s, 2), 0))
                for _ in range(pieces)
            ]
            + [pl.BlockSpec((images, cols, seq), lambda s, c: (0, part, 0))]
            + [whole_block(normed), whole_block(grad_attn)],
            [
                pl.BlockSpec((16, attn_per, dim), every),
                pl.BlockSpec((1, 8, cols), lambda s, c: (jnp.minimum(s, 2), 0, 0)),
            ],
            [shape_of((16, attn_per, dim), bf16), shape_of((3, 8, cols), f32)],
            (4,),
            60,
            )
        qv_sums[part] = sums
        order.after(sums)
        return grads

    grad_other = attn_part(1)
    made = []
    last = sum_flow(ATTN_WAYS, lambda: made[0], grad_other)
    order.tick(last, *flows)
    made.append(attn_part(0))
    order.tick(last, *flows)

    first_spec = lambda part: pl.BlockSpec((cols, dim), lambda s, c: (rows_of(part, 3)(s, c), 0))
    grad_tokens, grad_own_tokens, low_sums = run_kernel(
        functools.partial(first_back_kernel, pieces, images),
        order.sc,
        grad_qkv + wq + [tokens, modulation, grad_residual],
        [pl.BlockSpec((each, cols, seq), lambda s, c: (0, jnp.minimum(s, 5), 0)) for _ in range(pieces)]
        + [first_spec(0), first_spec(1)]
        + [image_spec(6, tail_local), pl.BlockSpec((1, 6, dim), tail_local(6)), image_spec(6)],
        [image_spec(6, tail_local), image_spec(6), pl.BlockSpec((1, 2, dim), tail(6))],
        [shape_of((slots, seq, dim), f32), token_f, shape_of((images, 2, dim), f32)],
        (6 + images,),
        60,
        scratch=[pltpu.VMEM((count, dim), f32)],
    )
    order.after(low_sums)
    order.tick(last, *flows)
    other_tokens = swap_cores(grad_own_tokens)
    down_spec = lambda part: pl.BlockSpec((reach, dim), lambda s, c: (rows_of(part, turns)(s, c), 0))
    output, own_output, gate_sums = run_kernel(
        functools.partial(output_kernel, turns, images),
        order.sc,
        [act] + wd + [residual, cotangent, modulation, down_bias],
        [
            span_spec,
            down_spec(0),
            down_spec(1),
            image_spec(2 * turns),
            image_spec(2 * turns, tail_local),
            pl.BlockSpec((1, 6, dim), tail_local(2 * turns)),
            whole_block(down_bias),
        ],
        [image_spec(2 * turns, tail_local), image_spec(2 * turns), pl.BlockSpec((1, 1, dim), tail(2 * turns))],
        [shape_of((slots, seq, dim), bf16), token_b, shape_of((images, 1, dim), f32)],
        (2 * turns + images,),
        60,
        scratch=[pltpu.VMEM((count, dim), f32)],
    )
    order.after(gate_sums)
    order.tick(last, *flows)
    other_output = swap_cores(own_output)

    low_sums, mid_sums, gate_sums, down_sums = order.fence((low_sums, mid_sums, gate_sums, down_sums))
    grad_modulation = jnp.concatenate([low_sums, mid_sums[:, 2:3], mid_sums[:, 0:2], gate_sums], axis=1)
    grad_modulation = grad_modulation.reshape(images, 6 * dim).astype(bf16)
    bias_sums = [
        jnp.concatenate(
            [qv_sums[part][0, 0:1], qv_sums[part][2, 0:1]]
            + [up_sums[chunk, part] for chunk in range(CHUNKS)],
            axis=1,
        )
        for part in range(2)
    ]
    shared = jnp.concatenate(
        [
            jnp.sum(mid_sums[:, 3], axis=0, keepdims=True),
            jnp.sum(down_sums[:, 0], axis=0, keepdims=True),
            jnp.zeros((1, own_cols - 2 * dim), f32),
        ],
        axis=1,
    )
    halves = grad_modulation.reshape(images, 2, own_cols)
    kept = lax.dynamic_index_in_dim(halves, core, 1, keepdims=False)
    given = lax.dynamic_index_in_dim(halves, 1 - core, 1, keepdims=False)
    got = swap_cores(jnp.concatenate([given.astype(f32), bias_sums[1], shared]))
    came = got[:images].astype(bf16)
    group_mod = jnp.where(core == 0, jnp.concatenate([kept, came]), jnp.concatenate([came, kept]))
    own_bias_sum = bias_sums[0] + got[images : images + 1]
    shared_sum = shared + got[images + 1 :]
    wide_scaled = jnp.pad(scaled.reshape(-1), (0, 3 * own_cols - slots * dim)).reshape(3, own_cols)
    packed_rows = jnp.concatenate(
        [group_mod, own_bias_sum.astype(bf16), shared_sum.astype(bf16), wide_scaled]
    )
    (packed_rows,) = order.fence([packed_rows])
    small = rows_flow(packed_rows)
    order.tick(last, small, *flows)
    (group_mod,) = order.fence([group_mod])
    part_scaled = outer_cols(group_mod, w_mod).astype(bf16)
    came_scaled = swap_cores(part_scaled)
    output = fill_other(output, order.fence(other_output), core)
    order.after((output[0, 0, :1], part_scaled[0, :1]))
    order.tick(last, small, *flows)
    grad_tokens = fill_other(grad_tokens, order.fence(other_tokens), core)
    part_scaled, came_scaled = order.fence((part_scaled, came_scaled))
    grad_scaled = part_scaled.astype(f32) + came_scaled.astype(f32)
    _, silu_back = jax.vjp(jax.nn.silu, cond_f)
    grad_condition = silu_back(grad_scaled)[0]
    order.after((grad_tokens[0, 0, :1], grad_condition[0, :1]))
    order.tick(last, small, *flows)

    def cuts(ways):
        return tuple((way[0], lo, hi) for lo, hi, way in ways)

    grad_w_down = grad_w_up = jnp.zeros((8, 128), f32)

    def final_mlp(chunk, body, args):
        nonlocal grad_w_down, grad_w_up
        first = grad_w_down.shape[0] == 8
        spot = len(args) + 1
        grad_w_down, grad_w_up, mark = run_kernel(
            body,
            order.sc,
            list(args) + [grad_w_down, grad_w_up],
            [
                whole_block(a)
                if a.shape[0] == 8
                else pl.BlockSpec((16 // steps,) + a.shape[1:], lambda s, c: (s, 0, 0))
                for a in args
            ]
            + [anywhere, anywhere],
            [
                pl.BlockSpec((block, dim), lambda s, c: (chunk * steps + s, 0)),
                pl.BlockSpec((dim, block), lambda s, c: (0, chunk * steps + s)),
                pl.BlockSpec((8, 128), lambda s, c: (0, 0)),
            ],
            [shape_of((ff, dim), f32), shape_of((dim, ff), f32), shape_of((8, 128), f32)],
            (steps,),
            4,
            scratch=[pltpu.VMEM((block, dim), f32)],
            alias=None if first else {spot: 0, spot + 1: 1},
        )
        order.after(mark)

    for chunk, flow in enumerate(flows):
        body = functools.partial(final_mlp_kernel, cuts(MLP_WAYS), per)
        final_mlp(chunk, body, order.finish(flow))
    order.tick(last, small)
    for chunk, total in zip(summed, order.fence(plain_sums)):
        final_mlp(chunk, functools.partial(final_plain_kernel, per), [total])
    order.tick(last)
    all_rows = order.fence(order.finish(small)).reshape(16, slots + 5, own_cols)
    all_mod = all_rows[:, :slots].reshape(-1, own_cols)
    all_scaled = all_rows[:, slots + 2 :].reshape(16, -1)[:, : slots * dim].reshape(-1, dim)
    grad_w_mod = inner_rows(all_scaled, all_mod)
    grad_b_mod = jnp.sum(all_mod.astype(f32), axis=0)
    bias_total = jnp.sum(all_rows[:, slots : slots + 2].astype(f32), axis=0)
    grad_b_qv = bias_total[0, : 2 * cols].reshape(2, cols)
    grad_b_up = bias_total[0, 2 * cols :]
    grad_b_proj = bias_total[1, :dim]
    grad_b_down = bias_total[1, dim : 2 * dim]
    order.after((grad_w_mod[0, :1], grad_b_mod[:1], bias_total[0, :1]))
    args = order.finish(last)
    grad_qkv_rows, grad_w_proj = run_kernel(
        functools.partial(final_attn_kernel, cuts(ATTN_WAYS), attn_per),
        order.sc,
        list(args),
        [whole_block(a) for a in args],
        [
            pl.BlockSpec((cols, dim), lambda s, c: (jnp.minimum(s, 2), 0)),
            pl.BlockSpec((cols, dim), lambda s, c: (0, 0)),
        ],
        [shape_of((3 * cols, dim), f32), shape_of((cols, dim), f32)],
        (4,),
        9,
    )
    grad_w_qkv = jnp.transpose(grad_qkv_rows.reshape(3, cols, dim), (2, 0, 1))
    return (
        output,
        grad_tokens,
        grad_condition,
        grad_w_qkv,
        grad_b_qv,
        grad_w_proj,
        grad_b_proj,
        grad_w_up,
        grad_b_up,
        grad_w_down,
        grad_b_down,
        grad_w_mod,
        grad_b_mod,
    )


def layer_norm(values):
    center = values - jnp.mean(values, axis=-1, keepdims=True)
    return center * lax.rsqrt(jnp.mean(center * center, axis=-1, keepdims=True) + epsilon)


def modulate(values, shift_part, scale_part):
    return layer_norm(values) * (1.0 + scale_part) + shift_part


def gelu_tanh(values):
    return (
        0.5
        * values
        * (1.0 + jnp.tanh(0.7978845608028654 * (values + 0.044715 * values * values * values)))
    )


def inner_rows(left, right):
    return lax.dot_general(
        left, right, (((0,), (0,)), ((), ())), preferred_element_type=jnp.float32
    )


def outer_cols(left, right):
    return lax.dot_general(
        left, right, (((1,), (1,)), ((), ())), preferred_element_type=jnp.float32
    )


def attention_forward(query_rows, key_rows, value_rows):
    factor = HEAD_DIM ** (-0.5)
    scores = (
        jnp.einsum("bqhd,bkhd->bhqk", query_rows, key_rows, preferred_element_type=jnp.float32)
        * factor
    )
    row_max = jnp.max(scores, axis=-1, keepdims=True)
    row_total = jnp.sum(jnp.exp(scores - row_max), axis=-1, keepdims=True)
    logsum = row_max + jnp.log(row_total)
    prob_b = jnp.exp(scores - logsum).astype(jnp.bfloat16)
    mixed_out = jnp.einsum(
        "bhqk,bkhd->bqhd", prob_b, value_rows, preferred_element_type=jnp.float32
    )
    return (mixed_out, logsum)


def attention_backward(query_rows, key_rows, value_rows, logsum, grad_mixed):
    factor = HEAD_DIM ** (-0.5)
    scores = (
        jnp.einsum("bqhd,bkhd->bhqk", query_rows, key_rows, preferred_element_type=jnp.float32)
        * factor
    )
    prob_f = jnp.exp(scores - logsum)
    prob_b = prob_f.astype(jnp.bfloat16)
    grad_prob = jnp.einsum(
        "bqhd,bkhd->bhqk", grad_mixed, value_rows, preferred_element_type=jnp.float32
    )
    row_delta = jnp.sum(prob_f * grad_prob, axis=-1, keepdims=True)
    grad_scores = (prob_f * (grad_prob - row_delta)).astype(jnp.bfloat16)
    grad_query = (
        jnp.einsum("bhqk,bkhd->bqhd", grad_scores, key_rows, preferred_element_type=jnp.float32)
        * factor
    )
    grad_key = (
        jnp.einsum("bhqk,bqhd->bkhd", grad_scores, query_rows, preferred_element_type=jnp.float32)
        * factor
    )
    grad_value = jnp.einsum(
        "bhqk,bqhd->bkhd", prob_b, grad_mixed, preferred_element_type=jnp.float32
    )
    return (
        grad_query.astype(jnp.bfloat16),
        grad_key.astype(jnp.bfloat16),
        grad_value.astype(jnp.bfloat16),
    )


def forward(tokens_f, spans, weights, repeat):
    w_qkv, b_qv, w_proj, b_proj, w_up, b_up, w_down, b_down = weights
    shift_attn, scale_attn, gate_attn, shift_mlp, scale_mlp, gate_mlp = spans
    slot_count, seq_len, model_dim = tokens_f.shape
    row_count = slot_count * seq_len
    head_cols = w_qkv.shape[2]
    head_count = head_cols // HEAD_DIM
    shape_four = (slot_count, seq_len, head_count, HEAD_DIM)
    normed = (
        modulate(tokens_f, shift_attn, scale_attn)
        .astype(jnp.bfloat16)
        .reshape(row_count, model_dim)
    )
    projected = jnp.dot(
        normed, w_qkv.reshape(model_dim, 3 * head_cols), preferred_element_type=jnp.float32
    )
    qkv_bias = jnp.stack([b_qv[0], jnp.zeros_like(b_qv[0]), b_qv[1]]).astype(jnp.float32)
    projected = (projected.reshape(row_count, 3, head_cols) + qkv_bias).astype(jnp.bfloat16)
    query_rows = projected[:, 0].reshape(shape_four)
    key_rows = projected[:, 1].reshape(shape_four)
    value_rows = projected[:, 2].reshape(shape_four)
    mixed_out, logsum = attention_forward(query_rows, key_rows, value_rows)
    mixed_b = mixed_out.astype(jnp.bfloat16).reshape(row_count, head_cols)
    partial_value = jnp.dot(mixed_b, w_proj, preferred_element_type=jnp.float32)
    if repeat:
        summed = lax.psum(partial_value.astype(jnp.bfloat16), "mp").astype(jnp.float32)
    else:
        summed = lax.psum(partial_value.astype(jnp.bfloat16), "mp").astype(jnp.float32)
    attn_out = (summed + b_proj.astype(jnp.float32)).reshape(slot_count, seq_len, model_dim)
    residual = tokens_f + gate_attn * attn_out
    normed_mlp = (
        modulate(residual, shift_mlp, scale_mlp).astype(jnp.bfloat16).reshape(row_count, model_dim)
    )
    hidden = jnp.dot(normed_mlp, w_up, preferred_element_type=jnp.float32) + b_up.astype(
        jnp.float32
    )
    act_bf = gelu_tanh(hidden).astype(jnp.bfloat16)
    partial_mlp = jnp.dot(act_bf, w_down, preferred_element_type=jnp.float32)
    if repeat:
        summed_mlp = lax.psum(partial_mlp.astype(jnp.bfloat16), "mp").astype(jnp.float32)
    else:
        summed_mlp = lax.psum(partial_mlp.astype(jnp.bfloat16), "mp").astype(jnp.float32)
    mlp_out = (summed_mlp + b_down.astype(jnp.float32)).reshape(slot_count, seq_len, model_dim)
    output = residual + gate_mlp * mlp_out
    return {
        "normed": normed,
        "query_rows": query_rows,
        "key_rows": key_rows,
        "value_rows": value_rows,
        "logsum": logsum,
        "mixed_b": mixed_b,
        "attn_out": attn_out,
        "residual": residual,
        "normed_mlp": normed_mlp,
        "hidden": hidden,
        "act_bf": act_bf,
        "mlp_out": mlp_out,
        "output": output,
    }


def image_pass(tokens_f, grad_out, spans, weights):
    w_qkv, b_qv, w_proj, b_proj, w_up, b_up, w_down, b_down = weights
    shift_attn, scale_attn, gate_attn, shift_mlp, scale_mlp, gate_mlp = spans
    slot_count, seq_len, model_dim = tokens_f.shape
    row_count = slot_count * seq_len
    head_cols = w_qkv.shape[2]
    head_count = head_cols // HEAD_DIM
    kept_fwd = forward(tokens_f, spans, weights, False)
    out_one = kept_fwd["output"]
    stored = forward(tokens_f, spans, weights, True)
    grad_gate_mlp = jnp.sum(grad_out * stored["mlp_out"], axis=1)
    grad_mlp = (gate_mlp * grad_out).astype(jnp.bfloat16).reshape(row_count, model_dim)
    grad_b_down = jnp.sum(grad_mlp.astype(jnp.float32), axis=0)
    grad_w_down = inner_rows(stored["act_bf"], grad_mlp)
    grad_act = outer_cols(grad_mlp, w_down)
    gelu_value, gelu_back = jax.vjp(gelu_tanh, stored["hidden"])
    grad_hidden = gelu_back(grad_act)[0].astype(jnp.bfloat16)
    grad_b_up = jnp.sum(grad_hidden.astype(jnp.float32), axis=0)
    grad_w_up = inner_rows(stored["normed_mlp"], grad_hidden)
    part_normed_mlp = outer_cols(grad_hidden, w_up)
    grad_normed_mlp = (
        lax.psum(part_normed_mlp.astype(jnp.bfloat16), "mp")
        .astype(jnp.float32)
        .reshape(slot_count, seq_len, model_dim)
    )
    norm_value, norm_back = jax.vjp(modulate, stored["residual"], shift_mlp, scale_mlp)
    grad_resid_norm, grad_shift_mlp, grad_scale_mlp = norm_back(grad_normed_mlp)
    grad_residual = grad_out + grad_resid_norm
    grad_gate_attn = jnp.sum(grad_residual * stored["attn_out"], axis=1)
    grad_attn = (gate_attn * grad_residual).astype(jnp.bfloat16).reshape(row_count, model_dim)
    grad_b_proj = jnp.sum(grad_attn.astype(jnp.float32), axis=0)
    grad_w_proj = inner_rows(stored["mixed_b"], grad_attn)
    grad_mixed = (
        outer_cols(grad_attn, w_proj)
        .astype(jnp.bfloat16)
        .reshape(slot_count, seq_len, head_count, HEAD_DIM)
    )
    grad_query, grad_key, grad_value = attention_backward(
        stored["query_rows"], stored["key_rows"], stored["value_rows"], stored["logsum"], grad_mixed
    )
    grad_qkv = jnp.stack(
        [
            grad_query.reshape(row_count, head_cols),
            grad_key.reshape(row_count, head_cols),
            grad_value.reshape(row_count, head_cols),
        ],
        axis=1,
    )
    grad_b_qv = jnp.stack(
        [
            jnp.sum(grad_qkv[:, 0].astype(jnp.float32), axis=0),
            jnp.sum(grad_qkv[:, 2].astype(jnp.float32), axis=0),
        ]
    )
    grad_w_qkv = inner_rows(stored["normed"], grad_qkv)
    part_normed = outer_cols(
        grad_qkv.reshape(row_count, 3 * head_cols), w_qkv.reshape(model_dim, 3 * head_cols)
    )
    grad_normed = (
        lax.psum(part_normed.astype(jnp.bfloat16), "mp")
        .astype(jnp.float32)
        .reshape(slot_count, seq_len, model_dim)
    )
    first_value, first_back = jax.vjp(modulate, tokens_f, shift_attn, scale_attn)
    grad_tok_norm, grad_shift_attn, grad_scale_attn = first_back(grad_normed)
    grad_tok_one = grad_residual + grad_tok_norm
    grad_mod_one = jnp.concatenate(
        [
            grad_shift_attn[:, 0],
            grad_scale_attn[:, 0],
            grad_gate_attn,
            grad_shift_mlp[:, 0],
            grad_scale_mlp[:, 0],
            grad_gate_mlp,
        ],
        axis=1,
    )
    grad_terms = (
        grad_w_qkv,
        grad_b_qv,
        grad_w_proj,
        grad_b_proj,
        grad_w_up,
        grad_b_up,
        grad_w_down,
        grad_b_down,
    )
    return (out_one, grad_tok_one, grad_mod_one, grad_terms)


def run_layer(tokens, condition, cotangent, live_count, turns, weights, w_mod, b_mod):
    slot_count, seq_len, model_dim = tokens.shape
    cond_f = condition.astype(jnp.float32)
    scaled = jax.nn.silu(cond_f).astype(jnp.bfloat16)
    own_mod = jnp.dot(scaled, w_mod, preferred_element_type=jnp.float32) + b_mod.astype(jnp.float32)
    modulation = lax.all_gather(own_mod, "mp", axis=1, tiled=True)
    tokens_f = tokens.astype(jnp.float32)
    cot_f = cotangent.astype(jnp.float32)

    def image_step(slot_idx, carry):
        out_buf, grad_buf, mod_buf, grad_sums = carry
        live_flag = (slot_idx < live_count).astype(jnp.float32)
        tok_one = lax.dynamic_slice_in_dim(tokens_f, slot_idx, 1, 0)
        cot_one = lax.dynamic_slice_in_dim(cot_f, slot_idx, 1, 0) * live_flag
        mod_row = lax.dynamic_slice_in_dim(modulation, slot_idx, 1, 0)
        spans = [
            mod_row[:, None, part_idx * model_dim : (part_idx + 1) * model_dim]
            for part_idx in range(6)
        ]
        out_one, grad_tok_one, grad_mod_one, grad_terms = image_pass(
            tok_one, cot_one, spans, weights
        )
        out_one = (out_one * live_flag).astype(jnp.bfloat16)
        out_buf = lax.dynamic_update_slice_in_dim(out_buf, out_one, slot_idx, 0)
        grad_buf = lax.dynamic_update_slice_in_dim(grad_buf, grad_tok_one, slot_idx, 0)
        mod_buf = lax.dynamic_update_slice_in_dim(mod_buf, grad_mod_one, slot_idx, 0)
        grad_sums = tuple((total_a + term_b for total_a, term_b in zip(grad_sums, grad_terms)))
        return (out_buf, grad_buf, mod_buf, grad_sums)

    start_sums = tuple((jnp.zeros(weight_in.shape, jnp.float32) for weight_in in weights))
    start_state = (
        jnp.zeros(tokens.shape, jnp.bfloat16),
        jnp.zeros(tokens.shape, jnp.float32),
        jnp.zeros((slot_count, 6 * model_dim), jnp.float32),
        start_sums,
    )
    out_buf, grad_buf, mod_buf, grad_sums = lax.fori_loop(0, turns, image_step, start_state)
    grad_modulation = mod_buf.astype(jnp.bfloat16)
    own_cols = w_mod.shape[1]
    grad_own = lax.dynamic_slice_in_dim(
        grad_modulation, lax.axis_index("mp") * own_cols, own_cols, 1
    )
    part_scaled = outer_cols(grad_own, w_mod)
    grad_scaled = lax.psum(part_scaled.astype(jnp.bfloat16), "mp").astype(jnp.float32)
    silu_value, silu_back = jax.vjp(jax.nn.silu, cond_f)
    grad_condition = silu_back(grad_scaled)[0]
    return (out_buf, grad_buf, grad_condition, grad_sums, scaled, grad_own)


def on_device(
    tokens,
    condition,
    counts,
    w_qkv,
    b_qv,
    w_proj,
    b_proj,
    w_up,
    b_up,
    w_down,
    b_down,
    w_mod,
    b_mod,
    cotangent,
):
    slot_count, seq_len, model_dim = tokens.shape
    weights = (w_qkv, b_qv, w_proj, b_proj, w_up, b_up, w_down, b_down)
    own_count = counts[0]
    output, grad_tokens, grad_condition, grad_sums, scaled, grad_own = run_layer(
        tokens, condition, cotangent, own_count, slot_count, weights, w_mod, b_mod
    )
    (
        grad_w_qkv,
        grad_b_qv,
        grad_w_proj,
        grad_b_proj,
        grad_w_up,
        grad_b_up,
        grad_w_down,
        grad_b_down,
    ) = grad_sums
    grad_w_mod = inner_rows(scaled, grad_own)
    grad_b_mod = jnp.sum(grad_own.astype(jnp.float32), axis=0)
    (
        grad_w_qkv,
        grad_b_qv,
        grad_w_proj,
        grad_b_proj,
        grad_w_up,
        grad_b_up,
        grad_w_down,
        grad_b_down,
        grad_w_mod,
        grad_b_mod,
    ) = (
        lax.psum(grad_w_qkv.astype(jnp.bfloat16), "dp").astype(jnp.float32),
        lax.psum(grad_b_qv.astype(jnp.bfloat16), "dp").astype(jnp.float32),
        lax.psum(grad_w_proj.astype(jnp.bfloat16), "dp").astype(jnp.float32),
        lax.psum(grad_b_proj.astype(jnp.bfloat16), "dp").astype(jnp.float32),
        lax.psum(grad_w_up.astype(jnp.bfloat16), "dp").astype(jnp.float32),
        lax.psum(grad_b_up.astype(jnp.bfloat16), "dp").astype(jnp.float32),
        lax.psum(grad_w_down.astype(jnp.bfloat16), "dp").astype(jnp.float32),
        lax.psum(grad_b_down.astype(jnp.bfloat16), "dp").astype(jnp.float32),
        lax.psum(grad_w_mod.astype(jnp.bfloat16), "dp").astype(jnp.float32),
        lax.psum(grad_b_mod.astype(jnp.bfloat16), "dp").astype(jnp.float32),
    )
    return (
        output,
        grad_tokens,
        grad_condition,
        grad_w_qkv,
        grad_b_qv,
        grad_w_proj,
        grad_b_proj,
        grad_w_up,
        grad_b_up,
        grad_w_down,
        grad_b_down,
        grad_w_mod,
        grad_b_mod,
    )


def solution(mesh):
    placed = (
        P("dp", None, None),
        P("dp", None),
        P("dp"),
        P(None, None, "mp"),
        P(None, "mp"),
        P("mp", None),
        P(),
        P(None, "mp"),
        P("mp"),
        P("mp", None),
        P(),
        P(None, "mp"),
        P("mp"),
        P("dp", None, None),
    )
    fast = mesh.shape["dp"] == 16 and mesh.shape["mp"] == 2
    return jax.shard_map(
        fast_device if fast else on_device,
        mesh=mesh,
        in_specs=placed,
        out_specs=(
            P("dp", None, None),
            P("dp", None, None),
            P("dp", None),
            P(None, None, "mp"),
            P(None, "mp"),
            P("mp", None),
            P(),
            P(None, "mp"),
            P("mp"),
            P("mp", None),
            P(),
            P(None, "mp"),
            P("mp"),
        ),
        check_vma=False,
    )
```

```python
import functools

import jax
import jax.numpy as jnp
from jax import lax
from jax.experimental import pallas as pl
from jax.experimental.pallas import tpu as pltpu
from jax.sharding import PartitionSpec as P

HEAD_DIM = 72


epsilon = 1e-06

f32 = jnp.float32
bf16 = jnp.bfloat16


def dot_nn(left, right):
    return lax.dot_general(left, right, (((1,), (0,)), ((), ())), preferred_element_type=f32)


def dot_nt(left, right):
    return lax.dot_general(left, right, (((1,), (1,)), ((), ())), preferred_element_type=f32)


def dot_tn(left, right):
    return lax.dot_general(left, right, (((0,), (0,)), ((), ())), preferred_element_type=f32)


def normalize(values):
    center = values - jnp.mean(values, axis=-1, keepdims=True)
    recip = lax.rsqrt(jnp.mean(center * center, axis=-1, keepdims=True) + epsilon)
    return center * recip, recip


def norm_pullback(grad_normed, unit, recip, scale_row):
    scaled_grad = grad_normed * (1.0 + scale_row)
    mean_grad = jnp.mean(scaled_grad, axis=-1, keepdims=True)
    mean_unit = jnp.mean(scaled_grad * unit, axis=-1, keepdims=True)
    return recip * (scaled_grad - mean_grad - unit * mean_unit)


def column(row):
    return jnp.broadcast_to(row[...].astype(f32), (8, row.shape[1])).T[:, 0:1]


def token_sum(values):
    return jnp.sum(values, axis=0, keepdims=True)


def attention_kernel(parts, own_images, sc, tok, cot, mod, b_proj, *refs):
    w_qkv, w_proj, bias = refs[:parts], refs[parts : 2 * parts], refs[2 * parts : 3 * parts]
    qkv, prob, mixed, attn_out, residual, normed_mlp, normed, grad_mlp, down_sums = refs[3 * parts :]
    image = sc[0] * own_images + pl.program_id(0)
    live = jnp.where(image < sc[1], 1.0, 0.0).astype(f32)
    unit, _ = normalize(tok[0].astype(f32))
    normed[0] = (unit * (1.0 + mod[0, 1:2, :]) + mod[0, 0:1, :]).astype(bf16)
    grad = (mod[0, 5:6, :] * (cot[0].astype(f32) * live)).astype(bf16)
    grad_mlp[0] = grad
    down_sums[0] = token_sum(grad.astype(f32))
    cols = w_proj[0].shape[0]
    pairs = cols // (2 * HEAD_DIM)
    span = 2 * HEAD_DIM
    factor = HEAD_DIM ** (-0.5)
    rows = normed[0]
    total = b_proj[...]
    for part in range(parts):
        base = part * 3 * cols
        shift = bias[part][...].astype(f32).T
        for proj in range(3):
            lo = proj * cols
            value = dot_nt(w_qkv[part][lo : lo + cols, :], rows)
            if proj != 1:
                value = value + shift[:, proj // 2 : proj // 2 + 1]
            qkv[0, base + lo : base + lo + cols, :] = value.astype(bf16)

        def pair_step(pair, carry, base=base, part=part):
            at = pl.multiple_of(base + pair * span, 16)
            query = qkv[0, pl.ds(at, span), :].astype(f32)
            key = qkv[0, pl.ds(at + cols, span), :].astype(f32)
            value = qkv[0, pl.ds(at + 2 * cols, span), :].astype(f32)
            outs = []
            for one in range(2):
                rows_of = slice(one * HEAD_DIM, (one + 1) * HEAD_DIM)
                scores = dot_tn(key[rows_of].astype(bf16), query[rows_of].astype(bf16)) * factor
                raised = jnp.exp(scores - jnp.max(scores, axis=0, keepdims=True))
                share = 1.0 / jnp.sum(raised, axis=0, keepdims=True)
                prob_b = (raised * share).astype(bf16)
                prob[0, part * 2 * pairs + 2 * pair + one] = prob_b
                outs.append(dot_nn(value[rows_of].astype(bf16), prob_b))
            to = pl.multiple_of(part * cols + pair * span, 16)
            mixed[0, pl.ds(to, span), :] = jnp.concatenate(outs, axis=0).astype(bf16)
            return carry

        lax.fori_loop(0, pairs, pair_step, 0, unroll=True)
        total = total + dot_tn(mixed[0, part * cols : (part + 1) * cols, :], w_proj[part][...])
    attn_out[0] = total
    summed = tok[0].astype(f32) + mod[0, 2:3, :] * total
    residual[0] = summed
    unit, _ = normalize(summed)
    normed_mlp[0] = (unit * (1.0 + mod[0, 4:5, :]) + mod[0, 3:4, :]).astype(bf16)


def mlp_kernel(per, jobs, sc, rows, grad_mlp, *refs):
    count = len(jobs)
    weights = [refs[3 * k : 3 * k + 3] for k in range(count)]
    refs = refs[3 * count :]
    came = []
    for _, summed in jobs:
        came.append(refs[0] if summed else None)
        refs = refs[1:] if summed else refs
    act, back = refs[2], refs[3]
    grads, sums = refs[4 : 4 + count], refs[4 + count :]
    job, step = pl.program_id(0), pl.program_id(1)
    for k in range(count):

        @pl.when(job == k)
        def _(k=k):
            mlp_block(
                per, jobs[k][0], step, sc, rows, grad_mlp, *weights[k], act, back, grads[k], sums[k], came[k]
            )


def mlp_block(per, natural, step, sc, rows, grad_mlp, w_up, w_down, bias, act, back, grads, sums, came):
    here = w_down.shape[0] // per
    hidden = lax.dot_general(
        w_up[...], rows[...], (((0,), (1,)), ((), ())), preferred_element_type=f32
    ) + column(bias)
    square = hidden * hidden
    bend = jnp.tanh(0.7978845608028654 * hidden * (1.0 + 0.044715 * square))
    half = 0.5 * (1.0 + bend)
    act_b = (hidden * half).astype(bf16)
    slope = half + 0.5 * hidden * (1.0 - bend * bend) * (
        0.7978845608028654 * (1.0 + 3.0 * 0.044715 * square)
    )
    back_b = (dot_nt(w_down[...], grad_mlp[...]) * slope).astype(bf16)
    act[0] = act_b
    back[0] = back_b
    sums[...] = dot_nt(jnp.ones((8, rows.shape[0]), bf16), back_b)
    for lo_row, left, right in ((0, act_b, grad_mlp), (per, back_b, rows)):
        grad = dot_nn(left, right[...])
        for piece in range(here):
            value = grad[piece * per : (piece + 1) * per]
            if natural:
                if came is not None:
                    value = value + came[piece, lo_row : lo_row + per, :].astype(f32)
                grads[piece, lo_row : lo_row + per, :] = value.astype(bf16)
            else:
                at = jnp.bitwise_xor(step * here + piece, sc[2])
                grads[at, lo_row : lo_row + per, :] = value.astype(bf16)


def grow(total, part_steps, left, rights, dims):
    step = pl.program_id(0)

    def term(right):
        return lax.dot_general(left, right[...], (dims, ((), ())), preferred_element_type=f32)

    @pl.when(step == 0)
    def _():
        total[...] = term(rights[0])

    @pl.when(jnp.logical_and(step > 0, step < part_steps))
    def _():
        total[...] += term(rights[0])

    @pl.when(jnp.logical_and(step >= part_steps, step < 2 * part_steps))
    def _():
        total[...] += term(rights[1])


def norm_back_kernel(
    part_steps, own_images, sc, back, w_up0, w_up1, residual, cot, mod, attn_out,
    grad_residual, grad_attn, sums, total
):
    grow(total, part_steps, back[0], (w_up0, w_up1), ((0,), (1,)))
    one = pl.program_id(0) - 2 * part_steps
    seq = residual.shape[1]

    @pl.when(one >= 0)
    def _():
        live = jnp.where(sc[0] * own_images + one < sc[1], 1.0, 0.0).astype(f32)
        grad_normed = total[pl.ds(pl.multiple_of(one * seq, seq), seq), :]
        unit, recip = normalize(residual[0])
        sums[0, 0:1, :] = token_sum(grad_normed)
        sums[0, 1:2, :] = token_sum(grad_normed * unit)
        grad_res = cot[0].astype(f32) * live + norm_pullback(grad_normed, unit, recip, mod[0, 4:5, :])
        grad_residual[0] = grad_res
        sums[0, 2:3, :] = token_sum(grad_res * attn_out[0])
        grad_att = (mod[0, 2:3, :] * grad_res).astype(bf16)
        grad_attn[0] = grad_att
        sums[0, 3:4, :] = token_sum(grad_att.astype(f32))


def back_kernel(parts, sc, grad_attn, qkv, prob, *refs):
    w_proj = refs[:parts]
    grad_qkv, grad_mixed = refs[parts:]
    cols = w_proj[0].shape[0]
    pairs = cols // (2 * HEAD_DIM)
    span = 2 * HEAD_DIM
    factor = HEAD_DIM ** (-0.5)
    grad_att = grad_attn[0]
    for part in range(parts):
        base = part * 3 * cols
        grad_mixed[part * cols : (part + 1) * cols, :] = dot_nt(w_proj[part][...], grad_att).astype(bf16)

        def pair_step(pair, carry, base=base, part=part):
            at = pl.multiple_of(base + pair * span, 16)
            query = qkv[0, pl.ds(at, span), :].astype(f32)
            key = qkv[0, pl.ds(at + cols, span), :].astype(f32)
            value = qkv[0, pl.ds(at + 2 * cols, span), :].astype(f32)
            grads = grad_mixed[pl.ds(pl.multiple_of(part * cols + pair * span, 16), span), :].astype(f32)
            to_query, to_key, to_value = [], [], []
            for one in range(2):
                rows_of = slice(one * HEAD_DIM, (one + 1) * HEAD_DIM)
                prob_b = prob[0, part * 2 * pairs + 2 * pair + one]
                prob_f = prob_b.astype(f32)
                grad_b = grads[rows_of].astype(bf16)
                grad_prob = dot_tn(value[rows_of].astype(bf16), grad_b)
                delta = jnp.sum(prob_f * grad_prob, axis=0, keepdims=True)
                grad_scores = (prob_f * (grad_prob - delta)).astype(bf16)
                to_query.append(dot_nn(key[rows_of].astype(bf16), grad_scores) * factor)
                to_key.append(dot_nt(query[rows_of].astype(bf16), grad_scores) * factor)
                to_value.append(dot_nt(grad_b, prob_b))
            grad_qkv[0, pl.ds(at, span), :] = jnp.concatenate(to_query, axis=0).astype(bf16)
            grad_qkv[0, pl.ds(at + cols, span), :] = jnp.concatenate(to_key, axis=0).astype(bf16)
            grad_qkv[0, pl.ds(at + 2 * cols, span), :] = jnp.concatenate(to_value, axis=0).astype(bf16)
            return carry

        lax.fori_loop(0, pairs, pair_step, 0, unroll=True)


def attn_grad_kernel(pieces, per, sc, *refs):
    grad_qkv, mixed, normed, grad_attn = refs[:pieces], refs[pieces], refs[pieces + 1], refs[pieces + 2]
    grads, sums = refs[pieces + 3 :]
    step = pl.program_id(0)
    here = mixed.shape[1] // per
    images = mixed.shape[0]
    each = images // pieces

    def spread(total):
        total = total.astype(bf16)
        for piece in range(here):
            at = jnp.bitwise_xor(step * here + piece, sc[2])
            grads[at] = total[piece * per : (piece + 1) * per]

    @pl.when(step < 3)
    def _():
        ones = jnp.ones((8, mixed.shape[2]), bf16)
        total = count = None
        for image in range(images):
            left = grad_qkv[image // each][image % each]
            term, one = dot_nn(left, normed[image]), dot_nt(ones, left)
            total = term if image == 0 else total + term
            count = one if image == 0 else count + one
        sums[0] = count
        spread(total)

    @pl.when(step == 3)
    def _():
        total = dot_nn(mixed[0], grad_attn[0])
        for image in range(1, images):
            total = total + dot_nn(mixed[image], grad_attn[image])
        spread(total)


def first_back_kernel(pieces, images, sc, *refs):
    grad_qkv = refs[:pieces]
    w_qkv0, w_qkv1, tok, mod, grad_residual = refs[pieces : pieces + 5]
    grad_tokens, grad_own, sums, total = refs[pieces + 5 :]
    step = pl.program_id(0)
    each = images // pieces
    seq = tok.shape[1]

    def add(w_qkv, fresh):
        for one in range(images):
            term = dot_tn(grad_qkv[one // each][one % each], w_qkv[...])
            if fresh:
                total[one * seq : (one + 1) * seq, :] = term
            else:
                total[one * seq : (one + 1) * seq, :] += term

    @pl.when(step == 0)
    def _():
        add(w_qkv0, True)

    @pl.when(jnp.logical_and(step > 0, step < 3))
    def _():
        add(w_qkv0, False)

    @pl.when(jnp.logical_and(step >= 3, step < 6))
    def _():
        add(w_qkv1, False)

    @pl.when(step >= 6)
    def _():
        grad_normed = total[pl.ds(pl.multiple_of((step - 6) * seq, seq), seq), :]
        unit, recip = normalize(tok[0].astype(f32))
        sums[0, 0:1, :] = token_sum(grad_normed)
        sums[0, 1:2, :] = token_sum(grad_normed * unit)
        grad = grad_residual[0] + norm_pullback(grad_normed, unit, recip, mod[0, 1:2, :])
        grad_tokens[0] = grad
        grad_own[0] = grad


def output_kernel(
    part_steps, own_images, sc, act, w_down0, w_down1, residual, cot, mod, b_down, output, own, sums, total
):
    grow(total, part_steps, act[0], (w_down0, w_down1), ((0,), (0,)))
    one = pl.program_id(0) - 2 * part_steps
    seq = residual.shape[1]

    @pl.when(one >= 0)
    def _():
        live = jnp.where(sc[0] * own_images + one < sc[1], 1.0, 0.0).astype(f32)
        mlp_out = total[pl.ds(pl.multiple_of(one * seq, seq), seq), :] + b_down[...]
        sums[0] = token_sum((cot[0].astype(f32) * live) * mlp_out)
        rows = ((residual[0] + mod[0, 5:6, :] * mlp_out) * live).astype(bf16)
        output[0] = rows
        own[0] = rows


def final_piece(sc, halves, piece, store):
    rel = jnp.bitwise_xor(piece, sc[2])
    for low, high, bit, lo, hi in halves:
        index = ((rel >> (bit + 1)) << bit) | (rel & ((1 << bit) - 1))
        side = (rel >> bit) & 1

        @pl.when(side == 0)
        def _(low=low, index=index, lo=lo, hi=hi):
            store(low[index].astype(f32), lo, hi)

        @pl.when(side == 1)
        def _(high=high, index=index, lo=lo, hi=hi):
            store(high[index].astype(f32), lo, hi)


def final_plain_kernel(per, sc, summed, down_in, up_in, down, up, mark, turned):
    for piece in range(summed.shape[0]):
        lo = piece * per
        down[lo : lo + per, :] = summed[piece, 0:per, :].astype(f32)
        turned[lo : lo + per, :] = summed[piece, per : 2 * per, :].astype(f32)
    up[...] = turned[...].T
    mark[...] = jnp.zeros_like(mark)


def final_attn_kernel(cuts, per, sc, *refs):
    count = 2 * len(cuts)
    arrays, (qkv, proj) = refs[:count], refs[count:]
    here = proj.shape[0] // per
    halves = [(arrays[2 * k], arrays[2 * k + 1]) + cut for k, cut in enumerate(cuts)]
    for target, wanted in ((qkv, True), (proj, False)):

        @pl.when((pl.program_id(0) < 3) == wanted)
        def _(target=target):
            for piece in range(here):

                def store(value, lo, hi, piece=piece):
                    target[piece * per : (piece + 1) * per, lo:hi] = value

                final_piece(sc, halves, pl.program_id(0) * here + piece, store)


def run_kernel(
    body, sc, args, in_specs, out_specs, out_shape, grid, micros, scratch=(), alias=None, room=60
):
    size = sum(a.size * a.dtype.itemsize for a in args) + sum(
        s.size * s.dtype.itemsize for s in out_shape
    )
    return pl.pallas_call(
        body,
        out_shape=out_shape,
        grid_spec=pltpu.PrefetchScalarGridSpec(
            num_scalar_prefetch=1,
            grid=grid,
            in_specs=in_specs,
            out_specs=out_specs,
            scratch_shapes=list(scratch),
        ),
        compiler_params=pltpu.CompilerParams(vmem_limit_bytes=room << 20),
        cost_estimate=pl.CostEstimate(
            flops=int(micros * 1.15e9), bytes_accessed=int(min(size, micros * 1e6)), transcendentals=0
        ),
        input_output_aliases=alias or {},
    )(sc, *args)


def whole_block(array):
    zeros = (0,) * array.ndim
    return pl.BlockSpec(array.shape, lambda *_: zeros, pipeline_mode=pl.Buffered(1))


def shape_of(dims, kind):
    return jax.ShapeDtypeStruct(dims, kind)


SWAP = [(0, 1), (1, 0)]


def swap_cores(value):
    return lax.ppermute(value, "mp", SWAP)


def bit_pairs(bit):
    return [(index, index ^ (1 << bit)) for index in range(16)]


ATTN_WAYS = ((0, 512, (0, 1, 2, 3)), (512, 896, (1, 0, 2, 3)), (896, 1152, (2, 3, 0, 1)))


def cut(array, bits, bit, side, cols=None):
    lo = [0] * array.ndim
    hi = list(array.shape)
    place = bits.index(bit)
    lo[place], hi[place] = side, side + 1
    if cols is not None:
        lo[-1], hi[-1] = cols
    out = lax.slice(array, lo, hi)
    return out.reshape(out.shape[:place] + out.shape[place + 1 :])


def left_bits(done):
    return [bit for bit in (3, 2, 1, 0) if bit not in done]


def exchange(values, bits):
    return [lax.ppermute(value, "dp", bit_pairs(bit)) for value, bit in zip(values, bits)]


def reduce_flow(ways, get_own, other):
    shape = (2, 2, 2, 2) + other.shape[1:]
    (other,) = yield [other]
    came = swap_cores(other)
    yield None
    own, came = yield [get_own(), came]
    firsts, seconds = [own.reshape(shape)] * len(ways), [came.reshape(shape)] * len(ways)
    routes = [way for _, _, way in ways]
    for stage in range(4):
        sends, keeps = [], []
        for (lo, hi, _), route, one, two in zip(ways, routes, firsts, seconds):
            bits = left_bits(route[:stage])
            cols = (lo, hi) if stage == 0 else None
            for side, into in ((1, sends), (0, keeps)):
                into.append(
                    cut(one, bits, route[stage], side, cols) + cut(two, bits, route[stage], side, cols)
                )
        if stage == 2 and routes[0][2:] == routes[1][2:]:
            sends = [jnp.concatenate(sends[:2], axis=-1)] + sends[2:]
            keeps = [jnp.concatenate(keeps[:2], axis=-1)] + keeps[2:]
            routes = [routes[0]] + routes[2:]
            ways = [(0, 0, way) for way in routes]
        sends, keeps = yield [sends, keeps]
        comes = exchange(sends, [route[stage] for route in routes])
        yield None
        firsts, seconds = yield [keeps, comes]
    return [one + two for one, two in zip(firsts, seconds)]


def gather_flow(ways, have):
    routes = [ways[0][2]] + [way for _, _, way in ways[2:]]
    middle = ways[0][1]
    known = [[] for _ in routes]
    (have,) = yield [have]
    comes = exchange(have, [route[3] for route in routes])
    yield None
    for stage in (2, 1, 0):
        have, comes = yield [have, comes]
        joined = []
        for route, bits, one, two in zip(routes, known, have, comes):
            bit = route[stage + 1]
            place = sum(1 for other in bits if other > bit)
            joined.append(jnp.stack([one, two], axis=place))
            bits.insert(place, bit)
        if stage == 1:
            joined = [joined[0][..., :middle], joined[0][..., middle:]] + joined[1:]
            routes = [way for _, _, way in ways]
            known = [list(known[0]), list(known[0])] + known[1:]
        (have,) = yield [joined]
        comes = exchange(have, [route[stage] for route in routes])
        yield None
    have, comes = yield [have, comes]
    return [part.reshape((8,) + part.shape[-2:]) for pair in zip(have, comes) for part in pair]


def sum_flow(ways, get_own, other):
    have = yield from reduce_flow(ways, get_own, other)
    return (yield from gather_flow(ways, have))


def swap_flow(other):
    (other,) = yield [other]
    came = swap_cores(other)
    yield None
    (came,) = yield [came]
    return came


def both_flow(own, given):
    (own, given) = yield [own, given]
    came = swap_cores(given)
    yield None
    own, came = yield [own, came]
    return (yield from rows_flow(own + came))


def rows_flow(rows):
    for bit in (3, 2, 1, 0):
        (rows,) = yield [rows]
        came = lax.ppermute(rows, "dp", bit_pairs(bit))
        yield None
        rows, came = yield [rows, came]
        rows = jnp.concatenate([rows, came])
    return rows


class Order:
    def __init__(self, sc):
        self.sc = sc
        self.results = {}

    def fence(self, values):
        self.sc, values = lax.optimization_barrier((self.sc, values))
        return values

    def after(self, value):
        self.sc, _ = lax.optimization_barrier((self.sc, value))

    def tick(self, *flows):
        replies = {flow: None for flow in flows if flow not in self.results}
        while replies:
            wants = {}
            for flow, reply in replies.items():
                try:
                    want = flow.send(reply)
                except StopIteration as stop:
                    self.results[flow] = stop.value
                    continue
                if want is not None:
                    wants[flow] = want
            replies = dict(zip(wants, self.fence(list(wants.values())))) if wants else {}

    def finish(self, flow):
        while flow not in self.results:
            self.tick(flow)
        return self.results[flow]


CHUNKS = 3


def fill_other(both, came, core):
    size = came.shape[0]
    return lax.dynamic_update_slice_in_dim(both, came, (1 - core) * size, 0)


def fast_device(
    tokens, condition, counts, w_qkv, b_qv, w_proj, b_proj, w_up, b_up, w_down, b_down, w_mod, b_mod,
    cotangent,
):
    slots, seq, dim = tokens.shape
    images = slots // 2
    count = images * seq
    cols = w_qkv.shape[2]
    ff = w_up.shape[1]
    own_cols = w_mod.shape[1]
    heads = cols // HEAD_DIM
    core = lax.axis_index("mp")
    order = Order(jnp.stack([core, counts[0], lax.axis_index("dp")]).astype(jnp.int32))

    qkv_rows = jnp.transpose(w_qkv, (1, 2, 0)).reshape(3 * cols, dim)
    wq = [qkv_rows, swap_cores(qkv_rows)]
    wp = [w_proj, swap_cores(w_proj)]
    qkv_bias = [b_qv, swap_cores(b_qv)]

    cond_f = condition.astype(f32)
    scaled = jax.nn.silu(cond_f).astype(bf16)
    own_mod = jnp.dot(scaled, w_mod, preferred_element_type=f32) + b_mod.astype(f32)
    other_mod = swap_cores(own_mod)
    sides = [jnp.where(core == side, own_mod, other_mod) for side in range(2)]
    modulation = jnp.concatenate(sides, axis=1).reshape(slots, 6, dim)
    proj_bias = b_proj.astype(f32)[None]
    down_bias = b_down.astype(f32)[None]

    late_up, late_down, late_bias = lax.optimization_barrier((wq[1], w_up, w_down, b_up, modulation))[1:4]
    wu = [w_up, swap_cores(late_up)]
    wd = [w_down, swap_cores(late_down)]
    up_bias = [b_up[None], swap_cores(late_bias[None])]

    local = lambda i, s: (s[0] * images + i, 0, 0)
    mine = lambda i, s: (i, 0, 0)
    tok_spec = pl.BlockSpec((1, seq, dim), local)
    own_spec = pl.BlockSpec((1, seq, dim), mine)
    mod_spec = pl.BlockSpec((1, 6, dim), local)
    row_spec = pl.BlockSpec((1, 1, dim), mine)
    qkv_spec = pl.BlockSpec((1, 6 * cols, seq), mine)
    prob_spec = pl.BlockSpec((1, 2 * heads, seq, seq), lambda i, s: (i, 0, 0, 0))
    mixed_spec = pl.BlockSpec((1, 2 * cols, seq), mine)
    token_f = shape_of((images, seq, dim), f32)
    token_b = shape_of((images, seq, dim), bf16)
    attn_args = wq + wp + qkv_bias
    qkv, prob, mixed, attn_out, residual, normed_mlp, normed, grad_mlp, down_sums = run_kernel(
        functools.partial(attention_kernel, 2, images),
        order.sc,
        [tokens, cotangent, modulation, proj_bias] + attn_args,
        [tok_spec, tok_spec, mod_spec, whole_block(proj_bias)] + [whole_block(a) for a in attn_args],
        [qkv_spec, prob_spec, mixed_spec] + [own_spec] * 5 + [row_spec],
        [
            shape_of((images, 6 * cols, seq), bf16),
            shape_of((images, 2 * heads, seq, seq), bf16),
            shape_of((images, 2 * cols, seq), bf16),
            token_f,
            token_f,
            token_b,
            token_b,
            token_b,
            shape_of((images, 1, dim), f32),
        ],
        (images,),
        45,
    )
    order.after(down_sums)

    rows_flat = normed_mlp.reshape(count, dim)
    grad_flat = grad_mlp.reshape(count, dim)
    width = ff // CHUNKS
    per = width // 16
    steps = 2
    block = width // steps
    anywhere = pl.BlockSpec(memory_space=pl.ANY)
    act = back = jnp.zeros((8, 128), bf16)
    up_sums = {}

    def mlp_call(jobs, came, micros):
        nonlocal act, back
        first = act.shape[0] == 8
        kinds = tuple((True, job in came) for job in jobs)

        def turn(k):
            return lambda p, s, c: jnp.clip((p - k) * steps + s, 0, steps - 1)

        def pick(values):
            return lambda p: sum(jnp.where(p == k, value, 0) for k, value in enumerate(values))

        parts = pick([part for _, part in jobs])
        starts = pick([chunk * steps for chunk, _ in jobs])
        spread = pl.BlockSpec((1, block, count), lambda p, s, c: (parts(p), starts(p) + s, 0))
        args, specs = [], []
        for k, (chunk, part) in enumerate(jobs):
            at = chunk * steps
            wide = lambda p, s, c, k=k, at=at: (0, at + turn(k)(p, s, c))
            tall = lambda p, s, c, k=k, at=at: (at + turn(k)(p, s, c), 0)
            args += [wu[part], wd[part], up_bias[part]]
            specs += [
                pl.BlockSpec((dim, block), wide),
                pl.BlockSpec((block, dim), tall),
                pl.BlockSpec((1, block), wide),
            ]
        grad_specs = []
        for k, (natural, _) in enumerate(kinds):
            own = lambda p, s, c, k=k: (turn(k)(p, s, c), 0, 0)
            fixed = lambda p, s, c: (0, 0, 0)
            grad_specs.append(
                pl.BlockSpec((16 // steps, 2 * per, dim), own)
                if natural
                else pl.BlockSpec((16, 2 * per, dim), fixed)
            )
        for k, job in enumerate(jobs):
            if job in came:
                args.append(came[job])
                specs.append(grad_specs[k])
        args += [act, back]
        spot = len(args) + 1
        outs = run_kernel(
            functools.partial(mlp_kernel, per, kinds),
            order.sc,
            [rows_flat, grad_flat] + args,
            [whole_block(rows_flat), whole_block(grad_flat)] + specs + [anywhere, anywhere],
            [spread, spread]
            + grad_specs
            + [pl.BlockSpec((8, block), lambda p, s, c, k=k: (0, turn(k)(p, s, c))) for k in range(len(jobs))],
            [shape_of((2, ff, count), bf16)] * 2
            + [shape_of((16, 2 * per, dim), bf16)] * len(jobs)
            + [shape_of((8, width), f32)] * len(jobs),
            (len(jobs), steps),
            micros,
            alias=None if first else {spot: 0, spot + 1: 1},
        )
        act, back = outs[:2]
        grads = outs[2 : 2 + len(jobs)]
        for job, sums in zip(jobs, outs[2 + len(jobs) :]):
            up_sums[job] = sums[0:1]
        order.after(outs[-1])
        return grads

    swaps = {}
    for chunks in ((0, 1), (2,)):
        grads = mlp_call([(chunk, 1) for chunk in chunks], {}, 13 * len(chunks))
        swaps.update({chunk: swap_flow(grad) for chunk, grad in zip(chunks, grads)})
        order.tick(*[swaps[chunk] for chunk in sorted(swaps)])
    wide_scaled = jnp.pad(scaled.reshape(-1), (0, 3 * own_cols - slots * dim)).reshape(3, own_cols)
    early = rows_flow(wide_scaled)
    sums_in = []
    for chunks in ((0, 1), (2,)):
        came = {(chunk, 0): order.finish(swaps[chunk]) for chunk in chunks}
        if chunks == (2,):
            order.tick(early)
        sums_in += mlp_call([(chunk, 0) for chunk in chunks], came, 13 * len(chunks))
    plain_sums = lax.psum(sums_in, "dp")
    down_row = jnp.sum(down_sums[:, 0], axis=0, keepdims=True)
    own_row, other_row = (
        jnp.concatenate([up_sums[chunk, part] for chunk in range(CHUNKS)] + [down_row], axis=1)
        for part in range(2)
    )
    bias_flow = both_flow(own_row, other_row)
    order.tick(early, bias_flow)

    reach = 768
    turns = ff // reach
    every = lambda s, c: (0, 0, 0)
    tail = lambda first: lambda s, c: (jnp.maximum(s - first, 0), 0, 0)
    tail_local = lambda first: lambda s, c: (c[0] * images + jnp.maximum(s - first, 0), 0, 0)

    def image_spec(first, where=tail):
        return pl.BlockSpec((1, seq, dim), where(first))

    def rows_of(part, size):
        if part == 0:
            return lambda s, c: jnp.minimum(s, size - 1)
        return lambda s, c: jnp.clip(s - size, 0, size - 1)

    span_spec = pl.BlockSpec(
        (1, reach, count),
        lambda s, c: (jnp.minimum(s // turns, 1), jnp.where(s < 2 * turns, s % turns, turns - 1), 0),
    )
    grad_residual, grad_attn, mid_sums = run_kernel(
        functools.partial(norm_back_kernel, turns, images),
        order.sc,
        [back] + wu + [residual, cotangent, modulation, attn_out],
        [
            span_spec,
            pl.BlockSpec((dim, reach), lambda s, c: (0, rows_of(0, turns)(s, c))),
            pl.BlockSpec((dim, reach), lambda s, c: (0, rows_of(1, turns)(s, c))),
            image_spec(2 * turns),
            image_spec(2 * turns, tail_local),
            pl.BlockSpec((1, 6, dim), tail_local(2 * turns)),
            image_spec(2 * turns),
        ],
        [image_spec(2 * turns)] * 2 + [pl.BlockSpec((1, 4, dim), tail(2 * turns))],
        [token_f, token_b, shape_of((images, 4, dim), f32)],
        (2 * turns + images,),
        60,
        scratch=[pltpu.VMEM((count, dim), f32)],
    )
    order.after(mid_sums)
    order.tick(early, bias_flow)
    pieces = 2
    each = images // pieces
    grad_qkv = []
    for piece in range(pieces):
        there = lambda i, s, piece=piece: (piece * each + i, 0, 0)
        (grad_piece,) = run_kernel(
            functools.partial(back_kernel, 2),
            order.sc,
            [grad_attn, qkv, prob] + wp,
            [
                pl.BlockSpec((1, seq, dim), there),
                pl.BlockSpec((1, 6 * cols, seq), there),
                pl.BlockSpec((1, 2 * heads, seq, seq), lambda i, s, piece=piece: (piece * each + i, 0, 0, 0)),
            ]
            + [whole_block(a) for a in wp],
            [qkv_spec],
            [shape_of((each, 6 * cols, seq), bf16)],
            (each,),
            60,
            scratch=[pltpu.VMEM((2 * cols, seq), bf16)],
            )
        grad_qkv.append(grad_piece)
        order.after(grad_piece)
        order.tick(early, bias_flow)

    attn_per = 4 * cols // 16
    qv_sums = [None, None]

    def attn_part(part):
        grads, sums = run_kernel(
            functools.partial(attn_grad_kernel, pieces, attn_per),
            order.sc,
            grad_qkv + [mixed, normed, grad_attn],
            [
                pl.BlockSpec((each, cols, seq), lambda s, c: (0, 3 * part + jnp.minimum(s, 2), 0))
                for _ in range(pieces)
            ]
            + [pl.BlockSpec((images, cols, seq), lambda s, c: (0, part, 0))]
            + [whole_block(normed), whole_block(grad_attn)],
            [
                pl.BlockSpec((16, attn_per, dim), every),
                pl.BlockSpec((1, 8, cols), lambda s, c: (jnp.minimum(s, 2), 0, 0)),
            ],
            [shape_of((16, attn_per, dim), bf16), shape_of((3, 8, cols), f32)],
            (4,),
            60,
            )
        qv_sums[part] = sums
        order.after(sums)
        return grads

    grad_other = attn_part(1)
    made = []
    last = sum_flow(ATTN_WAYS, lambda: made[0], grad_other)
    order.tick(last, early, bias_flow)
    made.append(attn_part(0))
    order.tick(last, early, bias_flow)

    first_spec = lambda part: pl.BlockSpec((cols, dim), lambda s, c: (rows_of(part, 3)(s, c), 0))
    grad_tokens, grad_own_tokens, low_sums = run_kernel(
        functools.partial(first_back_kernel, pieces, images),
        order.sc,
        grad_qkv + wq + [tokens, modulation, grad_residual],
        [pl.BlockSpec((each, cols, seq), lambda s, c: (0, jnp.minimum(s, 5), 0)) for _ in range(pieces)]
        + [first_spec(0), first_spec(1)]
        + [image_spec(6, tail_local), pl.BlockSpec((1, 6, dim), tail_local(6)), image_spec(6)],
        [image_spec(6, tail_local), image_spec(6), pl.BlockSpec((1, 2, dim), tail(6))],
        [shape_of((slots, seq, dim), f32), token_f, shape_of((images, 2, dim), f32)],
        (6 + images,),
        60,
        scratch=[pltpu.VMEM((count, dim), f32)],
    )
    order.after(low_sums)
    order.tick(last)
    other_tokens = swap_cores(grad_own_tokens)
    down_spec = lambda part: pl.BlockSpec((reach, dim), lambda s, c: (rows_of(part, turns)(s, c), 0))
    output, own_output, gate_sums = run_kernel(
        functools.partial(output_kernel, turns, images),
        order.sc,
        [act] + wd + [residual, cotangent, modulation, down_bias],
        [
            span_spec,
            down_spec(0),
            down_spec(1),
            image_spec(2 * turns),
            image_spec(2 * turns, tail_local),
            pl.BlockSpec((1, 6, dim), tail_local(2 * turns)),
            whole_block(down_bias),
        ],
        [image_spec(2 * turns, tail_local), image_spec(2 * turns), pl.BlockSpec((1, 1, dim), tail(2 * turns))],
        [shape_of((slots, seq, dim), bf16), token_b, shape_of((images, 1, dim), f32)],
        (2 * turns + images,),
        60,
        scratch=[pltpu.VMEM((count, dim), f32)],
    )
    order.after(gate_sums)
    order.tick(last)
    other_output = swap_cores(own_output)

    low_sums, mid_sums, gate_sums = order.fence((low_sums, mid_sums, gate_sums))
    grad_modulation = jnp.concatenate([low_sums, mid_sums[:, 2:3], mid_sums[:, 0:2], gate_sums], axis=1)
    grad_modulation = grad_modulation.reshape(images, 6 * dim).astype(bf16)
    proj_row = jnp.sum(mid_sums[:, 3], axis=0, keepdims=True)
    fill = jnp.zeros((1, own_cols - 2 * cols - dim), f32)
    rows_kept, rows_given = (
        jnp.concatenate([qv_sums[part][0, 0:1], qv_sums[part][2, 0:1], proj_row, fill], axis=1)
        for part in range(2)
    )
    halves = grad_modulation.reshape(images, 2, own_cols)
    kept = lax.dynamic_index_in_dim(halves, core, 1, keepdims=False)
    given = lax.dynamic_index_in_dim(halves, 1 - core, 1, keepdims=False)
    got = swap_cores(jnp.concatenate([given.astype(f32), rows_given]))
    came = got[:images].astype(bf16)
    group_mod = jnp.where(core == 0, jnp.concatenate([kept, came]), jnp.concatenate([came, kept]))
    packed_rows = jnp.concatenate([group_mod, (rows_kept + got[images:]).astype(bf16)])
    (packed_rows,) = order.fence([packed_rows])
    small = rows_flow(packed_rows)
    order.tick(last, small)
    (group_mod,) = order.fence([group_mod])
    part_scaled = outer_cols(group_mod, w_mod).astype(bf16)
    came_scaled = swap_cores(part_scaled)
    output = fill_other(output, order.fence(other_output), core)
    order.after((output[0, 0, :1], part_scaled[0, :1]))
    order.tick(last, small)
    grad_tokens = fill_other(grad_tokens, order.fence(other_tokens), core)
    part_scaled, came_scaled = order.fence((part_scaled, came_scaled))
    grad_scaled = part_scaled.astype(f32) + came_scaled.astype(f32)
    _, silu_back = jax.vjp(jax.nn.silu, cond_f)
    grad_condition = silu_back(grad_scaled)[0]
    order.after((grad_tokens[0, 0, :1], grad_condition[0, :1]))
    order.tick(last, small)

    def cuts(ways):
        return tuple((way[0], lo, hi) for lo, hi, way in ways)

    grad_w_down = grad_w_up = jnp.zeros((8, 128), f32)

    def final_mlp(chunk, body, args):
        nonlocal grad_w_down, grad_w_up
        first = grad_w_down.shape[0] == 8
        spot = len(args) + 1
        grad_w_down, grad_w_up, mark = run_kernel(
            body,
            order.sc,
            list(args) + [grad_w_down, grad_w_up],
            [
                whole_block(a)
                if a.shape[0] == 8
                else pl.BlockSpec((16 // steps,) + a.shape[1:], lambda s, c: (s, 0, 0))
                for a in args
            ]
            + [anywhere, anywhere],
            [
                pl.BlockSpec((block, dim), lambda s, c: (chunk * steps + s, 0)),
                pl.BlockSpec((dim, block), lambda s, c: (0, chunk * steps + s)),
                pl.BlockSpec((8, 128), lambda s, c: (0, 0)),
            ],
            [shape_of((ff, dim), f32), shape_of((dim, ff), f32), shape_of((8, 128), f32)],
            (steps,),
            4,
            scratch=[pltpu.VMEM((block, dim), f32)],
            alias=None if first else {spot: 0, spot + 1: 1},
        )
        order.after(mark)

    order.tick(last, small)
    all_rows = order.fence(order.finish(small)).reshape(16, slots + 1, own_cols)
    all_mod = all_rows[:, :slots].reshape(-1, own_cols)
    all_scaled = order.finish(early).reshape(16, -1)[:, : slots * dim].reshape(-1, dim)
    grad_w_mod = inner_rows(all_scaled, all_mod)
    grad_b_mod = jnp.sum(all_mod.astype(f32), axis=0)
    late_total = jnp.sum(all_rows[:, slots].astype(f32), axis=0)
    early_total = jnp.sum(order.finish(bias_flow), axis=0)
    grad_b_qv = late_total[: 2 * cols].reshape(2, cols)
    grad_b_proj = late_total[2 * cols : 2 * cols + dim]
    grad_b_up = early_total[:ff]
    grad_b_down = early_total[ff : ff + dim]
    order.after((grad_w_mod[0, :1], grad_b_mod[:1], late_total[:1]))
    args = order.finish(last)
    grad_qkv_rows, grad_w_proj = run_kernel(
        functools.partial(final_attn_kernel, cuts(ATTN_WAYS), attn_per),
        order.sc,
        list(args),
        [whole_block(a) for a in args],
        [
            pl.BlockSpec((cols, dim), lambda s, c: (jnp.minimum(s, 2), 0)),
            pl.BlockSpec((cols, dim), lambda s, c: (0, 0)),
        ],
        [shape_of((3 * cols, dim), f32), shape_of((cols, dim), f32)],
        (4,),
        9,
    )
    grad_w_qkv = jnp.transpose(grad_qkv_rows.reshape(3, cols, dim), (2, 0, 1))
    order.after(grad_w_proj[0, :1])
    for chunk, total in enumerate(plain_sums):
        final_mlp(chunk, functools.partial(final_plain_kernel, per), [total])
    return (
        output,
        grad_tokens,
        grad_condition,
        grad_w_qkv,
        grad_b_qv,
        grad_w_proj,
        grad_b_proj,
        grad_w_up,
        grad_b_up,
        grad_w_down,
        grad_b_down,
        grad_w_mod,
        grad_b_mod,
    )


def layer_norm(values):
    center = values - jnp.mean(values, axis=-1, keepdims=True)
    return center * lax.rsqrt(jnp.mean(center * center, axis=-1, keepdims=True) + epsilon)


def modulate(values, shift_part, scale_part):
    return layer_norm(values) * (1.0 + scale_part) + shift_part


def gelu_tanh(values):
    return (
        0.5
        * values
        * (1.0 + jnp.tanh(0.7978845608028654 * (values + 0.044715 * values * values * values)))
    )


def inner_rows(left, right):
    return lax.dot_general(
        left, right, (((0,), (0,)), ((), ())), preferred_element_type=jnp.float32
    )


def outer_cols(left, right):
    return lax.dot_general(
        left, right, (((1,), (1,)), ((), ())), preferred_element_type=jnp.float32
    )


def attention_forward(query_rows, key_rows, value_rows):
    factor = HEAD_DIM ** (-0.5)
    scores = (
        jnp.einsum("bqhd,bkhd->bhqk", query_rows, key_rows, preferred_element_type=jnp.float32)
        * factor
    )
    row_max = jnp.max(scores, axis=-1, keepdims=True)
    row_total = jnp.sum(jnp.exp(scores - row_max), axis=-1, keepdims=True)
    logsum = row_max + jnp.log(row_total)
    prob_b = jnp.exp(scores - logsum).astype(jnp.bfloat16)
    mixed_out = jnp.einsum(
        "bhqk,bkhd->bqhd", prob_b, value_rows, preferred_element_type=jnp.float32
    )
    return (mixed_out, logsum)


def attention_backward(query_rows, key_rows, value_rows, logsum, grad_mixed):
    factor = HEAD_DIM ** (-0.5)
    scores = (
        jnp.einsum("bqhd,bkhd->bhqk", query_rows, key_rows, preferred_element_type=jnp.float32)
        * factor
    )
    prob_f = jnp.exp(scores - logsum)
    prob_b = prob_f.astype(jnp.bfloat16)
    grad_prob = jnp.einsum(
        "bqhd,bkhd->bhqk", grad_mixed, value_rows, preferred_element_type=jnp.float32
    )
    row_delta = jnp.sum(prob_f * grad_prob, axis=-1, keepdims=True)
    grad_scores = (prob_f * (grad_prob - row_delta)).astype(jnp.bfloat16)
    grad_query = (
        jnp.einsum("bhqk,bkhd->bqhd", grad_scores, key_rows, preferred_element_type=jnp.float32)
        * factor
    )
    grad_key = (
        jnp.einsum("bhqk,bqhd->bkhd", grad_scores, query_rows, preferred_element_type=jnp.float32)
        * factor
    )
    grad_value = jnp.einsum(
        "bhqk,bqhd->bkhd", prob_b, grad_mixed, preferred_element_type=jnp.float32
    )
    return (
        grad_query.astype(jnp.bfloat16),
        grad_key.astype(jnp.bfloat16),
        grad_value.astype(jnp.bfloat16),
    )


def forward(tokens_f, spans, weights, repeat):
    w_qkv, b_qv, w_proj, b_proj, w_up, b_up, w_down, b_down = weights
    shift_attn, scale_attn, gate_attn, shift_mlp, scale_mlp, gate_mlp = spans
    slot_count, seq_len, model_dim = tokens_f.shape
    row_count = slot_count * seq_len
    head_cols = w_qkv.shape[2]
    head_count = head_cols // HEAD_DIM
    shape_four = (slot_count, seq_len, head_count, HEAD_DIM)
    normed = (
        modulate(tokens_f, shift_attn, scale_attn)
        .astype(jnp.bfloat16)
        .reshape(row_count, model_dim)
    )
    projected = jnp.dot(
        normed, w_qkv.reshape(model_dim, 3 * head_cols), preferred_element_type=jnp.float32
    )
    qkv_bias = jnp.stack([b_qv[0], jnp.zeros_like(b_qv[0]), b_qv[1]]).astype(jnp.float32)
    projected = (projected.reshape(row_count, 3, head_cols) + qkv_bias).astype(jnp.bfloat16)
    query_rows = projected[:, 0].reshape(shape_four)
    key_rows = projected[:, 1].reshape(shape_four)
    value_rows = projected[:, 2].reshape(shape_four)
    mixed_out, logsum = attention_forward(query_rows, key_rows, value_rows)
    mixed_b = mixed_out.astype(jnp.bfloat16).reshape(row_count, head_cols)
    partial_value = jnp.dot(mixed_b, w_proj, preferred_element_type=jnp.float32)
    if repeat:
        summed = lax.psum(partial_value.astype(jnp.bfloat16), "mp").astype(jnp.float32)
    else:
        summed = lax.psum(partial_value.astype(jnp.bfloat16), "mp").astype(jnp.float32)
    attn_out = (summed + b_proj.astype(jnp.float32)).reshape(slot_count, seq_len, model_dim)
    residual = tokens_f + gate_attn * attn_out
    normed_mlp = (
        modulate(residual, shift_mlp, scale_mlp).astype(jnp.bfloat16).reshape(row_count, model_dim)
    )
    hidden = jnp.dot(normed_mlp, w_up, preferred_element_type=jnp.float32) + b_up.astype(
        jnp.float32
    )
    act_bf = gelu_tanh(hidden).astype(jnp.bfloat16)
    partial_mlp = jnp.dot(act_bf, w_down, preferred_element_type=jnp.float32)
    if repeat:
        summed_mlp = lax.psum(partial_mlp.astype(jnp.bfloat16), "mp").astype(jnp.float32)
    else:
        summed_mlp = lax.psum(partial_mlp.astype(jnp.bfloat16), "mp").astype(jnp.float32)
    mlp_out = (summed_mlp + b_down.astype(jnp.float32)).reshape(slot_count, seq_len, model_dim)
    output = residual + gate_mlp * mlp_out
    return {
        "normed": normed,
        "query_rows": query_rows,
        "key_rows": key_rows,
        "value_rows": value_rows,
        "logsum": logsum,
        "mixed_b": mixed_b,
        "attn_out": attn_out,
        "residual": residual,
        "normed_mlp": normed_mlp,
        "hidden": hidden,
        "act_bf": act_bf,
        "mlp_out": mlp_out,
        "output": output,
    }


def image_pass(tokens_f, grad_out, spans, weights):
    w_qkv, b_qv, w_proj, b_proj, w_up, b_up, w_down, b_down = weights
    shift_attn, scale_attn, gate_attn, shift_mlp, scale_mlp, gate_mlp = spans
    slot_count, seq_len, model_dim = tokens_f.shape
    row_count = slot_count * seq_len
    head_cols = w_qkv.shape[2]
    head_count = head_cols // HEAD_DIM
    kept_fwd = forward(tokens_f, spans, weights, False)
    out_one = kept_fwd["output"]
    stored = forward(tokens_f, spans, weights, True)
    grad_gate_mlp = jnp.sum(grad_out * stored["mlp_out"], axis=1)
    grad_mlp = (gate_mlp * grad_out).astype(jnp.bfloat16).reshape(row_count, model_dim)
    grad_b_down = jnp.sum(grad_mlp.astype(jnp.float32), axis=0)
    grad_w_down = inner_rows(stored["act_bf"], grad_mlp)
    grad_act = outer_cols(grad_mlp, w_down)
    gelu_value, gelu_back = jax.vjp(gelu_tanh, stored["hidden"])
    grad_hidden = gelu_back(grad_act)[0].astype(jnp.bfloat16)
    grad_b_up = jnp.sum(grad_hidden.astype(jnp.float32), axis=0)
    grad_w_up = inner_rows(stored["normed_mlp"], grad_hidden)
    part_normed_mlp = outer_cols(grad_hidden, w_up)
    grad_normed_mlp = (
        lax.psum(part_normed_mlp.astype(jnp.bfloat16), "mp")
        .astype(jnp.float32)
        .reshape(slot_count, seq_len, model_dim)
    )
    norm_value, norm_back = jax.vjp(modulate, stored["residual"], shift_mlp, scale_mlp)
    grad_resid_norm, grad_shift_mlp, grad_scale_mlp = norm_back(grad_normed_mlp)
    grad_residual = grad_out + grad_resid_norm
    grad_gate_attn = jnp.sum(grad_residual * stored["attn_out"], axis=1)
    grad_attn = (gate_attn * grad_residual).astype(jnp.bfloat16).reshape(row_count, model_dim)
    grad_b_proj = jnp.sum(grad_attn.astype(jnp.float32), axis=0)
    grad_w_proj = inner_rows(stored["mixed_b"], grad_attn)
    grad_mixed = (
        outer_cols(grad_attn, w_proj)
        .astype(jnp.bfloat16)
        .reshape(slot_count, seq_len, head_count, HEAD_DIM)
    )
    grad_query, grad_key, grad_value = attention_backward(
        stored["query_rows"], stored["key_rows"], stored["value_rows"], stored["logsum"], grad_mixed
    )
    grad_qkv = jnp.stack(
        [
            grad_query.reshape(row_count, head_cols),
            grad_key.reshape(row_count, head_cols),
            grad_value.reshape(row_count, head_cols),
        ],
        axis=1,
    )
    grad_b_qv = jnp.stack(
        [
            jnp.sum(grad_qkv[:, 0].astype(jnp.float32), axis=0),
            jnp.sum(grad_qkv[:, 2].astype(jnp.float32), axis=0),
        ]
    )
    grad_w_qkv = inner_rows(stored["normed"], grad_qkv)
    part_normed = outer_cols(
        grad_qkv.reshape(row_count, 3 * head_cols), w_qkv.reshape(model_dim, 3 * head_cols)
    )
    grad_normed = (
        lax.psum(part_normed.astype(jnp.bfloat16), "mp")
        .astype(jnp.float32)
        .reshape(slot_count, seq_len, model_dim)
    )
    first_value, first_back = jax.vjp(modulate, tokens_f, shift_attn, scale_attn)
    grad_tok_norm, grad_shift_attn, grad_scale_attn = first_back(grad_normed)
    grad_tok_one = grad_residual + grad_tok_norm
    grad_mod_one = jnp.concatenate(
        [
            grad_shift_attn[:, 0],
            grad_scale_attn[:, 0],
            grad_gate_attn,
            grad_shift_mlp[:, 0],
            grad_scale_mlp[:, 0],
            grad_gate_mlp,
        ],
        axis=1,
    )
    grad_terms = (
        grad_w_qkv,
        grad_b_qv,
        grad_w_proj,
        grad_b_proj,
        grad_w_up,
        grad_b_up,
        grad_w_down,
        grad_b_down,
    )
    return (out_one, grad_tok_one, grad_mod_one, grad_terms)


def run_layer(tokens, condition, cotangent, live_count, turns, weights, w_mod, b_mod):
    slot_count, seq_len, model_dim = tokens.shape
    cond_f = condition.astype(jnp.float32)
    scaled = jax.nn.silu(cond_f).astype(jnp.bfloat16)
    own_mod = jnp.dot(scaled, w_mod, preferred_element_type=jnp.float32) + b_mod.astype(jnp.float32)
    modulation = lax.all_gather(own_mod, "mp", axis=1, tiled=True)
    tokens_f = tokens.astype(jnp.float32)
    cot_f = cotangent.astype(jnp.float32)

    def image_step(slot_idx, carry):
        out_buf, grad_buf, mod_buf, grad_sums = carry
        live_flag = (slot_idx < live_count).astype(jnp.float32)
        tok_one = lax.dynamic_slice_in_dim(tokens_f, slot_idx, 1, 0)
        cot_one = lax.dynamic_slice_in_dim(cot_f, slot_idx, 1, 0) * live_flag
        mod_row = lax.dynamic_slice_in_dim(modulation, slot_idx, 1, 0)
        spans = [
            mod_row[:, None, part_idx * model_dim : (part_idx + 1) * model_dim]
            for part_idx in range(6)
        ]
        out_one, grad_tok_one, grad_mod_one, grad_terms = image_pass(
            tok_one, cot_one, spans, weights
        )
        out_one = (out_one * live_flag).astype(jnp.bfloat16)
        out_buf = lax.dynamic_update_slice_in_dim(out_buf, out_one, slot_idx, 0)
        grad_buf = lax.dynamic_update_slice_in_dim(grad_buf, grad_tok_one, slot_idx, 0)
        mod_buf = lax.dynamic_update_slice_in_dim(mod_buf, grad_mod_one, slot_idx, 0)
        grad_sums = tuple((total_a + term_b for total_a, term_b in zip(grad_sums, grad_terms)))
        return (out_buf, grad_buf, mod_buf, grad_sums)

    start_sums = tuple((jnp.zeros(weight_in.shape, jnp.float32) for weight_in in weights))
    start_state = (
        jnp.zeros(tokens.shape, jnp.bfloat16),
        jnp.zeros(tokens.shape, jnp.float32),
        jnp.zeros((slot_count, 6 * model_dim), jnp.float32),
        start_sums,
    )
    out_buf, grad_buf, mod_buf, grad_sums = lax.fori_loop(0, turns, image_step, start_state)
    grad_modulation = mod_buf.astype(jnp.bfloat16)
    own_cols = w_mod.shape[1]
    grad_own = lax.dynamic_slice_in_dim(
        grad_modulation, lax.axis_index("mp") * own_cols, own_cols, 1
    )
    part_scaled = outer_cols(grad_own, w_mod)
    grad_scaled = lax.psum(part_scaled.astype(jnp.bfloat16), "mp").astype(jnp.float32)
    silu_value, silu_back = jax.vjp(jax.nn.silu, cond_f)
    grad_condition = silu_back(grad_scaled)[0]
    return (out_buf, grad_buf, grad_condition, grad_sums, scaled, grad_own)


def on_device(
    tokens,
    condition,
    counts,
    w_qkv,
    b_qv,
    w_proj,
    b_proj,
    w_up,
    b_up,
    w_down,
    b_down,
    w_mod,
    b_mod,
    cotangent,
):
    slot_count, seq_len, model_dim = tokens.shape
    weights = (w_qkv, b_qv, w_proj, b_proj, w_up, b_up, w_down, b_down)
    own_count = counts[0]
    output, grad_tokens, grad_condition, grad_sums, scaled, grad_own = run_layer(
        tokens, condition, cotangent, own_count, slot_count, weights, w_mod, b_mod
    )
    (
        grad_w_qkv,
        grad_b_qv,
        grad_w_proj,
        grad_b_proj,
        grad_w_up,
        grad_b_up,
        grad_w_down,
        grad_b_down,
    ) = grad_sums
    grad_w_mod = inner_rows(scaled, grad_own)
    grad_b_mod = jnp.sum(grad_own.astype(jnp.float32), axis=0)
    (
        grad_w_qkv,
        grad_b_qv,
        grad_w_proj,
        grad_b_proj,
        grad_w_up,
        grad_b_up,
        grad_w_down,
        grad_b_down,
        grad_w_mod,
        grad_b_mod,
    ) = (
        lax.psum(grad_w_qkv.astype(jnp.bfloat16), "dp").astype(jnp.float32),
        lax.psum(grad_b_qv.astype(jnp.bfloat16), "dp").astype(jnp.float32),
        lax.psum(grad_w_proj.astype(jnp.bfloat16), "dp").astype(jnp.float32),
        lax.psum(grad_b_proj.astype(jnp.bfloat16), "dp").astype(jnp.float32),
        lax.psum(grad_w_up.astype(jnp.bfloat16), "dp").astype(jnp.float32),
        lax.psum(grad_b_up.astype(jnp.bfloat16), "dp").astype(jnp.float32),
        lax.psum(grad_w_down.astype(jnp.bfloat16), "dp").astype(jnp.float32),
        lax.psum(grad_b_down.astype(jnp.bfloat16), "dp").astype(jnp.float32),
        lax.psum(grad_w_mod.astype(jnp.bfloat16), "dp").astype(jnp.float32),
        lax.psum(grad_b_mod.astype(jnp.bfloat16), "dp").astype(jnp.float32),
    )
    return (
        output,
        grad_tokens,
        grad_condition,
        grad_w_qkv,
        grad_b_qv,
        grad_w_proj,
        grad_b_proj,
        grad_w_up,
        grad_b_up,
        grad_w_down,
        grad_b_down,
        grad_w_mod,
        grad_b_mod,
    )


def solution(mesh):
    placed = (
        P("dp", None, None),
        P("dp", None),
        P("dp"),
        P(None, None, "mp"),
        P(None, "mp"),
        P("mp", None),
        P(),
        P(None, "mp"),
        P("mp"),
        P("mp", None),
        P(),
        P(None, "mp"),
        P("mp"),
        P("dp", None, None),
    )
    fast = mesh.shape["dp"] == 16 and mesh.shape["mp"] == 2
    return jax.shard_map(
        fast_device if fast else on_device,
        mesh=mesh,
        in_specs=placed,
        out_specs=(
            P("dp", None, None),
            P("dp", None, None),
            P("dp", None),
            P(None, None, "mp"),
            P(None, "mp"),
            P("mp", None),
            P(),
            P(None, "mp"),
            P("mp"),
            P("mp", None),
            P(),
            P(None, "mp"),
            P("mp"),
        ),
        check_vma=False,
    )
```

```python
import functools

import jax
import jax.numpy as jnp
from jax import lax
from jax.experimental import pallas as pl
from jax.experimental.pallas import tpu as pltpu
from jax.sharding import PartitionSpec as P

HEAD_DIM = 72


epsilon = 1e-06

f32 = jnp.float32
bf16 = jnp.bfloat16


def dot_nn(left, right):
    return lax.dot_general(left, right, (((1,), (0,)), ((), ())), preferred_element_type=f32)


def dot_nt(left, right):
    return lax.dot_general(left, right, (((1,), (1,)), ((), ())), preferred_element_type=f32)


def dot_tn(left, right):
    return lax.dot_general(left, right, (((0,), (0,)), ((), ())), preferred_element_type=f32)


def normalize(values):
    center = values - jnp.mean(values, axis=-1, keepdims=True)
    recip = lax.rsqrt(jnp.mean(center * center, axis=-1, keepdims=True) + epsilon)
    return center * recip, recip


def norm_pullback(grad_normed, unit, recip, scale_row):
    scaled_grad = grad_normed * (1.0 + scale_row)
    mean_grad = jnp.mean(scaled_grad, axis=-1, keepdims=True)
    mean_unit = jnp.mean(scaled_grad * unit, axis=-1, keepdims=True)
    return recip * (scaled_grad - mean_grad - unit * mean_unit)


def column(row):
    return jnp.broadcast_to(row[...].astype(f32), (8, row.shape[1])).T[:, 0:1]


def token_sum(values):
    return jnp.sum(values, axis=0, keepdims=True)


def attention_kernel(parts, own_images, sc, tok, cot, mod, b_proj, *refs):
    w_qkv, w_proj, bias = refs[:parts], refs[parts : 2 * parts], refs[2 * parts : 3 * parts]
    qkv, prob, mixed, attn_out, residual, normed_mlp, normed, grad_mlp, down_sums = refs[3 * parts :]
    image = sc[0] * own_images + pl.program_id(0)
    live = jnp.where(image < sc[1], 1.0, 0.0).astype(f32)
    unit, _ = normalize(tok[0].astype(f32))
    normed[0] = (unit * (1.0 + mod[0, 1:2, :]) + mod[0, 0:1, :]).astype(bf16)
    grad = (mod[0, 5:6, :] * (cot[0].astype(f32) * live)).astype(bf16)
    grad_mlp[0] = grad
    down_sums[0] = token_sum(grad.astype(f32))
    cols = w_proj[0].shape[0]
    pairs = cols // (2 * HEAD_DIM)
    span = 2 * HEAD_DIM
    factor = HEAD_DIM ** (-0.5)
    rows = normed[0]
    total = b_proj[...]
    for part in range(parts):
        base = part * 3 * cols
        shift = bias[part][...].astype(f32).T
        for proj in range(3):
            lo = proj * cols
            value = dot_nt(w_qkv[part][lo : lo + cols, :], rows)
            if proj != 1:
                value = value + shift[:, proj // 2 : proj // 2 + 1]
            qkv[0, base + lo : base + lo + cols, :] = value.astype(bf16)

        def pair_step(pair, carry, base=base, part=part):
            at = pl.multiple_of(base + pair * span, 16)
            query = qkv[0, pl.ds(at, span), :].astype(f32)
            key = qkv[0, pl.ds(at + cols, span), :].astype(f32)
            value = qkv[0, pl.ds(at + 2 * cols, span), :].astype(f32)
            outs = []
            for one in range(2):
                rows_of = slice(one * HEAD_DIM, (one + 1) * HEAD_DIM)
                scores = dot_tn(key[rows_of].astype(bf16), query[rows_of].astype(bf16)) * factor
                raised = jnp.exp(scores - jnp.max(scores, axis=0, keepdims=True))
                share = 1.0 / jnp.sum(raised, axis=0, keepdims=True)
                prob_b = (raised * share).astype(bf16)
                prob[0, part * 2 * pairs + 2 * pair + one] = prob_b
                outs.append(dot_nn(value[rows_of].astype(bf16), prob_b))
            to = pl.multiple_of(part * cols + pair * span, 16)
            mixed[0, pl.ds(to, span), :] = jnp.concatenate(outs, axis=0).astype(bf16)
            return carry

        lax.fori_loop(0, pairs, pair_step, 0, unroll=True)
        total = total + dot_tn(mixed[0, part * cols : (part + 1) * cols, :], w_proj[part][...])
    attn_out[0] = total
    summed = tok[0].astype(f32) + mod[0, 2:3, :] * total
    residual[0] = summed
    unit, _ = normalize(summed)
    normed_mlp[0] = (unit * (1.0 + mod[0, 4:5, :]) + mod[0, 3:4, :]).astype(bf16)


def mlp_kernel(per, jobs, sc, rows, grad_mlp, *refs):
    count = len(jobs)
    weights = [refs[3 * k : 3 * k + 3] for k in range(count)]
    refs = refs[3 * count :]
    came = []
    for _, summed in jobs:
        came.append(refs[0] if summed else None)
        refs = refs[1:] if summed else refs
    act, back = refs[2], refs[3]
    refs = refs[4:]
    grads = []
    for cuts, _ in jobs:
        size = 1 if cuts is None else len(cuts)
        grads.append(refs[:size])
        refs = refs[size:]
    job, step = pl.program_id(0), pl.program_id(1)
    for k in range(count):

        @pl.when(job == k)
        def _(k=k):
            mlp_block(
                per, jobs[k][0], step, sc, rows, grad_mlp, *weights[k], act, back, grads[k], refs[k], came[k]
            )


def mlp_block(per, cuts, step, sc, rows, grad_mlp, w_up, w_down, bias, act, back, grads, sums, came):
    here = w_down.shape[0] // per
    hidden = lax.dot_general(
        w_up[...], rows[...], (((0,), (1,)), ((), ())), preferred_element_type=f32
    ) + column(bias)
    square = hidden * hidden
    bend = jnp.tanh(0.7978845608028654 * hidden * (1.0 + 0.044715 * square))
    half = 0.5 * (1.0 + bend)
    act_b = (hidden * half).astype(bf16)
    slope = half + 0.5 * hidden * (1.0 - bend * bend) * (
        0.7978845608028654 * (1.0 + 3.0 * 0.044715 * square)
    )
    back_b = (dot_nt(w_down[...], grad_mlp[...]) * slope).astype(bf16)
    act[0] = act_b
    back[0] = back_b
    sums[...] = dot_nt(jnp.ones((8, rows.shape[0]), bf16), back_b)[0:1]
    for lo_row, left, right in ((0, act_b, grad_mlp), (per, back_b, rows)):
        grad = dot_nn(left, right[...])
        for piece in range(here):
            value = grad[piece * per : (piece + 1) * per]
            if cuts is None:
                if came is not None:
                    value = value + came[piece, lo_row : lo_row + per, :].astype(f32)
                grads[0][piece, lo_row : lo_row + per, :] = value.astype(bf16)
            else:
                at = jnp.bitwise_xor(step * here + piece, sc[2])
                for (lo, hi), into in zip(cuts, grads):
                    into[at, lo_row : lo_row + per, :] = value[:, lo:hi].astype(bf16)


def grow(total, part_steps, left, rights, dims):
    step = pl.program_id(0)

    def term(right):
        return lax.dot_general(left, right[...], (dims, ((), ())), preferred_element_type=f32)

    @pl.when(step == 0)
    def _():
        total[...] = term(rights[0])

    @pl.when(jnp.logical_and(step > 0, step < part_steps))
    def _():
        total[...] += term(rights[0])

    @pl.when(jnp.logical_and(step >= part_steps, step < 2 * part_steps))
    def _():
        total[...] += term(rights[1])


def norm_back_kernel(
    part_steps, own_images, sc, back, w_up0, w_up1, residual, cot, mod, attn_out,
    grad_residual, grad_attn, sums, total
):
    grow(total, part_steps, back[0], (w_up0, w_up1), ((0,), (1,)))
    one = pl.program_id(0) - 2 * part_steps
    seq = residual.shape[1]

    @pl.when(one >= 0)
    def _():
        live = jnp.where(sc[0] * own_images + one < sc[1], 1.0, 0.0).astype(f32)
        grad_normed = total[pl.ds(pl.multiple_of(one * seq, seq), seq), :]
        unit, recip = normalize(residual[0])
        sums[0, 0:1, :] = token_sum(grad_normed)
        sums[0, 1:2, :] = token_sum(grad_normed * unit)
        grad_res = cot[0].astype(f32) * live + norm_pullback(grad_normed, unit, recip, mod[0, 4:5, :])
        grad_residual[0] = grad_res
        sums[0, 2:3, :] = token_sum(grad_res * attn_out[0])
        grad_att = (mod[0, 2:3, :] * grad_res).astype(bf16)
        grad_attn[0] = grad_att
        sums[0, 3:4, :] = token_sum(grad_att.astype(f32))


def back_kernel(parts, sc, grad_attn, qkv, prob, *refs):
    w_proj = refs[:parts]
    grad_qkv, grad_mixed = refs[parts:]
    cols = w_proj[0].shape[0]
    pairs = cols // (2 * HEAD_DIM)
    span = 2 * HEAD_DIM
    factor = HEAD_DIM ** (-0.5)
    grad_att = grad_attn[0]
    for part in range(parts):
        base = part * 3 * cols
        grad_mixed[part * cols : (part + 1) * cols, :] = dot_nt(w_proj[part][...], grad_att).astype(bf16)

        def pair_step(pair, carry, base=base, part=part):
            at = pl.multiple_of(base + pair * span, 16)
            query = qkv[0, pl.ds(at, span), :].astype(f32)
            key = qkv[0, pl.ds(at + cols, span), :].astype(f32)
            value = qkv[0, pl.ds(at + 2 * cols, span), :].astype(f32)
            grads = grad_mixed[pl.ds(pl.multiple_of(part * cols + pair * span, 16), span), :].astype(f32)
            to_query, to_key, to_value = [], [], []
            for one in range(2):
                rows_of = slice(one * HEAD_DIM, (one + 1) * HEAD_DIM)
                prob_b = prob[0, part * 2 * pairs + 2 * pair + one]
                prob_f = prob_b.astype(f32)
                grad_b = grads[rows_of].astype(bf16)
                grad_prob = dot_tn(value[rows_of].astype(bf16), grad_b)
                delta = jnp.sum(prob_f * grad_prob, axis=0, keepdims=True)
                grad_scores = (prob_f * (grad_prob - delta)).astype(bf16)
                to_query.append(dot_nn(key[rows_of].astype(bf16), grad_scores) * factor)
                to_key.append(dot_nt(query[rows_of].astype(bf16), grad_scores) * factor)
                to_value.append(dot_nt(grad_b, prob_b))
            grad_qkv[0, pl.ds(at, span), :] = jnp.concatenate(to_query, axis=0).astype(bf16)
            grad_qkv[0, pl.ds(at + cols, span), :] = jnp.concatenate(to_key, axis=0).astype(bf16)
            grad_qkv[0, pl.ds(at + 2 * cols, span), :] = jnp.concatenate(to_value, axis=0).astype(bf16)
            return carry

        lax.fori_loop(0, pairs, pair_step, 0, unroll=True)


def attn_grad_kernel(pieces, per, cuts, sc, *refs):
    grad_qkv, mixed, normed, grad_attn = refs[:pieces], refs[pieces], refs[pieces + 1], refs[pieces + 2]
    grads, sums = refs[pieces + 3 : -1], refs[-1]
    step = pl.program_id(0)
    here = mixed.shape[1] // per
    images = mixed.shape[0]
    each = images // pieces

    def spread(total):
        total = total.astype(bf16)
        for piece in range(here):
            at = jnp.bitwise_xor(step * here + piece, sc[2])
            for (lo, hi), into in zip(cuts, grads):
                into[at] = total[piece * per : (piece + 1) * per, lo:hi]

    @pl.when(step < 3)
    def _():
        ones = jnp.ones((8, mixed.shape[2]), bf16)
        total = count = None
        for image in range(images):
            left = grad_qkv[image // each][image % each]
            term, one = dot_nn(left, normed[image]), dot_nt(ones, left)
            total = term if image == 0 else total + term
            count = one if image == 0 else count + one
        sums[0] = count[0:1]
        spread(total)

    @pl.when(step == 3)
    def _():
        total = dot_nn(mixed[0], grad_attn[0])
        for image in range(1, images):
            total = total + dot_nn(mixed[image], grad_attn[image])
        spread(total)


def first_back_kernel(pieces, images, sc, *refs):
    grad_qkv = refs[:pieces]
    w_qkv0, w_qkv1, tok, mod, grad_residual = refs[pieces : pieces + 5]
    grad_tokens, grad_own, sums, total = refs[pieces + 5 :]
    step = pl.program_id(0)
    each = images // pieces
    seq = tok.shape[1]

    def add(w_qkv, fresh):
        for one in range(images):
            term = dot_tn(grad_qkv[one // each][one % each], w_qkv[...])
            if fresh:
                total[one * seq : (one + 1) * seq, :] = term
            else:
                total[one * seq : (one + 1) * seq, :] += term

    @pl.when(step == 0)
    def _():
        add(w_qkv0, True)

    @pl.when(jnp.logical_and(step > 0, step < 3))
    def _():
        add(w_qkv0, False)

    @pl.when(jnp.logical_and(step >= 3, step < 6))
    def _():
        add(w_qkv1, False)

    @pl.when(step >= 6)
    def _():
        grad_normed = total[pl.ds(pl.multiple_of((step - 6) * seq, seq), seq), :]
        unit, recip = normalize(tok[0].astype(f32))
        sums[0, 0:1, :] = token_sum(grad_normed)
        sums[0, 1:2, :] = token_sum(grad_normed * unit)
        grad = grad_residual[0] + norm_pullback(grad_normed, unit, recip, mod[0, 1:2, :])
        grad_tokens[0] = grad
        grad_own[0] = grad


def output_kernel(
    part_steps, own_images, sc, act, w_down0, w_down1, residual, cot, mod, b_down, output, own, sums, total
):
    grow(total, part_steps, act[0], (w_down0, w_down1), ((0,), (0,)))
    one = pl.program_id(0) - 2 * part_steps
    seq = residual.shape[1]

    @pl.when(one >= 0)
    def _():
        live = jnp.where(sc[0] * own_images + one < sc[1], 1.0, 0.0).astype(f32)
        mlp_out = total[pl.ds(pl.multiple_of(one * seq, seq), seq), :] + b_down[...]
        sums[0] = token_sum((cot[0].astype(f32) * live) * mlp_out)
        rows = ((residual[0] + mod[0, 5:6, :] * mlp_out) * live).astype(bf16)
        output[0] = rows
        own[0] = rows


def final_piece(sc, halves, piece, store):
    rel = jnp.bitwise_xor(piece, sc[2])
    for low, high, route, lo, hi in halves:
        bits = [(rel >> bit) & 1 for bit in route]
        index = bits[1] * 4 + bits[2] * 2 + bits[3]

        @pl.when(bits[0] == 0)
        def _(low=low, index=index, lo=lo, hi=hi):
            store(low[index].astype(f32), lo, hi)

        @pl.when(bits[0] == 1)
        def _(high=high, index=index, lo=lo, hi=hi):
            store(high[index].astype(f32), lo, hi)


def final_mlp_kernel(cuts, per, sc, *refs):
    count = 2 * len(cuts)
    arrays, (_, _, down, up, mark, turned) = refs[:count], refs[count:]
    here = down.shape[0] // per
    halves = [(arrays[2 * k], arrays[2 * k + 1]) + cut for k, cut in enumerate(cuts)]
    for piece in range(here):

        def store(value, lo, hi, piece=piece):
            down[piece * per : (piece + 1) * per, lo:hi] = value[0:per]
            turned[piece * per : (piece + 1) * per, lo:hi] = value[per : 2 * per]

        final_piece(sc, halves, pl.program_id(0) * here + piece, store)
    up[...] = turned[...].T
    mark[...] = jnp.zeros_like(mark)


def final_plain_kernel(per, sc, summed, down_in, up_in, down, up, mark, turned):
    for piece in range(summed.shape[0]):
        lo = piece * per
        down[lo : lo + per, :] = summed[piece, 0:per, :].astype(f32)
        turned[lo : lo + per, :] = summed[piece, per : 2 * per, :].astype(f32)
    up[...] = turned[...].T
    mark[...] = jnp.zeros_like(mark)


def final_attn_kernel(cuts, per, sc, *refs):
    count = 2 * len(cuts)
    arrays, (qkv, proj) = refs[:count], refs[count:]
    here = proj.shape[0] // per
    halves = [(arrays[2 * k], arrays[2 * k + 1]) + cut for k, cut in enumerate(cuts)]
    for target, wanted in ((qkv, True), (proj, False)):

        @pl.when((pl.program_id(0) < 3) == wanted)
        def _(target=target):
            for piece in range(here):

                def store(value, lo, hi, piece=piece):
                    target[piece * per : (piece + 1) * per, lo:hi] = value

                final_piece(sc, halves, pl.program_id(0) * here + piece, store)


def run_kernel(
    body, sc, args, in_specs, out_specs, out_shape, grid, micros, scratch=(), alias=None, room=60
):
    size = sum(a.size * a.dtype.itemsize for a in args) + sum(
        s.size * s.dtype.itemsize for s in out_shape
    )
    return pl.pallas_call(
        body,
        out_shape=out_shape,
        grid_spec=pltpu.PrefetchScalarGridSpec(
            num_scalar_prefetch=1,
            grid=grid,
            in_specs=in_specs,
            out_specs=out_specs,
            scratch_shapes=list(scratch),
        ),
        compiler_params=pltpu.CompilerParams(vmem_limit_bytes=room << 20),
        cost_estimate=pl.CostEstimate(
            flops=int(micros * 1.15e9), bytes_accessed=int(min(size, micros * 1e6)), transcendentals=0
        ),
        input_output_aliases=alias or {},
    )(sc, *args)


def whole_block(array):
    zeros = (0,) * array.ndim
    return pl.BlockSpec(array.shape, lambda *_: zeros, pipeline_mode=pl.Buffered(1))


def shape_of(dims, kind):
    return jax.ShapeDtypeStruct(dims, kind)


SWAP = [(0, 1), (1, 0)]


def swap_cores(value):
    return lax.ppermute(value, "mp", SWAP)


def bit_pairs(bit):
    return [(index, index ^ (1 << bit)) for index in range(16)]


MLP_WAYS = ((0, 640, (0, 1, 2, 3)), (640, 1152, (1, 0, 2, 3)))
ATTN_WAYS = ((0, 512, (0, 1, 2, 3)), (512, 896, (1, 0, 2, 3)), (896, 1152, (2, 3, 0, 1)))


def columns(ways):
    return tuple((lo, hi) for lo, hi, _ in ways)


def cut(array, bits, bit, side):
    return lax.index_in_dim(array, side, bits.index(bit), keepdims=False)


def left_bits(done):
    return [bit for bit in (3, 2, 1, 0) if bit not in done]


def exchange(values, bits):
    return [lax.ppermute(value, "dp", bit_pairs(bit)) for value, bit in zip(values, bits)]


def reduce_flow(ways, get_own, others):
    others = yield others
    came = [swap_cores(other) for other in others]
    yield None
    own, came = yield [get_own(), came]
    firsts, seconds = ([a.reshape((2, 2, 2, 2) + a.shape[1:]) for a in arrays] for arrays in (own, came))
    routes = [way for _, _, way in ways]
    for stage in range(4):
        sends, keeps = [], []
        for route, one, two in zip(routes, firsts, seconds):
            bits = left_bits(route[:stage])
            for side, into in ((1, sends), (0, keeps)):
                into.append(cut(one, bits, route[stage], side) + cut(two, bits, route[stage], side))
        if stage == 2 and routes[0][2:] == routes[1][2:]:
            sends = [jnp.concatenate(sends[:2], axis=-1)] + sends[2:]
            keeps = [jnp.concatenate(keeps[:2], axis=-1)] + keeps[2:]
            routes = [routes[0]] + routes[2:]
        sends, keeps = yield [sends, keeps]
        comes = exchange(sends, [route[stage] for route in routes])
        yield None
        firsts, seconds = yield [keeps, comes]
    return [one + two for one, two in zip(firsts, seconds)]


def gather_flow(ways, have):
    routes = [ways[0][2]] + [way for _, _, way in ways[2:]]
    middle = ways[0][1]
    (have,) = yield [have]
    comes = exchange(have, [route[3] for route in routes])
    have = [one[None] for one in have]
    comes = [one[None] for one in comes]
    yield None
    for stage in (2, 1, 0):
        have, comes = yield [have, comes]
        joined = [jnp.concatenate([one, two]) for one, two in zip(have, comes)]
        if stage == 1:
            joined = [joined[0][..., :middle], joined[0][..., middle:]] + joined[1:]
            routes = [way for _, _, way in ways]
        (have,) = yield [joined]
        comes = exchange(have, [route[stage] for route in routes])
        yield None
    have, comes = yield [have, comes]
    return [part for pair in zip(have, comes) for part in pair]


def sum_flow(ways, get_own, others):
    have = yield from reduce_flow(ways, get_own, others)
    return (yield from gather_flow(ways, have))


def swap_flow(other):
    (other,) = yield [other]
    came = swap_cores(other)
    yield None
    (came,) = yield [came]
    return came


def rows_flow(rows):
    for bit in (3, 2, 1, 0):
        (rows,) = yield [rows]
        came = lax.ppermute(rows, "dp", bit_pairs(bit))
        yield None
        rows, came = yield [rows, came]
        rows = jnp.concatenate([rows, came])
    return rows


class Order:
    def __init__(self, sc):
        self.sc = sc
        self.results = {}

    def fence(self, values):
        self.sc, values = lax.optimization_barrier((self.sc, values))
        return values

    def after(self, value):
        self.sc, _ = lax.optimization_barrier((self.sc, value))

    def tick(self, *flows):
        replies = {flow: None for flow in flows if flow not in self.results}
        while replies:
            wants = {}
            for flow, reply in replies.items():
                try:
                    want = flow.send(reply)
                except StopIteration as stop:
                    self.results[flow] = stop.value
                    continue
                if want is not None:
                    wants[flow] = want
            replies = dict(zip(wants, self.fence(list(wants.values())))) if wants else {}

    def finish(self, flow):
        while flow not in self.results:
            self.tick(flow)
        return self.results[flow]


CHUNKS = 3
PLAIN = 2


def fill_other(both, came, core):
    size = came.shape[0]
    return lax.dynamic_update_slice_in_dim(both, came, (1 - core) * size, 0)


def fast_device(
    tokens, condition, counts, w_qkv, b_qv, w_proj, b_proj, w_up, b_up, w_down, b_down, w_mod, b_mod,
    cotangent,
):
    slots, seq, dim = tokens.shape
    images = slots // 2
    count = images * seq
    cols = w_qkv.shape[2]
    ff = w_up.shape[1]
    own_cols = w_mod.shape[1]
    heads = cols // HEAD_DIM
    core = lax.axis_index("mp")
    order = Order(jnp.stack([core, counts[0], lax.axis_index("dp")]).astype(jnp.int32))

    qkv_rows = jnp.transpose(w_qkv, (1, 2, 0)).reshape(3 * cols, dim)
    wq = [qkv_rows, swap_cores(qkv_rows)]
    wp = [w_proj, swap_cores(w_proj)]
    qkv_bias = [b_qv, swap_cores(b_qv)]

    cond_f = condition.astype(f32)
    scaled = jax.nn.silu(cond_f).astype(bf16)
    own_mod = jnp.dot(scaled, w_mod, preferred_element_type=f32) + b_mod.astype(f32)
    other_mod = swap_cores(own_mod)
    sides = [jnp.where(core == side, own_mod, other_mod) for side in range(2)]
    modulation = jnp.concatenate(sides, axis=1).reshape(slots, 6, dim)
    proj_bias = b_proj.astype(f32)[None]
    down_bias = b_down.astype(f32)[None]

    late_up, late_down, late_bias = lax.optimization_barrier((wq[1], w_up, w_down, b_up, modulation))[1:4]
    wu = [w_up, swap_cores(late_up)]
    wd = [w_down, swap_cores(late_down)]
    up_bias = [b_up[None], swap_cores(late_bias[None])]

    local = lambda i, s: (s[0] * images + i, 0, 0)
    mine = lambda i, s: (i, 0, 0)
    tok_spec = pl.BlockSpec((1, seq, dim), local)
    own_spec = pl.BlockSpec((1, seq, dim), mine)
    mod_spec = pl.BlockSpec((1, 6, dim), local)
    row_spec = pl.BlockSpec((1, 1, dim), mine)
    qkv_spec = pl.BlockSpec((1, 6 * cols, seq), mine)
    prob_spec = pl.BlockSpec((1, 2 * heads, seq, seq), lambda i, s: (i, 0, 0, 0))
    mixed_spec = pl.BlockSpec((1, 2 * cols, seq), mine)
    token_f = shape_of((images, seq, dim), f32)
    token_b = shape_of((images, seq, dim), bf16)
    attn_args = wq + wp + qkv_bias
    qkv, prob, mixed, attn_out, residual, normed_mlp, normed, grad_mlp, down_sums = run_kernel(
        functools.partial(attention_kernel, 2, images),
        order.sc,
        [tokens, cotangent, modulation, proj_bias] + attn_args,
        [tok_spec, tok_spec, mod_spec, whole_block(proj_bias)] + [whole_block(a) for a in attn_args],
        [qkv_spec, prob_spec, mixed_spec] + [own_spec] * 5 + [row_spec],
        [
            shape_of((images, 6 * cols, seq), bf16),
            shape_of((images, 2 * heads, seq, seq), bf16),
            shape_of((images, 2 * cols, seq), bf16),
            token_f,
            token_f,
            token_b,
            token_b,
            token_b,
            shape_of((images, 1, dim), f32),
        ],
        (images,),
        45,
    )
    order.after(down_sums)

    rows_flat = normed_mlp.reshape(count, dim)
    grad_flat = grad_mlp.reshape(count, dim)
    width = ff // CHUNKS
    per = width // 16
    steps = 2
    block = width // steps
    anywhere = pl.BlockSpec(memory_space=pl.ANY)
    act = back = jnp.zeros((8, 128), bf16)
    up_sums = {}

    def mlp_call(jobs, came, micros):
        nonlocal act, back
        first = act.shape[0] == 8
        kinds = tuple((None if job[0] < PLAIN else columns(MLP_WAYS), job in came) for job in jobs)

        def turn(k):
            return lambda p, s, c: jnp.clip((p - k) * steps + s, 0, steps - 1)

        def pick(values):
            return lambda p: sum(jnp.where(p == k, value, 0) for k, value in enumerate(values))

        parts = pick([part for _, part in jobs])
        starts = pick([chunk * steps for chunk, _ in jobs])
        spread = pl.BlockSpec((1, block, count), lambda p, s, c: (parts(p), starts(p) + s, 0))
        args, specs = [], []
        for k, (chunk, part) in enumerate(jobs):
            at = chunk * steps
            wide = lambda p, s, c, k=k, at=at: (0, at + turn(k)(p, s, c))
            tall = lambda p, s, c, k=k, at=at: (at + turn(k)(p, s, c), 0)
            args += [wu[part], wd[part], up_bias[part]]
            specs += [
                pl.BlockSpec((dim, block), wide),
                pl.BlockSpec((block, dim), tall),
                pl.BlockSpec((1, block), wide),
            ]
        grad_specs, grad_shapes, sizes = [], [], []
        for k, (split, _) in enumerate(kinds):
            own = lambda p, s, c, k=k: (turn(k)(p, s, c), 0, 0)
            fixed = lambda p, s, c: (0, 0, 0)
            wides = [dim] if split is None else [hi - lo for lo, hi in split]
            lead = (16 // steps, own) if split is None else (16, fixed)
            grad_specs.append([pl.BlockSpec((lead[0], 2 * per, wide), lead[1]) for wide in wides])
            grad_shapes += [shape_of((16, 2 * per, wide), bf16) for wide in wides]
            sizes.append(len(wides))
        for k, job in enumerate(jobs):
            if job in came:
                args.append(came[job])
                specs += grad_specs[k]
        args += [act, back]
        spot = len(args) + 1
        outs = run_kernel(
            functools.partial(mlp_kernel, per, kinds),
            order.sc,
            [rows_flat, grad_flat] + args,
            [whole_block(rows_flat), whole_block(grad_flat)] + specs + [anywhere, anywhere],
            [spread, spread]
            + [spec for specs in grad_specs for spec in specs]
            + [pl.BlockSpec((1, block), lambda p, s, c, k=k: (0, turn(k)(p, s, c))) for k in range(len(jobs))],
            [shape_of((2, ff, count), bf16)] * 2 + grad_shapes + [shape_of((1, width), f32)] * len(jobs),
            (len(jobs), steps),
            micros,
            alias=None if first else {spot: 0, spot + 1: 1},
        )
        act, back = outs[:2]
        grads, outs = list(outs[2 : 2 + sum(sizes)]), outs[2 + sum(sizes) :]
        up_sums.update(zip(jobs, outs))
        order.after(outs[-1])
        return [[grads.pop(0) for _ in range(size)] for size in sizes]

    summed = range(PLAIN)
    swaps = [swap_flow(grad) for (grad,) in mlp_call([(chunk, 1) for chunk in summed], {}, 26)]
    order.tick(*swaps)
    rest = [(chunk, part) for chunk in range(PLAIN, CHUNKS) for part in (1, 0)]
    grads = mlp_call(rest, {}, 26)
    flows = [
        sum_flow(MLP_WAYS, lambda own=own: own, others) for others, own in zip(grads[0::2], grads[1::2])
    ]
    order.tick(*swaps, *flows)
    came = {(chunk, 0): order.results[swap] for chunk, swap in zip(summed, swaps)}
    grads = mlp_call([(chunk, 0) for chunk in summed], came, 26)
    plain_sums = lax.psum([grad for (grad,) in grads], "dp")
    order.tick(*flows)

    reach = 768
    turns = ff // reach
    every = lambda s, c: (0, 0, 0)
    tail = lambda first: lambda s, c: (jnp.maximum(s - first, 0), 0, 0)
    tail_local = lambda first: lambda s, c: (c[0] * images + jnp.maximum(s - first, 0), 0, 0)

    def image_spec(first, where=tail):
        return pl.BlockSpec((1, seq, dim), where(first))

    def rows_of(part, size):
        if part == 0:
            return lambda s, c: jnp.minimum(s, size - 1)
        return lambda s, c: jnp.clip(s - size, 0, size - 1)

    span_spec = pl.BlockSpec(
        (1, reach, count),
        lambda s, c: (jnp.minimum(s // turns, 1), jnp.where(s < 2 * turns, s % turns, turns - 1), 0),
    )
    grad_residual, grad_attn, mid_sums = run_kernel(
        functools.partial(norm_back_kernel, turns, images),
        order.sc,
        [back] + wu + [residual, cotangent, modulation, attn_out],
        [
            span_spec,
            pl.BlockSpec((dim, reach), lambda s, c: (0, rows_of(0, turns)(s, c))),
            pl.BlockSpec((dim, reach), lambda s, c: (0, rows_of(1, turns)(s, c))),
            image_spec(2 * turns),
            image_spec(2 * turns, tail_local),
            pl.BlockSpec((1, 6, dim), tail_local(2 * turns)),
            image_spec(2 * turns),
        ],
        [image_spec(2 * turns)] * 2 + [pl.BlockSpec((1, 4, dim), tail(2 * turns))],
        [token_f, token_b, shape_of((images, 4, dim), f32)],
        (2 * turns + images,),
        60,
        scratch=[pltpu.VMEM((count, dim), f32)],
    )
    order.after(mid_sums)
    order.tick(*flows)
    pieces = 2
    each = images // pieces
    grad_qkv = []
    for piece in range(pieces):
        there = lambda i, s, piece=piece: (piece * each + i, 0, 0)
        (grad_piece,) = run_kernel(
            functools.partial(back_kernel, 2),
            order.sc,
            [grad_attn, qkv, prob] + wp,
            [
                pl.BlockSpec((1, seq, dim), there),
                pl.BlockSpec((1, 6 * cols, seq), there),
                pl.BlockSpec((1, 2 * heads, seq, seq), lambda i, s, piece=piece: (piece * each + i, 0, 0, 0)),
            ]
            + [whole_block(a) for a in wp],
            [qkv_spec],
            [shape_of((each, 6 * cols, seq), bf16)],
            (each,),
            60,
            scratch=[pltpu.VMEM((2 * cols, seq), bf16)],
            )
        grad_qkv.append(grad_piece)
        order.after(grad_piece)
        order.tick(*flows)

    attn_per = 4 * cols // 16
    qv_sums = [None, None]

    def attn_part(part):
        *grads, sums = run_kernel(
            functools.partial(attn_grad_kernel, pieces, attn_per, columns(ATTN_WAYS)),
            order.sc,
            grad_qkv + [mixed, normed, grad_attn],
            [
                pl.BlockSpec((each, cols, seq), lambda s, c: (0, 3 * part + jnp.minimum(s, 2), 0))
                for _ in range(pieces)
            ]
            + [pl.BlockSpec((images, cols, seq), lambda s, c: (0, part, 0))]
            + [whole_block(normed), whole_block(grad_attn)],
            [pl.BlockSpec((16, attn_per, hi - lo), every) for lo, hi in columns(ATTN_WAYS)]
            + [pl.BlockSpec((1, 1, cols), lambda s, c: (jnp.minimum(s, 2), 0, 0))],
            [shape_of((16, attn_per, hi - lo), bf16) for lo, hi in columns(ATTN_WAYS)]
            + [shape_of((3, 1, cols), f32)],
            (4,),
            60,
            )
        qv_sums[part] = sums
        order.after(sums)
        return grads

    grad_other = attn_part(1)
    made = []
    last = sum_flow(ATTN_WAYS, lambda: made[0], grad_other)
    order.tick(last, *flows)
    made.append(attn_part(0))
    order.tick(last, *flows)

    first_spec = lambda part: pl.BlockSpec((cols, dim), lambda s, c: (rows_of(part, 3)(s, c), 0))
    grad_tokens, grad_own_tokens, low_sums = run_kernel(
        functools.partial(first_back_kernel, pieces, images),
        order.sc,
        grad_qkv + wq + [tokens, modulation, grad_residual],
        [pl.BlockSpec((each, cols, seq), lambda s, c: (0, jnp.minimum(s, 5), 0)) for _ in range(pieces)]
        + [first_spec(0), first_spec(1)]
        + [image_spec(6, tail_local), pl.BlockSpec((1, 6, dim), tail_local(6)), image_spec(6)],
        [image_spec(6, tail_local), image_spec(6), pl.BlockSpec((1, 2, dim), tail(6))],
        [shape_of((slots, seq, dim), f32), token_f, shape_of((images, 2, dim), f32)],
        (6 + images,),
        60,
        scratch=[pltpu.VMEM((count, dim), f32)],
    )
    order.after(low_sums)
    order.tick(last, *flows)
    other_tokens = swap_cores(grad_own_tokens)
    down_spec = lambda part: pl.BlockSpec((reach, dim), lambda s, c: (rows_of(part, turns)(s, c), 0))
    output, own_output, gate_sums = run_kernel(
        functools.partial(output_kernel, turns, images),
        order.sc,
        [act] + wd + [residual, cotangent, modulation, down_bias],
        [
            span_spec,
            down_spec(0),
            down_spec(1),
            image_spec(2 * turns),
            image_spec(2 * turns, tail_local),
            pl.BlockSpec((1, 6, dim), tail_local(2 * turns)),
            whole_block(down_bias),
        ],
        [image_spec(2 * turns, tail_local), image_spec(2 * turns), pl.BlockSpec((1, 1, dim), tail(2 * turns))],
        [shape_of((slots, seq, dim), bf16), token_b, shape_of((images, 1, dim), f32)],
        (2 * turns + images,),
        60,
        scratch=[pltpu.VMEM((count, dim), f32)],
    )
    order.after(gate_sums)
    order.tick(last, *flows)
    other_output = swap_cores(own_output)

    low_sums, mid_sums, gate_sums, down_sums = order.fence((low_sums, mid_sums, gate_sums, down_sums))
    grad_modulation = jnp.concatenate([low_sums, mid_sums[:, 2:3], mid_sums[:, 0:2], gate_sums], axis=1)
    grad_modulation = grad_modulation.reshape(images, 6 * dim).astype(bf16)
    bias_sums = [
        jnp.concatenate(
            [qv_sums[part][0], qv_sums[part][2]]
            + [up_sums[chunk, part] for chunk in range(CHUNKS)],
            axis=1,
        )
        for part in range(2)
    ]
    shared = jnp.concatenate(
        [
            jnp.sum(mid_sums[:, 3], axis=0, keepdims=True),
            jnp.sum(down_sums[:, 0], axis=0, keepdims=True),
            jnp.zeros((1, own_cols - 2 * dim), f32),
        ],
        axis=1,
    )
    halves = grad_modulation.reshape(images, 2, own_cols)
    kept = lax.dynamic_index_in_dim(halves, core, 1, keepdims=False)
    given = lax.dynamic_index_in_dim(halves, 1 - core, 1, keepdims=False)
    got = swap_cores(jnp.concatenate([given.astype(f32), bias_sums[1], shared]))
    came = got[:images].astype(bf16)
    group_mod = jnp.where(core == 0, jnp.concatenate([kept, came]), jnp.concatenate([came, kept]))
    own_bias_sum = bias_sums[0] + got[images : images + 1]
    shared_sum = shared + got[images + 1 :]
    wide_scaled = jnp.pad(scaled.reshape(-1), (0, 3 * own_cols - slots * dim)).reshape(3, own_cols)
    packed_rows = jnp.concatenate(
        [group_mod, own_bias_sum.astype(bf16), shared_sum.astype(bf16), wide_scaled]
    )
    (packed_rows,) = order.fence([packed_rows])
    small = rows_flow(packed_rows)
    order.tick(last, small, *flows)
    (group_mod,) = order.fence([group_mod])
    part_scaled = outer_cols(group_mod, w_mod).astype(bf16)
    came_scaled = swap_cores(part_scaled)
    output = fill_other(output, order.fence(other_output), core)
    order.after((output[0, 0, :1], part_scaled[0, :1]))
    order.tick(last, small, *flows)
    grad_tokens = fill_other(grad_tokens, order.fence(other_tokens), core)
    part_scaled, came_scaled = order.fence((part_scaled, came_scaled))
    grad_scaled = part_scaled.astype(f32) + came_scaled.astype(f32)
    _, silu_back = jax.vjp(jax.nn.silu, cond_f)
    grad_condition = silu_back(grad_scaled)[0]
    order.after((grad_tokens[0, 0, :1], grad_condition[0, :1]))
    order.tick(last, small, *flows)

    def cuts(ways):
        return tuple((way, lo, hi) for lo, hi, way in ways)

    grad_w_down = grad_w_up = jnp.zeros((8, 128), f32)

    def final_mlp(chunk, body, args):
        nonlocal grad_w_down, grad_w_up
        first = grad_w_down.shape[0] == 8
        spot = len(args) + 1
        grad_w_down, grad_w_up, mark = run_kernel(
            body,
            order.sc,
            list(args) + [grad_w_down, grad_w_up],
            [
                whole_block(a)
                if a.shape[0] == 8
                else pl.BlockSpec((16 // steps,) + a.shape[1:], lambda s, c: (s, 0, 0))
                for a in args
            ]
            + [anywhere, anywhere],
            [
                pl.BlockSpec((block, dim), lambda s, c: (chunk * steps + s, 0)),
                pl.BlockSpec((dim, block), lambda s, c: (0, chunk * steps + s)),
                pl.BlockSpec((8, 128), lambda s, c: (0, 0)),
            ],
            [shape_of((ff, dim), f32), shape_of((dim, ff), f32), shape_of((8, 128), f32)],
            (steps,),
            4,
            scratch=[pltpu.VMEM((block, dim), f32)],
            alias=None if first else {spot: 0, spot + 1: 1},
        )
        order.after(mark)

    for chunk, flow in enumerate(flows):
        body = functools.partial(final_mlp_kernel, cuts(MLP_WAYS), per)
        final_mlp(PLAIN + chunk, body, order.finish(flow))
    order.tick(last, small)
    for chunk, total in zip(summed, order.fence(plain_sums)):
        final_mlp(chunk, functools.partial(final_plain_kernel, per), [total])
    order.tick(last)
    all_rows = order.fence(order.finish(small)).reshape(16, slots + 5, own_cols)
    all_mod = all_rows[:, :slots].reshape(-1, own_cols)
    all_scaled = all_rows[:, slots + 2 :].reshape(16, -1)[:, : slots * dim].reshape(-1, dim)
    grad_w_mod = inner_rows(all_scaled, all_mod)
    grad_b_mod = jnp.sum(all_mod.astype(f32), axis=0)
    bias_total = jnp.sum(all_rows[:, slots : slots + 2].astype(f32), axis=0)
    grad_b_qv = bias_total[0, : 2 * cols].reshape(2, cols)
    grad_b_up = bias_total[0, 2 * cols :]
    grad_b_proj = bias_total[1, :dim]
    grad_b_down = bias_total[1, dim : 2 * dim]
    order.after((grad_w_mod[0, :1], grad_b_mod[:1], bias_total[0, :1]))
    args = order.finish(last)
    grad_qkv_rows, grad_w_proj = run_kernel(
        functools.partial(final_attn_kernel, cuts(ATTN_WAYS), attn_per),
        order.sc,
        list(args),
        [whole_block(a) for a in args],
        [
            pl.BlockSpec((cols, dim), lambda s, c: (jnp.minimum(s, 2), 0)),
            pl.BlockSpec((cols, dim), lambda s, c: (0, 0)),
        ],
        [shape_of((3 * cols, dim), f32), shape_of((cols, dim), f32)],
        (4,),
        9,
    )
    grad_w_qkv = jnp.transpose(grad_qkv_rows.reshape(3, cols, dim), (2, 0, 1))
    return (
        output,
        grad_tokens,
        grad_condition,
        grad_w_qkv,
        grad_b_qv,
        grad_w_proj,
        grad_b_proj,
        grad_w_up,
        grad_b_up,
        grad_w_down,
        grad_b_down,
        grad_w_mod,
        grad_b_mod,
    )


def layer_norm(values):
    center = values - jnp.mean(values, axis=-1, keepdims=True)
    return center * lax.rsqrt(jnp.mean(center * center, axis=-1, keepdims=True) + epsilon)


def modulate(values, shift_part, scale_part):
    return layer_norm(values) * (1.0 + scale_part) + shift_part


def gelu_tanh(values):
    return (
        0.5
        * values
        * (1.0 + jnp.tanh(0.7978845608028654 * (values + 0.044715 * values * values * values)))
    )


def inner_rows(left, right):
    return lax.dot_general(
        left, right, (((0,), (0,)), ((), ())), preferred_element_type=jnp.float32
    )


def outer_cols(left, right):
    return lax.dot_general(
        left, right, (((1,), (1,)), ((), ())), preferred_element_type=jnp.float32
    )


def attention_forward(query_rows, key_rows, value_rows):
    factor = HEAD_DIM ** (-0.5)
    scores = (
        jnp.einsum("bqhd,bkhd->bhqk", query_rows, key_rows, preferred_element_type=jnp.float32)
        * factor
    )
    row_max = jnp.max(scores, axis=-1, keepdims=True)
    row_total = jnp.sum(jnp.exp(scores - row_max), axis=-1, keepdims=True)
    logsum = row_max + jnp.log(row_total)
    prob_b = jnp.exp(scores - logsum).astype(jnp.bfloat16)
    mixed_out = jnp.einsum(
        "bhqk,bkhd->bqhd", prob_b, value_rows, preferred_element_type=jnp.float32
    )
    return (mixed_out, logsum)


def attention_backward(query_rows, key_rows, value_rows, logsum, grad_mixed):
    factor = HEAD_DIM ** (-0.5)
    scores = (
        jnp.einsum("bqhd,bkhd->bhqk", query_rows, key_rows, preferred_element_type=jnp.float32)
        * factor
    )
    prob_f = jnp.exp(scores - logsum)
    prob_b = prob_f.astype(jnp.bfloat16)
    grad_prob = jnp.einsum(
        "bqhd,bkhd->bhqk", grad_mixed, value_rows, preferred_element_type=jnp.float32
    )
    row_delta = jnp.sum(prob_f * grad_prob, axis=-1, keepdims=True)
    grad_scores = (prob_f * (grad_prob - row_delta)).astype(jnp.bfloat16)
    grad_query = (
        jnp.einsum("bhqk,bkhd->bqhd", grad_scores, key_rows, preferred_element_type=jnp.float32)
        * factor
    )
    grad_key = (
        jnp.einsum("bhqk,bqhd->bkhd", grad_scores, query_rows, preferred_element_type=jnp.float32)
        * factor
    )
    grad_value = jnp.einsum(
        "bhqk,bqhd->bkhd", prob_b, grad_mixed, preferred_element_type=jnp.float32
    )
    return (
        grad_query.astype(jnp.bfloat16),
        grad_key.astype(jnp.bfloat16),
        grad_value.astype(jnp.bfloat16),
    )


def forward(tokens_f, spans, weights, repeat):
    w_qkv, b_qv, w_proj, b_proj, w_up, b_up, w_down, b_down = weights
    shift_attn, scale_attn, gate_attn, shift_mlp, scale_mlp, gate_mlp = spans
    slot_count, seq_len, model_dim = tokens_f.shape
    row_count = slot_count * seq_len
    head_cols = w_qkv.shape[2]
    head_count = head_cols // HEAD_DIM
    shape_four = (slot_count, seq_len, head_count, HEAD_DIM)
    normed = (
        modulate(tokens_f, shift_attn, scale_attn)
        .astype(jnp.bfloat16)
        .reshape(row_count, model_dim)
    )
    projected = jnp.dot(
        normed, w_qkv.reshape(model_dim, 3 * head_cols), preferred_element_type=jnp.float32
    )
    qkv_bias = jnp.stack([b_qv[0], jnp.zeros_like(b_qv[0]), b_qv[1]]).astype(jnp.float32)
    projected = (projected.reshape(row_count, 3, head_cols) + qkv_bias).astype(jnp.bfloat16)
    query_rows = projected[:, 0].reshape(shape_four)
    key_rows = projected[:, 1].reshape(shape_four)
    value_rows = projected[:, 2].reshape(shape_four)
    mixed_out, logsum = attention_forward(query_rows, key_rows, value_rows)
    mixed_b = mixed_out.astype(jnp.bfloat16).reshape(row_count, head_cols)
    partial_value = jnp.dot(mixed_b, w_proj, preferred_element_type=jnp.float32)
    if repeat:
        summed = lax.psum(partial_value.astype(jnp.bfloat16), "mp").astype(jnp.float32)
    else:
        summed = lax.psum(partial_value.astype(jnp.bfloat16), "mp").astype(jnp.float32)
    attn_out = (summed + b_proj.astype(jnp.float32)).reshape(slot_count, seq_len, model_dim)
    residual = tokens_f + gate_attn * attn_out
    normed_mlp = (
        modulate(residual, shift_mlp, scale_mlp).astype(jnp.bfloat16).reshape(row_count, model_dim)
    )
    hidden = jnp.dot(normed_mlp, w_up, preferred_element_type=jnp.float32) + b_up.astype(
        jnp.float32
    )
    act_bf = gelu_tanh(hidden).astype(jnp.bfloat16)
    partial_mlp = jnp.dot(act_bf, w_down, preferred_element_type=jnp.float32)
    if repeat:
        summed_mlp = lax.psum(partial_mlp.astype(jnp.bfloat16), "mp").astype(jnp.float32)
    else:
        summed_mlp = lax.psum(partial_mlp.astype(jnp.bfloat16), "mp").astype(jnp.float32)
    mlp_out = (summed_mlp + b_down.astype(jnp.float32)).reshape(slot_count, seq_len, model_dim)
    output = residual + gate_mlp * mlp_out
    return {
        "normed": normed,
        "query_rows": query_rows,
        "key_rows": key_rows,
        "value_rows": value_rows,
        "logsum": logsum,
        "mixed_b": mixed_b,
        "attn_out": attn_out,
        "residual": residual,
        "normed_mlp": normed_mlp,
        "hidden": hidden,
        "act_bf": act_bf,
        "mlp_out": mlp_out,
        "output": output,
    }


def image_pass(tokens_f, grad_out, spans, weights):
    w_qkv, b_qv, w_proj, b_proj, w_up, b_up, w_down, b_down = weights
    shift_attn, scale_attn, gate_attn, shift_mlp, scale_mlp, gate_mlp = spans
    slot_count, seq_len, model_dim = tokens_f.shape
    row_count = slot_count * seq_len
    head_cols = w_qkv.shape[2]
    head_count = head_cols // HEAD_DIM
    kept_fwd = forward(tokens_f, spans, weights, False)
    out_one = kept_fwd["output"]
    stored = forward(tokens_f, spans, weights, True)
    grad_gate_mlp = jnp.sum(grad_out * stored["mlp_out"], axis=1)
    grad_mlp = (gate_mlp * grad_out).astype(jnp.bfloat16).reshape(row_count, model_dim)
    grad_b_down = jnp.sum(grad_mlp.astype(jnp.float32), axis=0)
    grad_w_down = inner_rows(stored["act_bf"], grad_mlp)
    grad_act = outer_cols(grad_mlp, w_down)
    gelu_value, gelu_back = jax.vjp(gelu_tanh, stored["hidden"])
    grad_hidden = gelu_back(grad_act)[0].astype(jnp.bfloat16)
    grad_b_up = jnp.sum(grad_hidden.astype(jnp.float32), axis=0)
    grad_w_up = inner_rows(stored["normed_mlp"], grad_hidden)
    part_normed_mlp = outer_cols(grad_hidden, w_up)
    grad_normed_mlp = (
        lax.psum(part_normed_mlp.astype(jnp.bfloat16), "mp")
        .astype(jnp.float32)
        .reshape(slot_count, seq_len, model_dim)
    )
    norm_value, norm_back = jax.vjp(modulate, stored["residual"], shift_mlp, scale_mlp)
    grad_resid_norm, grad_shift_mlp, grad_scale_mlp = norm_back(grad_normed_mlp)
    grad_residual = grad_out + grad_resid_norm
    grad_gate_attn = jnp.sum(grad_residual * stored["attn_out"], axis=1)
    grad_attn = (gate_attn * grad_residual).astype(jnp.bfloat16).reshape(row_count, model_dim)
    grad_b_proj = jnp.sum(grad_attn.astype(jnp.float32), axis=0)
    grad_w_proj = inner_rows(stored["mixed_b"], grad_attn)
    grad_mixed = (
        outer_cols(grad_attn, w_proj)
        .astype(jnp.bfloat16)
        .reshape(slot_count, seq_len, head_count, HEAD_DIM)
    )
    grad_query, grad_key, grad_value = attention_backward(
        stored["query_rows"], stored["key_rows"], stored["value_rows"], stored["logsum"], grad_mixed
    )
    grad_qkv = jnp.stack(
        [
            grad_query.reshape(row_count, head_cols),
            grad_key.reshape(row_count, head_cols),
            grad_value.reshape(row_count, head_cols),
        ],
        axis=1,
    )
    grad_b_qv = jnp.stack(
        [
            jnp.sum(grad_qkv[:, 0].astype(jnp.float32), axis=0),
            jnp.sum(grad_qkv[:, 2].astype(jnp.float32), axis=0),
        ]
    )
    grad_w_qkv = inner_rows(stored["normed"], grad_qkv)
    part_normed = outer_cols(
        grad_qkv.reshape(row_count, 3 * head_cols), w_qkv.reshape(model_dim, 3 * head_cols)
    )
    grad_normed = (
        lax.psum(part_normed.astype(jnp.bfloat16), "mp")
        .astype(jnp.float32)
        .reshape(slot_count, seq_len, model_dim)
    )
    first_value, first_back = jax.vjp(modulate, tokens_f, shift_attn, scale_attn)
    grad_tok_norm, grad_shift_attn, grad_scale_attn = first_back(grad_normed)
    grad_tok_one = grad_residual + grad_tok_norm
    grad_mod_one = jnp.concatenate(
        [
            grad_shift_attn[:, 0],
            grad_scale_attn[:, 0],
            grad_gate_attn,
            grad_shift_mlp[:, 0],
            grad_scale_mlp[:, 0],
            grad_gate_mlp,
        ],
        axis=1,
    )
    grad_terms = (
        grad_w_qkv,
        grad_b_qv,
        grad_w_proj,
        grad_b_proj,
        grad_w_up,
        grad_b_up,
        grad_w_down,
        grad_b_down,
    )
    return (out_one, grad_tok_one, grad_mod_one, grad_terms)


def run_layer(tokens, condition, cotangent, live_count, turns, weights, w_mod, b_mod):
    slot_count, seq_len, model_dim = tokens.shape
    cond_f = condition.astype(jnp.float32)
    scaled = jax.nn.silu(cond_f).astype(jnp.bfloat16)
    own_mod = jnp.dot(scaled, w_mod, preferred_element_type=jnp.float32) + b_mod.astype(jnp.float32)
    modulation = lax.all_gather(own_mod, "mp", axis=1, tiled=True)
    tokens_f = tokens.astype(jnp.float32)
    cot_f = cotangent.astype(jnp.float32)

    def image_step(slot_idx, carry):
        out_buf, grad_buf, mod_buf, grad_sums = carry
        live_flag = (slot_idx < live_count).astype(jnp.float32)
        tok_one = lax.dynamic_slice_in_dim(tokens_f, slot_idx, 1, 0)
        cot_one = lax.dynamic_slice_in_dim(cot_f, slot_idx, 1, 0) * live_flag
        mod_row = lax.dynamic_slice_in_dim(modulation, slot_idx, 1, 0)
        spans = [
            mod_row[:, None, part_idx * model_dim : (part_idx + 1) * model_dim]
            for part_idx in range(6)
        ]
        out_one, grad_tok_one, grad_mod_one, grad_terms = image_pass(
            tok_one, cot_one, spans, weights
        )
        out_one = (out_one * live_flag).astype(jnp.bfloat16)
        out_buf = lax.dynamic_update_slice_in_dim(out_buf, out_one, slot_idx, 0)
        grad_buf = lax.dynamic_update_slice_in_dim(grad_buf, grad_tok_one, slot_idx, 0)
        mod_buf = lax.dynamic_update_slice_in_dim(mod_buf, grad_mod_one, slot_idx, 0)
        grad_sums = tuple((total_a + term_b for total_a, term_b in zip(grad_sums, grad_terms)))
        return (out_buf, grad_buf, mod_buf, grad_sums)

    start_sums = tuple((jnp.zeros(weight_in.shape, jnp.float32) for weight_in in weights))
    start_state = (
        jnp.zeros(tokens.shape, jnp.bfloat16),
        jnp.zeros(tokens.shape, jnp.float32),
        jnp.zeros((slot_count, 6 * model_dim), jnp.float32),
        start_sums,
    )
    out_buf, grad_buf, mod_buf, grad_sums = lax.fori_loop(0, turns, image_step, start_state)
    grad_modulation = mod_buf.astype(jnp.bfloat16)
    own_cols = w_mod.shape[1]
    grad_own = lax.dynamic_slice_in_dim(
        grad_modulation, lax.axis_index("mp") * own_cols, own_cols, 1
    )
    part_scaled = outer_cols(grad_own, w_mod)
    grad_scaled = lax.psum(part_scaled.astype(jnp.bfloat16), "mp").astype(jnp.float32)
    silu_value, silu_back = jax.vjp(jax.nn.silu, cond_f)
    grad_condition = silu_back(grad_scaled)[0]
    return (out_buf, grad_buf, grad_condition, grad_sums, scaled, grad_own)


def on_device(
    tokens,
    condition,
    counts,
    w_qkv,
    b_qv,
    w_proj,
    b_proj,
    w_up,
    b_up,
    w_down,
    b_down,
    w_mod,
    b_mod,
    cotangent,
):
    slot_count, seq_len, model_dim = tokens.shape
    weights = (w_qkv, b_qv, w_proj, b_proj, w_up, b_up, w_down, b_down)
    own_count = counts[0]
    output, grad_tokens, grad_condition, grad_sums, scaled, grad_own = run_layer(
        tokens, condition, cotangent, own_count, slot_count, weights, w_mod, b_mod
    )
    (
        grad_w_qkv,
        grad_b_qv,
        grad_w_proj,
        grad_b_proj,
        grad_w_up,
        grad_b_up,
        grad_w_down,
        grad_b_down,
    ) = grad_sums
    grad_w_mod = inner_rows(scaled, grad_own)
    grad_b_mod = jnp.sum(grad_own.astype(jnp.float32), axis=0)
    (
        grad_w_qkv,
        grad_b_qv,
        grad_w_proj,
        grad_b_proj,
        grad_w_up,
        grad_b_up,
        grad_w_down,
        grad_b_down,
        grad_w_mod,
        grad_b_mod,
    ) = (
        lax.psum(grad_w_qkv.astype(jnp.bfloat16), "dp").astype(jnp.float32),
        lax.psum(grad_b_qv.astype(jnp.bfloat16), "dp").astype(jnp.float32),
        lax.psum(grad_w_proj.astype(jnp.bfloat16), "dp").astype(jnp.float32),
        lax.psum(grad_b_proj.astype(jnp.bfloat16), "dp").astype(jnp.float32),
        lax.psum(grad_w_up.astype(jnp.bfloat16), "dp").astype(jnp.float32),
        lax.psum(grad_b_up.astype(jnp.bfloat16), "dp").astype(jnp.float32),
        lax.psum(grad_w_down.astype(jnp.bfloat16), "dp").astype(jnp.float32),
        lax.psum(grad_b_down.astype(jnp.bfloat16), "dp").astype(jnp.float32),
        lax.psum(grad_w_mod.astype(jnp.bfloat16), "dp").astype(jnp.float32),
        lax.psum(grad_b_mod.astype(jnp.bfloat16), "dp").astype(jnp.float32),
    )
    return (
        output,
        grad_tokens,
        grad_condition,
        grad_w_qkv,
        grad_b_qv,
        grad_w_proj,
        grad_b_proj,
        grad_w_up,
        grad_b_up,
        grad_w_down,
        grad_b_down,
        grad_w_mod,
        grad_b_mod,
    )


def solution(mesh):
    placed = (
        P("dp", None, None),
        P("dp", None),
        P("dp"),
        P(None, None, "mp"),
        P(None, "mp"),
        P("mp", None),
        P(),
        P(None, "mp"),
        P("mp"),
        P("mp", None),
        P(),
        P(None, "mp"),
        P("mp"),
        P("dp", None, None),
    )
    fast = mesh.shape["dp"] == 16 and mesh.shape["mp"] == 2
    return jax.shard_map(
        fast_device if fast else on_device,
        mesh=mesh,
        in_specs=placed,
        out_specs=(
            P("dp", None, None),
            P("dp", None, None),
            P("dp", None),
            P(None, None, "mp"),
            P(None, "mp"),
            P("mp", None),
            P(),
            P(None, "mp"),
            P("mp"),
            P("mp", None),
            P(),
            P(None, "mp"),
            P("mp"),
        ),
        check_vma=False,
    )
```

```python
import functools

import jax
import jax.numpy as jnp
from jax import lax
from jax.experimental import pallas as pl
from jax.experimental.pallas import tpu as pltpu
from jax.sharding import PartitionSpec as P

HEAD_DIM = 72


epsilon = 1e-06

f32 = jnp.float32
bf16 = jnp.bfloat16


def dot_nn(left, right):
    return lax.dot_general(left, right, (((1,), (0,)), ((), ())), preferred_element_type=f32)


def dot_nt(left, right):
    return lax.dot_general(left, right, (((1,), (1,)), ((), ())), preferred_element_type=f32)


def dot_tn(left, right):
    return lax.dot_general(left, right, (((0,), (0,)), ((), ())), preferred_element_type=f32)


def normalize(values):
    center = values - jnp.mean(values, axis=-1, keepdims=True)
    recip = lax.rsqrt(jnp.mean(center * center, axis=-1, keepdims=True) + epsilon)
    return center * recip, recip


def norm_pullback(grad_normed, unit, recip, scale_row):
    scaled_grad = grad_normed * (1.0 + scale_row)
    mean_grad = jnp.mean(scaled_grad, axis=-1, keepdims=True)
    mean_unit = jnp.mean(scaled_grad * unit, axis=-1, keepdims=True)
    return recip * (scaled_grad - mean_grad - unit * mean_unit)


def column(row):
    return jnp.broadcast_to(row[...].astype(f32), (8, row.shape[1])).T[:, 0:1]


def token_sum(values):
    return jnp.sum(values, axis=0, keepdims=True)


def attention_kernel(parts, own_images, sc, tok, cot, mod, b_proj, *refs):
    w_qkv, w_proj, bias = refs[:parts], refs[parts : 2 * parts], refs[2 * parts : 3 * parts]
    qkv, prob, mixed, attn_out, residual, normed_mlp, normed, grad_mlp, down_sums = refs[3 * parts :]
    image = sc[0] * own_images + pl.program_id(0)
    live = jnp.where(image < sc[1], 1.0, 0.0).astype(f32)
    unit, _ = normalize(tok[0].astype(f32))
    normed[0] = (unit * (1.0 + mod[0, 1:2, :]) + mod[0, 0:1, :]).astype(bf16)
    grad = (mod[0, 5:6, :] * (cot[0].astype(f32) * live)).astype(bf16)
    grad_mlp[0] = grad
    down_sums[0] = token_sum(grad.astype(f32))
    cols = w_proj[0].shape[0]
    pairs = cols // (2 * HEAD_DIM)
    span = 2 * HEAD_DIM
    factor = HEAD_DIM ** (-0.5)
    rows = normed[0]
    total = b_proj[...]
    for part in range(parts):
        base = part * 3 * cols
        shift = bias[part][...].astype(f32).T
        for proj in range(3):
            lo = proj * cols
            value = dot_nt(w_qkv[part][lo : lo + cols, :], rows)
            if proj != 1:
                value = value + shift[:, proj // 2 : proj // 2 + 1]
            qkv[0, base + lo : base + lo + cols, :] = value.astype(bf16)

        def pair_step(pair, carry, base=base, part=part):
            at = pl.multiple_of(base + pair * span, 16)
            query = qkv[0, pl.ds(at, span), :].astype(f32)
            key = qkv[0, pl.ds(at + cols, span), :].astype(f32)
            value = qkv[0, pl.ds(at + 2 * cols, span), :].astype(f32)
            outs = []
            for one in range(2):
                rows_of = slice(one * HEAD_DIM, (one + 1) * HEAD_DIM)
                scores = dot_tn(key[rows_of].astype(bf16), query[rows_of].astype(bf16)) * factor
                raised = jnp.exp(scores - jnp.max(scores, axis=0, keepdims=True))
                share = 1.0 / jnp.sum(raised, axis=0, keepdims=True)
                prob_b = (raised * share).astype(bf16)
                prob[0, part * 2 * pairs + 2 * pair + one] = prob_b
                outs.append(dot_nn(value[rows_of].astype(bf16), prob_b))
            to = pl.multiple_of(part * cols + pair * span, 16)
            mixed[0, pl.ds(to, span), :] = jnp.concatenate(outs, axis=0).astype(bf16)
            return carry

        lax.fori_loop(0, pairs, pair_step, 0, unroll=True)
        total = total + dot_tn(mixed[0, part * cols : (part + 1) * cols, :], w_proj[part][...])
    attn_out[0] = total
    summed = tok[0].astype(f32) + mod[0, 2:3, :] * total
    residual[0] = summed
    unit, _ = normalize(summed)
    normed_mlp[0] = (unit * (1.0 + mod[0, 4:5, :]) + mod[0, 3:4, :]).astype(bf16)


def mlp_kernel(per, jobs, sc, rows, grad_mlp, *refs):
    count = len(jobs)
    weights = [refs[3 * k : 3 * k + 3] for k in range(count)]
    refs = refs[3 * count :]
    came = []
    for _, summed in jobs:
        came.append(refs[0] if summed else None)
        refs = refs[1:] if summed else refs
    act, back = refs[2], refs[3]
    refs = refs[4:]
    grads = []
    for cuts, _ in jobs:
        size = 1 if cuts is None else len(cuts)
        grads.append(refs[:size])
        refs = refs[size:]
    job, step = pl.program_id(0), pl.program_id(1)
    for k in range(count):

        @pl.when(job == k)
        def _(k=k):
            mlp_block(
                per, jobs[k][0], step, sc, rows, grad_mlp, *weights[k], act, back, grads[k], refs[k], came[k]
            )


def mlp_block(per, cuts, step, sc, rows, grad_mlp, w_up, w_down, bias, act, back, grads, sums, came):
    here = w_down.shape[0] // per
    hidden = lax.dot_general(
        w_up[...], rows[...], (((0,), (1,)), ((), ())), preferred_element_type=f32
    ) + column(bias)
    square = hidden * hidden
    bend = jnp.tanh(0.7978845608028654 * hidden * (1.0 + 0.044715 * square))
    half = 0.5 * (1.0 + bend)
    act_b = (hidden * half).astype(bf16)
    slope = half + 0.5 * hidden * (1.0 - bend * bend) * (
        0.7978845608028654 * (1.0 + 3.0 * 0.044715 * square)
    )
    back_b = (dot_nt(w_down[...], grad_mlp[...]) * slope).astype(bf16)
    act[0] = act_b
    back[0] = back_b
    sums[...] = dot_nt(jnp.ones((8, rows.shape[0]), bf16), back_b)[0:1]
    for lo_row, left, right in ((0, act_b, grad_mlp), (per, back_b, rows)):
        grad = dot_nn(left, right[...])
        for piece in range(here):
            value = grad[piece * per : (piece + 1) * per]
            if cuts is None:
                if came is not None:
                    value = value + came[piece, lo_row : lo_row + per, :].astype(f32)
                grads[0][piece, lo_row : lo_row + per, :] = value.astype(bf16)
            else:
                at = jnp.bitwise_xor(step * here + piece, sc[2])
                for (lo, hi), into in zip(cuts, grads):
                    into[at, lo_row : lo_row + per, :] = value[:, lo:hi].astype(bf16)


def grow(total, part_steps, left, rights, dims):
    step = pl.program_id(0)

    def term(right):
        return lax.dot_general(left, right[...], (dims, ((), ())), preferred_element_type=f32)

    @pl.when(step == 0)
    def _():
        total[...] = term(rights[0])

    @pl.when(jnp.logical_and(step > 0, step < part_steps))
    def _():
        total[...] += term(rights[0])

    @pl.when(jnp.logical_and(step >= part_steps, step < 2 * part_steps))
    def _():
        total[...] += term(rights[1])


def norm_back_kernel(
    part_steps, own_images, sc, back, w_up0, w_up1, residual, cot, mod, attn_out,
    grad_residual, grad_attn, sums, total
):
    grow(total, part_steps, back[0], (w_up0, w_up1), ((0,), (1,)))
    one = pl.program_id(0) - 2 * part_steps
    seq = residual.shape[1]

    @pl.when(one >= 0)
    def _():
        live = jnp.where(sc[0] * own_images + one < sc[1], 1.0, 0.0).astype(f32)
        grad_normed = total[pl.ds(pl.multiple_of(one * seq, seq), seq), :]
        unit, recip = normalize(residual[0])
        sums[0, 0:1, :] = token_sum(grad_normed)
        sums[0, 1:2, :] = token_sum(grad_normed * unit)
        grad_res = cot[0].astype(f32) * live + norm_pullback(grad_normed, unit, recip, mod[0, 4:5, :])
        grad_residual[0] = grad_res
        sums[0, 2:3, :] = token_sum(grad_res * attn_out[0])
        grad_att = (mod[0, 2:3, :] * grad_res).astype(bf16)
        grad_attn[0] = grad_att
        sums[0, 3:4, :] = token_sum(grad_att.astype(f32))


def back_kernel(parts, sc, grad_attn, qkv, prob, *refs):
    w_proj = refs[:parts]
    grad_qkv, grad_mixed = refs[parts:]
    cols = w_proj[0].shape[0]
    pairs = cols // (2 * HEAD_DIM)
    span = 2 * HEAD_DIM
    factor = HEAD_DIM ** (-0.5)
    grad_att = grad_attn[0]
    for part in range(parts):
        base = part * 3 * cols
        grad_mixed[part * cols : (part + 1) * cols, :] = dot_nt(w_proj[part][...], grad_att).astype(bf16)

        def pair_step(pair, carry, base=base, part=part):
            at = pl.multiple_of(base + pair * span, 16)
            query = qkv[0, pl.ds(at, span), :].astype(f32)
            key = qkv[0, pl.ds(at + cols, span), :].astype(f32)
            value = qkv[0, pl.ds(at + 2 * cols, span), :].astype(f32)
            grads = grad_mixed[pl.ds(pl.multiple_of(part * cols + pair * span, 16), span), :].astype(f32)
            to_query, to_key, to_value = [], [], []
            for one in range(2):
                rows_of = slice(one * HEAD_DIM, (one + 1) * HEAD_DIM)
                prob_b = prob[0, part * 2 * pairs + 2 * pair + one]
                prob_f = prob_b.astype(f32)
                grad_b = grads[rows_of].astype(bf16)
                grad_prob = dot_tn(value[rows_of].astype(bf16), grad_b)
                delta = jnp.sum(prob_f * grad_prob, axis=0, keepdims=True)
                grad_scores = (prob_f * (grad_prob - delta)).astype(bf16)
                to_query.append(dot_nn(key[rows_of].astype(bf16), grad_scores) * factor)
                to_key.append(dot_nt(query[rows_of].astype(bf16), grad_scores) * factor)
                to_value.append(dot_nt(grad_b, prob_b))
            grad_qkv[0, pl.ds(at, span), :] = jnp.concatenate(to_query, axis=0).astype(bf16)
            grad_qkv[0, pl.ds(at + cols, span), :] = jnp.concatenate(to_key, axis=0).astype(bf16)
            grad_qkv[0, pl.ds(at + 2 * cols, span), :] = jnp.concatenate(to_value, axis=0).astype(bf16)
            return carry

        lax.fori_loop(0, pairs, pair_step, 0, unroll=True)


def attn_grad_kernel(pieces, per, cuts, sc, *refs):
    grad_qkv, mixed, normed, grad_attn = refs[:pieces], refs[pieces], refs[pieces + 1], refs[pieces + 2]
    grads, sums = refs[pieces + 3 : -1], refs[-1]
    step = pl.program_id(0)
    here = mixed.shape[1] // per
    images = mixed.shape[0]
    each = images // pieces

    def spread(total):
        total = total.astype(bf16)
        for piece in range(here):
            at = jnp.bitwise_xor(step * here + piece, sc[2])
            for (lo, hi), into in zip(cuts, grads):
                into[at] = total[piece * per : (piece + 1) * per, lo:hi]

    @pl.when(step < 3)
    def _():
        ones = jnp.ones((8, mixed.shape[2]), bf16)
        total = count = None
        for image in range(images):
            left = grad_qkv[image // each][image % each]
            term, one = dot_nn(left, normed[image]), dot_nt(ones, left)
            total = term if image == 0 else total + term
            count = one if image == 0 else count + one
        sums[0] = count[0:1]
        spread(total)

    @pl.when(step == 3)
    def _():
        total = dot_nn(mixed[0], grad_attn[0])
        for image in range(1, images):
            total = total + dot_nn(mixed[image], grad_attn[image])
        spread(total)


def first_back_kernel(pieces, images, sc, *refs):
    grad_qkv = refs[:pieces]
    w_qkv0, w_qkv1, tok, mod, grad_residual = refs[pieces : pieces + 5]
    grad_tokens, grad_own, sums, total = refs[pieces + 5 :]
    step = pl.program_id(0)
    each = images // pieces
    seq = tok.shape[1]

    def add(w_qkv, fresh):
        for one in range(images):
            term = dot_tn(grad_qkv[one // each][one % each], w_qkv[...])
            if fresh:
                total[one * seq : (one + 1) * seq, :] = term
            else:
                total[one * seq : (one + 1) * seq, :] += term

    @pl.when(step == 0)
    def _():
        add(w_qkv0, True)

    @pl.when(jnp.logical_and(step > 0, step < 3))
    def _():
        add(w_qkv0, False)

    @pl.when(jnp.logical_and(step >= 3, step < 6))
    def _():
        add(w_qkv1, False)

    @pl.when(step >= 6)
    def _():
        grad_normed = total[pl.ds(pl.multiple_of((step - 6) * seq, seq), seq), :]
        unit, recip = normalize(tok[0].astype(f32))
        sums[0, 0:1, :] = token_sum(grad_normed)
        sums[0, 1:2, :] = token_sum(grad_normed * unit)
        grad = grad_residual[0] + norm_pullback(grad_normed, unit, recip, mod[0, 1:2, :])
        grad_tokens[0] = grad
        grad_own[0] = grad


def output_kernel(
    part_steps, own_images, sc, act, w_down0, w_down1, residual, cot, mod, b_down, output, own, sums, total
):
    grow(total, part_steps, act[0], (w_down0, w_down1), ((0,), (0,)))
    one = pl.program_id(0) - 2 * part_steps
    seq = residual.shape[1]

    @pl.when(one >= 0)
    def _():
        live = jnp.where(sc[0] * own_images + one < sc[1], 1.0, 0.0).astype(f32)
        mlp_out = total[pl.ds(pl.multiple_of(one * seq, seq), seq), :] + b_down[...]
        sums[0] = token_sum((cot[0].astype(f32) * live) * mlp_out)
        rows = ((residual[0] + mod[0, 5:6, :] * mlp_out) * live).astype(bf16)
        output[0] = rows
        own[0] = rows


def final_piece(sc, halves, piece, store):
    rel = jnp.bitwise_xor(piece, sc[2])
    for low, high, route, lo, hi in halves:
        bits = [(rel >> bit) & 1 for bit in route]
        index = bits[1] * 4 + bits[2] * 2 + bits[3]

        @pl.when(bits[0] == 0)
        def _(low=low, index=index, lo=lo, hi=hi):
            store(low[index].astype(f32), lo, hi)

        @pl.when(bits[0] == 1)
        def _(high=high, index=index, lo=lo, hi=hi):
            store(high[index].astype(f32), lo, hi)


def final_mlp_kernel(cuts, per, sc, *refs):
    count = 2 * len(cuts)
    arrays, (_, _, down, up, mark, turned) = refs[:count], refs[count:]
    here = down.shape[0] // per
    halves = [(arrays[2 * k], arrays[2 * k + 1]) + cut for k, cut in enumerate(cuts)]
    for piece in range(here):

        def store(value, lo, hi, piece=piece):
            down[piece * per : (piece + 1) * per, lo:hi] = value[0:per]
            turned[piece * per : (piece + 1) * per, lo:hi] = value[per : 2 * per]

        final_piece(sc, halves, pl.program_id(0) * here + piece, store)
    up[...] = turned[...].T
    mark[...] = jnp.zeros_like(mark)


def final_plain_kernel(per, sc, summed, down_in, up_in, down, up, mark, turned):
    for piece in range(summed.shape[0]):
        lo = piece * per
        down[lo : lo + per, :] = summed[piece, 0:per, :].astype(f32)
        turned[lo : lo + per, :] = summed[piece, per : 2 * per, :].astype(f32)
    up[...] = turned[...].T
    mark[...] = jnp.zeros_like(mark)


def final_attn_kernel(cuts, per, sc, *refs):
    count = 2 * len(cuts)
    arrays, (qkv, proj) = refs[:count], refs[count:]
    here = proj.shape[0] // per
    halves = [(arrays[2 * k], arrays[2 * k + 1]) + cut for k, cut in enumerate(cuts)]
    for target, wanted in ((qkv, True), (proj, False)):

        @pl.when((pl.program_id(0) < 3) == wanted)
        def _(target=target):
            for piece in range(here):

                def store(value, lo, hi, piece=piece):
                    target[piece * per : (piece + 1) * per, lo:hi] = value

                final_piece(sc, halves, pl.program_id(0) * here + piece, store)


def run_kernel(
    body, sc, args, in_specs, out_specs, out_shape, grid, micros, scratch=(), alias=None, room=60
):
    size = sum(a.size * a.dtype.itemsize for a in args) + sum(
        s.size * s.dtype.itemsize for s in out_shape
    )
    return pl.pallas_call(
        body,
        out_shape=out_shape,
        grid_spec=pltpu.PrefetchScalarGridSpec(
            num_scalar_prefetch=1,
            grid=grid,
            in_specs=in_specs,
            out_specs=out_specs,
            scratch_shapes=list(scratch),
        ),
        compiler_params=pltpu.CompilerParams(vmem_limit_bytes=room << 20),
        cost_estimate=pl.CostEstimate(
            flops=int(micros * 1.15e9), bytes_accessed=int(min(size, micros * 1e6)), transcendentals=0
        ),
        input_output_aliases=alias or {},
    )(sc, *args)


def whole_block(array):
    zeros = (0,) * array.ndim
    return pl.BlockSpec(array.shape, lambda *_: zeros, pipeline_mode=pl.Buffered(1))


def shape_of(dims, kind):
    return jax.ShapeDtypeStruct(dims, kind)


SWAP = [(0, 1), (1, 0)]


def swap_cores(value):
    return lax.ppermute(value, "mp", SWAP)


def bit_pairs(bit):
    return [(index, index ^ (1 << bit)) for index in range(16)]


MLP_WAYS = ((0, 640, (0, 1, 2, 3)), (640, 1152, (1, 0, 2, 3)))
ATTN_WAYS = ((0, 512, (0, 1, 2, 3)), (512, 896, (1, 0, 2, 3)), (896, 1152, (2, 3, 0, 1)))


def columns(ways):
    return tuple((lo, hi) for lo, hi, _ in ways)


def cut(array, bits, bit, side):
    return lax.index_in_dim(array, side, bits.index(bit), keepdims=False)


def left_bits(done):
    return [bit for bit in (3, 2, 1, 0) if bit not in done]


def exchange(values, bits):
    return [lax.ppermute(value, "dp", bit_pairs(bit)) for value, bit in zip(values, bits)]


def reduce_flow(ways, get_own, others):
    others = yield others
    came = [swap_cores(other) for other in others]
    yield None
    own, came = yield [get_own(), came]
    firsts, seconds = ([a.reshape((2, 2, 2, 2) + a.shape[1:]) for a in arrays] for arrays in (own, came))
    routes = [way for _, _, way in ways]
    for stage in range(4):
        sends, keeps = [], []
        for route, one, two in zip(routes, firsts, seconds):
            bits = left_bits(route[:stage])
            for side, into in ((1, sends), (0, keeps)):
                into.append(cut(one, bits, route[stage], side) + cut(two, bits, route[stage], side))
        if stage == 2 and routes[0][2:] == routes[1][2:]:
            sends = [jnp.concatenate(sends[:2], axis=-1)] + sends[2:]
            keeps = [jnp.concatenate(keeps[:2], axis=-1)] + keeps[2:]
            routes = [routes[0]] + routes[2:]
        sends, keeps = yield [sends, keeps]
        comes = exchange(sends, [route[stage] for route in routes])
        yield None
        firsts, seconds = yield [keeps, comes]
    return [one + two for one, two in zip(firsts, seconds)]


def gather_flow(ways, have):
    routes = [ways[0][2]] + [way for _, _, way in ways[2:]]
    middle = ways[0][1]
    (have,) = yield [have]
    comes = exchange(have, [route[3] for route in routes])
    have = [one[None] for one in have]
    comes = [one[None] for one in comes]
    yield None
    for stage in (2, 1, 0):
        have, comes = yield [have, comes]
        joined = [jnp.concatenate([one, two]) for one, two in zip(have, comes)]
        if stage == 1:
            joined = [joined[0][..., :middle], joined[0][..., middle:]] + joined[1:]
            routes = [way for _, _, way in ways]
        (have,) = yield [joined]
        comes = exchange(have, [route[stage] for route in routes])
        yield None
    have, comes = yield [have, comes]
    return [part for pair in zip(have, comes) for part in pair]


def sum_flow(ways, get_own, others):
    have = yield from reduce_flow(ways, get_own, others)
    return (yield from gather_flow(ways, have))


def swap_flow(other):
    (other,) = yield [other]
    came = swap_cores(other)
    yield None
    (came,) = yield [came]
    return came


def rows_flow(rows):
    for bit in (3, 2, 1, 0):
        (rows,) = yield [rows]
        came = lax.ppermute(rows, "dp", bit_pairs(bit))
        yield None
        rows, came = yield [rows, came]
        rows = jnp.concatenate([rows, came])
    return rows


class Order:
    def __init__(self, sc):
        self.sc = sc
        self.results = {}

    def fence(self, values):
        self.sc, values = lax.optimization_barrier((self.sc, values))
        return values

    def after(self, value):
        self.sc, _ = lax.optimization_barrier((self.sc, value))

    def tick(self, *flows):
        replies = {flow: None for flow in flows if flow not in self.results}
        while replies:
            wants = {}
            for flow, reply in replies.items():
                try:
                    want = flow.send(reply)
                except StopIteration as stop:
                    self.results[flow] = stop.value
                    continue
                if want is not None:
                    wants[flow] = want
            replies = dict(zip(wants, self.fence(list(wants.values())))) if wants else {}

    def finish(self, flow):
        while flow not in self.results:
            self.tick(flow)
        return self.results[flow]


CHUNKS = 3
PLAIN = 2


def fill_other(both, came, core):
    size = came.shape[0]
    return lax.dynamic_update_slice_in_dim(both, came, (1 - core) * size, 0)


def fast_device(
    tokens, condition, counts, w_qkv, b_qv, w_proj, b_proj, w_up, b_up, w_down, b_down, w_mod, b_mod,
    cotangent,
):
    slots, seq, dim = tokens.shape
    images = slots // 2
    count = images * seq
    cols = w_qkv.shape[2]
    ff = w_up.shape[1]
    own_cols = w_mod.shape[1]
    heads = cols // HEAD_DIM
    core = lax.axis_index("mp")
    order = Order(jnp.stack([core, counts[0], lax.axis_index("dp")]).astype(jnp.int32))

    qkv_rows = jnp.transpose(w_qkv, (1, 2, 0)).reshape(3 * cols, dim)
    wq = [qkv_rows, swap_cores(qkv_rows)]
    wp = [w_proj, swap_cores(w_proj)]
    qkv_bias = [b_qv, swap_cores(b_qv)]

    cond_f = condition.astype(f32)
    scaled = jax.nn.silu(cond_f).astype(bf16)
    own_mod = jnp.dot(scaled, w_mod, preferred_element_type=f32) + b_mod.astype(f32)
    other_mod = swap_cores(own_mod)
    sides = [jnp.where(core == side, own_mod, other_mod) for side in range(2)]
    modulation = jnp.concatenate(sides, axis=1).reshape(slots, 6, dim)
    proj_bias = b_proj.astype(f32)[None]
    down_bias = b_down.astype(f32)[None]

    late_up, late_down, late_bias = lax.optimization_barrier((wq[1], w_up, w_down, b_up, modulation))[1:4]
    wu = [w_up, swap_cores(late_up)]
    wd = [w_down, swap_cores(late_down)]
    up_bias = [b_up[None], swap_cores(late_bias[None])]

    local = lambda i, s: (s[0] * images + i, 0, 0)
    mine = lambda i, s: (i, 0, 0)
    tok_spec = pl.BlockSpec((1, seq, dim), local)
    own_spec = pl.BlockSpec((1, seq, dim), mine)
    mod_spec = pl.BlockSpec((1, 6, dim), local)
    row_spec = pl.BlockSpec((1, 1, dim), mine)
    qkv_spec = pl.BlockSpec((1, 6 * cols, seq), mine)
    prob_spec = pl.BlockSpec((1, 2 * heads, seq, seq), lambda i, s: (i, 0, 0, 0))
    mixed_spec = pl.BlockSpec((1, 2 * cols, seq), mine)
    token_f = shape_of((images, seq, dim), f32)
    token_b = shape_of((images, seq, dim), bf16)
    attn_args = wq + wp + qkv_bias
    qkv, prob, mixed, attn_out, residual, normed_mlp, normed, grad_mlp, down_sums = run_kernel(
        functools.partial(attention_kernel, 2, images),
        order.sc,
        [tokens, cotangent, modulation, proj_bias] + attn_args,
        [tok_spec, tok_spec, mod_spec, whole_block(proj_bias)] + [whole_block(a) for a in attn_args],
        [qkv_spec, prob_spec, mixed_spec] + [own_spec] * 5 + [row_spec],
        [
            shape_of((images, 6 * cols, seq), bf16),
            shape_of((images, 2 * heads, seq, seq), bf16),
            shape_of((images, 2 * cols, seq), bf16),
            token_f,
            token_f,
            token_b,
            token_b,
            token_b,
            shape_of((images, 1, dim), f32),
        ],
        (images,),
        45,
    )
    order.after(down_sums)

    rows_flat = normed_mlp.reshape(count, dim)
    grad_flat = grad_mlp.reshape(count, dim)
    width = ff // CHUNKS
    per = width // 16
    steps = 2
    block = width // steps
    anywhere = pl.BlockSpec(memory_space=pl.ANY)
    act = back = jnp.zeros((8, 128), bf16)
    up_sums = {}

    def mlp_call(jobs, came, micros):
        nonlocal act, back
        first = act.shape[0] == 8
        kinds = tuple((None if job[0] < PLAIN else columns(MLP_WAYS), job in came) for job in jobs)

        def turn(k):
            return lambda p, s, c: jnp.clip((p - k) * steps + s, 0, steps - 1)

        def pick(values):
            return lambda p: sum(jnp.where(p == k, value, 0) for k, value in enumerate(values))

        parts = pick([part for _, part in jobs])
        starts = pick([chunk * steps for chunk, _ in jobs])
        spread = pl.BlockSpec((1, block, count), lambda p, s, c: (parts(p), starts(p) + s, 0))
        args, specs = [], []
        for k, (chunk, part) in enumerate(jobs):
            at = chunk * steps
            wide = lambda p, s, c, k=k, at=at: (0, at + turn(k)(p, s, c))
            tall = lambda p, s, c, k=k, at=at: (at + turn(k)(p, s, c), 0)
            args += [wu[part], wd[part], up_bias[part]]
            specs += [
                pl.BlockSpec((dim, block), wide),
                pl.BlockSpec((block, dim), tall),
                pl.BlockSpec((1, block), wide),
            ]
        grad_specs, grad_shapes, sizes = [], [], []
        for k, (split, _) in enumerate(kinds):
            own = lambda p, s, c, k=k: (turn(k)(p, s, c), 0, 0)
            fixed = lambda p, s, c: (0, 0, 0)
            wides = [dim] if split is None else [hi - lo for lo, hi in split]
            lead = (16 // steps, own) if split is None else (16, fixed)
            grad_specs.append([pl.BlockSpec((lead[0], 2 * per, wide), lead[1]) for wide in wides])
            grad_shapes += [shape_of((16, 2 * per, wide), bf16) for wide in wides]
            sizes.append(len(wides))
        for k, job in enumerate(jobs):
            if job in came:
                args.append(came[job])
                specs += grad_specs[k]
        args += [act, back]
        spot = len(args) + 1
        outs = run_kernel(
            functools.partial(mlp_kernel, per, kinds),
            order.sc,
            [rows_flat, grad_flat] + args,
            [whole_block(rows_flat), whole_block(grad_flat)] + specs + [anywhere, anywhere],
            [spread, spread]
            + [spec for specs in grad_specs for spec in specs]
            + [pl.BlockSpec((1, block), lambda p, s, c, k=k: (0, turn(k)(p, s, c))) for k in range(len(jobs))],
            [shape_of((2, ff, count), bf16)] * 2 + grad_shapes + [shape_of((1, width), f32)] * len(jobs),
            (len(jobs), steps),
            micros,
            alias=None if first else {spot: 0, spot + 1: 1},
        )
        act, back = outs[:2]
        grads, outs = list(outs[2 : 2 + sum(sizes)]), outs[2 + sum(sizes) :]
        up_sums.update(zip(jobs, outs))
        order.after(outs[-1])
        return [[grads.pop(0) for _ in range(size)] for size in sizes]

    summed = range(PLAIN)
    swaps = [swap_flow(grad) for (grad,) in mlp_call([(chunk, 1) for chunk in summed], {}, 26)]
    order.tick(*swaps)
    rest = [(chunk, part) for chunk in range(PLAIN, CHUNKS) for part in (1, 0)]
    grads = mlp_call(rest, {}, 26)
    flows = [
        sum_flow(MLP_WAYS, lambda own=own: own, others) for others, own in zip(grads[0::2], grads[1::2])
    ]
    order.tick(*swaps, *flows)
    came = {(chunk, 0): order.results[swap] for chunk, swap in zip(summed, swaps)}
    grads = mlp_call([(chunk, 0) for chunk in summed], came, 26)
    plain_sums = lax.psum([grad for (grad,) in grads], "dp")
    order.tick(*flows)

    reach = 768
    turns = ff // reach
    every = lambda s, c: (0, 0, 0)
    tail = lambda first: lambda s, c: (jnp.maximum(s - first, 0), 0, 0)
    tail_local = lambda first: lambda s, c: (c[0] * images + jnp.maximum(s - first, 0), 0, 0)

    def image_spec(first, where=tail):
        return pl.BlockSpec((1, seq, dim), where(first))

    def rows_of(part, size):
        if part == 0:
            return lambda s, c: jnp.minimum(s, size - 1)
        return lambda s, c: jnp.clip(s - size, 0, size - 1)

    span_spec = pl.BlockSpec(
        (1, reach, count),
        lambda s, c: (jnp.minimum(s // turns, 1), jnp.where(s < 2 * turns, s % turns, turns - 1), 0),
    )
    grad_residual, grad_attn, mid_sums = run_kernel(
        functools.partial(norm_back_kernel, turns, images),
        order.sc,
        [back] + wu + [residual, cotangent, modulation, attn_out],
        [
            span_spec,
            pl.BlockSpec((dim, reach), lambda s, c: (0, rows_of(0, turns)(s, c))),
            pl.BlockSpec((dim, reach), lambda s, c: (0, rows_of(1, turns)(s, c))),
            image_spec(2 * turns),
            image_spec(2 * turns, tail_local),
            pl.BlockSpec((1, 6, dim), tail_local(2 * turns)),
            image_spec(2 * turns),
        ],
        [image_spec(2 * turns)] * 2 + [pl.BlockSpec((1, 4, dim), tail(2 * turns))],
        [token_f, token_b, shape_of((images, 4, dim), f32)],
        (2 * turns + images,),
        60,
        scratch=[pltpu.VMEM((count, dim), f32)],
    )
    order.after(mid_sums)
    order.tick(*flows)
    pieces = 2
    each = images // pieces
    grad_qkv = []
    for piece in range(pieces):
        there = lambda i, s, piece=piece: (piece * each + i, 0, 0)
        (grad_piece,) = run_kernel(
            functools.partial(back_kernel, 2),
            order.sc,
            [grad_attn, qkv, prob] + wp,
            [
                pl.BlockSpec((1, seq, dim), there),
                pl.BlockSpec((1, 6 * cols, seq), there),
                pl.BlockSpec((1, 2 * heads, seq, seq), lambda i, s, piece=piece: (piece * each + i, 0, 0, 0)),
            ]
            + [whole_block(a) for a in wp],
            [qkv_spec],
            [shape_of((each, 6 * cols, seq), bf16)],
            (each,),
            60,
            scratch=[pltpu.VMEM((2 * cols, seq), bf16)],
            )
        grad_qkv.append(grad_piece)
        order.after(grad_piece)
        order.tick(*flows)

    attn_per = 4 * cols // 16
    qv_sums = [None, None]

    def attn_part(part):
        *grads, sums = run_kernel(
            functools.partial(attn_grad_kernel, pieces, attn_per, columns(ATTN_WAYS)),
            order.sc,
            grad_qkv + [mixed, normed, grad_attn],
            [
                pl.BlockSpec((each, cols, seq), lambda s, c: (0, 3 * part + jnp.minimum(s, 2), 0))
                for _ in range(pieces)
            ]
            + [pl.BlockSpec((images, cols, seq), lambda s, c: (0, part, 0))]
            + [whole_block(normed), whole_block(grad_attn)],
            [pl.BlockSpec((16, attn_per, hi - lo), every) for lo, hi in columns(ATTN_WAYS)]
            + [pl.BlockSpec((1, 1, cols), lambda s, c: (jnp.minimum(s, 2), 0, 0))],
            [shape_of((16, attn_per, hi - lo), bf16) for lo, hi in columns(ATTN_WAYS)]
            + [shape_of((3, 1, cols), f32)],
            (4,),
            60,
            )
        qv_sums[part] = sums
        order.after(sums)
        return grads

    grad_other = attn_part(1)
    made = []
    last = sum_flow(ATTN_WAYS, lambda: made[0], grad_other)
    order.tick(last, *flows)
    made.append(attn_part(0))
    order.tick(last, *flows)

    first_spec = lambda part: pl.BlockSpec((cols, dim), lambda s, c: (rows_of(part, 3)(s, c), 0))
    grad_tokens, grad_own_tokens, low_sums = run_kernel(
        functools.partial(first_back_kernel, pieces, images),
        order.sc,
        grad_qkv + wq + [tokens, modulation, grad_residual],
        [pl.BlockSpec((each, cols, seq), lambda s, c: (0, jnp.minimum(s, 5), 0)) for _ in range(pieces)]
        + [first_spec(0), first_spec(1)]
        + [image_spec(6, tail_local), pl.BlockSpec((1, 6, dim), tail_local(6)), image_spec(6)],
        [image_spec(6, tail_local), image_spec(6), pl.BlockSpec((1, 2, dim), tail(6))],
        [shape_of((slots, seq, dim), f32), token_f, shape_of((images, 2, dim), f32)],
        (6 + images,),
        60,
        scratch=[pltpu.VMEM((count, dim), f32)],
    )
    order.after(low_sums)
    order.tick(last, *flows)
    down_spec = lambda part: pl.BlockSpec((reach, dim), lambda s, c: (rows_of(part, turns)(s, c), 0))
    output, own_output, gate_sums = run_kernel(
        functools.partial(output_kernel, turns, images),
        order.sc,
        [act] + wd + [residual, cotangent, modulation, down_bias],
        [
            span_spec,
            down_spec(0),
            down_spec(1),
            image_spec(2 * turns),
            image_spec(2 * turns, tail_local),
            pl.BlockSpec((1, 6, dim), tail_local(2 * turns)),
            whole_block(down_bias),
        ],
        [image_spec(2 * turns, tail_local), image_spec(2 * turns), pl.BlockSpec((1, 1, dim), tail(2 * turns))],
        [shape_of((slots, seq, dim), bf16), token_b, shape_of((images, 1, dim), f32)],
        (2 * turns + images,),
        60,
        scratch=[pltpu.VMEM((count, dim), f32)],
    )
    order.after(gate_sums)
    order.tick(last, *flows)

    low_sums, mid_sums, gate_sums, down_sums, qv_sums, up_sums, scaled_rows = order.fence(
        (low_sums, mid_sums, gate_sums, down_sums, qv_sums, up_sums, scaled)
    )
    grad_modulation = jnp.concatenate([low_sums, mid_sums[:, 2:3], mid_sums[:, 0:2], gate_sums], axis=1)
    grad_modulation = grad_modulation.reshape(images, 6 * dim).astype(bf16)
    bias_sums = [
        jnp.concatenate(
            [qv_sums[part][0], qv_sums[part][2]]
            + [up_sums[chunk, part] for chunk in range(CHUNKS)],
            axis=1,
        )
        for part in range(2)
    ]
    shared = jnp.concatenate(
        [
            jnp.sum(mid_sums[:, 3], axis=0, keepdims=True),
            jnp.sum(down_sums[:, 0], axis=0, keepdims=True),
            jnp.zeros((1, own_cols - 2 * dim), f32),
        ],
        axis=1,
    )
    halves = grad_modulation.reshape(images, 2, own_cols)
    kept = lax.dynamic_index_in_dim(halves, core, 1, keepdims=False)
    given = lax.dynamic_index_in_dim(halves, 1 - core, 1, keepdims=False)
    got = swap_cores(jnp.concatenate([given.astype(f32), bias_sums[1], shared]))
    came = got[:images].astype(bf16)
    group_mod = jnp.where(core == 0, jnp.concatenate([kept, came]), jnp.concatenate([came, kept]))
    own_bias_sum = bias_sums[0] + got[images : images + 1]
    shared_sum = shared + got[images + 1 :]
    wide_scaled = jnp.pad(scaled_rows.reshape(-1), (0, 3 * own_cols - slots * dim)).reshape(3, own_cols)
    packed_rows = jnp.concatenate(
        [group_mod, own_bias_sum.astype(bf16), shared_sum.astype(bf16), wide_scaled]
    )
    (packed_rows,) = order.fence([packed_rows])
    small = rows_flow(packed_rows)
    order.tick(last, small)
    (group_mod,) = order.fence([group_mod])
    part_scaled = outer_cols(group_mod, w_mod).astype(bf16)
    order.after(part_scaled[0, :1])
    order.tick(last, small, *flows)
    own_output, part_scaled = order.fence((own_output, part_scaled))
    other_output, came_scaled = swap_cores(own_output), swap_cores(part_scaled)

    def cuts(ways):
        return tuple((way, lo, hi) for lo, hi, way in ways)

    grad_w_down = grad_w_up = jnp.zeros((8, 128), f32)

    def final_mlp(chunk, body, args):
        nonlocal grad_w_down, grad_w_up
        first = grad_w_down.shape[0] == 8
        spot = len(args) + 1
        grad_w_down, grad_w_up, mark = run_kernel(
            body,
            order.sc,
            list(args) + [grad_w_down, grad_w_up],
            [
                whole_block(a)
                if a.shape[0] == 8
                else pl.BlockSpec((16 // steps,) + a.shape[1:], lambda s, c: (s, 0, 0))
                for a in args
            ]
            + [anywhere, anywhere],
            [
                pl.BlockSpec((block, dim), lambda s, c: (chunk * steps + s, 0)),
                pl.BlockSpec((dim, block), lambda s, c: (0, chunk * steps + s)),
                pl.BlockSpec((8, 128), lambda s, c: (0, 0)),
            ],
            [shape_of((ff, dim), f32), shape_of((dim, ff), f32), shape_of((8, 128), f32)],
            (steps,),
            4,
            scratch=[pltpu.VMEM((block, dim), f32)],
            alias=None if first else {spot: 0, spot + 1: 1},
        )
        order.after(mark)

    for chunk, flow in enumerate(flows):
        body = functools.partial(final_mlp_kernel, cuts(MLP_WAYS), per)
        final_mlp(PLAIN + chunk, body, order.finish(flow))
    order.tick(last, small)
    other_output, came_scaled, grad_own_tokens = order.fence((other_output, came_scaled, grad_own_tokens))
    other_tokens = swap_cores(grad_own_tokens)
    for chunk, total in zip(summed, order.fence(plain_sums)):
        final_mlp(chunk, functools.partial(final_plain_kernel, per), [total])
    order.tick(last, small)
    output = fill_other(output, other_output, core)
    grad_scaled = part_scaled.astype(f32) + came_scaled.astype(f32)
    _, silu_back = jax.vjp(jax.nn.silu, cond_f)
    grad_condition = silu_back(grad_scaled)[0]
    order.after((output[0, 0, :1], grad_condition[0, :1]))
    order.tick(last)
    grad_tokens = fill_other(grad_tokens, order.fence(other_tokens), core)
    order.after(grad_tokens[0, 0, :1])
    all_rows = order.fence(order.finish(small)).reshape(16, slots + 5, own_cols)
    all_mod = all_rows[:, :slots].reshape(-1, own_cols)
    all_scaled = all_rows[:, slots + 2 :].reshape(16, -1)[:, : slots * dim].reshape(-1, dim)
    grad_w_mod = inner_rows(all_scaled, all_mod)
    grad_b_mod = jnp.sum(all_mod.astype(f32), axis=0)
    bias_total = jnp.sum(all_rows[:, slots : slots + 2].astype(f32), axis=0)
    grad_b_qv = bias_total[0, : 2 * cols].reshape(2, cols)
    grad_b_up = bias_total[0, 2 * cols :]
    grad_b_proj = bias_total[1, :dim]
    grad_b_down = bias_total[1, dim : 2 * dim]
    order.after((grad_w_mod[0, :1], grad_b_mod[:1], bias_total[0, :1]))
    args = order.finish(last)
    grad_qkv_rows, grad_w_proj = run_kernel(
        functools.partial(final_attn_kernel, cuts(ATTN_WAYS), attn_per),
        order.sc,
        list(args),
        [whole_block(a) for a in args],
        [
            pl.BlockSpec((cols, dim), lambda s, c: (jnp.minimum(s, 2), 0)),
            pl.BlockSpec((cols, dim), lambda s, c: (0, 0)),
        ],
        [shape_of((3 * cols, dim), f32), shape_of((cols, dim), f32)],
        (4,),
        9,
    )
    grad_w_qkv = jnp.transpose(grad_qkv_rows.reshape(3, cols, dim), (2, 0, 1))
    return (
        output,
        grad_tokens,
        grad_condition,
        grad_w_qkv,
        grad_b_qv,
        grad_w_proj,
        grad_b_proj,
        grad_w_up,
        grad_b_up,
        grad_w_down,
        grad_b_down,
        grad_w_mod,
        grad_b_mod,
    )


def layer_norm(values):
    center = values - jnp.mean(values, axis=-1, keepdims=True)
    return center * lax.rsqrt(jnp.mean(center * center, axis=-1, keepdims=True) + epsilon)


def modulate(values, shift_part, scale_part):
    return layer_norm(values) * (1.0 + scale_part) + shift_part


def gelu_tanh(values):
    return (
        0.5
        * values
        * (1.0 + jnp.tanh(0.7978845608028654 * (values + 0.044715 * values * values * values)))
    )


def inner_rows(left, right):
    return lax.dot_general(
        left, right, (((0,), (0,)), ((), ())), preferred_element_type=jnp.float32
    )


def outer_cols(left, right):
    return lax.dot_general(
        left, right, (((1,), (1,)), ((), ())), preferred_element_type=jnp.float32
    )


def attention_forward(query_rows, key_rows, value_rows):
    factor = HEAD_DIM ** (-0.5)
    scores = (
        jnp.einsum("bqhd,bkhd->bhqk", query_rows, key_rows, preferred_element_type=jnp.float32)
        * factor
    )
    row_max = jnp.max(scores, axis=-1, keepdims=True)
    row_total = jnp.sum(jnp.exp(scores - row_max), axis=-1, keepdims=True)
    logsum = row_max + jnp.log(row_total)
    prob_b = jnp.exp(scores - logsum).astype(jnp.bfloat16)
    mixed_out = jnp.einsum(
        "bhqk,bkhd->bqhd", prob_b, value_rows, preferred_element_type=jnp.float32
    )
    return (mixed_out, logsum)


def attention_backward(query_rows, key_rows, value_rows, logsum, grad_mixed):
    factor = HEAD_DIM ** (-0.5)
    scores = (
        jnp.einsum("bqhd,bkhd->bhqk", query_rows, key_rows, preferred_element_type=jnp.float32)
        * factor
    )
    prob_f = jnp.exp(scores - logsum)
    prob_b = prob_f.astype(jnp.bfloat16)
    grad_prob = jnp.einsum(
        "bqhd,bkhd->bhqk", grad_mixed, value_rows, preferred_element_type=jnp.float32
    )
    row_delta = jnp.sum(prob_f * grad_prob, axis=-1, keepdims=True)
    grad_scores = (prob_f * (grad_prob - row_delta)).astype(jnp.bfloat16)
    grad_query = (
        jnp.einsum("bhqk,bkhd->bqhd", grad_scores, key_rows, preferred_element_type=jnp.float32)
        * factor
    )
    grad_key = (
        jnp.einsum("bhqk,bqhd->bkhd", grad_scores, query_rows, preferred_element_type=jnp.float32)
        * factor
    )
    grad_value = jnp.einsum(
        "bhqk,bqhd->bkhd", prob_b, grad_mixed, preferred_element_type=jnp.float32
    )
    return (
        grad_query.astype(jnp.bfloat16),
        grad_key.astype(jnp.bfloat16),
        grad_value.astype(jnp.bfloat16),
    )


def forward(tokens_f, spans, weights, repeat):
    w_qkv, b_qv, w_proj, b_proj, w_up, b_up, w_down, b_down = weights
    shift_attn, scale_attn, gate_attn, shift_mlp, scale_mlp, gate_mlp = spans
    slot_count, seq_len, model_dim = tokens_f.shape
    row_count = slot_count * seq_len
    head_cols = w_qkv.shape[2]
    head_count = head_cols // HEAD_DIM
    shape_four = (slot_count, seq_len, head_count, HEAD_DIM)
    normed = (
        modulate(tokens_f, shift_attn, scale_attn)
        .astype(jnp.bfloat16)
        .reshape(row_count, model_dim)
    )
    projected = jnp.dot(
        normed, w_qkv.reshape(model_dim, 3 * head_cols), preferred_element_type=jnp.float32
    )
    qkv_bias = jnp.stack([b_qv[0], jnp.zeros_like(b_qv[0]), b_qv[1]]).astype(jnp.float32)
    projected = (projected.reshape(row_count, 3, head_cols) + qkv_bias).astype(jnp.bfloat16)
    query_rows = projected[:, 0].reshape(shape_four)
    key_rows = projected[:, 1].reshape(shape_four)
    value_rows = projected[:, 2].reshape(shape_four)
    mixed_out, logsum = attention_forward(query_rows, key_rows, value_rows)
    mixed_b = mixed_out.astype(jnp.bfloat16).reshape(row_count, head_cols)
    partial_value = jnp.dot(mixed_b, w_proj, preferred_element_type=jnp.float32)
    if repeat:
        summed = lax.psum(partial_value.astype(jnp.bfloat16), "mp").astype(jnp.float32)
    else:
        summed = lax.psum(partial_value.astype(jnp.bfloat16), "mp").astype(jnp.float32)
    attn_out = (summed + b_proj.astype(jnp.float32)).reshape(slot_count, seq_len, model_dim)
    residual = tokens_f + gate_attn * attn_out
    normed_mlp = (
        modulate(residual, shift_mlp, scale_mlp).astype(jnp.bfloat16).reshape(row_count, model_dim)
    )
    hidden = jnp.dot(normed_mlp, w_up, preferred_element_type=jnp.float32) + b_up.astype(
        jnp.float32
    )
    act_bf = gelu_tanh(hidden).astype(jnp.bfloat16)
    partial_mlp = jnp.dot(act_bf, w_down, preferred_element_type=jnp.float32)
    if repeat:
        summed_mlp = lax.psum(partial_mlp.astype(jnp.bfloat16), "mp").astype(jnp.float32)
    else:
        summed_mlp = lax.psum(partial_mlp.astype(jnp.bfloat16), "mp").astype(jnp.float32)
    mlp_out = (summed_mlp + b_down.astype(jnp.float32)).reshape(slot_count, seq_len, model_dim)
    output = residual + gate_mlp * mlp_out
    return {
        "normed": normed,
        "query_rows": query_rows,
        "key_rows": key_rows,
        "value_rows": value_rows,
        "logsum": logsum,
        "mixed_b": mixed_b,
        "attn_out": attn_out,
        "residual": residual,
        "normed_mlp": normed_mlp,
        "hidden": hidden,
        "act_bf": act_bf,
        "mlp_out": mlp_out,
        "output": output,
    }


def image_pass(tokens_f, grad_out, spans, weights):
    w_qkv, b_qv, w_proj, b_proj, w_up, b_up, w_down, b_down = weights
    shift_attn, scale_attn, gate_attn, shift_mlp, scale_mlp, gate_mlp = spans
    slot_count, seq_len, model_dim = tokens_f.shape
    row_count = slot_count * seq_len
    head_cols = w_qkv.shape[2]
    head_count = head_cols // HEAD_DIM
    kept_fwd = forward(tokens_f, spans, weights, False)
    out_one = kept_fwd["output"]
    stored = forward(tokens_f, spans, weights, True)
    grad_gate_mlp = jnp.sum(grad_out * stored["mlp_out"], axis=1)
    grad_mlp = (gate_mlp * grad_out).astype(jnp.bfloat16).reshape(row_count, model_dim)
    grad_b_down = jnp.sum(grad_mlp.astype(jnp.float32), axis=0)
    grad_w_down = inner_rows(stored["act_bf"], grad_mlp)
    grad_act = outer_cols(grad_mlp, w_down)
    gelu_value, gelu_back = jax.vjp(gelu_tanh, stored["hidden"])
    grad_hidden = gelu_back(grad_act)[0].astype(jnp.bfloat16)
    grad_b_up = jnp.sum(grad_hidden.astype(jnp.float32), axis=0)
    grad_w_up = inner_rows(stored["normed_mlp"], grad_hidden)
    part_normed_mlp = outer_cols(grad_hidden, w_up)
    grad_normed_mlp = (
        lax.psum(part_normed_mlp.astype(jnp.bfloat16), "mp")
        .astype(jnp.float32)
        .reshape(slot_count, seq_len, model_dim)
    )
    norm_value, norm_back = jax.vjp(modulate, stored["residual"], shift_mlp, scale_mlp)
    grad_resid_norm, grad_shift_mlp, grad_scale_mlp = norm_back(grad_normed_mlp)
    grad_residual = grad_out + grad_resid_norm
    grad_gate_attn = jnp.sum(grad_residual * stored["attn_out"], axis=1)
    grad_attn = (gate_attn * grad_residual).astype(jnp.bfloat16).reshape(row_count, model_dim)
    grad_b_proj = jnp.sum(grad_attn.astype(jnp.float32), axis=0)
    grad_w_proj = inner_rows(stored["mixed_b"], grad_attn)
    grad_mixed = (
        outer_cols(grad_attn, w_proj)
        .astype(jnp.bfloat16)
        .reshape(slot_count, seq_len, head_count, HEAD_DIM)
    )
    grad_query, grad_key, grad_value = attention_backward(
        stored["query_rows"], stored["key_rows"], stored["value_rows"], stored["logsum"], grad_mixed
    )
    grad_qkv = jnp.stack(
        [
            grad_query.reshape(row_count, head_cols),
            grad_key.reshape(row_count, head_cols),
            grad_value.reshape(row_count, head_cols),
        ],
        axis=1,
    )
    grad_b_qv = jnp.stack(
        [
            jnp.sum(grad_qkv[:, 0].astype(jnp.float32), axis=0),
            jnp.sum(grad_qkv[:, 2].astype(jnp.float32), axis=0),
        ]
    )
    grad_w_qkv = inner_rows(stored["normed"], grad_qkv)
    part_normed = outer_cols(
        grad_qkv.reshape(row_count, 3 * head_cols), w_qkv.reshape(model_dim, 3 * head_cols)
    )
    grad_normed = (
        lax.psum(part_normed.astype(jnp.bfloat16), "mp")
        .astype(jnp.float32)
        .reshape(slot_count, seq_len, model_dim)
    )
    first_value, first_back = jax.vjp(modulate, tokens_f, shift_attn, scale_attn)
    grad_tok_norm, grad_shift_attn, grad_scale_attn = first_back(grad_normed)
    grad_tok_one = grad_residual + grad_tok_norm
    grad_mod_one = jnp.concatenate(
        [
            grad_shift_attn[:, 0],
            grad_scale_attn[:, 0],
            grad_gate_attn,
            grad_shift_mlp[:, 0],
            grad_scale_mlp[:, 0],
            grad_gate_mlp,
        ],
        axis=1,
    )
    grad_terms = (
        grad_w_qkv,
        grad_b_qv,
        grad_w_proj,
        grad_b_proj,
        grad_w_up,
        grad_b_up,
        grad_w_down,
        grad_b_down,
    )
    return (out_one, grad_tok_one, grad_mod_one, grad_terms)


def run_layer(tokens, condition, cotangent, live_count, turns, weights, w_mod, b_mod):
    slot_count, seq_len, model_dim = tokens.shape
    cond_f = condition.astype(jnp.float32)
    scaled = jax.nn.silu(cond_f).astype(jnp.bfloat16)
    own_mod = jnp.dot(scaled, w_mod, preferred_element_type=jnp.float32) + b_mod.astype(jnp.float32)
    modulation = lax.all_gather(own_mod, "mp", axis=1, tiled=True)
    tokens_f = tokens.astype(jnp.float32)
    cot_f = cotangent.astype(jnp.float32)

    def image_step(slot_idx, carry):
        out_buf, grad_buf, mod_buf, grad_sums = carry
        live_flag = (slot_idx < live_count).astype(jnp.float32)
        tok_one = lax.dynamic_slice_in_dim(tokens_f, slot_idx, 1, 0)
        cot_one = lax.dynamic_slice_in_dim(cot_f, slot_idx, 1, 0) * live_flag
        mod_row = lax.dynamic_slice_in_dim(modulation, slot_idx, 1, 0)
        spans = [
            mod_row[:, None, part_idx * model_dim : (part_idx + 1) * model_dim]
            for part_idx in range(6)
        ]
        out_one, grad_tok_one, grad_mod_one, grad_terms = image_pass(
            tok_one, cot_one, spans, weights
        )
        out_one = (out_one * live_flag).astype(jnp.bfloat16)
        out_buf = lax.dynamic_update_slice_in_dim(out_buf, out_one, slot_idx, 0)
        grad_buf = lax.dynamic_update_slice_in_dim(grad_buf, grad_tok_one, slot_idx, 0)
        mod_buf = lax.dynamic_update_slice_in_dim(mod_buf, grad_mod_one, slot_idx, 0)
        grad_sums = tuple((total_a + term_b for total_a, term_b in zip(grad_sums, grad_terms)))
        return (out_buf, grad_buf, mod_buf, grad_sums)

    start_sums = tuple((jnp.zeros(weight_in.shape, jnp.float32) for weight_in in weights))
    start_state = (
        jnp.zeros(tokens.shape, jnp.bfloat16),
        jnp.zeros(tokens.shape, jnp.float32),
        jnp.zeros((slot_count, 6 * model_dim), jnp.float32),
        start_sums,
    )
    out_buf, grad_buf, mod_buf, grad_sums = lax.fori_loop(0, turns, image_step, start_state)
    grad_modulation = mod_buf.astype(jnp.bfloat16)
    own_cols = w_mod.shape[1]
    grad_own = lax.dynamic_slice_in_dim(
        grad_modulation, lax.axis_index("mp") * own_cols, own_cols, 1
    )
    part_scaled = outer_cols(grad_own, w_mod)
    grad_scaled = lax.psum(part_scaled.astype(jnp.bfloat16), "mp").astype(jnp.float32)
    silu_value, silu_back = jax.vjp(jax.nn.silu, cond_f)
    grad_condition = silu_back(grad_scaled)[0]
    return (out_buf, grad_buf, grad_condition, grad_sums, scaled, grad_own)


def on_device(
    tokens,
    condition,
    counts,
    w_qkv,
    b_qv,
    w_proj,
    b_proj,
    w_up,
    b_up,
    w_down,
    b_down,
    w_mod,
    b_mod,
    cotangent,
):
    slot_count, seq_len, model_dim = tokens.shape
    weights = (w_qkv, b_qv, w_proj, b_proj, w_up, b_up, w_down, b_down)
    own_count = counts[0]
    output, grad_tokens, grad_condition, grad_sums, scaled, grad_own = run_layer(
        tokens, condition, cotangent, own_count, slot_count, weights, w_mod, b_mod
    )
    (
        grad_w_qkv,
        grad_b_qv,
        grad_w_proj,
        grad_b_proj,
        grad_w_up,
        grad_b_up,
        grad_w_down,
        grad_b_down,
    ) = grad_sums
    grad_w_mod = inner_rows(scaled, grad_own)
    grad_b_mod = jnp.sum(grad_own.astype(jnp.float32), axis=0)
    (
        grad_w_qkv,
        grad_b_qv,
        grad_w_proj,
        grad_b_proj,
        grad_w_up,
        grad_b_up,
        grad_w_down,
        grad_b_down,
        grad_w_mod,
        grad_b_mod,
    ) = (
        lax.psum(grad_w_qkv.astype(jnp.bfloat16), "dp").astype(jnp.float32),
        lax.psum(grad_b_qv.astype(jnp.bfloat16), "dp").astype(jnp.float32),
        lax.psum(grad_w_proj.astype(jnp.bfloat16), "dp").astype(jnp.float32),
        lax.psum(grad_b_proj.astype(jnp.bfloat16), "dp").astype(jnp.float32),
        lax.psum(grad_w_up.astype(jnp.bfloat16), "dp").astype(jnp.float32),
        lax.psum(grad_b_up.astype(jnp.bfloat16), "dp").astype(jnp.float32),
        lax.psum(grad_w_down.astype(jnp.bfloat16), "dp").astype(jnp.float32),
        lax.psum(grad_b_down.astype(jnp.bfloat16), "dp").astype(jnp.float32),
        lax.psum(grad_w_mod.astype(jnp.bfloat16), "dp").astype(jnp.float32),
        lax.psum(grad_b_mod.astype(jnp.bfloat16), "dp").astype(jnp.float32),
    )
    return (
        output,
        grad_tokens,
        grad_condition,
        grad_w_qkv,
        grad_b_qv,
        grad_w_proj,
        grad_b_proj,
        grad_w_up,
        grad_b_up,
        grad_w_down,
        grad_b_down,
        grad_w_mod,
        grad_b_mod,
    )


def solution(mesh):
    placed = (
        P("dp", None, None),
        P("dp", None),
        P("dp"),
        P(None, None, "mp"),
        P(None, "mp"),
        P("mp", None),
        P(),
        P(None, "mp"),
        P("mp"),
        P("mp", None),
        P(),
        P(None, "mp"),
        P("mp"),
        P("dp", None, None),
    )
    fast = mesh.shape["dp"] == 16 and mesh.shape["mp"] == 2
    return jax.shard_map(
        fast_device if fast else on_device,
        mesh=mesh,
        in_specs=placed,
        out_specs=(
            P("dp", None, None),
            P("dp", None, None),
            P("dp", None),
            P(None, None, "mp"),
            P(None, "mp"),
            P("mp", None),
            P(),
            P(None, "mp"),
            P("mp"),
            P("mp", None),
            P(),
            P(None, "mp"),
            P("mp"),
        ),
        check_vma=False,
    )
```

```python
import functools

import jax
import jax.numpy as jnp
from jax import lax
from jax.experimental import pallas as pl
from jax.experimental.pallas import tpu as pltpu
from jax.sharding import PartitionSpec as P

HEAD_DIM = 72
LOG2_E = 1.4426950408889634


epsilon = 1e-06

f32 = jnp.float32
bf16 = jnp.bfloat16


def dot_nn(left, right):
    return lax.dot_general(left, right, (((1,), (0,)), ((), ())), preferred_element_type=f32)


def dot_nt(left, right):
    return lax.dot_general(left, right, (((1,), (1,)), ((), ())), preferred_element_type=f32)


def dot_tn(left, right):
    return lax.dot_general(left, right, (((0,), (0,)), ((), ())), preferred_element_type=f32)


def normalize(values):
    center = values - jnp.mean(values, axis=-1, keepdims=True)
    recip = lax.rsqrt(jnp.mean(center * center, axis=-1, keepdims=True) + epsilon)
    return center * recip, recip


def norm_pullback(grad_normed, unit, recip, scale_row):
    scaled_grad = grad_normed * (1.0 + scale_row)
    mean_grad = jnp.mean(scaled_grad, axis=-1, keepdims=True)
    mean_unit = jnp.mean(scaled_grad * unit, axis=-1, keepdims=True)
    return recip * (scaled_grad - mean_grad - unit * mean_unit)


def column(row):
    return jnp.broadcast_to(row[...].astype(f32), (8, row.shape[1])).T[:, 0:1]


def head_rows(values, one):
    return values[one * HEAD_DIM : (one + 1) * HEAD_DIM].astype(bf16)


def token_sum(values):
    return jnp.sum(values, axis=0, keepdims=True)


def attention_kernel(parts, own_images, sc, tok, cot, mod, b_proj, *refs):
    w_qkv, w_proj, bias = refs[:parts], refs[parts : 2 * parts], refs[2 * parts : 3 * parts]
    qkv, prob, mixed, attn_out, residual, normed_mlp, normed, grad_mlp, down_sums = refs[3 * parts :]
    image = sc[0] * own_images + pl.program_id(0)
    live = jnp.where(image < sc[1], 1.0, 0.0).astype(f32)
    unit, _ = normalize(tok[0].astype(f32))
    normed[0] = (unit * (1.0 + mod[0, 1:2, :]) + mod[0, 0:1, :]).astype(bf16)
    grad = (mod[0, 5:6, :] * (cot[0].astype(f32) * live)).astype(bf16)
    grad_mlp[0] = grad
    down_sums[0] = token_sum(grad.astype(f32))
    cols = w_proj[0].shape[0]
    pairs = cols // (2 * HEAD_DIM)
    span = 2 * HEAD_DIM
    scale = HEAD_DIM ** (-0.5) * LOG2_E
    rows = normed[0]
    for part in range(parts):
        base = part * 3 * cols
        shift = bias[part][...].astype(f32).T
        for proj in range(3):
            lo = proj * cols
            value = dot_nt(w_qkv[part][lo : lo + cols, :], rows)
            if proj != 1:
                value = value + shift[:, proj // 2 : proj // 2 + 1]
            qkv[0, base + lo : base + lo + cols, :] = value.astype(bf16)

    def load(part, pair):
        at = part * 3 * cols + pair * span
        return [qkv[0, at + k * cols : at + k * cols + span, :].astype(f32) for k in range(3)]

    def score(loaded):
        query, key, _ = loaded
        return [dot_tn(head_rows(key, one), head_rows(query, one)) for one in range(2)]

    def spread(scores, head):
        raised = jnp.exp2((scores - jnp.max(scores, axis=0, keepdims=True)) * scale)
        share = 1.0 / jnp.sum(raised, axis=0, keepdims=True)
        prob_b = (raised * share).astype(bf16)
        prob[0, head] = prob_b
        return prob_b

    def mix(part, pair, loaded, probs):
        outs = [dot_nn(head_rows(loaded[2], one), probs[one]) for one in range(2)]
        to = part * cols + pair * span
        mixed[0, to : to + span, :] = jnp.concatenate(outs, axis=0).astype(bf16)

    work = [(part, pair) for part in range(parts) for pair in range(pairs)]
    loaded = load(*work[0])
    scores = score(loaded)
    waiting = None
    for turn, (part, pair) in enumerate(work):
        after = turn + 1 < len(work)
        if after:
            next_loaded = load(*work[turn + 1])
            next_scores = score(next_loaded)
        probs = [spread(scores[one], part * 2 * pairs + 2 * pair + one) for one in range(2)]
        if waiting is not None:
            mix(*waiting)
        waiting = (part, pair, loaded, probs)
        if after:
            loaded, scores = next_loaded, next_scores
    mix(*waiting)
    total = b_proj[...]
    for part in range(parts):
        total = total + dot_tn(mixed[0, part * cols : (part + 1) * cols, :], w_proj[part][...])
    attn_out[0] = total
    summed = tok[0].astype(f32) + mod[0, 2:3, :] * total
    residual[0] = summed
    unit, _ = normalize(summed)
    normed_mlp[0] = (unit * (1.0 + mod[0, 4:5, :]) + mod[0, 3:4, :]).astype(bf16)


def mlp_kernel(per, jobs, sc, rows, grad_mlp, *refs):
    count = len(jobs)
    weights = [refs[3 * k : 3 * k + 3] for k in range(count)]
    refs = refs[3 * count :]
    came = []
    for _, summed in jobs:
        came.append(refs[0] if summed else None)
        refs = refs[1:] if summed else refs
    act, back = refs[2], refs[3]
    refs = refs[4:]
    grads = []
    for cuts, _ in jobs:
        size = 1 if cuts is None else len(cuts)
        grads.append(refs[:size])
        refs = refs[size:]
    job, step = pl.program_id(0), pl.program_id(1)
    for k in range(count):

        @pl.when(job == k)
        def _(k=k):
            mlp_block(
                per, jobs[k][0], step, sc, rows, grad_mlp, *weights[k], act, back, grads[k], refs[k], came[k]
            )


def mlp_block(per, cuts, step, sc, rows, grad_mlp, w_up, w_down, bias, act, back, grads, sums, came):
    here = w_down.shape[0] // per
    hidden = lax.dot_general(
        w_up[...], rows[...], (((0,), (1,)), ((), ())), preferred_element_type=f32
    ) + column(bias)
    square = hidden * hidden
    bend = jnp.tanh(0.7978845608028654 * hidden * (1.0 + 0.044715 * square))
    half = 0.5 * (1.0 + bend)
    act_b = (hidden * half).astype(bf16)
    slope = half + 0.5 * hidden * (1.0 - bend * bend) * (
        0.7978845608028654 * (1.0 + 3.0 * 0.044715 * square)
    )
    back_b = (dot_nt(w_down[...], grad_mlp[...]) * slope).astype(bf16)
    act[0] = act_b
    back[0] = back_b
    sums[...] = dot_nt(jnp.ones((8, rows.shape[0]), bf16), back_b)[0:1]
    for lo_row, left, right in ((0, act_b, grad_mlp), (per, back_b, rows)):
        grad = dot_nn(left, right[...])
        for piece in range(here):
            value = grad[piece * per : (piece + 1) * per]
            if cuts is None:
                if came is not None:
                    value = value + came[piece, lo_row : lo_row + per, :].astype(f32)
                grads[0][piece, lo_row : lo_row + per, :] = value.astype(bf16)
            else:
                at = jnp.bitwise_xor(step * here + piece, sc[2])
                for (lo, hi), into in zip(cuts, grads):
                    into[at, lo_row : lo_row + per, :] = value[:, lo:hi].astype(bf16)


def grow(total, part_steps, left, rights, dims):
    step = pl.program_id(0)

    def term(right):
        return lax.dot_general(left, right[...], (dims, ((), ())), preferred_element_type=f32)

    @pl.when(step == 0)
    def _():
        total[...] = term(rights[0])

    @pl.when(jnp.logical_and(step > 0, step < part_steps))
    def _():
        total[...] += term(rights[0])

    @pl.when(jnp.logical_and(step >= part_steps, step < 2 * part_steps))
    def _():
        total[...] += term(rights[1])


def norm_back_kernel(
    part_steps, own_images, sc, back, w_up0, w_up1, residual, cot, mod, attn_out,
    grad_residual, grad_attn, sums, total
):
    grow(total, part_steps, back[0], (w_up0, w_up1), ((0,), (1,)))
    one = pl.program_id(0) - 2 * part_steps
    seq = residual.shape[1]

    @pl.when(one >= 0)
    def _():
        live = jnp.where(sc[0] * own_images + one < sc[1], 1.0, 0.0).astype(f32)
        grad_normed = total[pl.ds(pl.multiple_of(one * seq, seq), seq), :]
        unit, recip = normalize(residual[0])
        sums[0, 0:1, :] = token_sum(grad_normed)
        sums[0, 1:2, :] = token_sum(grad_normed * unit)
        grad_res = cot[0].astype(f32) * live + norm_pullback(grad_normed, unit, recip, mod[0, 4:5, :])
        grad_residual[0] = grad_res
        sums[0, 2:3, :] = token_sum(grad_res * attn_out[0])
        grad_att = (mod[0, 2:3, :] * grad_res).astype(bf16)
        grad_attn[0] = grad_att
        sums[0, 3:4, :] = token_sum(grad_att.astype(f32))


def back_kernel(parts, sc, grad_attn, qkv, prob, *refs):
    w_proj = refs[:parts]
    grad_qkv, grad_mixed = refs[parts:]
    cols = w_proj[0].shape[0]
    pairs = cols // (2 * HEAD_DIM)
    span = 2 * HEAD_DIM
    factor = HEAD_DIM ** (-0.5)
    grad_att = grad_attn[0]
    for part in range(parts):
        rows = slice(part * cols, (part + 1) * cols)
        grad_mixed[rows, :] = dot_nt(w_proj[part][...], grad_att).astype(bf16)

    def load(part, pair):
        at = part * 3 * cols + pair * span
        mix_at = part * cols + pair * span
        loaded = [qkv[0, at + k * cols : at + k * cols + span, :].astype(f32) for k in range(3)]
        return loaded + [grad_mixed[mix_at : mix_at + span, :].astype(f32)]

    def back_prob(loaded):
        return [dot_tn(head_rows(loaded[2], one), head_rows(loaded[3], one)) for one in range(2)]

    def back_scores(grad_prob, head):
        prob_b = prob[0, head]
        prob_f = prob_b.astype(f32)
        delta = jnp.sum(prob_f * grad_prob, axis=0, keepdims=True)
        return prob_b, (prob_f * (grad_prob - delta)).astype(bf16)

    work = [(part, pair) for part in range(parts) for pair in range(pairs)]
    loaded = load(*work[0])
    grad_probs = back_prob(loaded)
    for turn, (part, pair) in enumerate(work):
        after = turn + 1 < len(work)
        if after:
            next_loaded = load(*work[turn + 1])
            next_probs = back_prob(next_loaded)
        middle = [back_scores(grad_probs[one], part * 2 * pairs + 2 * pair + one) for one in range(2)]
        query, key, _, grads = loaded
        to_query = [dot_nn(head_rows(key, one), middle[one][1]) * factor for one in range(2)]
        to_key = [dot_nt(head_rows(query, one), middle[one][1]) * factor for one in range(2)]
        to_value = [dot_nt(head_rows(grads, one), middle[one][0]) for one in range(2)]
        at = part * 3 * cols + pair * span
        for k, outs in enumerate((to_query, to_key, to_value)):
            into = slice(at + k * cols, at + k * cols + span)
            grad_qkv[0, into, :] = jnp.concatenate(outs, axis=0).astype(bf16)
        if after:
            loaded, grad_probs = next_loaded, next_probs


def attn_grad_kernel(pieces, per, cuts, sc, *refs):
    grad_qkv, mixed, normed, grad_attn = refs[:pieces], refs[pieces], refs[pieces + 1], refs[pieces + 2]
    grads, sums = refs[pieces + 3 : -1], refs[-1]
    step = pl.program_id(0)
    here = mixed.shape[1] // per
    images = mixed.shape[0]
    each = images // pieces

    def spread(total):
        total = total.astype(bf16)
        for piece in range(here):
            at = jnp.bitwise_xor(step * here + piece, sc[2])
            for (lo, hi), into in zip(cuts, grads):
                into[at] = total[piece * per : (piece + 1) * per, lo:hi]

    @pl.when(step < 3)
    def _():
        ones = jnp.ones((8, mixed.shape[2]), bf16)
        total = count = None
        for image in range(images):
            left = grad_qkv[image // each][image % each]
            term, one = dot_nn(left, normed[image]), dot_nt(ones, left)
            total = term if image == 0 else total + term
            count = one if image == 0 else count + one
        sums[0] = count[0:1]
        spread(total)

    @pl.when(step == 3)
    def _():
        total = dot_nn(mixed[0], grad_attn[0])
        for image in range(1, images):
            total = total + dot_nn(mixed[image], grad_attn[image])
        spread(total)


def first_back_kernel(pieces, images, sc, *refs):
    grad_qkv = refs[:pieces]
    w_qkv0, w_qkv1, tok, mod, grad_residual = refs[pieces : pieces + 5]
    grad_tokens, grad_own, sums, total = refs[pieces + 5 :]
    step = pl.program_id(0)
    each = images // pieces
    seq = tok.shape[1]

    def add(w_qkv, fresh):
        for one in range(images):
            term = dot_tn(grad_qkv[one // each][one % each], w_qkv[...])
            if fresh:
                total[one * seq : (one + 1) * seq, :] = term
            else:
                total[one * seq : (one + 1) * seq, :] += term

    @pl.when(step == 0)
    def _():
        add(w_qkv0, True)

    @pl.when(jnp.logical_and(step > 0, step < 3))
    def _():
        add(w_qkv0, False)

    @pl.when(jnp.logical_and(step >= 3, step < 6))
    def _():
        add(w_qkv1, False)

    @pl.when(step >= 6)
    def _():
        grad_normed = total[pl.ds(pl.multiple_of((step - 6) * seq, seq), seq), :]
        unit, recip = normalize(tok[0].astype(f32))
        sums[0, 0:1, :] = token_sum(grad_normed)
        sums[0, 1:2, :] = token_sum(grad_normed * unit)
        grad = grad_residual[0] + norm_pullback(grad_normed, unit, recip, mod[0, 1:2, :])
        grad_tokens[0] = grad
        grad_own[0] = grad


def output_kernel(
    part_steps, own_images, sc, act, w_down0, w_down1, residual, cot, mod, b_down, output, own, sums, total
):
    grow(total, part_steps, act[0], (w_down0, w_down1), ((0,), (0,)))
    one = pl.program_id(0) - 2 * part_steps
    seq = residual.shape[1]

    @pl.when(one >= 0)
    def _():
        live = jnp.where(sc[0] * own_images + one < sc[1], 1.0, 0.0).astype(f32)
        mlp_out = total[pl.ds(pl.multiple_of(one * seq, seq), seq), :] + b_down[...]
        sums[0] = token_sum((cot[0].astype(f32) * live) * mlp_out)
        rows = ((residual[0] + mod[0, 5:6, :] * mlp_out) * live).astype(bf16)
        output[0] = rows
        own[0] = rows


def final_piece(sc, halves, piece, store):
    rel = jnp.bitwise_xor(piece, sc[2])
    for low, high, route, lo, hi in halves:
        bits = [(rel >> bit) & 1 for bit in route]
        index = bits[1] * 4 + bits[2] * 2 + bits[3]

        @pl.when(bits[0] == 0)
        def _(low=low, index=index, lo=lo, hi=hi):
            store(low[index].astype(f32), lo, hi)

        @pl.when(bits[0] == 1)
        def _(high=high, index=index, lo=lo, hi=hi):
            store(high[index].astype(f32), lo, hi)


def final_mlp_kernel(cuts, per, sc, *refs):
    count = 2 * len(cuts)
    arrays, (_, _, down, up, mark, turned) = refs[:count], refs[count:]
    here = down.shape[0] // per
    halves = [(arrays[2 * k], arrays[2 * k + 1]) + cut for k, cut in enumerate(cuts)]
    for piece in range(here):

        def store(value, lo, hi, piece=piece):
            down[piece * per : (piece + 1) * per, lo:hi] = value[0:per]
            turned[piece * per : (piece + 1) * per, lo:hi] = value[per : 2 * per]

        final_piece(sc, halves, pl.program_id(0) * here + piece, store)
    up[...] = turned[...].T
    mark[...] = jnp.zeros_like(mark)


def final_plain_kernel(per, sc, summed, down_in, up_in, down, up, mark, turned):
    for piece in range(summed.shape[0]):
        lo = piece * per
        down[lo : lo + per, :] = summed[piece, 0:per, :].astype(f32)
        turned[lo : lo + per, :] = summed[piece, per : 2 * per, :].astype(f32)
    up[...] = turned[...].T
    mark[...] = jnp.zeros_like(mark)


def final_attn_kernel(cuts, per, sc, *refs):
    count = 2 * len(cuts)
    arrays, (qkv, proj) = refs[:count], refs[count:]
    here = proj.shape[0] // per
    halves = [(arrays[2 * k], arrays[2 * k + 1]) + cut for k, cut in enumerate(cuts)]
    for target, wanted in ((qkv, True), (proj, False)):

        @pl.when((pl.program_id(0) < 3) == wanted)
        def _(target=target):
            for piece in range(here):

                def store(value, lo, hi, piece=piece):
                    target[piece * per : (piece + 1) * per, lo:hi] = value

                final_piece(sc, halves, pl.program_id(0) * here + piece, store)


def run_kernel(
    body, sc, args, in_specs, out_specs, out_shape, grid, micros, scratch=(), alias=None, room=60
):
    size = sum(a.size * a.dtype.itemsize for a in args) + sum(
        s.size * s.dtype.itemsize for s in out_shape
    )
    return pl.pallas_call(
        body,
        out_shape=out_shape,
        grid_spec=pltpu.PrefetchScalarGridSpec(
            num_scalar_prefetch=1,
            grid=grid,
            in_specs=in_specs,
            out_specs=out_specs,
            scratch_shapes=list(scratch),
        ),
        compiler_params=pltpu.CompilerParams(vmem_limit_bytes=room << 20),
        cost_estimate=pl.CostEstimate(
            flops=int(micros * 1.15e9), bytes_accessed=int(min(size, micros * 1e6)), transcendentals=0
        ),
        input_output_aliases=alias or {},
    )(sc, *args)


def whole_block(array):
    zeros = (0,) * array.ndim
    return pl.BlockSpec(array.shape, lambda *_: zeros, pipeline_mode=pl.Buffered(1))


def shape_of(dims, kind):
    return jax.ShapeDtypeStruct(dims, kind)


SWAP = [(0, 1), (1, 0)]


def swap_cores(value):
    return lax.ppermute(value, "mp", SWAP)


def bit_pairs(bit):
    return [(index, index ^ (1 << bit)) for index in range(16)]


MLP_WAYS = ((0, 640, (0, 1, 2, 3)), (640, 1152, (1, 0, 2, 3)))
ATTN_WAYS = ((0, 512, (0, 1, 2, 3)), (512, 896, (1, 0, 2, 3)), (896, 1152, (2, 3, 0, 1)))


def columns(ways):
    return tuple((lo, hi) for lo, hi, _ in ways)


def cut(array, bits, bit, side):
    return lax.index_in_dim(array, side, bits.index(bit), keepdims=False)


def left_bits(done):
    return [bit for bit in (3, 2, 1, 0) if bit not in done]


def exchange(values, bits):
    return [lax.ppermute(value, "dp", bit_pairs(bit)) for value, bit in zip(values, bits)]


def reduce_flow(ways, get_own, others):
    others = yield others
    came = [swap_cores(other) for other in others]
    yield None
    own, came = yield [get_own(), came]
    firsts, seconds = ([a.reshape((2, 2, 2, 2) + a.shape[1:]) for a in arrays] for arrays in (own, came))
    routes = [way for _, _, way in ways]
    for stage in range(4):
        sends, keeps = [], []
        for route, one, two in zip(routes, firsts, seconds):
            bits = left_bits(route[:stage])
            for side, into in ((1, sends), (0, keeps)):
                into.append(cut(one, bits, route[stage], side) + cut(two, bits, route[stage], side))
        if stage == 2 and routes[0][2:] == routes[1][2:]:
            sends = [jnp.concatenate(sends[:2], axis=-1)] + sends[2:]
            keeps = [jnp.concatenate(keeps[:2], axis=-1)] + keeps[2:]
            routes = [routes[0]] + routes[2:]
        sends, keeps = yield [sends, keeps]
        comes = exchange(sends, [route[stage] for route in routes])
        yield None
        firsts, seconds = yield [keeps, comes]
    return [one + two for one, two in zip(firsts, seconds)]


def gather_flow(ways, have):
    routes = [ways[0][2]] + [way for _, _, way in ways[2:]]
    middle = ways[0][1]
    (have,) = yield [have]
    comes = exchange(have, [route[3] for route in routes])
    have = [one[None] for one in have]
    comes = [one[None] for one in comes]
    yield None
    for stage in (2, 1, 0):
        have, comes = yield [have, comes]
        joined = [jnp.concatenate([one, two]) for one, two in zip(have, comes)]
        if stage == 1:
            joined = [joined[0][..., :middle], joined[0][..., middle:]] + joined[1:]
            routes = [way for _, _, way in ways]
        (have,) = yield [joined]
        comes = exchange(have, [route[stage] for route in routes])
        yield None
    have, comes = yield [have, comes]
    return [part for pair in zip(have, comes) for part in pair]


def sum_flow(ways, get_own, others):
    have = yield from reduce_flow(ways, get_own, others)
    return (yield from gather_flow(ways, have))


def swap_flow(other):
    (other,) = yield [other]
    came = swap_cores(other)
    yield None
    (came,) = yield [came]
    return came


def rows_flow(rows):
    for bit in (3, 2, 1, 0):
        (rows,) = yield [rows]
        came = lax.ppermute(rows, "dp", bit_pairs(bit))
        yield None
        rows, came = yield [rows, came]
        rows = jnp.concatenate([rows, came])
    return rows


class Order:
    def __init__(self, sc):
        self.sc = sc
        self.results = {}

    def fence(self, values):
        self.sc, values = lax.optimization_barrier((self.sc, values))
        return values

    def after(self, value):
        self.sc, _ = lax.optimization_barrier((self.sc, value))

    def tick(self, *flows):
        replies = {flow: None for flow in flows if flow not in self.results}
        while replies:
            wants = {}
            for flow, reply in replies.items():
                try:
                    want = flow.send(reply)
                except StopIteration as stop:
                    self.results[flow] = stop.value
                    continue
                if want is not None:
                    wants[flow] = want
            replies = dict(zip(wants, self.fence(list(wants.values())))) if wants else {}

    def finish(self, flow):
        while flow not in self.results:
            self.tick(flow)
        return self.results[flow]


CHUNKS = 3
PLAIN = 2


def fill_other(both, came, core):
    size = came.shape[0]
    return lax.dynamic_update_slice_in_dim(both, came, (1 - core) * size, 0)


def fast_device(
    tokens, condition, counts, w_qkv, b_qv, w_proj, b_proj, w_up, b_up, w_down, b_down, w_mod, b_mod,
    cotangent,
):
    slots, seq, dim = tokens.shape
    images = slots // 2
    count = images * seq
    cols = w_qkv.shape[2]
    ff = w_up.shape[1]
    own_cols = w_mod.shape[1]
    heads = cols // HEAD_DIM
    core = lax.axis_index("mp")
    order = Order(jnp.stack([core, counts[0], lax.axis_index("dp")]).astype(jnp.int32))

    qkv_rows = jnp.transpose(w_qkv, (1, 2, 0)).reshape(3 * cols, dim)
    wq = [qkv_rows, swap_cores(qkv_rows)]
    wp = [w_proj, swap_cores(w_proj)]
    qkv_bias = [b_qv, swap_cores(b_qv)]

    cond_f = condition.astype(f32)
    scaled = jax.nn.silu(cond_f).astype(bf16)
    own_mod = jnp.dot(scaled, w_mod, preferred_element_type=f32) + b_mod.astype(f32)
    other_mod = swap_cores(own_mod)
    sides = [jnp.where(core == side, own_mod, other_mod) for side in range(2)]
    modulation = jnp.concatenate(sides, axis=1).reshape(slots, 6, dim)
    proj_bias = b_proj.astype(f32)[None]
    down_bias = b_down.astype(f32)[None]

    late_up, late_down, late_bias = lax.optimization_barrier((wq[1], w_up, w_down, b_up, modulation))[1:4]
    wu = [w_up, swap_cores(late_up)]
    wd = [w_down, swap_cores(late_down)]
    up_bias = [b_up[None], swap_cores(late_bias[None])]

    local = lambda i, s: (s[0] * images + i, 0, 0)
    mine = lambda i, s: (i, 0, 0)
    tok_spec = pl.BlockSpec((1, seq, dim), local)
    own_spec = pl.BlockSpec((1, seq, dim), mine)
    mod_spec = pl.BlockSpec((1, 6, dim), local)
    row_spec = pl.BlockSpec((1, 1, dim), mine)
    qkv_spec = pl.BlockSpec((1, 6 * cols, seq), mine)
    prob_spec = pl.BlockSpec((1, 2 * heads, seq, seq), lambda i, s: (i, 0, 0, 0))
    mixed_spec = pl.BlockSpec((1, 2 * cols, seq), mine)
    token_f = shape_of((images, seq, dim), f32)
    token_b = shape_of((images, seq, dim), bf16)
    attn_args = wq + wp + qkv_bias
    qkv, prob, mixed, attn_out, residual, normed_mlp, normed, grad_mlp, down_sums = run_kernel(
        functools.partial(attention_kernel, 2, images),
        order.sc,
        [tokens, cotangent, modulation, proj_bias] + attn_args,
        [tok_spec, tok_spec, mod_spec, whole_block(proj_bias)] + [whole_block(a) for a in attn_args],
        [qkv_spec, prob_spec, mixed_spec] + [own_spec] * 5 + [row_spec],
        [
            shape_of((images, 6 * cols, seq), bf16),
            shape_of((images, 2 * heads, seq, seq), bf16),
            shape_of((images, 2 * cols, seq), bf16),
            token_f,
            token_f,
            token_b,
            token_b,
            token_b,
            shape_of((images, 1, dim), f32),
        ],
        (images,),
        33,
    )
    order.after(down_sums)

    rows_flat = normed_mlp.reshape(count, dim)
    grad_flat = grad_mlp.reshape(count, dim)
    width = ff // CHUNKS
    per = width // 16
    steps = 2
    block = width // steps
    anywhere = pl.BlockSpec(memory_space=pl.ANY)
    act = back = jnp.zeros((8, 128), bf16)
    up_sums = {}

    def mlp_call(jobs, came, micros):
        nonlocal act, back
        first = act.shape[0] == 8
        kinds = tuple((None if job[0] < PLAIN else columns(MLP_WAYS), job in came) for job in jobs)

        def turn(k):
            return lambda p, s, c: jnp.clip((p - k) * steps + s, 0, steps - 1)

        def pick(values):
            return lambda p: sum(jnp.where(p == k, value, 0) for k, value in enumerate(values))

        parts = pick([part for _, part in jobs])
        starts = pick([chunk * steps for chunk, _ in jobs])
        spread = pl.BlockSpec((1, block, count), lambda p, s, c: (parts(p), starts(p) + s, 0))
        args, specs = [], []
        for k, (chunk, part) in enumerate(jobs):
            at = chunk * steps
            wide = lambda p, s, c, k=k, at=at: (0, at + turn(k)(p, s, c))
            tall = lambda p, s, c, k=k, at=at: (at + turn(k)(p, s, c), 0)
            args += [wu[part], wd[part], up_bias[part]]
            specs += [
                pl.BlockSpec((dim, block), wide),
                pl.BlockSpec((block, dim), tall),
                pl.BlockSpec((1, block), wide),
            ]
        grad_specs, grad_shapes, sizes = [], [], []
        for k, (split, _) in enumerate(kinds):
            own = lambda p, s, c, k=k: (turn(k)(p, s, c), 0, 0)
            fixed = lambda p, s, c: (0, 0, 0)
            wides = [dim] if split is None else [hi - lo for lo, hi in split]
            lead = (16 // steps, own) if split is None else (16, fixed)
            grad_specs.append([pl.BlockSpec((lead[0], 2 * per, wide), lead[1]) for wide in wides])
            grad_shapes += [shape_of((16, 2 * per, wide), bf16) for wide in wides]
            sizes.append(len(wides))
        for k, job in enumerate(jobs):
            if job in came:
                args.append(came[job])
                specs += grad_specs[k]
        args += [act, back]
        spot = len(args) + 1
        outs = run_kernel(
            functools.partial(mlp_kernel, per, kinds),
            order.sc,
            [rows_flat, grad_flat] + args,
            [whole_block(rows_flat), whole_block(grad_flat)] + specs + [anywhere, anywhere],
            [spread, spread]
            + [spec for specs in grad_specs for spec in specs]
            + [pl.BlockSpec((1, block), lambda p, s, c, k=k: (0, turn(k)(p, s, c))) for k in range(len(jobs))],
            [shape_of((2, ff, count), bf16)] * 2 + grad_shapes + [shape_of((1, width), f32)] * len(jobs),
            (len(jobs), steps),
            micros,
            alias=None if first else {spot: 0, spot + 1: 1},
        )
        act, back = outs[:2]
        grads, outs = list(outs[2 : 2 + sum(sizes)]), outs[2 + sum(sizes) :]
        up_sums.update(zip(jobs, outs))
        order.after(outs[-1])
        return [[grads.pop(0) for _ in range(size)] for size in sizes]

    summed = range(PLAIN)
    swaps = [swap_flow(grad) for (grad,) in mlp_call([(chunk, 1) for chunk in summed], {}, 26)]
    order.tick(*swaps)
    rest = [(chunk, part) for chunk in range(PLAIN, CHUNKS) for part in (1, 0)]
    grads = mlp_call(rest, {}, 26)
    flows = [
        sum_flow(MLP_WAYS, lambda own=own: own, others) for others, own in zip(grads[0::2], grads[1::2])
    ]
    order.tick(*swaps, *flows)
    came = {(chunk, 0): order.results[swap] for chunk, swap in zip(summed, swaps)}
    grads = mlp_call([(chunk, 0) for chunk in summed], came, 26)
    plain_sums = lax.psum([grad for (grad,) in grads], "dp")
    order.tick(*flows)

    reach = 768
    turns = ff // reach
    every = lambda s, c: (0, 0, 0)
    tail = lambda first: lambda s, c: (jnp.maximum(s - first, 0), 0, 0)
    tail_local = lambda first: lambda s, c: (c[0] * images + jnp.maximum(s - first, 0), 0, 0)

    def image_spec(first, where=tail):
        return pl.BlockSpec((1, seq, dim), where(first))

    def rows_of(part, size):
        if part == 0:
            return lambda s, c: jnp.minimum(s, size - 1)
        return lambda s, c: jnp.clip(s - size, 0, size - 1)

    span_spec = pl.BlockSpec(
        (1, reach, count),
        lambda s, c: (jnp.minimum(s // turns, 1), jnp.where(s < 2 * turns, s % turns, turns - 1), 0),
    )
    grad_residual, grad_attn, mid_sums = run_kernel(
        functools.partial(norm_back_kernel, turns, images),
        order.sc,
        [back] + wu + [residual, cotangent, modulation, attn_out],
        [
            span_spec,
            pl.BlockSpec((dim, reach), lambda s, c: (0, rows_of(0, turns)(s, c))),
            pl.BlockSpec((dim, reach), lambda s, c: (0, rows_of(1, turns)(s, c))),
            image_spec(2 * turns),
            image_spec(2 * turns, tail_local),
            pl.BlockSpec((1, 6, dim), tail_local(2 * turns)),
            image_spec(2 * turns),
        ],
        [image_spec(2 * turns)] * 2 + [pl.BlockSpec((1, 4, dim), tail(2 * turns))],
        [token_f, token_b, shape_of((images, 4, dim), f32)],
        (2 * turns + images,),
        60,
        scratch=[pltpu.VMEM((count, dim), f32)],
    )
    order.after(mid_sums)
    order.tick(*flows)
    pieces = 2
    each = images // pieces
    grad_qkv = []
    for piece in range(pieces):
        there = lambda i, s, piece=piece: (piece * each + i, 0, 0)
        (grad_piece,) = run_kernel(
            functools.partial(back_kernel, 2),
            order.sc,
            [grad_attn, qkv, prob] + wp,
            [
                pl.BlockSpec((1, seq, dim), there),
                pl.BlockSpec((1, 6 * cols, seq), there),
                pl.BlockSpec((1, 2 * heads, seq, seq), lambda i, s, piece=piece: (piece * each + i, 0, 0, 0)),
            ]
            + [whole_block(a) for a in wp],
            [qkv_spec],
            [shape_of((each, 6 * cols, seq), bf16)],
            (each,),
            60,
            scratch=[pltpu.VMEM((2 * cols, seq), bf16)],
            )
        grad_qkv.append(grad_piece)
        order.after(grad_piece)
        order.tick(*flows)

    attn_per = 4 * cols // 16
    qv_sums = [None, None]

    def attn_part(part):
        *grads, sums = run_kernel(
            functools.partial(attn_grad_kernel, pieces, attn_per, columns(ATTN_WAYS)),
            order.sc,
            grad_qkv + [mixed, normed, grad_attn],
            [
                pl.BlockSpec((each, cols, seq), lambda s, c: (0, 3 * part + jnp.minimum(s, 2), 0))
                for _ in range(pieces)
            ]
            + [pl.BlockSpec((images, cols, seq), lambda s, c: (0, part, 0))]
            + [whole_block(normed), whole_block(grad_attn)],
            [pl.BlockSpec((16, attn_per, hi - lo), every) for lo, hi in columns(ATTN_WAYS)]
            + [pl.BlockSpec((1, 1, cols), lambda s, c: (jnp.minimum(s, 2), 0, 0))],
            [shape_of((16, attn_per, hi - lo), bf16) for lo, hi in columns(ATTN_WAYS)]
            + [shape_of((3, 1, cols), f32)],
            (4,),
            60,
            )
        qv_sums[part] = sums
        order.after(sums)
        return grads

    grad_other = attn_part(1)
    made = []
    last = sum_flow(ATTN_WAYS, lambda: made[0], grad_other)
    order.tick(last, *flows)
    made.append(attn_part(0))
    order.tick(last, *flows)

    first_spec = lambda part: pl.BlockSpec((cols, dim), lambda s, c: (rows_of(part, 3)(s, c), 0))
    grad_tokens, grad_own_tokens, low_sums = run_kernel(
        functools.partial(first_back_kernel, pieces, images),
        order.sc,
        grad_qkv + wq + [tokens, modulation, grad_residual],
        [pl.BlockSpec((each, cols, seq), lambda s, c: (0, jnp.minimum(s, 5), 0)) for _ in range(pieces)]
        + [first_spec(0), first_spec(1)]
        + [image_spec(6, tail_local), pl.BlockSpec((1, 6, dim), tail_local(6)), image_spec(6)],
        [image_spec(6, tail_local), image_spec(6), pl.BlockSpec((1, 2, dim), tail(6))],
        [shape_of((slots, seq, dim), f32), token_f, shape_of((images, 2, dim), f32)],
        (6 + images,),
        60,
        scratch=[pltpu.VMEM((count, dim), f32)],
    )
    order.after(low_sums)
    order.tick(last, *flows)
    down_spec = lambda part: pl.BlockSpec((reach, dim), lambda s, c: (rows_of(part, turns)(s, c), 0))
    output, own_output, gate_sums = run_kernel(
        functools.partial(output_kernel, turns, images),
        order.sc,
        [act] + wd + [residual, cotangent, modulation, down_bias],
        [
            span_spec,
            down_spec(0),
            down_spec(1),
            image_spec(2 * turns),
            image_spec(2 * turns, tail_local),
            pl.BlockSpec((1, 6, dim), tail_local(2 * turns)),
            whole_block(down_bias),
        ],
        [image_spec(2 * turns, tail_local), image_spec(2 * turns), pl.BlockSpec((1, 1, dim), tail(2 * turns))],
        [shape_of((slots, seq, dim), bf16), token_b, shape_of((images, 1, dim), f32)],
        (2 * turns + images,),
        60,
        scratch=[pltpu.VMEM((count, dim), f32)],
    )
    order.after(gate_sums)
    order.tick(last, *flows)

    low_sums, mid_sums, gate_sums, down_sums, qv_sums, up_sums, scaled_rows = order.fence(
        (low_sums, mid_sums, gate_sums, down_sums, qv_sums, up_sums, scaled)
    )
    grad_modulation = jnp.concatenate([low_sums, mid_sums[:, 2:3], mid_sums[:, 0:2], gate_sums], axis=1)
    grad_modulation = grad_modulation.reshape(images, 6 * dim).astype(bf16)
    bias_sums = [
        jnp.concatenate(
            [qv_sums[part][0], qv_sums[part][2]]
            + [up_sums[chunk, part] for chunk in range(CHUNKS)],
            axis=1,
        )
        for part in range(2)
    ]
    shared = jnp.concatenate(
        [
            jnp.sum(mid_sums[:, 3], axis=0, keepdims=True),
            jnp.sum(down_sums[:, 0], axis=0, keepdims=True),
            jnp.zeros((1, own_cols - 2 * dim), f32),
        ],
        axis=1,
    )
    halves = grad_modulation.reshape(images, 2, own_cols)
    kept = lax.dynamic_index_in_dim(halves, core, 1, keepdims=False)
    given = lax.dynamic_index_in_dim(halves, 1 - core, 1, keepdims=False)
    got = swap_cores(jnp.concatenate([given.astype(f32), bias_sums[1], shared]))
    came = got[:images].astype(bf16)
    group_mod = jnp.where(core == 0, jnp.concatenate([kept, came]), jnp.concatenate([came, kept]))
    own_bias_sum = bias_sums[0] + got[images : images + 1]
    shared_sum = shared + got[images + 1 :]
    wide_scaled = jnp.pad(scaled_rows.reshape(-1), (0, 3 * own_cols - slots * dim)).reshape(3, own_cols)
    packed_rows = jnp.concatenate(
        [group_mod, own_bias_sum.astype(bf16), shared_sum.astype(bf16), wide_scaled]
    )
    (packed_rows,) = order.fence([packed_rows])
    small = rows_flow(packed_rows)
    order.tick(last, small)
    (group_mod,) = order.fence([group_mod])
    part_scaled = outer_cols(group_mod, w_mod).astype(bf16)
    order.after(part_scaled[0, :1])
    order.tick(last, small, *flows)
    own_output, part_scaled = order.fence((own_output, part_scaled))
    other_output, came_scaled = swap_cores(own_output), swap_cores(part_scaled)

    def cuts(ways):
        return tuple((way, lo, hi) for lo, hi, way in ways)

    grad_w_down = grad_w_up = jnp.zeros((8, 128), f32)

    def final_mlp(chunk, body, args):
        nonlocal grad_w_down, grad_w_up
        first = grad_w_down.shape[0] == 8
        spot = len(args) + 1
        grad_w_down, grad_w_up, mark = run_kernel(
            body,
            order.sc,
            list(args) + [grad_w_down, grad_w_up],
            [
                whole_block(a)
                if a.shape[0] == 8
                else pl.BlockSpec((16 // steps,) + a.shape[1:], lambda s, c: (s, 0, 0))
                for a in args
            ]
            + [anywhere, anywhere],
            [
                pl.BlockSpec((block, dim), lambda s, c: (chunk * steps + s, 0)),
                pl.BlockSpec((dim, block), lambda s, c: (0, chunk * steps + s)),
                pl.BlockSpec((8, 128), lambda s, c: (0, 0)),
            ],
            [shape_of((ff, dim), f32), shape_of((dim, ff), f32), shape_of((8, 128), f32)],
            (steps,),
            4,
            scratch=[pltpu.VMEM((block, dim), f32)],
            alias=None if first else {spot: 0, spot + 1: 1},
        )
        order.after(mark)

    for chunk, flow in enumerate(flows):
        body = functools.partial(final_mlp_kernel, cuts(MLP_WAYS), per)
        final_mlp(PLAIN + chunk, body, order.finish(flow))
    order.tick(last, small)
    other_output, came_scaled, grad_own_tokens = order.fence((other_output, came_scaled, grad_own_tokens))
    other_tokens = swap_cores(grad_own_tokens)
    for chunk, total in zip(summed, order.fence(plain_sums)):
        final_mlp(chunk, functools.partial(final_plain_kernel, per), [total])
    order.tick(last, small)
    output = fill_other(output, other_output, core)
    grad_scaled = part_scaled.astype(f32) + came_scaled.astype(f32)
    _, silu_back = jax.vjp(jax.nn.silu, cond_f)
    grad_condition = silu_back(grad_scaled)[0]
    order.after((output[0, 0, :1], grad_condition[0, :1]))
    order.tick(last)
    grad_tokens = fill_other(grad_tokens, order.fence(other_tokens), core)
    order.after(grad_tokens[0, 0, :1])
    all_rows = order.fence(order.finish(small)).reshape(16, slots + 5, own_cols)
    all_mod = all_rows[:, :slots].reshape(-1, own_cols)
    all_scaled = all_rows[:, slots + 2 :].reshape(16, -1)[:, : slots * dim].reshape(-1, dim)
    grad_w_mod = inner_rows(all_scaled, all_mod)
    grad_b_mod = jnp.sum(all_mod.astype(f32), axis=0)
    bias_total = jnp.sum(all_rows[:, slots : slots + 2].astype(f32), axis=0)
    grad_b_qv = bias_total[0, : 2 * cols].reshape(2, cols)
    grad_b_up = bias_total[0, 2 * cols :]
    grad_b_proj = bias_total[1, :dim]
    grad_b_down = bias_total[1, dim : 2 * dim]
    order.after((grad_w_mod[0, :1], grad_b_mod[:1], bias_total[0, :1]))
    args = order.finish(last)
    grad_qkv_rows, grad_w_proj = run_kernel(
        functools.partial(final_attn_kernel, cuts(ATTN_WAYS), attn_per),
        order.sc,
        list(args),
        [whole_block(a) for a in args],
        [
            pl.BlockSpec((cols, dim), lambda s, c: (jnp.minimum(s, 2), 0)),
            pl.BlockSpec((cols, dim), lambda s, c: (0, 0)),
        ],
        [shape_of((3 * cols, dim), f32), shape_of((cols, dim), f32)],
        (4,),
        9,
    )
    grad_w_qkv = jnp.transpose(grad_qkv_rows.reshape(3, cols, dim), (2, 0, 1))
    return (
        output,
        grad_tokens,
        grad_condition,
        grad_w_qkv,
        grad_b_qv,
        grad_w_proj,
        grad_b_proj,
        grad_w_up,
        grad_b_up,
        grad_w_down,
        grad_b_down,
        grad_w_mod,
        grad_b_mod,
    )


def layer_norm(values):
    center = values - jnp.mean(values, axis=-1, keepdims=True)
    return center * lax.rsqrt(jnp.mean(center * center, axis=-1, keepdims=True) + epsilon)


def modulate(values, shift_part, scale_part):
    return layer_norm(values) * (1.0 + scale_part) + shift_part


def gelu_tanh(values):
    return (
        0.5
        * values
        * (1.0 + jnp.tanh(0.7978845608028654 * (values + 0.044715 * values * values * values)))
    )


def inner_rows(left, right):
    return lax.dot_general(
        left, right, (((0,), (0,)), ((), ())), preferred_element_type=jnp.float32
    )


def outer_cols(left, right):
    return lax.dot_general(
        left, right, (((1,), (1,)), ((), ())), preferred_element_type=jnp.float32
    )


def attention_forward(query_rows, key_rows, value_rows):
    factor = HEAD_DIM ** (-0.5)
    scores = (
        jnp.einsum("bqhd,bkhd->bhqk", query_rows, key_rows, preferred_element_type=jnp.float32)
        * factor
    )
    row_max = jnp.max(scores, axis=-1, keepdims=True)
    row_total = jnp.sum(jnp.exp(scores - row_max), axis=-1, keepdims=True)
    logsum = row_max + jnp.log(row_total)
    prob_b = jnp.exp(scores - logsum).astype(jnp.bfloat16)
    mixed_out = jnp.einsum(
        "bhqk,bkhd->bqhd", prob_b, value_rows, preferred_element_type=jnp.float32
    )
    return (mixed_out, logsum)


def attention_backward(query_rows, key_rows, value_rows, logsum, grad_mixed):
    factor = HEAD_DIM ** (-0.5)
    scores = (
        jnp.einsum("bqhd,bkhd->bhqk", query_rows, key_rows, preferred_element_type=jnp.float32)
        * factor
    )
    prob_f = jnp.exp(scores - logsum)
    prob_b = prob_f.astype(jnp.bfloat16)
    grad_prob = jnp.einsum(
        "bqhd,bkhd->bhqk", grad_mixed, value_rows, preferred_element_type=jnp.float32
    )
    row_delta = jnp.sum(prob_f * grad_prob, axis=-1, keepdims=True)
    grad_scores = (prob_f * (grad_prob - row_delta)).astype(jnp.bfloat16)
    grad_query = (
        jnp.einsum("bhqk,bkhd->bqhd", grad_scores, key_rows, preferred_element_type=jnp.float32)
        * factor
    )
    grad_key = (
        jnp.einsum("bhqk,bqhd->bkhd", grad_scores, query_rows, preferred_element_type=jnp.float32)
        * factor
    )
    grad_value = jnp.einsum(
        "bhqk,bqhd->bkhd", prob_b, grad_mixed, preferred_element_type=jnp.float32
    )
    return (
        grad_query.astype(jnp.bfloat16),
        grad_key.astype(jnp.bfloat16),
        grad_value.astype(jnp.bfloat16),
    )


def forward(tokens_f, spans, weights, repeat):
    w_qkv, b_qv, w_proj, b_proj, w_up, b_up, w_down, b_down = weights
    shift_attn, scale_attn, gate_attn, shift_mlp, scale_mlp, gate_mlp = spans
    slot_count, seq_len, model_dim = tokens_f.shape
    row_count = slot_count * seq_len
    head_cols = w_qkv.shape[2]
    head_count = head_cols // HEAD_DIM
    shape_four = (slot_count, seq_len, head_count, HEAD_DIM)
    normed = (
        modulate(tokens_f, shift_attn, scale_attn)
        .astype(jnp.bfloat16)
        .reshape(row_count, model_dim)
    )
    projected = jnp.dot(
        normed, w_qkv.reshape(model_dim, 3 * head_cols), preferred_element_type=jnp.float32
    )
    qkv_bias = jnp.stack([b_qv[0], jnp.zeros_like(b_qv[0]), b_qv[1]]).astype(jnp.float32)
    projected = (projected.reshape(row_count, 3, head_cols) + qkv_bias).astype(jnp.bfloat16)
    query_rows = projected[:, 0].reshape(shape_four)
    key_rows = projected[:, 1].reshape(shape_four)
    value_rows = projected[:, 2].reshape(shape_four)
    mixed_out, logsum = attention_forward(query_rows, key_rows, value_rows)
    mixed_b = mixed_out.astype(jnp.bfloat16).reshape(row_count, head_cols)
    partial_value = jnp.dot(mixed_b, w_proj, preferred_element_type=jnp.float32)
    if repeat:
        summed = lax.psum(partial_value.astype(jnp.bfloat16), "mp").astype(jnp.float32)
    else:
        summed = lax.psum(partial_value.astype(jnp.bfloat16), "mp").astype(jnp.float32)
    attn_out = (summed + b_proj.astype(jnp.float32)).reshape(slot_count, seq_len, model_dim)
    residual = tokens_f + gate_attn * attn_out
    normed_mlp = (
        modulate(residual, shift_mlp, scale_mlp).astype(jnp.bfloat16).reshape(row_count, model_dim)
    )
    hidden = jnp.dot(normed_mlp, w_up, preferred_element_type=jnp.float32) + b_up.astype(
        jnp.float32
    )
    act_bf = gelu_tanh(hidden).astype(jnp.bfloat16)
    partial_mlp = jnp.dot(act_bf, w_down, preferred_element_type=jnp.float32)
    if repeat:
        summed_mlp = lax.psum(partial_mlp.astype(jnp.bfloat16), "mp").astype(jnp.float32)
    else:
        summed_mlp = lax.psum(partial_mlp.astype(jnp.bfloat16), "mp").astype(jnp.float32)
    mlp_out = (summed_mlp + b_down.astype(jnp.float32)).reshape(slot_count, seq_len, model_dim)
    output = residual + gate_mlp * mlp_out
    return {
        "normed": normed,
        "query_rows": query_rows,
        "key_rows": key_rows,
        "value_rows": value_rows,
        "logsum": logsum,
        "mixed_b": mixed_b,
        "attn_out": attn_out,
        "residual": residual,
        "normed_mlp": normed_mlp,
        "hidden": hidden,
        "act_bf": act_bf,
        "mlp_out": mlp_out,
        "output": output,
    }


def image_pass(tokens_f, grad_out, spans, weights):
    w_qkv, b_qv, w_proj, b_proj, w_up, b_up, w_down, b_down = weights
    shift_attn, scale_attn, gate_attn, shift_mlp, scale_mlp, gate_mlp = spans
    slot_count, seq_len, model_dim = tokens_f.shape
    row_count = slot_count * seq_len
    head_cols = w_qkv.shape[2]
    head_count = head_cols // HEAD_DIM
    kept_fwd = forward(tokens_f, spans, weights, False)
    out_one = kept_fwd["output"]
    stored = forward(tokens_f, spans, weights, True)
    grad_gate_mlp = jnp.sum(grad_out * stored["mlp_out"], axis=1)
    grad_mlp = (gate_mlp * grad_out).astype(jnp.bfloat16).reshape(row_count, model_dim)
    grad_b_down = jnp.sum(grad_mlp.astype(jnp.float32), axis=0)
    grad_w_down = inner_rows(stored["act_bf"], grad_mlp)
    grad_act = outer_cols(grad_mlp, w_down)
    gelu_value, gelu_back = jax.vjp(gelu_tanh, stored["hidden"])
    grad_hidden = gelu_back(grad_act)[0].astype(jnp.bfloat16)
    grad_b_up = jnp.sum(grad_hidden.astype(jnp.float32), axis=0)
    grad_w_up = inner_rows(stored["normed_mlp"], grad_hidden)
    part_normed_mlp = outer_cols(grad_hidden, w_up)
    grad_normed_mlp = (
        lax.psum(part_normed_mlp.astype(jnp.bfloat16), "mp")
        .astype(jnp.float32)
        .reshape(slot_count, seq_len, model_dim)
    )
    norm_value, norm_back = jax.vjp(modulate, stored["residual"], shift_mlp, scale_mlp)
    grad_resid_norm, grad_shift_mlp, grad_scale_mlp = norm_back(grad_normed_mlp)
    grad_residual = grad_out + grad_resid_norm
    grad_gate_attn = jnp.sum(grad_residual * stored["attn_out"], axis=1)
    grad_attn = (gate_attn * grad_residual).astype(jnp.bfloat16).reshape(row_count, model_dim)
    grad_b_proj = jnp.sum(grad_attn.astype(jnp.float32), axis=0)
    grad_w_proj = inner_rows(stored["mixed_b"], grad_attn)
    grad_mixed = (
        outer_cols(grad_attn, w_proj)
        .astype(jnp.bfloat16)
        .reshape(slot_count, seq_len, head_count, HEAD_DIM)
    )
    grad_query, grad_key, grad_value = attention_backward(
        stored["query_rows"], stored["key_rows"], stored["value_rows"], stored["logsum"], grad_mixed
    )
    grad_qkv = jnp.stack(
        [
            grad_query.reshape(row_count, head_cols),
            grad_key.reshape(row_count, head_cols),
            grad_value.reshape(row_count, head_cols),
        ],
        axis=1,
    )
    grad_b_qv = jnp.stack(
        [
            jnp.sum(grad_qkv[:, 0].astype(jnp.float32), axis=0),
            jnp.sum(grad_qkv[:, 2].astype(jnp.float32), axis=0),
        ]
    )
    grad_w_qkv = inner_rows(stored["normed"], grad_qkv)
    part_normed = outer_cols(
        grad_qkv.reshape(row_count, 3 * head_cols), w_qkv.reshape(model_dim, 3 * head_cols)
    )
    grad_normed = (
        lax.psum(part_normed.astype(jnp.bfloat16), "mp")
        .astype(jnp.float32)
        .reshape(slot_count, seq_len, model_dim)
    )
    first_value, first_back = jax.vjp(modulate, tokens_f, shift_attn, scale_attn)
    grad_tok_norm, grad_shift_attn, grad_scale_attn = first_back(grad_normed)
    grad_tok_one = grad_residual + grad_tok_norm
    grad_mod_one = jnp.concatenate(
        [
            grad_shift_attn[:, 0],
            grad_scale_attn[:, 0],
            grad_gate_attn,
            grad_shift_mlp[:, 0],
            grad_scale_mlp[:, 0],
            grad_gate_mlp,
        ],
        axis=1,
    )
    grad_terms = (
        grad_w_qkv,
        grad_b_qv,
        grad_w_proj,
        grad_b_proj,
        grad_w_up,
        grad_b_up,
        grad_w_down,
        grad_b_down,
    )
    return (out_one, grad_tok_one, grad_mod_one, grad_terms)


def run_layer(tokens, condition, cotangent, live_count, turns, weights, w_mod, b_mod):
    slot_count, seq_len, model_dim = tokens.shape
    cond_f = condition.astype(jnp.float32)
    scaled = jax.nn.silu(cond_f).astype(jnp.bfloat16)
    own_mod = jnp.dot(scaled, w_mod, preferred_element_type=jnp.float32) + b_mod.astype(jnp.float32)
    modulation = lax.all_gather(own_mod, "mp", axis=1, tiled=True)
    tokens_f = tokens.astype(jnp.float32)
    cot_f = cotangent.astype(jnp.float32)

    def image_step(slot_idx, carry):
        out_buf, grad_buf, mod_buf, grad_sums = carry
        live_flag = (slot_idx < live_count).astype(jnp.float32)
        tok_one = lax.dynamic_slice_in_dim(tokens_f, slot_idx, 1, 0)
        cot_one = lax.dynamic_slice_in_dim(cot_f, slot_idx, 1, 0) * live_flag
        mod_row = lax.dynamic_slice_in_dim(modulation, slot_idx, 1, 0)
        spans = [
            mod_row[:, None, part_idx * model_dim : (part_idx + 1) * model_dim]
            for part_idx in range(6)
        ]
        out_one, grad_tok_one, grad_mod_one, grad_terms = image_pass(
            tok_one, cot_one, spans, weights
        )
        out_one = (out_one * live_flag).astype(jnp.bfloat16)
        out_buf = lax.dynamic_update_slice_in_dim(out_buf, out_one, slot_idx, 0)
        grad_buf = lax.dynamic_update_slice_in_dim(grad_buf, grad_tok_one, slot_idx, 0)
        mod_buf = lax.dynamic_update_slice_in_dim(mod_buf, grad_mod_one, slot_idx, 0)
        grad_sums = tuple((total_a + term_b for total_a, term_b in zip(grad_sums, grad_terms)))
        return (out_buf, grad_buf, mod_buf, grad_sums)

    start_sums = tuple((jnp.zeros(weight_in.shape, jnp.float32) for weight_in in weights))
    start_state = (
        jnp.zeros(tokens.shape, jnp.bfloat16),
        jnp.zeros(tokens.shape, jnp.float32),
        jnp.zeros((slot_count, 6 * model_dim), jnp.float32),
        start_sums,
    )
    out_buf, grad_buf, mod_buf, grad_sums = lax.fori_loop(0, turns, image_step, start_state)
    grad_modulation = mod_buf.astype(jnp.bfloat16)
    own_cols = w_mod.shape[1]
    grad_own = lax.dynamic_slice_in_dim(
        grad_modulation, lax.axis_index("mp") * own_cols, own_cols, 1
    )
    part_scaled = outer_cols(grad_own, w_mod)
    grad_scaled = lax.psum(part_scaled.astype(jnp.bfloat16), "mp").astype(jnp.float32)
    silu_value, silu_back = jax.vjp(jax.nn.silu, cond_f)
    grad_condition = silu_back(grad_scaled)[0]
    return (out_buf, grad_buf, grad_condition, grad_sums, scaled, grad_own)


def on_device(
    tokens,
    condition,
    counts,
    w_qkv,
    b_qv,
    w_proj,
    b_proj,
    w_up,
    b_up,
    w_down,
    b_down,
    w_mod,
    b_mod,
    cotangent,
):
    slot_count, seq_len, model_dim = tokens.shape
    weights = (w_qkv, b_qv, w_proj, b_proj, w_up, b_up, w_down, b_down)
    own_count = counts[0]
    output, grad_tokens, grad_condition, grad_sums, scaled, grad_own = run_layer(
        tokens, condition, cotangent, own_count, slot_count, weights, w_mod, b_mod
    )
    (
        grad_w_qkv,
        grad_b_qv,
        grad_w_proj,
        grad_b_proj,
        grad_w_up,
        grad_b_up,
        grad_w_down,
        grad_b_down,
    ) = grad_sums
    grad_w_mod = inner_rows(scaled, grad_own)
    grad_b_mod = jnp.sum(grad_own.astype(jnp.float32), axis=0)
    (
        grad_w_qkv,
        grad_b_qv,
        grad_w_proj,
        grad_b_proj,
        grad_w_up,
        grad_b_up,
        grad_w_down,
        grad_b_down,
        grad_w_mod,
        grad_b_mod,
    ) = (
        lax.psum(grad_w_qkv.astype(jnp.bfloat16), "dp").astype(jnp.float32),
        lax.psum(grad_b_qv.astype(jnp.bfloat16), "dp").astype(jnp.float32),
        lax.psum(grad_w_proj.astype(jnp.bfloat16), "dp").astype(jnp.float32),
        lax.psum(grad_b_proj.astype(jnp.bfloat16), "dp").astype(jnp.float32),
        lax.psum(grad_w_up.astype(jnp.bfloat16), "dp").astype(jnp.float32),
        lax.psum(grad_b_up.astype(jnp.bfloat16), "dp").astype(jnp.float32),
        lax.psum(grad_w_down.astype(jnp.bfloat16), "dp").astype(jnp.float32),
        lax.psum(grad_b_down.astype(jnp.bfloat16), "dp").astype(jnp.float32),
        lax.psum(grad_w_mod.astype(jnp.bfloat16), "dp").astype(jnp.float32),
        lax.psum(grad_b_mod.astype(jnp.bfloat16), "dp").astype(jnp.float32),
    )
    return (
        output,
        grad_tokens,
        grad_condition,
        grad_w_qkv,
        grad_b_qv,
        grad_w_proj,
        grad_b_proj,
        grad_w_up,
        grad_b_up,
        grad_w_down,
        grad_b_down,
        grad_w_mod,
        grad_b_mod,
    )


def solution(mesh):
    placed = (
        P("dp", None, None),
        P("dp", None),
        P("dp"),
        P(None, None, "mp"),
        P(None, "mp"),
        P("mp", None),
        P(),
        P(None, "mp"),
        P("mp"),
        P("mp", None),
        P(),
        P(None, "mp"),
        P("mp"),
        P("dp", None, None),
    )
    fast = mesh.shape["dp"] == 16 and mesh.shape["mp"] == 2
    return jax.shard_map(
        fast_device if fast else on_device,
        mesh=mesh,
        in_specs=placed,
        out_specs=(
            P("dp", None, None),
            P("dp", None, None),
            P("dp", None),
            P(None, None, "mp"),
            P(None, "mp"),
            P("mp", None),
            P(),
            P(None, "mp"),
            P("mp"),
            P("mp", None),
            P(),
            P(None, "mp"),
            P("mp"),
        ),
        check_vma=False,
    )
```

```python
import functools

import jax
import jax.numpy as jnp
from jax import lax
from jax.experimental import pallas as pl
from jax.experimental.pallas import tpu as pltpu
from jax.sharding import PartitionSpec as P

HEAD_DIM = 72
LOG2_E = 1.4426950408889634


epsilon = 1e-06

f32 = jnp.float32
bf16 = jnp.bfloat16


def dot_nn(left, right):
    return lax.dot_general(left, right, (((1,), (0,)), ((), ())), preferred_element_type=f32)


def dot_nt(left, right):
    return lax.dot_general(left, right, (((1,), (1,)), ((), ())), preferred_element_type=f32)


def dot_tn(left, right):
    return lax.dot_general(left, right, (((0,), (0,)), ((), ())), preferred_element_type=f32)


def normalize(values):
    center = values - jnp.mean(values, axis=-1, keepdims=True)
    recip = lax.rsqrt(jnp.mean(center * center, axis=-1, keepdims=True) + epsilon)
    return center * recip, recip


def norm_pullback(grad_normed, unit, recip, scale_row):
    scaled_grad = grad_normed * (1.0 + scale_row)
    mean_grad = jnp.mean(scaled_grad, axis=-1, keepdims=True)
    mean_unit = jnp.mean(scaled_grad * unit, axis=-1, keepdims=True)
    return recip * (scaled_grad - mean_grad - unit * mean_unit)


def column(row):
    return jnp.broadcast_to(row[...].astype(f32), (8, row.shape[1])).T[:, 0:1]


def head_rows(values, one):
    return values[one * HEAD_DIM : (one + 1) * HEAD_DIM].astype(bf16)


def token_sum(values):
    return jnp.sum(values, axis=0, keepdims=True)


def attention_kernel(parts, own_images, sc, tok, cot, mod, b_proj, *refs):
    w_qkv, w_proj, bias = refs[:parts], refs[parts : 2 * parts], refs[2 * parts : 3 * parts]
    qkv, prob, mixed, attn_out, residual, normed_mlp, normed, grad_mlp, down_sums = refs[3 * parts :]
    image = sc[0] * own_images + pl.program_id(0)
    live = jnp.where(image < sc[1], 1.0, 0.0).astype(f32)
    unit, _ = normalize(tok[0].astype(f32))
    normed[0] = (unit * (1.0 + mod[0, 1:2, :]) + mod[0, 0:1, :]).astype(bf16)
    grad = (mod[0, 5:6, :] * (cot[0].astype(f32) * live)).astype(bf16)
    grad_mlp[0] = grad
    down_sums[0] = token_sum(grad.astype(f32))
    cols = w_proj[0].shape[0]
    pairs = cols // (2 * HEAD_DIM)
    span = 2 * HEAD_DIM
    scale = HEAD_DIM ** (-0.5) * LOG2_E
    rows = normed[0]
    for part in range(parts):
        base = part * 3 * cols
        shift = bias[part][...].astype(f32).T
        for proj in range(3):
            lo = proj * cols
            value = dot_nt(w_qkv[part][lo : lo + cols, :], rows)
            if proj != 1:
                value = value + shift[:, proj // 2 : proj // 2 + 1]
            qkv[0, base + lo : base + lo + cols, :] = value.astype(bf16)

    def load(part, pair):
        at = part * 3 * cols + pair * span
        return [qkv[0, at + k * cols : at + k * cols + span, :].astype(f32) for k in range(3)]

    def score(loaded):
        query, key, _ = loaded
        return [dot_tn(head_rows(key, one), head_rows(query, one)) for one in range(2)]

    def spread(scores, head):
        raised = jnp.exp2((scores - jnp.max(scores, axis=0, keepdims=True)) * scale)
        share = 1.0 / jnp.sum(raised, axis=0, keepdims=True)
        prob_b = (raised * share).astype(bf16)
        prob[0, head] = prob_b
        return prob_b

    def mix(part, pair, loaded, probs):
        outs = [dot_nn(head_rows(loaded[2], one), probs[one]) for one in range(2)]
        to = part * cols + pair * span
        mixed[0, to : to + span, :] = jnp.concatenate(outs, axis=0).astype(bf16)

    work = [(part, pair) for part in range(parts) for pair in range(pairs)]
    loaded = load(*work[0])
    scores = score(loaded)
    waiting = None
    for turn, (part, pair) in enumerate(work):
        after = turn + 1 < len(work)
        if after:
            next_loaded = load(*work[turn + 1])
            next_scores = score(next_loaded)
        probs = [spread(scores[one], part * 2 * pairs + 2 * pair + one) for one in range(2)]
        if waiting is not None:
            mix(*waiting)
        waiting = (part, pair, loaded, probs)
        if after:
            loaded, scores = next_loaded, next_scores
    mix(*waiting)
    total = b_proj[...]
    for part in range(parts):
        total = total + dot_tn(mixed[0, part * cols : (part + 1) * cols, :], w_proj[part][...])
    attn_out[0] = total
    summed = tok[0].astype(f32) + mod[0, 2:3, :] * total
    residual[0] = summed
    unit, _ = normalize(summed)
    normed_mlp[0] = (unit * (1.0 + mod[0, 4:5, :]) + mod[0, 3:4, :]).astype(bf16)


def mlp_kernel(per, cuts, jobs, sc, rows, grad_mlp, *refs):
    count = len(jobs)
    weights = [refs[3 * k : 3 * k + 3] for k in range(count)]
    refs = refs[3 * count :]
    came = []
    for _, summed in jobs:
        came.append(refs[0] if summed else None)
        refs = refs[1:] if summed else refs
    act, back = refs[2], refs[3]
    refs = refs[4:]
    grads = []
    for kind, _ in jobs:
        size = (kind != "cut") + (kind != "plain") * len(cuts)
        grads.append(refs[:size])
        refs = refs[size:]
    job, step = pl.program_id(0), pl.program_id(1)
    for k in range(count):

        @pl.when(job == k)
        def _(k=k):
            mlp_block(
                per, cuts, jobs[k][0], step, sc, rows, grad_mlp, *weights[k], act, back, grads[k], refs[k], came[k]
            )


def mlp_block(
    per, cuts, kind, step, sc, rows, grad_mlp, w_up, w_down, bias, act, back, grads, sums, came
):
    here = w_down.shape[0] // per
    hidden = lax.dot_general(
        w_up[...], rows[...], (((0,), (1,)), ((), ())), preferred_element_type=f32
    ) + column(bias)
    square = hidden * hidden
    bend = jnp.tanh(0.7978845608028654 * hidden * (1.0 + 0.044715 * square))
    half = 0.5 * (1.0 + bend)
    act_b = (hidden * half).astype(bf16)
    slope = half + 0.5 * hidden * (1.0 - bend * bend) * (
        0.7978845608028654 * (1.0 + 3.0 * 0.044715 * square)
    )
    back_b = (dot_nt(w_down[...], grad_mlp[...]) * slope).astype(bf16)
    act[0] = act_b
    back[0] = back_b
    sums[...] = dot_nt(jnp.ones((8, rows.shape[0]), bf16), back_b)[0:1]
    for which, (left, right) in enumerate(((act_b, grad_mlp), (back_b, rows))):
        grad = dot_nn(left, right[...])
        lo_row = 0 if kind == "mixed" else which * per
        plain = kind == "plain" or (kind == "mixed" and which == 0)
        for piece in range(here):
            value = grad[piece * per : (piece + 1) * per]
            if plain:
                if came is not None:
                    value = value + came[piece, lo_row : lo_row + per, :].astype(f32)
                grads[0][piece, lo_row : lo_row + per, :] = value.astype(bf16)
            else:
                at = jnp.bitwise_xor(step * here + piece, sc[2])
                for (lo, hi), into in zip(cuts, grads[-len(cuts) :]):
                    into[at, lo_row : lo_row + per, :] = value[:, lo:hi].astype(bf16)


def grow(total, part_steps, left, rights, dims):
    step = pl.program_id(0)

    def term(right):
        return lax.dot_general(left, right[...], (dims, ((), ())), preferred_element_type=f32)

    @pl.when(step == 0)
    def _():
        total[...] = term(rights[0])

    @pl.when(jnp.logical_and(step > 0, step < part_steps))
    def _():
        total[...] += term(rights[0])

    @pl.when(jnp.logical_and(step >= part_steps, step < 2 * part_steps))
    def _():
        total[...] += term(rights[1])


def norm_back_kernel(
    part_steps, own_images, sc, back, w_up0, w_up1, residual, cot, mod, attn_out,
    grad_residual, grad_attn, sums, total
):
    grow(total, part_steps, back[0], (w_up0, w_up1), ((0,), (1,)))
    one = pl.program_id(0) - 2 * part_steps
    seq = residual.shape[1]

    @pl.when(one >= 0)
    def _():
        live = jnp.where(sc[0] * own_images + one < sc[1], 1.0, 0.0).astype(f32)
        grad_normed = total[pl.ds(pl.multiple_of(one * seq, seq), seq), :]
        unit, recip = normalize(residual[0])
        sums[0, 0:1, :] = token_sum(grad_normed)
        sums[0, 1:2, :] = token_sum(grad_normed * unit)
        grad_res = cot[0].astype(f32) * live + norm_pullback(grad_normed, unit, recip, mod[0, 4:5, :])
        grad_residual[0] = grad_res
        sums[0, 2:3, :] = token_sum(grad_res * attn_out[0])
        grad_att = (mod[0, 2:3, :] * grad_res).astype(bf16)
        grad_attn[0] = grad_att
        sums[0, 3:4, :] = token_sum(grad_att.astype(f32))


def back_kernel(parts, sc, grad_attn, qkv, prob, *refs):
    w_proj = refs[:parts]
    grad_qkv, grad_mixed = refs[parts:]
    cols = w_proj[0].shape[0]
    pairs = cols // (2 * HEAD_DIM)
    span = 2 * HEAD_DIM
    factor = HEAD_DIM ** (-0.5)
    grad_att = grad_attn[0]
    for part in range(parts):
        rows = slice(part * cols, (part + 1) * cols)
        grad_mixed[rows, :] = dot_nt(w_proj[part][...], grad_att).astype(bf16)

    def load(part, pair):
        at = part * 3 * cols + pair * span
        mix_at = part * cols + pair * span
        loaded = [qkv[0, at + k * cols : at + k * cols + span, :].astype(f32) for k in range(3)]
        return loaded + [grad_mixed[mix_at : mix_at + span, :].astype(f32)]

    def back_prob(loaded):
        return [dot_tn(head_rows(loaded[2], one), head_rows(loaded[3], one)) for one in range(2)]

    def back_scores(grad_prob, head):
        prob_b = prob[0, head]
        prob_f = prob_b.astype(f32)
        delta = jnp.sum(prob_f * grad_prob, axis=0, keepdims=True)
        return prob_b, (prob_f * (grad_prob - delta)).astype(bf16)

    work = [(part, pair) for part in range(parts) for pair in range(pairs)]
    loaded = load(*work[0])
    grad_probs = back_prob(loaded)
    for turn, (part, pair) in enumerate(work):
        after = turn + 1 < len(work)
        if after:
            next_loaded = load(*work[turn + 1])
            next_probs = back_prob(next_loaded)
        middle = [back_scores(grad_probs[one], part * 2 * pairs + 2 * pair + one) for one in range(2)]
        query, key, _, grads = loaded
        to_query = [dot_nn(head_rows(key, one), middle[one][1]) * factor for one in range(2)]
        to_key = [dot_nt(head_rows(query, one), middle[one][1]) * factor for one in range(2)]
        to_value = [dot_nt(head_rows(grads, one), middle[one][0]) for one in range(2)]
        at = part * 3 * cols + pair * span
        for k, outs in enumerate((to_query, to_key, to_value)):
            into = slice(at + k * cols, at + k * cols + span)
            grad_qkv[0, into, :] = jnp.concatenate(outs, axis=0).astype(bf16)
        if after:
            loaded, grad_probs = next_loaded, next_probs


def attn_grad_kernel(pieces, per, cuts, sc, *refs):
    grad_qkv, mixed, normed, grad_attn = refs[:pieces], refs[pieces], refs[pieces + 1], refs[pieces + 2]
    grads, sums = refs[pieces + 3 : -1], refs[-1]
    step = pl.program_id(0)
    here = mixed.shape[1] // per
    images = mixed.shape[0]
    each = images // pieces

    def spread(total):
        total = total.astype(bf16)
        for piece in range(here):
            at = jnp.bitwise_xor(step * here + piece, sc[2])
            for (lo, hi), into in zip(cuts, grads):
                into[at] = total[piece * per : (piece + 1) * per, lo:hi]

    @pl.when(step < 3)
    def _():
        ones = jnp.ones((8, mixed.shape[2]), bf16)
        total = count = None
        for image in range(images):
            left = grad_qkv[image // each][image % each]
            term, one = dot_nn(left, normed[image]), dot_nt(ones, left)
            total = term if image == 0 else total + term
            count = one if image == 0 else count + one
        sums[0] = count[0:1]
        spread(total)

    @pl.when(step == 3)
    def _():
        total = dot_nn(mixed[0], grad_attn[0])
        for image in range(1, images):
            total = total + dot_nn(mixed[image], grad_attn[image])
        spread(total)


def first_back_kernel(pieces, images, sc, *refs):
    grad_qkv = refs[:pieces]
    w_qkv0, w_qkv1, tok, mod, grad_residual = refs[pieces : pieces + 5]
    grad_tokens, grad_own, sums, total = refs[pieces + 5 :]
    step = pl.program_id(0)
    each = images // pieces
    seq = tok.shape[1]

    def add(w_qkv, fresh):
        for one in range(images):
            term = dot_tn(grad_qkv[one // each][one % each], w_qkv[...])
            if fresh:
                total[one * seq : (one + 1) * seq, :] = term
            else:
                total[one * seq : (one + 1) * seq, :] += term

    @pl.when(step == 0)
    def _():
        add(w_qkv0, True)

    @pl.when(jnp.logical_and(step > 0, step < 3))
    def _():
        add(w_qkv0, False)

    @pl.when(jnp.logical_and(step >= 3, step < 6))
    def _():
        add(w_qkv1, False)

    @pl.when(step >= 6)
    def _():
        grad_normed = total[pl.ds(pl.multiple_of((step - 6) * seq, seq), seq), :]
        unit, recip = normalize(tok[0].astype(f32))
        sums[0, 0:1, :] = token_sum(grad_normed)
        sums[0, 1:2, :] = token_sum(grad_normed * unit)
        grad = grad_residual[0] + norm_pullback(grad_normed, unit, recip, mod[0, 1:2, :])
        grad_tokens[0] = grad
        grad_own[0] = grad


def output_kernel(
    part_steps, own_images, sc, act, w_down0, w_down1, residual, cot, mod, b_down, output, own, sums, total
):
    grow(total, part_steps, act[0], (w_down0, w_down1), ((0,), (0,)))
    one = pl.program_id(0) - 2 * part_steps
    seq = residual.shape[1]

    @pl.when(one >= 0)
    def _():
        live = jnp.where(sc[0] * own_images + one < sc[1], 1.0, 0.0).astype(f32)
        mlp_out = total[pl.ds(pl.multiple_of(one * seq, seq), seq), :] + b_down[...]
        sums[0] = token_sum((cot[0].astype(f32) * live) * mlp_out)
        rows = ((residual[0] + mod[0, 5:6, :] * mlp_out) * live).astype(bf16)
        output[0] = rows
        own[0] = rows


def final_piece(sc, halves, piece, store):
    rel = jnp.bitwise_xor(piece, sc[2])
    for low, high, route, lo, hi in halves:
        bits = [(rel >> bit) & 1 for bit in route]
        index = bits[1] * 4 + bits[2] * 2 + bits[3]

        @pl.when(bits[0] == 0)
        def _(low=low, index=index, lo=lo, hi=hi):
            store(low[index].astype(f32), lo, hi)

        @pl.when(bits[0] == 1)
        def _(high=high, index=index, lo=lo, hi=hi):
            store(high[index].astype(f32), lo, hi)


def final_mlp_kernel(cuts, per, sc, *refs):
    count = 2 * len(cuts)
    arrays, (_, _, down, up, mark, turned) = refs[:count], refs[count:]
    here = down.shape[0] // per
    halves = [(arrays[2 * k], arrays[2 * k + 1]) + cut for k, cut in enumerate(cuts)]
    for piece in range(here):

        def store(value, lo, hi, piece=piece):
            down[piece * per : (piece + 1) * per, lo:hi] = value[0:per]
            turned[piece * per : (piece + 1) * per, lo:hi] = value[per : 2 * per]

        final_piece(sc, halves, pl.program_id(0) * here + piece, store)
    up[...] = turned[...].T
    mark[...] = jnp.zeros_like(mark)


def final_plain_kernel(per, sc, summed, down_in, up_in, down, up, mark, turned):
    for piece in range(summed.shape[0]):
        lo = piece * per
        down[lo : lo + per, :] = summed[piece, 0:per, :].astype(f32)
        turned[lo : lo + per, :] = summed[piece, per : 2 * per, :].astype(f32)
    up[...] = turned[...].T
    mark[...] = jnp.zeros_like(mark)


def final_mixed_kernel(cuts, per, sc, *refs):
    count = 2 * len(cuts)
    arrays, (summed, _, _, down, up, mark, turned) = refs[:count], refs[count:]
    here = down.shape[0] // per
    halves = [(arrays[2 * k], arrays[2 * k + 1]) + cut for k, cut in enumerate(cuts)]
    for piece in range(here):
        rows = slice(piece * per, (piece + 1) * per)
        down[rows, :] = summed[piece].astype(f32)

        def store(value, lo, hi, rows=rows):
            turned[rows, lo:hi] = value[2 * per :]

        final_piece(sc, halves, pl.program_id(0) * here + piece, store)
    up[...] = turned[...].T
    mark[...] = jnp.zeros_like(mark)


def final_attn_kernel(cuts, per, sc, *refs):
    count = 2 * len(cuts)
    arrays, (qkv, proj) = refs[:count], refs[count:]
    here = proj.shape[0] // per
    halves = [(arrays[2 * k], arrays[2 * k + 1]) + cut for k, cut in enumerate(cuts)]
    for target, wanted in ((qkv, True), (proj, False)):

        @pl.when((pl.program_id(0) < 3) == wanted)
        def _(target=target):
            for piece in range(here):

                def store(value, lo, hi, piece=piece):
                    target[piece * per : (piece + 1) * per, lo:hi] = value

                final_piece(sc, halves, pl.program_id(0) * here + piece, store)


def run_kernel(
    body, sc, args, in_specs, out_specs, out_shape, grid, micros, scratch=(), alias=None, room=60
):
    size = sum(a.size * a.dtype.itemsize for a in args) + sum(
        s.size * s.dtype.itemsize for s in out_shape
    )
    return pl.pallas_call(
        body,
        out_shape=out_shape,
        grid_spec=pltpu.PrefetchScalarGridSpec(
            num_scalar_prefetch=1,
            grid=grid,
            in_specs=in_specs,
            out_specs=out_specs,
            scratch_shapes=list(scratch),
        ),
        compiler_params=pltpu.CompilerParams(vmem_limit_bytes=room << 20),
        cost_estimate=pl.CostEstimate(
            flops=int(micros * 1.15e9), bytes_accessed=int(min(size, micros * 1e6)), transcendentals=0
        ),
        input_output_aliases=alias or {},
    )(sc, *args)


def whole_block(array):
    zeros = (0,) * array.ndim
    return pl.BlockSpec(array.shape, lambda *_: zeros, pipeline_mode=pl.Buffered(1))


def shape_of(dims, kind):
    return jax.ShapeDtypeStruct(dims, kind)


SWAP = [(0, 1), (1, 0)]


def swap_cores(value):
    return lax.ppermute(value, "mp", SWAP)


def bit_pairs(bit):
    return [(index, index ^ (1 << bit)) for index in range(16)]


MLP_WAYS = ((0, 640, (0, 1, 2, 3)), (640, 1152, (1, 0, 2, 3)))
ATTN_WAYS = ((0, 512, (0, 1, 2, 3)), (512, 896, (1, 0, 2, 3)), (896, 1152, (2, 3, 0, 1)))


def columns(ways):
    return tuple((lo, hi) for lo, hi, _ in ways)


def cut(array, bits, bit, side):
    return lax.index_in_dim(array, side, bits.index(bit), keepdims=False)


def left_bits(done):
    return [bit for bit in (3, 2, 1, 0) if bit not in done]


def exchange(values, bits):
    return [lax.ppermute(value, "dp", bit_pairs(bit)) for value, bit in zip(values, bits)]


def reduce_flow(ways, get_own, others):
    others = yield others
    came = jax.tree.map(swap_cores, others)
    yield None
    own, came = yield [get_own(), came]
    firsts, seconds = jax.tree.map(lambda a: a.reshape((2, 2, 2, 2) + a.shape[1:]), (own, came))
    routes = [way for _, _, way in ways]
    for stage in range(4):
        sends, keeps = [], []
        for route, one, two in zip(routes, firsts, seconds):
            bits = left_bits(route[:stage])
            one, two = (value if isinstance(value, list) else [value] for value in (one, two))
            for side, into in ((1, sends), (0, keeps)):
                sums = [cut(a, bits, route[stage], side) + cut(b, bits, route[stage], side) for a, b in zip(one, two)]
                into.append(sums[0] if len(sums) == 1 else jnp.concatenate(sums, axis=-2))
        if stage == 2 and routes[0][2:] == routes[1][2:]:
            sends = [jnp.concatenate(sends[:2], axis=-1)] + sends[2:]
            keeps = [jnp.concatenate(keeps[:2], axis=-1)] + keeps[2:]
            routes = [routes[0]] + routes[2:]
        sends, keeps = yield [sends, keeps]
        comes = exchange(sends, [route[stage] for route in routes])
        yield None
        firsts, seconds = yield [keeps, comes]
    return [one + two for one, two in zip(firsts, seconds)]


def gather_flow(ways, have):
    routes = [ways[0][2]] + [way for _, _, way in ways[2:]]
    middle = ways[0][1]
    (have,) = yield [have]
    comes = exchange(have, [route[3] for route in routes])
    have = [one[None] for one in have]
    comes = [one[None] for one in comes]
    yield None
    for stage in (2, 1, 0):
        have, comes = yield [have, comes]
        joined = [jnp.concatenate([one, two]) for one, two in zip(have, comes)]
        if stage == 1:
            joined = [joined[0][..., :middle], joined[0][..., middle:]] + joined[1:]
            routes = [way for _, _, way in ways]
        (have,) = yield [joined]
        comes = exchange(have, [route[stage] for route in routes])
        yield None
    have, comes = yield [have, comes]
    return [part for pair in zip(have, comes) for part in pair]


def sum_flow(ways, get_own, others):
    have = yield from reduce_flow(ways, get_own, others)
    return (yield from gather_flow(ways, have))


def swap_flow(other):
    (other,) = yield [other]
    came = swap_cores(other)
    yield None
    (came,) = yield [came]
    return came


def rows_flow(rows):
    for bit in (3, 2, 1, 0):
        (rows,) = yield [rows]
        came = lax.ppermute(rows, "dp", bit_pairs(bit))
        yield None
        rows, came = yield [rows, came]
        rows = jnp.concatenate([rows, came])
    return rows


class Order:
    def __init__(self, sc):
        self.sc = sc
        self.results = {}

    def fence(self, values):
        self.sc, values = lax.optimization_barrier((self.sc, values))
        return values

    def after(self, value):
        self.sc, _ = lax.optimization_barrier((self.sc, value))

    def tick(self, *flows):
        replies = {flow: None for flow in flows if flow not in self.results}
        while replies:
            wants = {}
            for flow, reply in replies.items():
                try:
                    want = flow.send(reply)
                except StopIteration as stop:
                    self.results[flow] = stop.value
                    continue
                if want is not None:
                    wants[flow] = want
            replies = dict(zip(wants, self.fence(list(wants.values())))) if wants else {}

    def finish(self, flow):
        while flow not in self.results:
            self.tick(flow)
        return self.results[flow]


CHUNKS = 3


def fill_other(both, came, core):
    size = came.shape[0]
    return lax.dynamic_update_slice_in_dim(both, came, (1 - core) * size, 0)


def fast_device(
    tokens, condition, counts, w_qkv, b_qv, w_proj, b_proj, w_up, b_up, w_down, b_down, w_mod, b_mod,
    cotangent,
):
    slots, seq, dim = tokens.shape
    images = slots // 2
    count = images * seq
    cols = w_qkv.shape[2]
    ff = w_up.shape[1]
    own_cols = w_mod.shape[1]
    heads = cols // HEAD_DIM
    core = lax.axis_index("mp")
    order = Order(jnp.stack([core, counts[0], lax.axis_index("dp")]).astype(jnp.int32))

    qkv_rows = jnp.transpose(w_qkv, (1, 2, 0)).reshape(3 * cols, dim)
    wq = [qkv_rows, swap_cores(qkv_rows)]
    wp = [w_proj, swap_cores(w_proj)]
    qkv_bias = [b_qv, swap_cores(b_qv)]

    cond_f = condition.astype(f32)
    scaled = jax.nn.silu(cond_f).astype(bf16)
    own_mod = jnp.dot(scaled, w_mod, preferred_element_type=f32) + b_mod.astype(f32)
    other_mod = swap_cores(own_mod)
    sides = [jnp.where(core == side, own_mod, other_mod) for side in range(2)]
    modulation = jnp.concatenate(sides, axis=1).reshape(slots, 6, dim)
    proj_bias = b_proj.astype(f32)[None]
    down_bias = b_down.astype(f32)[None]

    late_up, late_down, late_bias = lax.optimization_barrier((wq[1], w_up, w_down, b_up, modulation))[1:4]
    wu = [w_up, swap_cores(late_up)]
    wd = [w_down, swap_cores(late_down)]
    up_bias = [b_up[None], swap_cores(late_bias[None])]

    local = lambda i, s: (s[0] * images + i, 0, 0)
    mine = lambda i, s: (i, 0, 0)
    tok_spec = pl.BlockSpec((1, seq, dim), local)
    own_spec = pl.BlockSpec((1, seq, dim), mine)
    mod_spec = pl.BlockSpec((1, 6, dim), local)
    row_spec = pl.BlockSpec((1, 1, dim), mine)
    qkv_spec = pl.BlockSpec((1, 6 * cols, seq), mine)
    prob_spec = pl.BlockSpec((1, 2 * heads, seq, seq), lambda i, s: (i, 0, 0, 0))
    mixed_spec = pl.BlockSpec((1, 2 * cols, seq), mine)
    token_f = shape_of((images, seq, dim), f32)
    token_b = shape_of((images, seq, dim), bf16)
    attn_args = wq + wp + qkv_bias
    qkv, prob, mixed, attn_out, residual, normed_mlp, normed, grad_mlp, down_sums = run_kernel(
        functools.partial(attention_kernel, 2, images),
        order.sc,
        [tokens, cotangent, modulation, proj_bias] + attn_args,
        [tok_spec, tok_spec, mod_spec, whole_block(proj_bias)] + [whole_block(a) for a in attn_args],
        [qkv_spec, prob_spec, mixed_spec] + [own_spec] * 5 + [row_spec],
        [
            shape_of((images, 6 * cols, seq), bf16),
            shape_of((images, 2 * heads, seq, seq), bf16),
            shape_of((images, 2 * cols, seq), bf16),
            token_f,
            token_f,
            token_b,
            token_b,
            token_b,
            shape_of((images, 1, dim), f32),
        ],
        (images,),
        33,
    )
    order.after(down_sums)

    rows_flat = normed_mlp.reshape(count, dim)
    grad_flat = grad_mlp.reshape(count, dim)
    width = ff // CHUNKS
    per = width // 16
    steps = 2
    block = width // steps
    anywhere = pl.BlockSpec(memory_space=pl.ANY)
    act = back = jnp.zeros((8, 128), bf16)
    up_sums = {}

    def mlp_call(jobs, came, micros):
        nonlocal act, back
        first = act.shape[0] == 8
        kinds = tuple((("plain", "mixed", "cut")[job[0]], job in came) for job in jobs)

        def turn(k):
            return lambda p, s, c: jnp.clip((p - k) * steps + s, 0, steps - 1)

        def pick(values):
            return lambda p: sum(jnp.where(p == k, value, 0) for k, value in enumerate(values))

        parts = pick([part for _, part in jobs])
        starts = pick([chunk * steps for chunk, _ in jobs])
        spread = pl.BlockSpec((1, block, count), lambda p, s, c: (parts(p), starts(p) + s, 0))
        args, specs = [], []
        for k, (chunk, part) in enumerate(jobs):
            at = chunk * steps
            wide = lambda p, s, c, k=k, at=at: (0, at + turn(k)(p, s, c))
            tall = lambda p, s, c, k=k, at=at: (at + turn(k)(p, s, c), 0)
            args += [wu[part], wd[part], up_bias[part]]
            specs += [
                pl.BlockSpec((dim, block), wide),
                pl.BlockSpec((block, dim), tall),
                pl.BlockSpec((1, block), wide),
            ]
        grad_specs, grad_shapes, sizes = [], [], []
        for k, (kind, _) in enumerate(kinds):
            own = lambda p, s, c, k=k: (turn(k)(p, s, c), 0, 0)
            fixed = lambda p, s, c: (0, 0, 0)
            tall = per if kind == "mixed" else 2 * per
            plain = [] if kind == "cut" else [dim]
            split = [] if kind == "plain" else [hi - lo for lo, hi in columns(MLP_WAYS)]
            grad_specs.append(
                [pl.BlockSpec((16 // steps, tall, wide), own) for wide in plain]
                + [pl.BlockSpec((16, tall, wide), fixed) for wide in split]
            )
            grad_shapes += [shape_of((16, tall, wide), bf16) for wide in plain + split]
            sizes.append(len(plain + split))
        for k, job in enumerate(jobs):
            if job in came:
                args.append(came[job])
                specs.append(grad_specs[k][0])
        args += [act, back]
        spot = len(args) + 1
        outs = run_kernel(
            functools.partial(mlp_kernel, per, columns(MLP_WAYS), kinds),
            order.sc,
            [rows_flat, grad_flat] + args,
            [whole_block(rows_flat), whole_block(grad_flat)] + specs + [anywhere, anywhere],
            [spread, spread]
            + [spec for specs in grad_specs for spec in specs]
            + [pl.BlockSpec((1, block), lambda p, s, c, k=k: (0, turn(k)(p, s, c))) for k in range(len(jobs))],
            [shape_of((2, ff, count), bf16)] * 2 + grad_shapes + [shape_of((1, width), f32)] * len(jobs),
            (len(jobs), steps),
            micros,
            alias=None if first else {spot: 0, spot + 1: 1},
        )
        act, back = outs[:2]
        grads, outs = list(outs[2 : 2 + sum(sizes)]), outs[2 + sum(sizes) :]
        up_sums.update(zip(jobs, outs))
        order.after(outs[-1])
        return [[grads.pop(0) for _ in range(size)] for size in sizes]

    (other_0,), (other_1, *rest_1) = mlp_call([(0, 1), (1, 1)], {}, 26)
    swaps = [swap_flow(other_0), swap_flow(other_1)]
    order.tick(*swaps)
    others, own_2 = mlp_call([(2, 1), (2, 0)], {}, 26)
    made_rest = []
    flow = sum_flow(MLP_WAYS, lambda: made_rest, [list(pair) for pair in zip(others, rest_1)])
    flows = [flow]
    order.tick(*swaps, flow)
    came = {(chunk, 0): order.results[swap] for chunk, swap in enumerate(swaps)}
    (sum_0,), (sum_1, *own_1) = mlp_call([(0, 0), (1, 0)], came, 26)
    made_rest += [list(pair) for pair in zip(own_2, own_1)]
    plain_sums = lax.psum([sum_0, sum_1], "dp")
    order.tick(flow)

    reach = 768
    turns = ff // reach
    every = lambda s, c: (0, 0, 0)
    tail = lambda first: lambda s, c: (jnp.maximum(s - first, 0), 0, 0)
    tail_local = lambda first: lambda s, c: (c[0] * images + jnp.maximum(s - first, 0), 0, 0)

    def image_spec(first, where=tail):
        return pl.BlockSpec((1, seq, dim), where(first))

    def rows_of(part, size):
        if part == 0:
            return lambda s, c: jnp.minimum(s, size - 1)
        return lambda s, c: jnp.clip(s - size, 0, size - 1)

    span_spec = pl.BlockSpec(
        (1, reach, count),
        lambda s, c: (jnp.minimum(s // turns, 1), jnp.where(s < 2 * turns, s % turns, turns - 1), 0),
    )
    grad_residual, grad_attn, mid_sums = run_kernel(
        functools.partial(norm_back_kernel, turns, images),
        order.sc,
        [back] + wu + [residual, cotangent, modulation, attn_out],
        [
            span_spec,
            pl.BlockSpec((dim, reach), lambda s, c: (0, rows_of(0, turns)(s, c))),
            pl.BlockSpec((dim, reach), lambda s, c: (0, rows_of(1, turns)(s, c))),
            image_spec(2 * turns),
            image_spec(2 * turns, tail_local),
            pl.BlockSpec((1, 6, dim), tail_local(2 * turns)),
            image_spec(2 * turns),
        ],
        [image_spec(2 * turns)] * 2 + [pl.BlockSpec((1, 4, dim), tail(2 * turns))],
        [token_f, token_b, shape_of((images, 4, dim), f32)],
        (2 * turns + images,),
        60,
        scratch=[pltpu.VMEM((count, dim), f32)],
    )
    order.after(mid_sums)
    order.tick(*flows)
    pieces = 2
    each = images // pieces
    grad_qkv = []
    for piece in range(pieces):
        there = lambda i, s, piece=piece: (piece * each + i, 0, 0)
        (grad_piece,) = run_kernel(
            functools.partial(back_kernel, 2),
            order.sc,
            [grad_attn, qkv, prob] + wp,
            [
                pl.BlockSpec((1, seq, dim), there),
                pl.BlockSpec((1, 6 * cols, seq), there),
                pl.BlockSpec((1, 2 * heads, seq, seq), lambda i, s, piece=piece: (piece * each + i, 0, 0, 0)),
            ]
            + [whole_block(a) for a in wp],
            [qkv_spec],
            [shape_of((each, 6 * cols, seq), bf16)],
            (each,),
            60,
            scratch=[pltpu.VMEM((2 * cols, seq), bf16)],
            )
        grad_qkv.append(grad_piece)
        order.after(grad_piece)
        order.tick(*flows)

    attn_per = 4 * cols // 16
    qv_sums = [None, None]

    def attn_part(part):
        *grads, sums = run_kernel(
            functools.partial(attn_grad_kernel, pieces, attn_per, columns(ATTN_WAYS)),
            order.sc,
            grad_qkv + [mixed, normed, grad_attn],
            [
                pl.BlockSpec((each, cols, seq), lambda s, c: (0, 3 * part + jnp.minimum(s, 2), 0))
                for _ in range(pieces)
            ]
            + [pl.BlockSpec((images, cols, seq), lambda s, c: (0, part, 0))]
            + [whole_block(normed), whole_block(grad_attn)],
            [pl.BlockSpec((16, attn_per, hi - lo), every) for lo, hi in columns(ATTN_WAYS)]
            + [pl.BlockSpec((1, 1, cols), lambda s, c: (jnp.minimum(s, 2), 0, 0))],
            [shape_of((16, attn_per, hi - lo), bf16) for lo, hi in columns(ATTN_WAYS)]
            + [shape_of((3, 1, cols), f32)],
            (4,),
            60,
            )
        qv_sums[part] = sums
        order.after(sums)
        return grads

    grad_other = attn_part(1)
    made = []
    last = sum_flow(ATTN_WAYS, lambda: [[a] for a in made[0]], [[a] for a in grad_other])
    order.tick(last, *flows)
    made.append(attn_part(0))
    order.tick(last, *flows)

    first_spec = lambda part: pl.BlockSpec((cols, dim), lambda s, c: (rows_of(part, 3)(s, c), 0))
    grad_tokens, grad_own_tokens, low_sums = run_kernel(
        functools.partial(first_back_kernel, pieces, images),
        order.sc,
        grad_qkv + wq + [tokens, modulation, grad_residual],
        [pl.BlockSpec((each, cols, seq), lambda s, c: (0, jnp.minimum(s, 5), 0)) for _ in range(pieces)]
        + [first_spec(0), first_spec(1)]
        + [image_spec(6, tail_local), pl.BlockSpec((1, 6, dim), tail_local(6)), image_spec(6)],
        [image_spec(6, tail_local), image_spec(6), pl.BlockSpec((1, 2, dim), tail(6))],
        [shape_of((slots, seq, dim), f32), token_f, shape_of((images, 2, dim), f32)],
        (6 + images,),
        60,
        scratch=[pltpu.VMEM((count, dim), f32)],
    )
    order.after(low_sums)
    order.tick(last, *flows)
    down_spec = lambda part: pl.BlockSpec((reach, dim), lambda s, c: (rows_of(part, turns)(s, c), 0))
    output, own_output, gate_sums = run_kernel(
        functools.partial(output_kernel, turns, images),
        order.sc,
        [act] + wd + [residual, cotangent, modulation, down_bias],
        [
            span_spec,
            down_spec(0),
            down_spec(1),
            image_spec(2 * turns),
            image_spec(2 * turns, tail_local),
            pl.BlockSpec((1, 6, dim), tail_local(2 * turns)),
            whole_block(down_bias),
        ],
        [image_spec(2 * turns, tail_local), image_spec(2 * turns), pl.BlockSpec((1, 1, dim), tail(2 * turns))],
        [shape_of((slots, seq, dim), bf16), token_b, shape_of((images, 1, dim), f32)],
        (2 * turns + images,),
        60,
        scratch=[pltpu.VMEM((count, dim), f32)],
    )
    order.after(gate_sums)
    order.tick(last, *flows)

    low_sums, mid_sums, gate_sums, down_sums, qv_sums, up_sums, scaled_rows = order.fence(
        (low_sums, mid_sums, gate_sums, down_sums, qv_sums, up_sums, scaled)
    )
    grad_modulation = jnp.concatenate([low_sums, mid_sums[:, 2:3], mid_sums[:, 0:2], gate_sums], axis=1)
    grad_modulation = grad_modulation.reshape(images, 6 * dim).astype(bf16)
    bias_sums = [
        jnp.concatenate(
            [qv_sums[part][0], qv_sums[part][2]]
            + [up_sums[chunk, part] for chunk in range(CHUNKS)],
            axis=1,
        )
        for part in range(2)
    ]
    shared = jnp.concatenate(
        [
            jnp.sum(mid_sums[:, 3], axis=0, keepdims=True),
            jnp.sum(down_sums[:, 0], axis=0, keepdims=True),
            jnp.zeros((1, own_cols - 2 * dim), f32),
        ],
        axis=1,
    )
    halves = grad_modulation.reshape(images, 2, own_cols)
    kept = lax.dynamic_index_in_dim(halves, core, 1, keepdims=False)
    given = lax.dynamic_index_in_dim(halves, 1 - core, 1, keepdims=False)
    got = swap_cores(jnp.concatenate([given.astype(f32), bias_sums[1], shared]))
    came = got[:images].astype(bf16)
    group_mod = jnp.where(core == 0, jnp.concatenate([kept, came]), jnp.concatenate([came, kept]))
    own_bias_sum = bias_sums[0] + got[images : images + 1]
    shared_sum = shared + got[images + 1 :]
    wide_scaled = jnp.pad(scaled_rows.reshape(-1), (0, 3 * own_cols - slots * dim)).reshape(3, own_cols)
    packed_rows = jnp.concatenate(
        [group_mod, own_bias_sum.astype(bf16), shared_sum.astype(bf16), wide_scaled]
    )
    (packed_rows,) = order.fence([packed_rows])
    small = rows_flow(packed_rows)
    order.tick(last, small)
    (group_mod,) = order.fence([group_mod])
    part_scaled = outer_cols(group_mod, w_mod).astype(bf16)
    order.after(part_scaled[0, :1])
    order.tick(last, small, *flows)
    own_output, part_scaled = order.fence((own_output, part_scaled))
    other_output, came_scaled = swap_cores(own_output), swap_cores(part_scaled)

    def cuts(ways):
        return tuple((way, lo, hi) for lo, hi, way in ways)

    grad_w_down = grad_w_up = jnp.zeros((8, 128), f32)

    def final_mlp(chunk, body, args):
        nonlocal grad_w_down, grad_w_up
        first = grad_w_down.shape[0] == 8
        spot = len(args) + 1
        grad_w_down, grad_w_up, mark = run_kernel(
            body,
            order.sc,
            list(args) + [grad_w_down, grad_w_up],
            [
                whole_block(a)
                if a.shape[0] == 8
                else pl.BlockSpec((16 // steps,) + a.shape[1:], lambda s, c: (s, 0, 0))
                for a in args
            ]
            + [anywhere, anywhere],
            [
                pl.BlockSpec((block, dim), lambda s, c: (chunk * steps + s, 0)),
                pl.BlockSpec((dim, block), lambda s, c: (0, chunk * steps + s)),
                pl.BlockSpec((8, 128), lambda s, c: (0, 0)),
            ],
            [shape_of((ff, dim), f32), shape_of((dim, ff), f32), shape_of((8, 128), f32)],
            (steps,),
            4,
            scratch=[pltpu.VMEM((block, dim), f32)],
            alias=None if first else {spot: 0, spot + 1: 1},
        )
        order.after(mark)

    final_mlp(2, functools.partial(final_mlp_kernel, cuts(MLP_WAYS), per), order.finish(flow))
    order.tick(last, small)
    other_output, came_scaled, grad_own_tokens = order.fence((other_output, came_scaled, grad_own_tokens))
    other_tokens = swap_cores(grad_own_tokens)
    sum_0, sum_1 = order.fence(plain_sums)
    final_mlp(0, functools.partial(final_plain_kernel, per), [sum_0])
    body = functools.partial(final_mixed_kernel, cuts(MLP_WAYS), per)
    final_mlp(1, body, list(order.finish(flow)) + [sum_1])
    order.tick(last, small)
    output = fill_other(output, other_output, core)
    grad_scaled = part_scaled.astype(f32) + came_scaled.astype(f32)
    _, silu_back = jax.vjp(jax.nn.silu, cond_f)
    grad_condition = silu_back(grad_scaled)[0]
    order.after((output[0, 0, :1], grad_condition[0, :1]))
    order.tick(last)
    grad_tokens = fill_other(grad_tokens, order.fence(other_tokens), core)
    order.after(grad_tokens[0, 0, :1])
    all_rows = order.fence(order.finish(small)).reshape(16, slots + 5, own_cols)
    all_mod = all_rows[:, :slots].reshape(-1, own_cols)
    all_scaled = all_rows[:, slots + 2 :].reshape(16, -1)[:, : slots * dim].reshape(-1, dim)
    grad_w_mod = inner_rows(all_scaled, all_mod)
    grad_b_mod = jnp.sum(all_mod.astype(f32), axis=0)
    bias_total = jnp.sum(all_rows[:, slots : slots + 2].astype(f32), axis=0)
    grad_b_qv = bias_total[0, : 2 * cols].reshape(2, cols)
    grad_b_up = bias_total[0, 2 * cols :]
    grad_b_proj = bias_total[1, :dim]
    grad_b_down = bias_total[1, dim : 2 * dim]
    order.after((grad_w_mod[0, :1], grad_b_mod[:1], bias_total[0, :1]))
    args = order.finish(last)
    grad_qkv_rows, grad_w_proj = run_kernel(
        functools.partial(final_attn_kernel, cuts(ATTN_WAYS), attn_per),
        order.sc,
        list(args),
        [whole_block(a) for a in args],
        [
            pl.BlockSpec((cols, dim), lambda s, c: (jnp.minimum(s, 2), 0)),
            pl.BlockSpec((cols, dim), lambda s, c: (0, 0)),
        ],
        [shape_of((3 * cols, dim), f32), shape_of((cols, dim), f32)],
        (4,),
        9,
    )
    grad_w_qkv = jnp.transpose(grad_qkv_rows.reshape(3, cols, dim), (2, 0, 1))
    return (
        output,
        grad_tokens,
        grad_condition,
        grad_w_qkv,
        grad_b_qv,
        grad_w_proj,
        grad_b_proj,
        grad_w_up,
        grad_b_up,
        grad_w_down,
        grad_b_down,
        grad_w_mod,
        grad_b_mod,
    )


def layer_norm(values):
    center = values - jnp.mean(values, axis=-1, keepdims=True)
    return center * lax.rsqrt(jnp.mean(center * center, axis=-1, keepdims=True) + epsilon)


def modulate(values, shift_part, scale_part):
    return layer_norm(values) * (1.0 + scale_part) + shift_part


def gelu_tanh(values):
    return (
        0.5
        * values
        * (1.0 + jnp.tanh(0.7978845608028654 * (values + 0.044715 * values * values * values)))
    )


def inner_rows(left, right):
    return lax.dot_general(
        left, right, (((0,), (0,)), ((), ())), preferred_element_type=jnp.float32
    )


def outer_cols(left, right):
    return lax.dot_general(
        left, right, (((1,), (1,)), ((), ())), preferred_element_type=jnp.float32
    )


def attention_forward(query_rows, key_rows, value_rows):
    factor = HEAD_DIM ** (-0.5)
    scores = (
        jnp.einsum("bqhd,bkhd->bhqk", query_rows, key_rows, preferred_element_type=jnp.float32)
        * factor
    )
    row_max = jnp.max(scores, axis=-1, keepdims=True)
    row_total = jnp.sum(jnp.exp(scores - row_max), axis=-1, keepdims=True)
    logsum = row_max + jnp.log(row_total)
    prob_b = jnp.exp(scores - logsum).astype(jnp.bfloat16)
    mixed_out = jnp.einsum(
        "bhqk,bkhd->bqhd", prob_b, value_rows, preferred_element_type=jnp.float32
    )
    return (mixed_out, logsum)


def attention_backward(query_rows, key_rows, value_rows, logsum, grad_mixed):
    factor = HEAD_DIM ** (-0.5)
    scores = (
        jnp.einsum("bqhd,bkhd->bhqk", query_rows, key_rows, preferred_element_type=jnp.float32)
        * factor
    )
    prob_f = jnp.exp(scores - logsum)
    prob_b = prob_f.astype(jnp.bfloat16)
    grad_prob = jnp.einsum(
        "bqhd,bkhd->bhqk", grad_mixed, value_rows, preferred_element_type=jnp.float32
    )
    row_delta = jnp.sum(prob_f * grad_prob, axis=-1, keepdims=True)
    grad_scores = (prob_f * (grad_prob - row_delta)).astype(jnp.bfloat16)
    grad_query = (
        jnp.einsum("bhqk,bkhd->bqhd", grad_scores, key_rows, preferred_element_type=jnp.float32)
        * factor
    )
    grad_key = (
        jnp.einsum("bhqk,bqhd->bkhd", grad_scores, query_rows, preferred_element_type=jnp.float32)
        * factor
    )
    grad_value = jnp.einsum(
        "bhqk,bqhd->bkhd", prob_b, grad_mixed, preferred_element_type=jnp.float32
    )
    return (
        grad_query.astype(jnp.bfloat16),
        grad_key.astype(jnp.bfloat16),
        grad_value.astype(jnp.bfloat16),
    )


def forward(tokens_f, spans, weights, repeat):
    w_qkv, b_qv, w_proj, b_proj, w_up, b_up, w_down, b_down = weights
    shift_attn, scale_attn, gate_attn, shift_mlp, scale_mlp, gate_mlp = spans
    slot_count, seq_len, model_dim = tokens_f.shape
    row_count = slot_count * seq_len
    head_cols = w_qkv.shape[2]
    head_count = head_cols // HEAD_DIM
    shape_four = (slot_count, seq_len, head_count, HEAD_DIM)
    normed = (
        modulate(tokens_f, shift_attn, scale_attn)
        .astype(jnp.bfloat16)
        .reshape(row_count, model_dim)
    )
    projected = jnp.dot(
        normed, w_qkv.reshape(model_dim, 3 * head_cols), preferred_element_type=jnp.float32
    )
    qkv_bias = jnp.stack([b_qv[0], jnp.zeros_like(b_qv[0]), b_qv[1]]).astype(jnp.float32)
    projected = (projected.reshape(row_count, 3, head_cols) + qkv_bias).astype(jnp.bfloat16)
    query_rows = projected[:, 0].reshape(shape_four)
    key_rows = projected[:, 1].reshape(shape_four)
    value_rows = projected[:, 2].reshape(shape_four)
    mixed_out, logsum = attention_forward(query_rows, key_rows, value_rows)
    mixed_b = mixed_out.astype(jnp.bfloat16).reshape(row_count, head_cols)
    partial_value = jnp.dot(mixed_b, w_proj, preferred_element_type=jnp.float32)
    if repeat:
        summed = lax.psum(partial_value.astype(jnp.bfloat16), "mp").astype(jnp.float32)
    else:
        summed = lax.psum(partial_value.astype(jnp.bfloat16), "mp").astype(jnp.float32)
    attn_out = (summed + b_proj.astype(jnp.float32)).reshape(slot_count, seq_len, model_dim)
    residual = tokens_f + gate_attn * attn_out
    normed_mlp = (
        modulate(residual, shift_mlp, scale_mlp).astype(jnp.bfloat16).reshape(row_count, model_dim)
    )
    hidden = jnp.dot(normed_mlp, w_up, preferred_element_type=jnp.float32) + b_up.astype(
        jnp.float32
    )
    act_bf = gelu_tanh(hidden).astype(jnp.bfloat16)
    partial_mlp = jnp.dot(act_bf, w_down, preferred_element_type=jnp.float32)
    if repeat:
        summed_mlp = lax.psum(partial_mlp.astype(jnp.bfloat16), "mp").astype(jnp.float32)
    else:
        summed_mlp = lax.psum(partial_mlp.astype(jnp.bfloat16), "mp").astype(jnp.float32)
    mlp_out = (summed_mlp + b_down.astype(jnp.float32)).reshape(slot_count, seq_len, model_dim)
    output = residual + gate_mlp * mlp_out
    return {
        "normed": normed,
        "query_rows": query_rows,
        "key_rows": key_rows,
        "value_rows": value_rows,
        "logsum": logsum,
        "mixed_b": mixed_b,
        "attn_out": attn_out,
        "residual": residual,
        "normed_mlp": normed_mlp,
        "hidden": hidden,
        "act_bf": act_bf,
        "mlp_out": mlp_out,
        "output": output,
    }


def image_pass(tokens_f, grad_out, spans, weights):
    w_qkv, b_qv, w_proj, b_proj, w_up, b_up, w_down, b_down = weights
    shift_attn, scale_attn, gate_attn, shift_mlp, scale_mlp, gate_mlp = spans
    slot_count, seq_len, model_dim = tokens_f.shape
    row_count = slot_count * seq_len
    head_cols = w_qkv.shape[2]
    head_count = head_cols // HEAD_DIM
    kept_fwd = forward(tokens_f, spans, weights, False)
    out_one = kept_fwd["output"]
    stored = forward(tokens_f, spans, weights, True)
    grad_gate_mlp = jnp.sum(grad_out * stored["mlp_out"], axis=1)
    grad_mlp = (gate_mlp * grad_out).astype(jnp.bfloat16).reshape(row_count, model_dim)
    grad_b_down = jnp.sum(grad_mlp.astype(jnp.float32), axis=0)
    grad_w_down = inner_rows(stored["act_bf"], grad_mlp)
    grad_act = outer_cols(grad_mlp, w_down)
    gelu_value, gelu_back = jax.vjp(gelu_tanh, stored["hidden"])
    grad_hidden = gelu_back(grad_act)[0].astype(jnp.bfloat16)
    grad_b_up = jnp.sum(grad_hidden.astype(jnp.float32), axis=0)
    grad_w_up = inner_rows(stored["normed_mlp"], grad_hidden)
    part_normed_mlp = outer_cols(grad_hidden, w_up)
    grad_normed_mlp = (
        lax.psum(part_normed_mlp.astype(jnp.bfloat16), "mp")
        .astype(jnp.float32)
        .reshape(slot_count, seq_len, model_dim)
    )
    norm_value, norm_back = jax.vjp(modulate, stored["residual"], shift_mlp, scale_mlp)
    grad_resid_norm, grad_shift_mlp, grad_scale_mlp = norm_back(grad_normed_mlp)
    grad_residual = grad_out + grad_resid_norm
    grad_gate_attn = jnp.sum(grad_residual * stored["attn_out"], axis=1)
    grad_attn = (gate_attn * grad_residual).astype(jnp.bfloat16).reshape(row_count, model_dim)
    grad_b_proj = jnp.sum(grad_attn.astype(jnp.float32), axis=0)
    grad_w_proj = inner_rows(stored["mixed_b"], grad_attn)
    grad_mixed = (
        outer_cols(grad_attn, w_proj)
        .astype(jnp.bfloat16)
        .reshape(slot_count, seq_len, head_count, HEAD_DIM)
    )
    grad_query, grad_key, grad_value = attention_backward(
        stored["query_rows"], stored["key_rows"], stored["value_rows"], stored["logsum"], grad_mixed
    )
    grad_qkv = jnp.stack(
        [
            grad_query.reshape(row_count, head_cols),
            grad_key.reshape(row_count, head_cols),
            grad_value.reshape(row_count, head_cols),
        ],
        axis=1,
    )
    grad_b_qv = jnp.stack(
        [
            jnp.sum(grad_qkv[:, 0].astype(jnp.float32), axis=0),
            jnp.sum(grad_qkv[:, 2].astype(jnp.float32), axis=0),
        ]
    )
    grad_w_qkv = inner_rows(stored["normed"], grad_qkv)
    part_normed = outer_cols(
        grad_qkv.reshape(row_count, 3 * head_cols), w_qkv.reshape(model_dim, 3 * head_cols)
    )
    grad_normed = (
        lax.psum(part_normed.astype(jnp.bfloat16), "mp")
        .astype(jnp.float32)
        .reshape(slot_count, seq_len, model_dim)
    )
    first_value, first_back = jax.vjp(modulate, tokens_f, shift_attn, scale_attn)
    grad_tok_norm, grad_shift_attn, grad_scale_attn = first_back(grad_normed)
    grad_tok_one = grad_residual + grad_tok_norm
    grad_mod_one = jnp.concatenate(
        [
            grad_shift_attn[:, 0],
            grad_scale_attn[:, 0],
            grad_gate_attn,
            grad_shift_mlp[:, 0],
            grad_scale_mlp[:, 0],
            grad_gate_mlp,
        ],
        axis=1,
    )
    grad_terms = (
        grad_w_qkv,
        grad_b_qv,
        grad_w_proj,
        grad_b_proj,
        grad_w_up,
        grad_b_up,
        grad_w_down,
        grad_b_down,
    )
    return (out_one, grad_tok_one, grad_mod_one, grad_terms)


def run_layer(tokens, condition, cotangent, live_count, turns, weights, w_mod, b_mod):
    slot_count, seq_len, model_dim = tokens.shape
    cond_f = condition.astype(jnp.float32)
    scaled = jax.nn.silu(cond_f).astype(jnp.bfloat16)
    own_mod = jnp.dot(scaled, w_mod, preferred_element_type=jnp.float32) + b_mod.astype(jnp.float32)
    modulation = lax.all_gather(own_mod, "mp", axis=1, tiled=True)
    tokens_f = tokens.astype(jnp.float32)
    cot_f = cotangent.astype(jnp.float32)

    def image_step(slot_idx, carry):
        out_buf, grad_buf, mod_buf, grad_sums = carry
        live_flag = (slot_idx < live_count).astype(jnp.float32)
        tok_one = lax.dynamic_slice_in_dim(tokens_f, slot_idx, 1, 0)
        cot_one = lax.dynamic_slice_in_dim(cot_f, slot_idx, 1, 0) * live_flag
        mod_row = lax.dynamic_slice_in_dim(modulation, slot_idx, 1, 0)
        spans = [
            mod_row[:, None, part_idx * model_dim : (part_idx + 1) * model_dim]
            for part_idx in range(6)
        ]
        out_one, grad_tok_one, grad_mod_one, grad_terms = image_pass(
            tok_one, cot_one, spans, weights
        )
        out_one = (out_one * live_flag).astype(jnp.bfloat16)
        out_buf = lax.dynamic_update_slice_in_dim(out_buf, out_one, slot_idx, 0)
        grad_buf = lax.dynamic_update_slice_in_dim(grad_buf, grad_tok_one, slot_idx, 0)
        mod_buf = lax.dynamic_update_slice_in_dim(mod_buf, grad_mod_one, slot_idx, 0)
        grad_sums = tuple((total_a + term_b for total_a, term_b in zip(grad_sums, grad_terms)))
        return (out_buf, grad_buf, mod_buf, grad_sums)

    start_sums = tuple((jnp.zeros(weight_in.shape, jnp.float32) for weight_in in weights))
    start_state = (
        jnp.zeros(tokens.shape, jnp.bfloat16),
        jnp.zeros(tokens.shape, jnp.float32),
        jnp.zeros((slot_count, 6 * model_dim), jnp.float32),
        start_sums,
    )
    out_buf, grad_buf, mod_buf, grad_sums = lax.fori_loop(0, turns, image_step, start_state)
    grad_modulation = mod_buf.astype(jnp.bfloat16)
    own_cols = w_mod.shape[1]
    grad_own = lax.dynamic_slice_in_dim(
        grad_modulation, lax.axis_index("mp") * own_cols, own_cols, 1
    )
    part_scaled = outer_cols(grad_own, w_mod)
    grad_scaled = lax.psum(part_scaled.astype(jnp.bfloat16), "mp").astype(jnp.float32)
    silu_value, silu_back = jax.vjp(jax.nn.silu, cond_f)
    grad_condition = silu_back(grad_scaled)[0]
    return (out_buf, grad_buf, grad_condition, grad_sums, scaled, grad_own)


def on_device(
    tokens,
    condition,
    counts,
    w_qkv,
    b_qv,
    w_proj,
    b_proj,
    w_up,
    b_up,
    w_down,
    b_down,
    w_mod,
    b_mod,
    cotangent,
):
    slot_count, seq_len, model_dim = tokens.shape
    weights = (w_qkv, b_qv, w_proj, b_proj, w_up, b_up, w_down, b_down)
    own_count = counts[0]
    output, grad_tokens, grad_condition, grad_sums, scaled, grad_own = run_layer(
        tokens, condition, cotangent, own_count, slot_count, weights, w_mod, b_mod
    )
    (
        grad_w_qkv,
        grad_b_qv,
        grad_w_proj,
        grad_b_proj,
        grad_w_up,
        grad_b_up,
        grad_w_down,
        grad_b_down,
    ) = grad_sums
    grad_w_mod = inner_rows(scaled, grad_own)
    grad_b_mod = jnp.sum(grad_own.astype(jnp.float32), axis=0)
    (
        grad_w_qkv,
        grad_b_qv,
        grad_w_proj,
        grad_b_proj,
        grad_w_up,
        grad_b_up,
        grad_w_down,
        grad_b_down,
        grad_w_mod,
        grad_b_mod,
    ) = (
        lax.psum(grad_w_qkv.astype(jnp.bfloat16), "dp").astype(jnp.float32),
        lax.psum(grad_b_qv.astype(jnp.bfloat16), "dp").astype(jnp.float32),
        lax.psum(grad_w_proj.astype(jnp.bfloat16), "dp").astype(jnp.float32),
        lax.psum(grad_b_proj.astype(jnp.bfloat16), "dp").astype(jnp.float32),
        lax.psum(grad_w_up.astype(jnp.bfloat16), "dp").astype(jnp.float32),
        lax.psum(grad_b_up.astype(jnp.bfloat16), "dp").astype(jnp.float32),
        lax.psum(grad_w_down.astype(jnp.bfloat16), "dp").astype(jnp.float32),
        lax.psum(grad_b_down.astype(jnp.bfloat16), "dp").astype(jnp.float32),
        lax.psum(grad_w_mod.astype(jnp.bfloat16), "dp").astype(jnp.float32),
        lax.psum(grad_b_mod.astype(jnp.bfloat16), "dp").astype(jnp.float32),
    )
    return (
        output,
        grad_tokens,
        grad_condition,
        grad_w_qkv,
        grad_b_qv,
        grad_w_proj,
        grad_b_proj,
        grad_w_up,
        grad_b_up,
        grad_w_down,
        grad_b_down,
        grad_w_mod,
        grad_b_mod,
    )


def solution(mesh):
    placed = (
        P("dp", None, None),
        P("dp", None),
        P("dp"),
        P(None, None, "mp"),
        P(None, "mp"),
        P("mp", None),
        P(),
        P(None, "mp"),
        P("mp"),
        P("mp", None),
        P(),
        P(None, "mp"),
        P("mp"),
        P("dp", None, None),
    )
    fast = mesh.shape["dp"] == 16 and mesh.shape["mp"] == 2
    return jax.shard_map(
        fast_device if fast else on_device,
        mesh=mesh,
        in_specs=placed,
        out_specs=(
            P("dp", None, None),
            P("dp", None, None),
            P("dp", None),
            P(None, None, "mp"),
            P(None, "mp"),
            P("mp", None),
            P(),
            P(None, "mp"),
            P("mp"),
            P("mp", None),
            P(),
            P(None, "mp"),
            P("mp"),
        ),
        check_vma=False,
    )
```

```python
import functools

import jax
import jax.numpy as jnp
from jax import lax
from jax.experimental import pallas as pl
from jax.experimental.pallas import tpu as pltpu
from jax.sharding import PartitionSpec as P

HEAD_DIM = 72
LOG2_E = 1.4426950408889634


epsilon = 1e-06

f32 = jnp.float32
bf16 = jnp.bfloat16


def dot_nn(left, right):
    return lax.dot_general(left, right, (((1,), (0,)), ((), ())), preferred_element_type=f32)


def dot_nt(left, right):
    return lax.dot_general(left, right, (((1,), (1,)), ((), ())), preferred_element_type=f32)


def dot_tn(left, right):
    return lax.dot_general(left, right, (((0,), (0,)), ((), ())), preferred_element_type=f32)


def normalize(values):
    center = values - jnp.mean(values, axis=-1, keepdims=True)
    recip = lax.rsqrt(jnp.mean(center * center, axis=-1, keepdims=True) + epsilon)
    return center * recip, recip


def norm_pullback(grad_normed, unit, recip, scale_row):
    scaled_grad = grad_normed * (1.0 + scale_row)
    mean_grad = jnp.mean(scaled_grad, axis=-1, keepdims=True)
    mean_unit = jnp.mean(scaled_grad * unit, axis=-1, keepdims=True)
    return recip * (scaled_grad - mean_grad - unit * mean_unit)


def column(row):
    return jnp.broadcast_to(row[...].astype(f32), (8, row.shape[1])).T[:, 0:1]


def head_rows(values, one):
    return values[one * HEAD_DIM : (one + 1) * HEAD_DIM].astype(bf16)


def token_sum(values):
    return jnp.sum(values, axis=0, keepdims=True)


def attention_kernel(parts, own_images, sc, tok, cot, mod, b_proj, *refs):
    w_qkv, w_proj, bias = refs[:parts], refs[parts : 2 * parts], refs[2 * parts : 3 * parts]
    qkv, prob, mixed, attn_out, residual, normed_mlp, normed, grad_mlp, down_sums = refs[3 * parts :]
    image = sc[0] * own_images + pl.program_id(0)
    live = jnp.where(image < sc[1], 1.0, 0.0).astype(f32)
    unit, _ = normalize(tok[0].astype(f32))
    normed[0] = (unit * (1.0 + mod[0, 1:2, :]) + mod[0, 0:1, :]).astype(bf16)
    grad = (mod[0, 5:6, :] * (cot[0].astype(f32) * live)).astype(bf16)
    grad_mlp[0] = grad
    down_sums[0] = token_sum(grad.astype(f32))
    cols = w_proj[0].shape[0]
    pairs = cols // (2 * HEAD_DIM)
    span = 2 * HEAD_DIM
    scale = HEAD_DIM ** (-0.5) * LOG2_E
    rows = normed[0]
    for part in range(parts):
        base = part * 3 * cols
        shift = bias[part][...].astype(f32).T
        for proj in range(3):
            lo = proj * cols
            value = dot_nt(w_qkv[part][lo : lo + cols, :], rows)
            if proj != 1:
                value = value + shift[:, proj // 2 : proj // 2 + 1]
            qkv[0, base + lo : base + lo + cols, :] = value.astype(bf16)

    def load(part, pair):
        at = part * 3 * cols + pair * span
        return [qkv[0, at + k * cols : at + k * cols + span, :].astype(f32) for k in range(3)]

    def score(loaded):
        query, key, _ = loaded
        return [dot_tn(head_rows(key, one), head_rows(query, one)) for one in range(2)]

    def spread(scores, head):
        raised = jnp.exp2((scores - jnp.max(scores, axis=0, keepdims=True)) * scale)
        share = 1.0 / jnp.sum(raised, axis=0, keepdims=True)
        prob_b = (raised * share).astype(bf16)
        prob[0, head] = prob_b
        return prob_b

    def mix(part, pair, loaded, probs):
        outs = [dot_nn(head_rows(loaded[2], one), probs[one]) for one in range(2)]
        to = part * cols + pair * span
        mixed[0, to : to + span, :] = jnp.concatenate(outs, axis=0).astype(bf16)

    work = [(part, pair) for part in range(parts) for pair in range(pairs)]
    loaded = load(*work[0])
    scores = score(loaded)
    waiting = None
    for turn, (part, pair) in enumerate(work):
        after = turn + 1 < len(work)
        if after:
            next_loaded = load(*work[turn + 1])
            next_scores = score(next_loaded)
        probs = [spread(scores[one], part * 2 * pairs + 2 * pair + one) for one in range(2)]
        if waiting is not None:
            mix(*waiting)
        waiting = (part, pair, loaded, probs)
        if after:
            loaded, scores = next_loaded, next_scores
    mix(*waiting)
    total = b_proj[...]
    for part in range(parts):
        total = total + dot_tn(mixed[0, part * cols : (part + 1) * cols, :], w_proj[part][...])
    attn_out[0] = total
    summed = tok[0].astype(f32) + mod[0, 2:3, :] * total
    residual[0] = summed
    unit, _ = normalize(summed)
    normed_mlp[0] = (unit * (1.0 + mod[0, 4:5, :]) + mod[0, 3:4, :]).astype(bf16)


def mlp_kernel(per, jobs, sc, rows, grad_mlp, *refs):
    count = len(jobs)
    weights = [refs[3 * k : 3 * k + 3] for k in range(count)]
    refs = refs[3 * count :]
    came = []
    for _, summed in jobs:
        came.append(refs[0] if summed else None)
        refs = refs[1:] if summed else refs
    act, back = refs[2], refs[3]
    refs = refs[4:]
    grads = []
    for cuts, _ in jobs:
        size = 1 if cuts is None else len(cuts)
        grads.append(refs[:size])
        refs = refs[size:]
    job, step = pl.program_id(0), pl.program_id(1)
    for k in range(count):

        @pl.when(job == k)
        def _(k=k):
            mlp_block(
                per, jobs[k][0], step, sc, rows, grad_mlp, *weights[k], act, back, grads[k], refs[k], came[k]
            )


def mlp_block(per, cuts, step, sc, rows, grad_mlp, w_up, w_down, bias, act, back, grads, sums, came):
    here = w_down.shape[0] // per
    hidden = lax.dot_general(
        w_up[...], rows[...], (((0,), (1,)), ((), ())), preferred_element_type=f32
    ) + column(bias)
    square = hidden * hidden
    bend = jnp.tanh(0.7978845608028654 * hidden * (1.0 + 0.044715 * square))
    half = 0.5 * (1.0 + bend)
    act_b = (hidden * half).astype(bf16)
    slope = half + 0.5 * hidden * (1.0 - bend * bend) * (
        0.7978845608028654 * (1.0 + 3.0 * 0.044715 * square)
    )
    back_b = (dot_nt(w_down[...], grad_mlp[...]) * slope).astype(bf16)
    act[0] = act_b
    back[0] = back_b
    sums[...] = dot_nt(jnp.ones((8, rows.shape[0]), bf16), back_b)[0:1]
    for lo_row, left, right in ((0, act_b, grad_mlp), (per, back_b, rows)):
        grad = dot_nn(left, right[...])
        for piece in range(here):
            value = grad[piece * per : (piece + 1) * per]
            if cuts is None:
                if came is not None:
                    value = value + came[piece, lo_row : lo_row + per, :].astype(f32)
                grads[0][piece, lo_row : lo_row + per, :] = value.astype(bf16)
            else:
                at = jnp.bitwise_xor(step * here + piece, sc[2])
                for (lo, hi), into in zip(cuts, grads):
                    into[at, lo_row : lo_row + per, :] = value[:, lo:hi].astype(bf16)


def grow(total, part_steps, left, rights, dims):
    step = pl.program_id(0)

    def term(right):
        return lax.dot_general(left, right[...], (dims, ((), ())), preferred_element_type=f32)

    @pl.when(step == 0)
    def _():
        total[...] = term(rights[0])

    @pl.when(jnp.logical_and(step > 0, step < part_steps))
    def _():
        total[...] += term(rights[0])

    @pl.when(jnp.logical_and(step >= part_steps, step < 2 * part_steps))
    def _():
        total[...] += term(rights[1])


def norm_back_kernel(
    part_steps, own_images, sc, back, w_up0, w_up1, residual, cot, mod, attn_out,
    grad_residual, grad_attn, sums, total
):
    grow(total, part_steps, back[0], (w_up0, w_up1), ((0,), (1,)))
    one = pl.program_id(0) - 2 * part_steps
    seq = residual.shape[1]

    @pl.when(one >= 0)
    def _():
        live = jnp.where(sc[0] * own_images + one < sc[1], 1.0, 0.0).astype(f32)
        grad_normed = total[pl.ds(pl.multiple_of(one * seq, seq), seq), :]
        unit, recip = normalize(residual[0])
        sums[0, 0:1, :] = token_sum(grad_normed)
        sums[0, 1:2, :] = token_sum(grad_normed * unit)
        grad_res = cot[0].astype(f32) * live + norm_pullback(grad_normed, unit, recip, mod[0, 4:5, :])
        grad_residual[0] = grad_res
        sums[0, 2:3, :] = token_sum(grad_res * attn_out[0])
        grad_att = (mod[0, 2:3, :] * grad_res).astype(bf16)
        grad_attn[0] = grad_att
        sums[0, 3:4, :] = token_sum(grad_att.astype(f32))


def back_kernel(parts, sc, grad_attn, qkv, prob, *refs):
    w_proj = refs[:parts]
    grad_qkv, grad_mixed = refs[parts:]
    cols = w_proj[0].shape[0]
    pairs = cols // (2 * HEAD_DIM)
    span = 2 * HEAD_DIM
    factor = HEAD_DIM ** (-0.5)
    grad_att = grad_attn[0]
    for part in range(parts):
        rows = slice(part * cols, (part + 1) * cols)
        grad_mixed[rows, :] = dot_nt(w_proj[part][...], grad_att).astype(bf16)

    def load(part, pair):
        at = part * 3 * cols + pair * span
        mix_at = part * cols + pair * span
        loaded = [qkv[0, at + k * cols : at + k * cols + span, :].astype(f32) for k in range(3)]
        return loaded + [grad_mixed[mix_at : mix_at + span, :].astype(f32)]

    def back_prob(loaded):
        return [dot_tn(head_rows(loaded[2], one), head_rows(loaded[3], one)) for one in range(2)]

    def back_scores(grad_prob, head):
        prob_b = prob[0, head]
        prob_f = prob_b.astype(f32)
        delta = jnp.sum(prob_f * grad_prob, axis=0, keepdims=True)
        return prob_b, (prob_f * (grad_prob - delta)).astype(bf16)

    work = [(part, pair) for part in range(parts) for pair in range(pairs)]
    loaded = load(*work[0])
    grad_probs = back_prob(loaded)
    for turn, (part, pair) in enumerate(work):
        after = turn + 1 < len(work)
        if after:
            next_loaded = load(*work[turn + 1])
            next_probs = back_prob(next_loaded)
        middle = [back_scores(grad_probs[one], part * 2 * pairs + 2 * pair + one) for one in range(2)]
        query, key, _, grads = loaded
        to_query = [dot_nn(head_rows(key, one), middle[one][1]) * factor for one in range(2)]
        to_key = [dot_nt(head_rows(query, one), middle[one][1]) * factor for one in range(2)]
        to_value = [dot_nt(head_rows(grads, one), middle[one][0]) for one in range(2)]
        at = part * 3 * cols + pair * span
        for k, outs in enumerate((to_query, to_key, to_value)):
            into = slice(at + k * cols, at + k * cols + span)
            grad_qkv[0, into, :] = jnp.concatenate(outs, axis=0).astype(bf16)
        if after:
            loaded, grad_probs = next_loaded, next_probs


def attn_grad_kernel(pieces, per, cuts, sc, *refs):
    grad_qkv, mixed, normed, grad_attn = refs[:pieces], refs[pieces], refs[pieces + 1], refs[pieces + 2]
    grads, sums = refs[pieces + 3 : -1], refs[-1]
    step = pl.program_id(0)
    here = mixed.shape[1] // per
    images = mixed.shape[0]
    each = images // pieces

    def spread(total):
        total = total.astype(bf16)
        for piece in range(here):
            at = jnp.bitwise_xor(step * here + piece, sc[2])
            for (lo, hi), into in zip(cuts, grads):
                into[at] = total[piece * per : (piece + 1) * per, lo:hi]

    @pl.when(step < 3)
    def _():
        ones = jnp.ones((8, mixed.shape[2]), bf16)
        total = count = None
        for image in range(images):
            left = grad_qkv[image // each][image % each]
            term, one = dot_nn(left, normed[image]), dot_nt(ones, left)
            total = term if image == 0 else total + term
            count = one if image == 0 else count + one
        sums[0] = count[0:1]
        spread(total)

    @pl.when(step == 3)
    def _():
        total = dot_nn(mixed[0], grad_attn[0])
        for image in range(1, images):
            total = total + dot_nn(mixed[image], grad_attn[image])
        spread(total)


def first_back_kernel(pieces, images, sc, *refs):
    grad_qkv = refs[:pieces]
    w_qkv0, w_qkv1, tok, mod, grad_residual = refs[pieces : pieces + 5]
    grad_tokens, grad_own, sums, total = refs[pieces + 5 :]
    step = pl.program_id(0)
    each = images // pieces
    seq = tok.shape[1]

    def add(w_qkv, fresh):
        for one in range(images):
            term = dot_tn(grad_qkv[one // each][one % each], w_qkv[...])
            if fresh:
                total[one * seq : (one + 1) * seq, :] = term
            else:
                total[one * seq : (one + 1) * seq, :] += term

    @pl.when(step == 0)
    def _():
        add(w_qkv0, True)

    @pl.when(jnp.logical_and(step > 0, step < 3))
    def _():
        add(w_qkv0, False)

    @pl.when(jnp.logical_and(step >= 3, step < 6))
    def _():
        add(w_qkv1, False)

    @pl.when(step >= 6)
    def _():
        grad_normed = total[pl.ds(pl.multiple_of((step - 6) * seq, seq), seq), :]
        unit, recip = normalize(tok[0].astype(f32))
        sums[0, 0:1, :] = token_sum(grad_normed)
        sums[0, 1:2, :] = token_sum(grad_normed * unit)
        grad = grad_residual[0] + norm_pullback(grad_normed, unit, recip, mod[0, 1:2, :])
        grad_tokens[0] = grad
        grad_own[0] = grad


def output_kernel(
    part_steps, own_images, sc, act, w_down0, w_down1, residual, cot, mod, b_down, output, own, sums, total
):
    grow(total, part_steps, act[0], (w_down0, w_down1), ((0,), (0,)))
    one = pl.program_id(0) - 2 * part_steps
    seq = residual.shape[1]

    @pl.when(one >= 0)
    def _():
        live = jnp.where(sc[0] * own_images + one < sc[1], 1.0, 0.0).astype(f32)
        mlp_out = total[pl.ds(pl.multiple_of(one * seq, seq), seq), :] + b_down[...]
        sums[0] = token_sum((cot[0].astype(f32) * live) * mlp_out)
        rows = ((residual[0] + mod[0, 5:6, :] * mlp_out) * live).astype(bf16)
        output[0] = rows
        own[0] = rows


def final_piece(sc, halves, piece, store):
    rel = jnp.bitwise_xor(piece, sc[2])
    for low, high, route, lo, hi in halves:
        bits = [(rel >> bit) & 1 for bit in route]
        index = bits[1] * 4 + bits[2] * 2 + bits[3]

        @pl.when(bits[0] == 0)
        def _(low=low, index=index, lo=lo, hi=hi):
            store(low[index].astype(f32), lo, hi)

        @pl.when(bits[0] == 1)
        def _(high=high, index=index, lo=lo, hi=hi):
            store(high[index].astype(f32), lo, hi)


def final_mlp_kernel(cuts, per, sc, *refs):
    count = 2 * len(cuts)
    arrays, (_, _, down, up, mark, turned) = refs[:count], refs[count:]
    here = down.shape[0] // per
    halves = [(arrays[2 * k], arrays[2 * k + 1]) + cut for k, cut in enumerate(cuts)]
    for piece in range(here):

        def store(value, lo, hi, piece=piece):
            down[piece * per : (piece + 1) * per, lo:hi] = value[0:per]
            turned[piece * per : (piece + 1) * per, lo:hi] = value[per : 2 * per]

        final_piece(sc, halves, pl.program_id(0) * here + piece, store)
    up[...] = turned[...].T
    mark[...] = jnp.zeros_like(mark)


def final_plain_kernel(per, sc, summed, down_in, up_in, down, up, mark, turned):
    for piece in range(summed.shape[0]):
        lo = piece * per
        down[lo : lo + per, :] = summed[piece, 0:per, :].astype(f32)
        turned[lo : lo + per, :] = summed[piece, per : 2 * per, :].astype(f32)
    up[...] = turned[...].T
    mark[...] = jnp.zeros_like(mark)


def final_attn_kernel(cuts, per, sc, *refs):
    count = 2 * len(cuts)
    arrays, (qkv, proj) = refs[:count], refs[count:]
    here = proj.shape[0] // per
    halves = [(arrays[2 * k], arrays[2 * k + 1]) + cut for k, cut in enumerate(cuts)]
    for target, wanted in ((qkv, True), (proj, False)):

        @pl.when((pl.program_id(0) < 3) == wanted)
        def _(target=target):
            for piece in range(here):

                def store(value, lo, hi, piece=piece):
                    target[piece * per : (piece + 1) * per, lo:hi] = value

                final_piece(sc, halves, pl.program_id(0) * here + piece, store)


def run_kernel(
    body, sc, args, in_specs, out_specs, out_shape, grid, micros, scratch=(), alias=None, room=60
):
    size = sum(a.size * a.dtype.itemsize for a in args) + sum(
        s.size * s.dtype.itemsize for s in out_shape
    )
    return pl.pallas_call(
        body,
        out_shape=out_shape,
        grid_spec=pltpu.PrefetchScalarGridSpec(
            num_scalar_prefetch=1,
            grid=grid,
            in_specs=in_specs,
            out_specs=out_specs,
            scratch_shapes=list(scratch),
        ),
        compiler_params=pltpu.CompilerParams(vmem_limit_bytes=room << 20),
        cost_estimate=pl.CostEstimate(
            flops=int(micros * 1.15e9), bytes_accessed=int(min(size, micros * 1e6)), transcendentals=0
        ),
        input_output_aliases=alias or {},
    )(sc, *args)


def whole_block(array):
    zeros = (0,) * array.ndim
    return pl.BlockSpec(array.shape, lambda *_: zeros, pipeline_mode=pl.Buffered(1))


def shape_of(dims, kind):
    return jax.ShapeDtypeStruct(dims, kind)


SWAP = [(0, 1), (1, 0)]


def swap_cores(value):
    return lax.ppermute(value, "mp", SWAP)


def bit_pairs(bit):
    return [(index, index ^ (1 << bit)) for index in range(16)]


MLP_WAYS = ((0, 640, (0, 1, 2, 3)), (640, 1152, (1, 0, 2, 3)))
ATTN_WAYS = ((0, 512, (0, 1, 2, 3)), (512, 896, (1, 0, 2, 3)), (896, 1152, (2, 3, 0, 1)))


def columns(ways):
    return tuple((lo, hi) for lo, hi, _ in ways)


def cut(array, bits, bit, side):
    return lax.index_in_dim(array, side, bits.index(bit), keepdims=False)


def left_bits(done):
    return [bit for bit in (3, 2, 1, 0) if bit not in done]


def exchange(values, bits):
    return [lax.ppermute(value, "dp", bit_pairs(bit)) for value, bit in zip(values, bits)]


def reduce_flow(ways, get_own, others):
    others = yield others
    came = [swap_cores(other) for other in others]
    yield None
    own, came = yield [get_own(), came]
    firsts, seconds = ([a.reshape((2, 2, 2, 2) + a.shape[1:]) for a in arrays] for arrays in (own, came))
    routes = [way for _, _, way in ways]
    for stage in range(4):
        sends, keeps = [], []
        for route, one, two in zip(routes, firsts, seconds):
            bits = left_bits(route[:stage])
            for side, into in ((1, sends), (0, keeps)):
                into.append(cut(one, bits, route[stage], side) + cut(two, bits, route[stage], side))
        if stage == 2 and routes[0][2:] == routes[1][2:]:
            sends = [jnp.concatenate(sends[:2], axis=-1)] + sends[2:]
            keeps = [jnp.concatenate(keeps[:2], axis=-1)] + keeps[2:]
            routes = [routes[0]] + routes[2:]
        sends, keeps = yield [sends, keeps]
        comes = exchange(sends, [route[stage] for route in routes])
        yield None
        firsts, seconds = yield [keeps, comes]
    return [one + two for one, two in zip(firsts, seconds)]


def gather_flow(ways, have):
    routes = [ways[0][2]] + [way for _, _, way in ways[2:]]
    middle = ways[0][1]
    (have,) = yield [have]
    comes = exchange(have, [route[3] for route in routes])
    have = [one[None] for one in have]
    comes = [one[None] for one in comes]
    yield None
    for stage in (2, 1, 0):
        have, comes = yield [have, comes]
        joined = [jnp.concatenate([one, two]) for one, two in zip(have, comes)]
        if stage == 1:
            joined = [joined[0][..., :middle], joined[0][..., middle:]] + joined[1:]
            routes = [way for _, _, way in ways]
        (have,) = yield [joined]
        comes = exchange(have, [route[stage] for route in routes])
        yield None
    have, comes = yield [have, comes]
    return [part for pair in zip(have, comes) for part in pair]


def sum_flow(ways, get_own, others):
    have = yield from reduce_flow(ways, get_own, others)
    return (yield from gather_flow(ways, have))


def swap_flow(other):
    (other,) = yield [other]
    came = swap_cores(other)
    yield None
    (came,) = yield [came]
    return came


def rows_flow(rows):
    for bit in (3, 2, 1, 0):
        (rows,) = yield [rows]
        came = lax.ppermute(rows, "dp", bit_pairs(bit))
        yield None
        rows, came = yield [rows, came]
        rows = jnp.concatenate([rows, came])
    return rows


class Order:
    def __init__(self, sc):
        self.sc = sc
        self.results = {}

    def fence(self, values):
        self.sc, values = lax.optimization_barrier((self.sc, values))
        return values

    def after(self, value):
        self.sc, _ = lax.optimization_barrier((self.sc, value))

    def tick(self, *flows):
        replies = {flow: None for flow in flows if flow not in self.results}
        while replies:
            wants = {}
            for flow, reply in replies.items():
                try:
                    want = flow.send(reply)
                except StopIteration as stop:
                    self.results[flow] = stop.value
                    continue
                if want is not None:
                    wants[flow] = want
            replies = dict(zip(wants, self.fence(list(wants.values())))) if wants else {}

    def finish(self, flow):
        while flow not in self.results:
            self.tick(flow)
        return self.results[flow]


CHUNKS = 3
PLAIN = 2


def fill_other(both, came, core):
    size = came.shape[0]
    return lax.dynamic_update_slice_in_dim(both, came, (1 - core) * size, 0)


def fast_device(
    tokens, condition, counts, w_qkv, b_qv, w_proj, b_proj, w_up, b_up, w_down, b_down, w_mod, b_mod,
    cotangent,
):
    slots, seq, dim = tokens.shape
    images = slots // 2
    count = images * seq
    cols = w_qkv.shape[2]
    ff = w_up.shape[1]
    own_cols = w_mod.shape[1]
    heads = cols // HEAD_DIM
    core = lax.axis_index("mp")
    order = Order(jnp.stack([core, counts[0], lax.axis_index("dp")]).astype(jnp.int32))

    qkv_rows = jnp.transpose(w_qkv, (1, 2, 0)).reshape(3 * cols, dim)
    wq = [qkv_rows, swap_cores(qkv_rows)]
    wp = [w_proj, swap_cores(w_proj)]
    qkv_bias = [b_qv, swap_cores(b_qv)]

    cond_f = condition.astype(f32)
    scaled = jax.nn.silu(cond_f).astype(bf16)
    own_mod = jnp.dot(scaled, w_mod, preferred_element_type=f32) + b_mod.astype(f32)
    other_mod = swap_cores(own_mod)
    sides = [jnp.where(core == side, own_mod, other_mod) for side in range(2)]
    modulation = jnp.concatenate(sides, axis=1).reshape(slots, 6, dim)
    proj_bias = b_proj.astype(f32)[None]
    down_bias = b_down.astype(f32)[None]

    late_up, late_down, late_bias = lax.optimization_barrier((wq[1], w_up, w_down, b_up, modulation))[1:4]
    wu = [w_up, swap_cores(late_up)]
    wd = [w_down, swap_cores(late_down)]
    up_bias = [b_up[None], swap_cores(late_bias[None])]

    local = lambda i, s: (s[0] * images + i, 0, 0)
    mine = lambda i, s: (i, 0, 0)
    tok_spec = pl.BlockSpec((1, seq, dim), local)
    own_spec = pl.BlockSpec((1, seq, dim), mine)
    mod_spec = pl.BlockSpec((1, 6, dim), local)
    row_spec = pl.BlockSpec((1, 1, dim), mine)
    qkv_spec = pl.BlockSpec((1, 6 * cols, seq), mine)
    prob_spec = pl.BlockSpec((1, 2 * heads, seq, seq), lambda i, s: (i, 0, 0, 0))
    mixed_spec = pl.BlockSpec((1, 2 * cols, seq), mine)
    token_f = shape_of((images, seq, dim), f32)
    token_b = shape_of((images, seq, dim), bf16)
    attn_args = wq + wp + qkv_bias
    qkv, prob, mixed, attn_out, residual, normed_mlp, normed, grad_mlp, down_sums = run_kernel(
        functools.partial(attention_kernel, 2, images),
        order.sc,
        [tokens, cotangent, modulation, proj_bias] + attn_args,
        [tok_spec, tok_spec, mod_spec, whole_block(proj_bias)] + [whole_block(a) for a in attn_args],
        [qkv_spec, prob_spec, mixed_spec] + [own_spec] * 5 + [row_spec],
        [
            shape_of((images, 6 * cols, seq), bf16),
            shape_of((images, 2 * heads, seq, seq), bf16),
            shape_of((images, 2 * cols, seq), bf16),
            token_f,
            token_f,
            token_b,
            token_b,
            token_b,
            shape_of((images, 1, dim), f32),
        ],
        (images,),
        33,
    )
    order.after(down_sums)

    rows_flat = normed_mlp.reshape(count, dim)
    grad_flat = grad_mlp.reshape(count, dim)
    width = ff // CHUNKS
    per = width // 16
    steps = 2
    block = width // steps
    anywhere = pl.BlockSpec(memory_space=pl.ANY)
    act = back = jnp.zeros((8, 128), bf16)
    up_sums = {}

    def mlp_call(jobs, came, micros):
        nonlocal act, back
        first = act.shape[0] == 8
        kinds = tuple((None if job[0] < PLAIN else columns(MLP_WAYS), job in came) for job in jobs)

        def turn(k):
            return lambda p, s, c: jnp.clip((p - k) * steps + s, 0, steps - 1)

        def pick(values):
            return lambda p: sum(jnp.where(p == k, value, 0) for k, value in enumerate(values))

        parts = pick([part for _, part in jobs])
        starts = pick([chunk * steps for chunk, _ in jobs])
        spread = pl.BlockSpec((1, block, count), lambda p, s, c: (parts(p), starts(p) + s, 0))
        args, specs = [], []
        for k, (chunk, part) in enumerate(jobs):
            at = chunk * steps
            wide = lambda p, s, c, k=k, at=at: (0, at + turn(k)(p, s, c))
            tall = lambda p, s, c, k=k, at=at: (at + turn(k)(p, s, c), 0)
            args += [wu[part], wd[part], up_bias[part]]
            specs += [
                pl.BlockSpec((dim, block), wide),
                pl.BlockSpec((block, dim), tall),
                pl.BlockSpec((1, block), wide),
            ]
        grad_specs, grad_shapes, sizes = [], [], []
        for k, (split, _) in enumerate(kinds):
            own = lambda p, s, c, k=k: (turn(k)(p, s, c), 0, 0)
            fixed = lambda p, s, c: (0, 0, 0)
            wides = [dim] if split is None else [hi - lo for lo, hi in split]
            lead = (16 // steps, own) if split is None else (16, fixed)
            grad_specs.append([pl.BlockSpec((lead[0], 2 * per, wide), lead[1]) for wide in wides])
            grad_shapes += [shape_of((16, 2 * per, wide), bf16) for wide in wides]
            sizes.append(len(wides))
        for k, job in enumerate(jobs):
            if job in came:
                args.append(came[job])
                specs += grad_specs[k]
        args += [act, back]
        spot = len(args) + 1
        outs = run_kernel(
            functools.partial(mlp_kernel, per, kinds),
            order.sc,
            [rows_flat, grad_flat] + args,
            [whole_block(rows_flat), whole_block(grad_flat)] + specs + [anywhere, anywhere],
            [spread, spread]
            + [spec for specs in grad_specs for spec in specs]
            + [pl.BlockSpec((1, block), lambda p, s, c, k=k: (0, turn(k)(p, s, c))) for k in range(len(jobs))],
            [shape_of((2, ff, count), bf16)] * 2 + grad_shapes + [shape_of((1, width), f32)] * len(jobs),
            (len(jobs), steps),
            micros,
            alias=None if first else {spot: 0, spot + 1: 1},
        )
        act, back = outs[:2]
        grads, outs = list(outs[2 : 2 + sum(sizes)]), outs[2 + sum(sizes) :]
        up_sums.update(zip(jobs, outs))
        order.after(outs[-1])
        return [[grads.pop(0) for _ in range(size)] for size in sizes]

    summed = range(PLAIN)
    swaps = [swap_flow(grad) for (grad,) in mlp_call([(chunk, 1) for chunk in summed], {}, 26)]
    order.tick(*swaps)
    rest = range(PLAIN, CHUNKS)
    made_rest = []
    flows = [
        sum_flow(MLP_WAYS, lambda k=k: made_rest[k], others)
        for k, others in enumerate(mlp_call([(chunk, 1) for chunk in rest], {}, 13))
    ]
    wide_scaled = jnp.pad(scaled.reshape(-1), (0, 3 * own_cols - slots * dim)).reshape(3, own_cols)
    early = rows_flow(wide_scaled)
    order.tick(*swaps, *flows, early)
    came = {(chunk, 0): order.results[swap] for chunk, swap in zip(summed, swaps)}
    grads = mlp_call([(chunk, 0) for chunk in summed], came, 26)
    plain_sums = lax.psum([grad for (grad,) in grads], "dp")
    order.tick(early)
    made_rest += mlp_call([(chunk, 0) for chunk in rest], {}, 13)
    order.tick(*flows, early)

    reach = 768
    turns = ff // reach
    every = lambda s, c: (0, 0, 0)
    tail = lambda first: lambda s, c: (jnp.maximum(s - first, 0), 0, 0)
    tail_local = lambda first: lambda s, c: (c[0] * images + jnp.maximum(s - first, 0), 0, 0)

    def image_spec(first, where=tail):
        return pl.BlockSpec((1, seq, dim), where(first))

    def rows_of(part, size):
        if part == 0:
            return lambda s, c: jnp.minimum(s, size - 1)
        return lambda s, c: jnp.clip(s - size, 0, size - 1)

    span_spec = pl.BlockSpec(
        (1, reach, count),
        lambda s, c: (jnp.minimum(s // turns, 1), jnp.where(s < 2 * turns, s % turns, turns - 1), 0),
    )
    grad_residual, grad_attn, mid_sums = run_kernel(
        functools.partial(norm_back_kernel, turns, images),
        order.sc,
        [back] + wu + [residual, cotangent, modulation, attn_out],
        [
            span_spec,
            pl.BlockSpec((dim, reach), lambda s, c: (0, rows_of(0, turns)(s, c))),
            pl.BlockSpec((dim, reach), lambda s, c: (0, rows_of(1, turns)(s, c))),
            image_spec(2 * turns),
            image_spec(2 * turns, tail_local),
            pl.BlockSpec((1, 6, dim), tail_local(2 * turns)),
            image_spec(2 * turns),
        ],
        [image_spec(2 * turns)] * 2 + [pl.BlockSpec((1, 4, dim), tail(2 * turns))],
        [token_f, token_b, shape_of((images, 4, dim), f32)],
        (2 * turns + images,),
        60,
        scratch=[pltpu.VMEM((count, dim), f32)],
    )
    order.after(mid_sums)
    order.tick(*flows, early)
    pieces = 2
    each = images // pieces
    grad_qkv = []
    for piece in range(pieces):
        there = lambda i, s, piece=piece: (piece * each + i, 0, 0)
        (grad_piece,) = run_kernel(
            functools.partial(back_kernel, 2),
            order.sc,
            [grad_attn, qkv, prob] + wp,
            [
                pl.BlockSpec((1, seq, dim), there),
                pl.BlockSpec((1, 6 * cols, seq), there),
                pl.BlockSpec((1, 2 * heads, seq, seq), lambda i, s, piece=piece: (piece * each + i, 0, 0, 0)),
            ]
            + [whole_block(a) for a in wp],
            [qkv_spec],
            [shape_of((each, 6 * cols, seq), bf16)],
            (each,),
            60,
            scratch=[pltpu.VMEM((2 * cols, seq), bf16)],
            )
        grad_qkv.append(grad_piece)
        order.after(grad_piece)
        order.tick(*flows, early)

    attn_per = 4 * cols // 16
    qv_sums = [None, None]

    def attn_part(part):
        *grads, sums = run_kernel(
            functools.partial(attn_grad_kernel, pieces, attn_per, columns(ATTN_WAYS)),
            order.sc,
            grad_qkv + [mixed, normed, grad_attn],
            [
                pl.BlockSpec((each, cols, seq), lambda s, c: (0, 3 * part + jnp.minimum(s, 2), 0))
                for _ in range(pieces)
            ]
            + [pl.BlockSpec((images, cols, seq), lambda s, c: (0, part, 0))]
            + [whole_block(normed), whole_block(grad_attn)],
            [pl.BlockSpec((16, attn_per, hi - lo), every) for lo, hi in columns(ATTN_WAYS)]
            + [pl.BlockSpec((1, 1, cols), lambda s, c: (jnp.minimum(s, 2), 0, 0))],
            [shape_of((16, attn_per, hi - lo), bf16) for lo, hi in columns(ATTN_WAYS)]
            + [shape_of((3, 1, cols), f32)],
            (4,),
            60,
            )
        qv_sums[part] = sums
        order.after(sums)
        return grads

    grad_other = attn_part(1)
    made = []
    last = sum_flow(ATTN_WAYS, lambda: made[0], grad_other)
    order.tick(last, *flows)
    made.append(attn_part(0))
    order.tick(last, *flows)

    first_spec = lambda part: pl.BlockSpec((cols, dim), lambda s, c: (rows_of(part, 3)(s, c), 0))
    grad_tokens, grad_own_tokens, low_sums = run_kernel(
        functools.partial(first_back_kernel, pieces, images),
        order.sc,
        grad_qkv + wq + [tokens, modulation, grad_residual],
        [pl.BlockSpec((each, cols, seq), lambda s, c: (0, jnp.minimum(s, 5), 0)) for _ in range(pieces)]
        + [first_spec(0), first_spec(1)]
        + [image_spec(6, tail_local), pl.BlockSpec((1, 6, dim), tail_local(6)), image_spec(6)],
        [image_spec(6, tail_local), image_spec(6), pl.BlockSpec((1, 2, dim), tail(6))],
        [shape_of((slots, seq, dim), f32), token_f, shape_of((images, 2, dim), f32)],
        (6 + images,),
        60,
        scratch=[pltpu.VMEM((count, dim), f32)],
    )
    order.after(low_sums)
    order.tick(last, *flows)
    down_spec = lambda part: pl.BlockSpec((reach, dim), lambda s, c: (rows_of(part, turns)(s, c), 0))
    output, own_output, gate_sums = run_kernel(
        functools.partial(output_kernel, turns, images),
        order.sc,
        [act] + wd + [residual, cotangent, modulation, down_bias],
        [
            span_spec,
            down_spec(0),
            down_spec(1),
            image_spec(2 * turns),
            image_spec(2 * turns, tail_local),
            pl.BlockSpec((1, 6, dim), tail_local(2 * turns)),
            whole_block(down_bias),
        ],
        [image_spec(2 * turns, tail_local), image_spec(2 * turns), pl.BlockSpec((1, 1, dim), tail(2 * turns))],
        [shape_of((slots, seq, dim), bf16), token_b, shape_of((images, 1, dim), f32)],
        (2 * turns + images,),
        60,
        scratch=[pltpu.VMEM((count, dim), f32)],
    )
    order.after(gate_sums)
    order.tick(last, *flows)

    low_sums, mid_sums, gate_sums, down_sums, qv_sums, up_sums = order.fence(
        (low_sums, mid_sums, gate_sums, down_sums, qv_sums, up_sums)
    )
    grad_modulation = jnp.concatenate([low_sums, mid_sums[:, 2:3], mid_sums[:, 0:2], gate_sums], axis=1)
    grad_modulation = grad_modulation.reshape(images, 6 * dim).astype(bf16)
    bias_sums = [
        jnp.concatenate(
            [qv_sums[part][0], qv_sums[part][2]]
            + [up_sums[chunk, part] for chunk in range(CHUNKS)],
            axis=1,
        )
        for part in range(2)
    ]
    shared = jnp.concatenate(
        [
            jnp.sum(mid_sums[:, 3], axis=0, keepdims=True),
            jnp.sum(down_sums[:, 0], axis=0, keepdims=True),
            jnp.zeros((1, own_cols - 2 * dim), f32),
        ],
        axis=1,
    )
    halves = grad_modulation.reshape(images, 2, own_cols)
    kept = lax.dynamic_index_in_dim(halves, core, 1, keepdims=False)
    given = lax.dynamic_index_in_dim(halves, 1 - core, 1, keepdims=False)
    got = swap_cores(jnp.concatenate([given.astype(f32), bias_sums[1], shared]))
    came = got[:images].astype(bf16)
    group_mod = jnp.where(core == 0, jnp.concatenate([kept, came]), jnp.concatenate([came, kept]))
    own_bias_sum = bias_sums[0] + got[images : images + 1]
    shared_sum = shared + got[images + 1 :]
    packed_rows = jnp.concatenate(
        [group_mod, own_bias_sum.astype(bf16), shared_sum.astype(bf16)]
    )
    (packed_rows,) = order.fence([packed_rows])
    small = rows_flow(packed_rows)
    def cuts(ways):
        return tuple((way, lo, hi) for lo, hi, way in ways)

    grad_w_down = grad_w_up = jnp.zeros((8, 128), f32)

    def final_mlp(chunk, body, args):
        nonlocal grad_w_down, grad_w_up
        first = grad_w_down.shape[0] == 8
        spot = len(args) + 1
        grad_w_down, grad_w_up, _ = run_kernel(
            body,
            order.sc,
            list(args) + [grad_w_down, grad_w_up],
            [
                whole_block(a)
                if a.shape[0] == 8
                else pl.BlockSpec((16 // steps,) + a.shape[1:], lambda s, c: (s, 0, 0))
                for a in args
            ]
            + [anywhere, anywhere],
            [
                pl.BlockSpec((block, dim), lambda s, c: (chunk * steps + s, 0)),
                pl.BlockSpec((dim, block), lambda s, c: (0, chunk * steps + s)),
                pl.BlockSpec((8, 128), lambda s, c: (0, 0)),
            ],
            [shape_of((ff, dim), f32), shape_of((dim, ff), f32), shape_of((8, 128), f32)],
            (steps,),
            4,
            scratch=[pltpu.VMEM((block, dim), f32)],
            alias=None if first else {spot: 0, spot + 1: 1},
        )
        grad_w_down, grad_w_up = order.fence((grad_w_down, grad_w_up))

    order.tick(last, small, *flows)
    own_output, grad_own_tokens, group_mod = order.fence((own_output, grad_own_tokens, group_mod))
    other_output, other_tokens = swap_cores(own_output), swap_cores(grad_own_tokens)
    part_scaled = outer_cols(group_mod, w_mod).astype(bf16)
    part_scaled = order.fence(part_scaled)
    for chunk, flow in enumerate(flows):
        body = functools.partial(final_mlp_kernel, cuts(MLP_WAYS), per)
        final_mlp(PLAIN + chunk, body, order.finish(flow))
    order.tick(last, small)
    came_scaled = swap_cores(order.fence(part_scaled))
    other_output, other_tokens = order.fence((other_output, other_tokens))
    output = fill_other(output, other_output, core)
    grad_tokens = fill_other(grad_tokens, other_tokens, core)
    output, grad_tokens = order.fence((output, grad_tokens))
    order.tick(last, small)
    grad_scaled = part_scaled.astype(f32) + order.fence(came_scaled).astype(f32)
    _, silu_back = jax.vjp(jax.nn.silu, cond_f)
    grad_condition = silu_back(grad_scaled)[0]
    grad_condition = order.fence(grad_condition)
    plain_sums = order.fence(plain_sums)
    final_mlp(0, functools.partial(final_plain_kernel, per), [plain_sums[0]])
    order.tick(last, small)
    final_mlp(1, functools.partial(final_plain_kernel, per), [plain_sums[1]])
    order.tick(last)
    all_rows = order.fence(order.finish(small)).reshape(16, slots + 2, own_cols)
    all_mod = all_rows[:, :slots].reshape(-1, own_cols)
    all_scaled = order.finish(early).reshape(16, -1)[:, : slots * dim].reshape(-1, dim)
    grad_w_mod = inner_rows(all_scaled, all_mod)
    grad_b_mod = jnp.sum(all_mod.astype(f32), axis=0)
    bias_total = jnp.sum(all_rows[:, slots : slots + 2].astype(f32), axis=0)
    grad_b_qv = bias_total[0, : 2 * cols].reshape(2, cols)
    grad_b_up = bias_total[0, 2 * cols :]
    grad_b_proj = bias_total[1, :dim]
    grad_b_down = bias_total[1, dim : 2 * dim]
    grad_w_mod = order.fence(grad_w_mod)
    args = order.finish(last)
    grad_qkv_rows, grad_w_proj = run_kernel(
        functools.partial(final_attn_kernel, cuts(ATTN_WAYS), attn_per),
        order.sc,
        list(args),
        [whole_block(a) for a in args],
        [
            pl.BlockSpec((cols, dim), lambda s, c: (jnp.minimum(s, 2), 0)),
            pl.BlockSpec((cols, dim), lambda s, c: (0, 0)),
        ],
        [shape_of((3 * cols, dim), f32), shape_of((cols, dim), f32)],
        (4,),
        9,
    )
    grad_w_qkv = jnp.transpose(grad_qkv_rows.reshape(3, cols, dim), (2, 0, 1))
    return (
        output,
        grad_tokens,
        grad_condition,
        grad_w_qkv,
        grad_b_qv,
        grad_w_proj,
        grad_b_proj,
        grad_w_up,
        grad_b_up,
        grad_w_down,
        grad_b_down,
        grad_w_mod,
        grad_b_mod,
    )


def layer_norm(values):
    center = values - jnp.mean(values, axis=-1, keepdims=True)
    return center * lax.rsqrt(jnp.mean(center * center, axis=-1, keepdims=True) + epsilon)


def modulate(values, shift_part, scale_part):
    return layer_norm(values) * (1.0 + scale_part) + shift_part


def gelu_tanh(values):
    return (
        0.5
        * values
        * (1.0 + jnp.tanh(0.7978845608028654 * (values + 0.044715 * values * values * values)))
    )


def inner_rows(left, right):
    return lax.dot_general(
        left, right, (((0,), (0,)), ((), ())), preferred_element_type=jnp.float32
    )


def outer_cols(left, right):
    return lax.dot_general(
        left, right, (((1,), (1,)), ((), ())), preferred_element_type=jnp.float32
    )


def attention_forward(query_rows, key_rows, value_rows):
    factor = HEAD_DIM ** (-0.5)
    scores = (
        jnp.einsum("bqhd,bkhd->bhqk", query_rows, key_rows, preferred_element_type=jnp.float32)
        * factor
    )
    row_max = jnp.max(scores, axis=-1, keepdims=True)
    row_total = jnp.sum(jnp.exp(scores - row_max), axis=-1, keepdims=True)
    logsum = row_max + jnp.log(row_total)
    prob_b = jnp.exp(scores - logsum).astype(jnp.bfloat16)
    mixed_out = jnp.einsum(
        "bhqk,bkhd->bqhd", prob_b, value_rows, preferred_element_type=jnp.float32
    )
    return (mixed_out, logsum)


def attention_backward(query_rows, key_rows, value_rows, logsum, grad_mixed):
    factor = HEAD_DIM ** (-0.5)
    scores = (
        jnp.einsum("bqhd,bkhd->bhqk", query_rows, key_rows, preferred_element_type=jnp.float32)
        * factor
    )
    prob_f = jnp.exp(scores - logsum)
    prob_b = prob_f.astype(jnp.bfloat16)
    grad_prob = jnp.einsum(
        "bqhd,bkhd->bhqk", grad_mixed, value_rows, preferred_element_type=jnp.float32
    )
    row_delta = jnp.sum(prob_f * grad_prob, axis=-1, keepdims=True)
    grad_scores = (prob_f * (grad_prob - row_delta)).astype(jnp.bfloat16)
    grad_query = (
        jnp.einsum("bhqk,bkhd->bqhd", grad_scores, key_rows, preferred_element_type=jnp.float32)
        * factor
    )
    grad_key = (
        jnp.einsum("bhqk,bqhd->bkhd", grad_scores, query_rows, preferred_element_type=jnp.float32)
        * factor
    )
    grad_value = jnp.einsum(
        "bhqk,bqhd->bkhd", prob_b, grad_mixed, preferred_element_type=jnp.float32
    )
    return (
        grad_query.astype(jnp.bfloat16),
        grad_key.astype(jnp.bfloat16),
        grad_value.astype(jnp.bfloat16),
    )


def forward(tokens_f, spans, weights, repeat):
    w_qkv, b_qv, w_proj, b_proj, w_up, b_up, w_down, b_down = weights
    shift_attn, scale_attn, gate_attn, shift_mlp, scale_mlp, gate_mlp = spans
    slot_count, seq_len, model_dim = tokens_f.shape
    row_count = slot_count * seq_len
    head_cols = w_qkv.shape[2]
    head_count = head_cols // HEAD_DIM
    shape_four = (slot_count, seq_len, head_count, HEAD_DIM)
    normed = (
        modulate(tokens_f, shift_attn, scale_attn)
        .astype(jnp.bfloat16)
        .reshape(row_count, model_dim)
    )
    projected = jnp.dot(
        normed, w_qkv.reshape(model_dim, 3 * head_cols), preferred_element_type=jnp.float32
    )
    qkv_bias = jnp.stack([b_qv[0], jnp.zeros_like(b_qv[0]), b_qv[1]]).astype(jnp.float32)
    projected = (projected.reshape(row_count, 3, head_cols) + qkv_bias).astype(jnp.bfloat16)
    query_rows = projected[:, 0].reshape(shape_four)
    key_rows = projected[:, 1].reshape(shape_four)
    value_rows = projected[:, 2].reshape(shape_four)
    mixed_out, logsum = attention_forward(query_rows, key_rows, value_rows)
    mixed_b = mixed_out.astype(jnp.bfloat16).reshape(row_count, head_cols)
    partial_value = jnp.dot(mixed_b, w_proj, preferred_element_type=jnp.float32)
    if repeat:
        summed = lax.psum(partial_value.astype(jnp.bfloat16), "mp").astype(jnp.float32)
    else:
        summed = lax.psum(partial_value.astype(jnp.bfloat16), "mp").astype(jnp.float32)
    attn_out = (summed + b_proj.astype(jnp.float32)).reshape(slot_count, seq_len, model_dim)
    residual = tokens_f + gate_attn * attn_out
    normed_mlp = (
        modulate(residual, shift_mlp, scale_mlp).astype(jnp.bfloat16).reshape(row_count, model_dim)
    )
    hidden = jnp.dot(normed_mlp, w_up, preferred_element_type=jnp.float32) + b_up.astype(
        jnp.float32
    )
    act_bf = gelu_tanh(hidden).astype(jnp.bfloat16)
    partial_mlp = jnp.dot(act_bf, w_down, preferred_element_type=jnp.float32)
    if repeat:
        summed_mlp = lax.psum(partial_mlp.astype(jnp.bfloat16), "mp").astype(jnp.float32)
    else:
        summed_mlp = lax.psum(partial_mlp.astype(jnp.bfloat16), "mp").astype(jnp.float32)
    mlp_out = (summed_mlp + b_down.astype(jnp.float32)).reshape(slot_count, seq_len, model_dim)
    output = residual + gate_mlp * mlp_out
    return {
        "normed": normed,
        "query_rows": query_rows,
        "key_rows": key_rows,
        "value_rows": value_rows,
        "logsum": logsum,
        "mixed_b": mixed_b,
        "attn_out": attn_out,
        "residual": residual,
        "normed_mlp": normed_mlp,
        "hidden": hidden,
        "act_bf": act_bf,
        "mlp_out": mlp_out,
        "output": output,
    }


def image_pass(tokens_f, grad_out, spans, weights):
    w_qkv, b_qv, w_proj, b_proj, w_up, b_up, w_down, b_down = weights
    shift_attn, scale_attn, gate_attn, shift_mlp, scale_mlp, gate_mlp = spans
    slot_count, seq_len, model_dim = tokens_f.shape
    row_count = slot_count * seq_len
    head_cols = w_qkv.shape[2]
    head_count = head_cols // HEAD_DIM
    kept_fwd = forward(tokens_f, spans, weights, False)
    out_one = kept_fwd["output"]
    stored = forward(tokens_f, spans, weights, True)
    grad_gate_mlp = jnp.sum(grad_out * stored["mlp_out"], axis=1)
    grad_mlp = (gate_mlp * grad_out).astype(jnp.bfloat16).reshape(row_count, model_dim)
    grad_b_down = jnp.sum(grad_mlp.astype(jnp.float32), axis=0)
    grad_w_down = inner_rows(stored["act_bf"], grad_mlp)
    grad_act = outer_cols(grad_mlp, w_down)
    gelu_value, gelu_back = jax.vjp(gelu_tanh, stored["hidden"])
    grad_hidden = gelu_back(grad_act)[0].astype(jnp.bfloat16)
    grad_b_up = jnp.sum(grad_hidden.astype(jnp.float32), axis=0)
    grad_w_up = inner_rows(stored["normed_mlp"], grad_hidden)
    part_normed_mlp = outer_cols(grad_hidden, w_up)
    grad_normed_mlp = (
        lax.psum(part_normed_mlp.astype(jnp.bfloat16), "mp")
        .astype(jnp.float32)
        .reshape(slot_count, seq_len, model_dim)
    )
    norm_value, norm_back = jax.vjp(modulate, stored["residual"], shift_mlp, scale_mlp)
    grad_resid_norm, grad_shift_mlp, grad_scale_mlp = norm_back(grad_normed_mlp)
    grad_residual = grad_out + grad_resid_norm
    grad_gate_attn = jnp.sum(grad_residual * stored["attn_out"], axis=1)
    grad_attn = (gate_attn * grad_residual).astype(jnp.bfloat16).reshape(row_count, model_dim)
    grad_b_proj = jnp.sum(grad_attn.astype(jnp.float32), axis=0)
    grad_w_proj = inner_rows(stored["mixed_b"], grad_attn)
    grad_mixed = (
        outer_cols(grad_attn, w_proj)
        .astype(jnp.bfloat16)
        .reshape(slot_count, seq_len, head_count, HEAD_DIM)
    )
    grad_query, grad_key, grad_value = attention_backward(
        stored["query_rows"], stored["key_rows"], stored["value_rows"], stored["logsum"], grad_mixed
    )
    grad_qkv = jnp.stack(
        [
            grad_query.reshape(row_count, head_cols),
            grad_key.reshape(row_count, head_cols),
            grad_value.reshape(row_count, head_cols),
        ],
        axis=1,
    )
    grad_b_qv = jnp.stack(
        [
            jnp.sum(grad_qkv[:, 0].astype(jnp.float32), axis=0),
            jnp.sum(grad_qkv[:, 2].astype(jnp.float32), axis=0),
        ]
    )
    grad_w_qkv = inner_rows(stored["normed"], grad_qkv)
    part_normed = outer_cols(
        grad_qkv.reshape(row_count, 3 * head_cols), w_qkv.reshape(model_dim, 3 * head_cols)
    )
    grad_normed = (
        lax.psum(part_normed.astype(jnp.bfloat16), "mp")
        .astype(jnp.float32)
        .reshape(slot_count, seq_len, model_dim)
    )
    first_value, first_back = jax.vjp(modulate, tokens_f, shift_attn, scale_attn)
    grad_tok_norm, grad_shift_attn, grad_scale_attn = first_back(grad_normed)
    grad_tok_one = grad_residual + grad_tok_norm
    grad_mod_one = jnp.concatenate(
        [
            grad_shift_attn[:, 0],
            grad_scale_attn[:, 0],
            grad_gate_attn,
            grad_shift_mlp[:, 0],
            grad_scale_mlp[:, 0],
            grad_gate_mlp,
        ],
        axis=1,
    )
    grad_terms = (
        grad_w_qkv,
        grad_b_qv,
        grad_w_proj,
        grad_b_proj,
        grad_w_up,
        grad_b_up,
        grad_w_down,
        grad_b_down,
    )
    return (out_one, grad_tok_one, grad_mod_one, grad_terms)


def run_layer(tokens, condition, cotangent, live_count, turns, weights, w_mod, b_mod):
    slot_count, seq_len, model_dim = tokens.shape
    cond_f = condition.astype(jnp.float32)
    scaled = jax.nn.silu(cond_f).astype(jnp.bfloat16)
    own_mod = jnp.dot(scaled, w_mod, preferred_element_type=jnp.float32) + b_mod.astype(jnp.float32)
    modulation = lax.all_gather(own_mod, "mp", axis=1, tiled=True)
    tokens_f = tokens.astype(jnp.float32)
    cot_f = cotangent.astype(jnp.float32)

    def image_step(slot_idx, carry):
        out_buf, grad_buf, mod_buf, grad_sums = carry
        live_flag = (slot_idx < live_count).astype(jnp.float32)
        tok_one = lax.dynamic_slice_in_dim(tokens_f, slot_idx, 1, 0)
        cot_one = lax.dynamic_slice_in_dim(cot_f, slot_idx, 1, 0) * live_flag
        mod_row = lax.dynamic_slice_in_dim(modulation, slot_idx, 1, 0)
        spans = [
            mod_row[:, None, part_idx * model_dim : (part_idx + 1) * model_dim]
            for part_idx in range(6)
        ]
        out_one, grad_tok_one, grad_mod_one, grad_terms = image_pass(
            tok_one, cot_one, spans, weights
        )
        out_one = (out_one * live_flag).astype(jnp.bfloat16)
        out_buf = lax.dynamic_update_slice_in_dim(out_buf, out_one, slot_idx, 0)
        grad_buf = lax.dynamic_update_slice_in_dim(grad_buf, grad_tok_one, slot_idx, 0)
        mod_buf = lax.dynamic_update_slice_in_dim(mod_buf, grad_mod_one, slot_idx, 0)
        grad_sums = tuple((total_a + term_b for total_a, term_b in zip(grad_sums, grad_terms)))
        return (out_buf, grad_buf, mod_buf, grad_sums)

    start_sums = tuple((jnp.zeros(weight_in.shape, jnp.float32) for weight_in in weights))
    start_state = (
        jnp.zeros(tokens.shape, jnp.bfloat16),
        jnp.zeros(tokens.shape, jnp.float32),
        jnp.zeros((slot_count, 6 * model_dim), jnp.float32),
        start_sums,
    )
    out_buf, grad_buf, mod_buf, grad_sums = lax.fori_loop(0, turns, image_step, start_state)
    grad_modulation = mod_buf.astype(jnp.bfloat16)
    own_cols = w_mod.shape[1]
    grad_own = lax.dynamic_slice_in_dim(
        grad_modulation, lax.axis_index("mp") * own_cols, own_cols, 1
    )
    part_scaled = outer_cols(grad_own, w_mod)
    grad_scaled = lax.psum(part_scaled.astype(jnp.bfloat16), "mp").astype(jnp.float32)
    silu_value, silu_back = jax.vjp(jax.nn.silu, cond_f)
    grad_condition = silu_back(grad_scaled)[0]
    return (out_buf, grad_buf, grad_condition, grad_sums, scaled, grad_own)


def on_device(
    tokens,
    condition,
    counts,
    w_qkv,
    b_qv,
    w_proj,
    b_proj,
    w_up,
    b_up,
    w_down,
    b_down,
    w_mod,
    b_mod,
    cotangent,
):
    slot_count, seq_len, model_dim = tokens.shape
    weights = (w_qkv, b_qv, w_proj, b_proj, w_up, b_up, w_down, b_down)
    own_count = counts[0]
    output, grad_tokens, grad_condition, grad_sums, scaled, grad_own = run_layer(
        tokens, condition, cotangent, own_count, slot_count, weights, w_mod, b_mod
    )
    (
        grad_w_qkv,
        grad_b_qv,
        grad_w_proj,
        grad_b_proj,
        grad_w_up,
        grad_b_up,
        grad_w_down,
        grad_b_down,
    ) = grad_sums
    grad_w_mod = inner_rows(scaled, grad_own)
    grad_b_mod = jnp.sum(grad_own.astype(jnp.float32), axis=0)
    (
        grad_w_qkv,
        grad_b_qv,
        grad_w_proj,
        grad_b_proj,
        grad_w_up,
        grad_b_up,
        grad_w_down,
        grad_b_down,
        grad_w_mod,
        grad_b_mod,
    ) = (
        lax.psum(grad_w_qkv.astype(jnp.bfloat16), "dp").astype(jnp.float32),
        lax.psum(grad_b_qv.astype(jnp.bfloat16), "dp").astype(jnp.float32),
        lax.psum(grad_w_proj.astype(jnp.bfloat16), "dp").astype(jnp.float32),
        lax.psum(grad_b_proj.astype(jnp.bfloat16), "dp").astype(jnp.float32),
        lax.psum(grad_w_up.astype(jnp.bfloat16), "dp").astype(jnp.float32),
        lax.psum(grad_b_up.astype(jnp.bfloat16), "dp").astype(jnp.float32),
        lax.psum(grad_w_down.astype(jnp.bfloat16), "dp").astype(jnp.float32),
        lax.psum(grad_b_down.astype(jnp.bfloat16), "dp").astype(jnp.float32),
        lax.psum(grad_w_mod.astype(jnp.bfloat16), "dp").astype(jnp.float32),
        lax.psum(grad_b_mod.astype(jnp.bfloat16), "dp").astype(jnp.float32),
    )
    return (
        output,
        grad_tokens,
        grad_condition,
        grad_w_qkv,
        grad_b_qv,
        grad_w_proj,
        grad_b_proj,
        grad_w_up,
        grad_b_up,
        grad_w_down,
        grad_b_down,
        grad_w_mod,
        grad_b_mod,
    )


def solution(mesh):
    placed = (
        P("dp", None, None),
        P("dp", None),
        P("dp"),
        P(None, None, "mp"),
        P(None, "mp"),
        P("mp", None),
        P(),
        P(None, "mp"),
        P("mp"),
        P("mp", None),
        P(),
        P(None, "mp"),
        P("mp"),
        P("dp", None, None),
    )
    fast = mesh.shape["dp"] == 16 and mesh.shape["mp"] == 2
    return jax.shard_map(
        fast_device if fast else on_device,
        mesh=mesh,
        in_specs=placed,
        out_specs=(
            P("dp", None, None),
            P("dp", None, None),
            P("dp", None),
            P(None, None, "mp"),
            P(None, "mp"),
            P("mp", None),
            P(),
            P(None, "mp"),
            P("mp"),
            P("mp", None),
            P(),
            P(None, "mp"),
            P("mp"),
        ),
        check_vma=False,
    )
```

```python
import functools

import jax
import jax.numpy as jnp
from jax import lax
from jax.experimental import pallas as pl
from jax.experimental.pallas import tpu as pltpu
from jax.sharding import PartitionSpec as P

HEAD_DIM = 72
LOG2_E = 1.4426950408889634


epsilon = 1e-06

f32 = jnp.float32
bf16 = jnp.bfloat16


def dot_nn(left, right):
    return lax.dot_general(left, right, (((1,), (0,)), ((), ())), preferred_element_type=f32)


def dot_nt(left, right):
    return lax.dot_general(left, right, (((1,), (1,)), ((), ())), preferred_element_type=f32)


def dot_tn(left, right):
    return lax.dot_general(left, right, (((0,), (0,)), ((), ())), preferred_element_type=f32)


def normalize(values):
    center = values - jnp.mean(values, axis=-1, keepdims=True)
    recip = lax.rsqrt(jnp.mean(center * center, axis=-1, keepdims=True) + epsilon)
    return center * recip, recip


def norm_pullback(grad_normed, unit, recip, scale_row):
    scaled_grad = grad_normed * (1.0 + scale_row)
    mean_grad = jnp.mean(scaled_grad, axis=-1, keepdims=True)
    mean_unit = jnp.mean(scaled_grad * unit, axis=-1, keepdims=True)
    return recip * (scaled_grad - mean_grad - unit * mean_unit)


def column(row):
    return jnp.broadcast_to(row[...].astype(f32), (8, row.shape[1])).T[:, 0:1]


def head_rows(values, one):
    return values[one * HEAD_DIM : (one + 1) * HEAD_DIM].astype(bf16)


def token_sum(values):
    return jnp.sum(values, axis=0, keepdims=True)


def attention_kernel(parts, own_images, sc, tok, cot, mod, b_proj, *refs):
    w_qkv, w_proj, bias = refs[:parts], refs[parts : 2 * parts], refs[2 * parts : 3 * parts]
    qkv, prob, mixed, attn_out, residual, normed_mlp, normed, grad_mlp, down_sums = refs[3 * parts :]
    image = sc[0] * own_images + pl.program_id(0)
    live = jnp.where(image < sc[1], 1.0, 0.0).astype(f32)
    unit, _ = normalize(tok[0].astype(f32))
    normed[0] = (unit * (1.0 + mod[0, 1:2, :]) + mod[0, 0:1, :]).astype(bf16)
    grad = (mod[0, 5:6, :] * (cot[0].astype(f32) * live)).astype(bf16)
    grad_mlp[0] = grad
    down_sums[0] = token_sum(grad.astype(f32))
    cols = w_proj[0].shape[0]
    pairs = cols // (2 * HEAD_DIM)
    span = 2 * HEAD_DIM
    scale = HEAD_DIM ** (-0.5) * LOG2_E
    rows = normed[0]
    for part in range(parts):
        base = part * 3 * cols
        shift = bias[part][...].astype(f32).T
        for proj in range(3):
            lo = proj * cols
            value = dot_nt(w_qkv[part][lo : lo + cols, :], rows)
            if proj != 1:
                value = value + shift[:, proj // 2 : proj // 2 + 1]
            qkv[0, base + lo : base + lo + cols, :] = value.astype(bf16)

    def load(part, pair):
        at = part * 3 * cols + pair * span
        return [qkv[0, at + k * cols : at + k * cols + span, :].astype(f32) for k in range(3)]

    def score(loaded):
        query, key, _ = loaded
        return [dot_tn(head_rows(key, one), head_rows(query, one)) for one in range(2)]

    def spread(scores, head):
        raised = jnp.exp2((scores - jnp.max(scores, axis=0, keepdims=True)) * scale)
        share = 1.0 / jnp.sum(raised, axis=0, keepdims=True)
        prob_b = (raised * share).astype(bf16)
        prob[0, head] = prob_b
        return prob_b

    def mix(part, pair, loaded, probs):
        outs = [dot_nn(head_rows(loaded[2], one), probs[one]) for one in range(2)]
        to = part * cols + pair * span
        mixed[0, to : to + span, :] = jnp.concatenate(outs, axis=0).astype(bf16)

    work = [(part, pair) for part in range(parts) for pair in range(pairs)]
    loaded = load(*work[0])
    scores = score(loaded)
    waiting = None
    for turn, (part, pair) in enumerate(work):
        after = turn + 1 < len(work)
        if after:
            next_loaded = load(*work[turn + 1])
            next_scores = score(next_loaded)
        probs = [spread(scores[one], part * 2 * pairs + 2 * pair + one) for one in range(2)]
        if waiting is not None:
            mix(*waiting)
        waiting = (part, pair, loaded, probs)
        if after:
            loaded, scores = next_loaded, next_scores
    mix(*waiting)
    total = b_proj[...]
    for part in range(parts):
        total = total + dot_tn(mixed[0, part * cols : (part + 1) * cols, :], w_proj[part][...])
    attn_out[0] = total
    summed = tok[0].astype(f32) + mod[0, 2:3, :] * total
    residual[0] = summed
    unit, _ = normalize(summed)
    normed_mlp[0] = (unit * (1.0 + mod[0, 4:5, :]) + mod[0, 3:4, :]).astype(bf16)


def mlp_kernel(per, jobs, sc, rows, grad_mlp, *refs):
    count = len(jobs)
    weights = [refs[3 * k : 3 * k + 3] for k in range(count)]
    refs = refs[3 * count :]
    came = []
    for _, summed in jobs:
        came.append(refs[0] if summed else None)
        refs = refs[1:] if summed else refs
    act, back = refs[2], refs[3]
    refs = refs[4:]
    grads = []
    for cuts, _ in jobs:
        size = 1 if cuts is None else len(cuts)
        grads.append(refs[:size])
        refs = refs[size:]
    job, step = pl.program_id(0), pl.program_id(1)
    for k in range(count):

        @pl.when(job == k)
        def _(k=k):
            mlp_block(
                per, jobs[k][0], step, sc, rows, grad_mlp, *weights[k], act, back, grads[k], refs[k], came[k]
            )


def mlp_block(per, cuts, step, sc, rows, grad_mlp, w_up, w_down, bias, act, back, grads, sums, came):
    here = w_down.shape[0] // per
    hidden = lax.dot_general(
        w_up[...], rows[...], (((0,), (1,)), ((), ())), preferred_element_type=f32
    ) + column(bias)
    square = hidden * hidden
    bend = jnp.tanh(0.7978845608028654 * hidden * (1.0 + 0.044715 * square))
    half = 0.5 * (1.0 + bend)
    act_b = (hidden * half).astype(bf16)
    slope = half + 0.5 * hidden * (1.0 - bend * bend) * (
        0.7978845608028654 * (1.0 + 3.0 * 0.044715 * square)
    )
    back_b = (dot_nt(w_down[...], grad_mlp[...]) * slope).astype(bf16)
    act[0] = act_b
    back[0] = back_b
    sums[...] = dot_nt(jnp.ones((8, rows.shape[0]), bf16), back_b)[0:1]
    for lo_row, left, right in ((0, act_b, grad_mlp), (per, back_b, rows)):
        grad = dot_nn(left, right[...])
        for piece in range(here):
            value = grad[piece * per : (piece + 1) * per]
            if cuts is None:
                if came is not None:
                    value = value + came[piece, lo_row : lo_row + per, :].astype(f32)
                grads[0][piece, lo_row : lo_row + per, :] = value.astype(bf16)
            else:
                at = jnp.bitwise_xor(step * here + piece, sc[2])
                for (lo, hi), into in zip(cuts, grads):
                    into[at, lo_row : lo_row + per, :] = value[:, lo:hi].astype(bf16)


def grow(total, part_steps, left, rights, dims):
    step = pl.program_id(0)

    def term(right):
        return lax.dot_general(left, right[...], (dims, ((), ())), preferred_element_type=f32)

    @pl.when(step == 0)
    def _():
        total[...] = term(rights[0])

    @pl.when(jnp.logical_and(step > 0, step < part_steps))
    def _():
        total[...] += term(rights[0])

    @pl.when(jnp.logical_and(step >= part_steps, step < 2 * part_steps))
    def _():
        total[...] += term(rights[1])


def norm_back_kernel(
    part_steps, own_images, sc, back, w_up0, w_up1, residual, cot, mod, attn_out,
    grad_residual, grad_attn, sums, total
):
    grow(total, part_steps, back[0], (w_up0, w_up1), ((0,), (1,)))
    one = pl.program_id(0) - 2 * part_steps
    seq = residual.shape[1]

    @pl.when(one >= 0)
    def _():
        live = jnp.where(sc[0] * own_images + one < sc[1], 1.0, 0.0).astype(f32)
        grad_normed = total[pl.ds(pl.multiple_of(one * seq, seq), seq), :]
        unit, recip = normalize(residual[0])
        sums[0, 0:1, :] = token_sum(grad_normed)
        sums[0, 1:2, :] = token_sum(grad_normed * unit)
        grad_res = cot[0].astype(f32) * live + norm_pullback(grad_normed, unit, recip, mod[0, 4:5, :])
        grad_residual[0] = grad_res
        sums[0, 2:3, :] = token_sum(grad_res * attn_out[0])
        grad_att = (mod[0, 2:3, :] * grad_res).astype(bf16)
        grad_attn[0] = grad_att
        sums[0, 3:4, :] = token_sum(grad_att.astype(f32))


def back_kernel(parts, sc, grad_attn, qkv, prob, *refs):
    w_proj = refs[:parts]
    grad_qkv, grad_mixed = refs[parts:]
    cols = w_proj[0].shape[0]
    pairs = cols // (2 * HEAD_DIM)
    span = 2 * HEAD_DIM
    factor = HEAD_DIM ** (-0.5)
    grad_att = grad_attn[0]
    for part in range(parts):
        rows = slice(part * cols, (part + 1) * cols)
        grad_mixed[rows, :] = dot_nt(w_proj[part][...], grad_att).astype(bf16)

    def load(part, pair):
        at = part * 3 * cols + pair * span
        mix_at = part * cols + pair * span
        loaded = [qkv[0, at + k * cols : at + k * cols + span, :].astype(f32) for k in range(3)]
        return loaded + [grad_mixed[mix_at : mix_at + span, :].astype(f32)]

    def back_prob(loaded):
        return [dot_tn(head_rows(loaded[2], one), head_rows(loaded[3], one)) for one in range(2)]

    def back_scores(grad_prob, head):
        prob_b = prob[0, head]
        prob_f = prob_b.astype(f32)
        delta = jnp.sum(prob_f * grad_prob, axis=0, keepdims=True)
        return prob_b, (prob_f * (grad_prob - delta)).astype(bf16)

    work = [(part, pair) for part in range(parts) for pair in range(pairs)]
    loaded = load(*work[0])
    grad_probs = back_prob(loaded)
    for turn, (part, pair) in enumerate(work):
        after = turn + 1 < len(work)
        if after:
            next_loaded = load(*work[turn + 1])
            next_probs = back_prob(next_loaded)
        middle = [back_scores(grad_probs[one], part * 2 * pairs + 2 * pair + one) for one in range(2)]
        query, key, _, grads = loaded
        to_query = [dot_nn(head_rows(key, one), middle[one][1]) * factor for one in range(2)]
        to_key = [dot_nt(head_rows(query, one), middle[one][1]) * factor for one in range(2)]
        to_value = [dot_nt(head_rows(grads, one), middle[one][0]) for one in range(2)]
        at = part * 3 * cols + pair * span
        for k, outs in enumerate((to_query, to_key, to_value)):
            into = slice(at + k * cols, at + k * cols + span)
            grad_qkv[0, into, :] = jnp.concatenate(outs, axis=0).astype(bf16)
        if after:
            loaded, grad_probs = next_loaded, next_probs


def attn_grad_kernel(pieces, per, cuts, sc, *refs):
    grad_qkv, mixed, normed, grad_attn = refs[:pieces], refs[pieces], refs[pieces + 1], refs[pieces + 2]
    grads, sums = refs[pieces + 3 : -1], refs[-1]
    step = pl.program_id(0)
    here = mixed.shape[1] // per
    images = mixed.shape[0]
    each = images // pieces

    def spread(total):
        total = total.astype(bf16)
        for piece in range(here):
            at = jnp.bitwise_xor(step * here + piece, sc[2])
            for (lo, hi), into in zip(cuts, grads):
                into[at] = total[piece * per : (piece + 1) * per, lo:hi]

    @pl.when(step < 3)
    def _():
        ones = jnp.ones((8, mixed.shape[2]), bf16)
        total = count = None
        for image in range(images):
            left = grad_qkv[image // each][image % each]
            term, one = dot_nn(left, normed[image]), dot_nt(ones, left)
            total = term if image == 0 else total + term
            count = one if image == 0 else count + one
        sums[0] = count[0:1]
        spread(total)

    @pl.when(step == 3)
    def _():
        total = dot_nn(mixed[0], grad_attn[0])
        for image in range(1, images):
            total = total + dot_nn(mixed[image], grad_attn[image])
        spread(total)


def first_back_kernel(pieces, images, sc, *refs):
    grad_qkv = refs[:pieces]
    w_qkv0, w_qkv1, tok, mod, grad_residual = refs[pieces : pieces + 5]
    grad_tokens, grad_own, sums, total = refs[pieces + 5 :]
    step = pl.program_id(0)
    each = images // pieces
    seq = tok.shape[1]

    def add(w_qkv, fresh):
        for one in range(images):
            term = dot_tn(grad_qkv[one // each][one % each], w_qkv[...])
            if fresh:
                total[one * seq : (one + 1) * seq, :] = term
            else:
                total[one * seq : (one + 1) * seq, :] += term

    @pl.when(step == 0)
    def _():
        add(w_qkv0, True)

    @pl.when(jnp.logical_and(step > 0, step < 3))
    def _():
        add(w_qkv0, False)

    @pl.when(jnp.logical_and(step >= 3, step < 6))
    def _():
        add(w_qkv1, False)

    @pl.when(step >= 6)
    def _():
        grad_normed = total[pl.ds(pl.multiple_of((step - 6) * seq, seq), seq), :]
        unit, recip = normalize(tok[0].astype(f32))
        sums[0, 0:1, :] = token_sum(grad_normed)
        sums[0, 1:2, :] = token_sum(grad_normed * unit)
        grad = grad_residual[0] + norm_pullback(grad_normed, unit, recip, mod[0, 1:2, :])
        grad_tokens[0] = grad
        grad_own[0] = grad


def output_kernel(
    part_steps, own_images, sc, act, w_down0, w_down1, residual, cot, mod, b_down, output, own, sums, total
):
    grow(total, part_steps, act[0], (w_down0, w_down1), ((0,), (0,)))
    one = pl.program_id(0) - 2 * part_steps
    seq = residual.shape[1]

    @pl.when(one >= 0)
    def _():
        live = jnp.where(sc[0] * own_images + one < sc[1], 1.0, 0.0).astype(f32)
        mlp_out = total[pl.ds(pl.multiple_of(one * seq, seq), seq), :] + b_down[...]
        sums[0] = token_sum((cot[0].astype(f32) * live) * mlp_out)
        rows = ((residual[0] + mod[0, 5:6, :] * mlp_out) * live).astype(bf16)
        output[0] = rows
        own[0] = rows


def final_piece(sc, halves, piece, store):
    rel = jnp.bitwise_xor(piece, sc[2])
    for low, high, route, lo, hi in halves:
        bits = [(rel >> bit) & 1 for bit in route]
        index = bits[1] * 4 + bits[2] * 2 + bits[3]

        @pl.when(bits[0] == 0)
        def _(low=low, index=index, lo=lo, hi=hi):
            store(low[index].astype(f32), lo, hi)

        @pl.when(bits[0] == 1)
        def _(high=high, index=index, lo=lo, hi=hi):
            store(high[index].astype(f32), lo, hi)


def final_mlp_kernel(cuts, per, sc, *refs):
    count = 2 * len(cuts)
    arrays, (_, _, down, up, mark, turned) = refs[:count], refs[count:]
    here = down.shape[0] // per
    halves = [(arrays[2 * k], arrays[2 * k + 1]) + cut for k, cut in enumerate(cuts)]
    for piece in range(here):

        def store(value, lo, hi, piece=piece):
            down[piece * per : (piece + 1) * per, lo:hi] = value[0:per]
            turned[piece * per : (piece + 1) * per, lo:hi] = value[per : 2 * per]

        final_piece(sc, halves, pl.program_id(0) * here + piece, store)
    up[...] = turned[...].T
    mark[...] = jnp.zeros_like(mark)


def final_plain_kernel(per, sc, summed, down_in, up_in, down, up, mark, turned):
    for piece in range(summed.shape[0]):
        lo = piece * per
        down[lo : lo + per, :] = summed[piece, 0:per, :].astype(f32)
        turned[lo : lo + per, :] = summed[piece, per : 2 * per, :].astype(f32)
    up[...] = turned[...].T
    mark[...] = jnp.zeros_like(mark)


def final_attn_kernel(cuts, per, sc, *refs):
    count = 2 * len(cuts)
    arrays, (qkv, proj) = refs[:count], refs[count:]
    here = proj.shape[0] // per
    halves = [(arrays[2 * k], arrays[2 * k + 1]) + cut for k, cut in enumerate(cuts)]
    for target, wanted in ((qkv, True), (proj, False)):

        @pl.when((pl.program_id(0) < 3) == wanted)
        def _(target=target):
            for piece in range(here):

                def store(value, lo, hi, piece=piece):
                    target[piece * per : (piece + 1) * per, lo:hi] = value

                final_piece(sc, halves, pl.program_id(0) * here + piece, store)


def run_kernel(
    body, sc, args, in_specs, out_specs, out_shape, grid, micros, scratch=(), alias=None, room=60
):
    size = sum(a.size * a.dtype.itemsize for a in args) + sum(
        s.size * s.dtype.itemsize for s in out_shape
    )
    return pl.pallas_call(
        body,
        out_shape=out_shape,
        grid_spec=pltpu.PrefetchScalarGridSpec(
            num_scalar_prefetch=1,
            grid=grid,
            in_specs=in_specs,
            out_specs=out_specs,
            scratch_shapes=list(scratch),
        ),
        compiler_params=pltpu.CompilerParams(vmem_limit_bytes=room << 20),
        cost_estimate=pl.CostEstimate(
            flops=int(micros * 1.15e9), bytes_accessed=int(min(size, micros * 1e6)), transcendentals=0
        ),
        input_output_aliases=alias or {},
    )(sc, *args)


def whole_block(array):
    zeros = (0,) * array.ndim
    return pl.BlockSpec(array.shape, lambda *_: zeros, pipeline_mode=pl.Buffered(1))


def shape_of(dims, kind):
    return jax.ShapeDtypeStruct(dims, kind)


SWAP = [(0, 1), (1, 0)]


def swap_cores(value):
    return lax.ppermute(value, "mp", SWAP)


def bit_pairs(bit):
    return [(index, index ^ (1 << bit)) for index in range(16)]


MLP_WAYS = ((0, 640, (0, 1, 2, 3)), (640, 1152, (1, 0, 2, 3)))
ATTN_WAYS = ((0, 512, (0, 1, 2, 3)), (512, 896, (1, 0, 2, 3)), (896, 1152, (2, 3, 0, 1)))


def columns(ways):
    return tuple((lo, hi) for lo, hi, _ in ways)


def cut(array, bits, bit, side):
    return lax.index_in_dim(array, side, bits.index(bit), keepdims=False)


def left_bits(done):
    return [bit for bit in (3, 2, 1, 0) if bit not in done]


def exchange(values, bits):
    return [lax.ppermute(value, "dp", bit_pairs(bit)) for value, bit in zip(values, bits)]


def reduce_flow(ways, get_own, others):
    others = yield others
    came = [swap_cores(other) for other in others]
    yield None
    own, came = yield [get_own(), came]
    firsts, seconds = ([a.reshape((2, 2, 2, 2) + a.shape[1:]) for a in arrays] for arrays in (own, came))
    routes = [way for _, _, way in ways]
    for stage in range(4):
        sends, keeps = [], []
        for route, one, two in zip(routes, firsts, seconds):
            bits = left_bits(route[:stage])
            for side, into in ((1, sends), (0, keeps)):
                into.append(cut(one, bits, route[stage], side) + cut(two, bits, route[stage], side))
        if stage == 2 and routes[0][2:] == routes[1][2:]:
            sends = [jnp.concatenate(sends[:2], axis=-1)] + sends[2:]
            keeps = [jnp.concatenate(keeps[:2], axis=-1)] + keeps[2:]
            routes = [routes[0]] + routes[2:]
        sends, keeps = yield [sends, keeps]
        comes = exchange(sends, [route[stage] for route in routes])
        yield None
        firsts, seconds = yield [keeps, comes]
    return [one + two for one, two in zip(firsts, seconds)]


def gather_flow(ways, have):
    routes = [ways[0][2]] + [way for _, _, way in ways[2:]]
    middle = ways[0][1]
    (have,) = yield [have]
    comes = exchange(have, [route[3] for route in routes])
    have = [one[None] for one in have]
    comes = [one[None] for one in comes]
    yield None
    for stage in (2, 1, 0):
        have, comes = yield [have, comes]
        joined = [jnp.concatenate([one, two]) for one, two in zip(have, comes)]
        if stage == 1:
            joined = [joined[0][..., :middle], joined[0][..., middle:]] + joined[1:]
            routes = [way for _, _, way in ways]
        (have,) = yield [joined]
        comes = exchange(have, [route[stage] for route in routes])
        yield None
    have, comes = yield [have, comes]
    return [part for pair in zip(have, comes) for part in pair]


def sum_flow(ways, get_own, others):
    have = yield from reduce_flow(ways, get_own, others)
    return (yield from gather_flow(ways, have))


def swap_flow(other):
    (other,) = yield [other]
    came = swap_cores(other)
    yield None
    (came,) = yield [came]
    return came


def rows_flow(rows):
    for bit in (3, 2, 1, 0):
        (rows,) = yield [rows]
        came = lax.ppermute(rows, "dp", bit_pairs(bit))
        yield None
        rows, came = yield [rows, came]
        rows = jnp.concatenate([rows, came])
    return rows


class Order:
    def __init__(self, sc):
        self.sc = sc
        self.results = {}

    def fence(self, values):
        self.sc, values = lax.optimization_barrier((self.sc, values))
        return values

    def after(self, value):
        self.sc, _ = lax.optimization_barrier((self.sc, value))

    def tick(self, *flows):
        replies = {flow: None for flow in flows if flow not in self.results}
        while replies:
            wants = {}
            for flow, reply in replies.items():
                try:
                    want = flow.send(reply)
                except StopIteration as stop:
                    self.results[flow] = stop.value
                    continue
                if want is not None:
                    wants[flow] = want
            replies = dict(zip(wants, self.fence(list(wants.values())))) if wants else {}

    def finish(self, flow):
        while flow not in self.results:
            self.tick(flow)
        return self.results[flow]


CHUNKS = 3
PLAIN = 2


def fill_other(both, came, core):
    size = came.shape[0]
    return lax.dynamic_update_slice_in_dim(both, came, (1 - core) * size, 0)


def fast_device(
    tokens, condition, counts, w_qkv, b_qv, w_proj, b_proj, w_up, b_up, w_down, b_down, w_mod, b_mod,
    cotangent,
):
    slots, seq, dim = tokens.shape
    images = slots // 2
    count = images * seq
    cols = w_qkv.shape[2]
    ff = w_up.shape[1]
    own_cols = w_mod.shape[1]
    heads = cols // HEAD_DIM
    core = lax.axis_index("mp")
    order = Order(jnp.stack([core, counts[0], lax.axis_index("dp")]).astype(jnp.int32))

    qkv_rows = jnp.transpose(w_qkv, (1, 2, 0)).reshape(3 * cols, dim)
    wq = [qkv_rows, swap_cores(qkv_rows)]
    wp = [w_proj, swap_cores(w_proj)]
    qkv_bias = [b_qv, swap_cores(b_qv)]

    cond_f = condition.astype(f32)
    scaled = jax.nn.silu(cond_f).astype(bf16)
    own_mod = jnp.dot(scaled, w_mod, preferred_element_type=f32) + b_mod.astype(f32)
    other_mod = swap_cores(own_mod)
    sides = [jnp.where(core == side, own_mod, other_mod) for side in range(2)]
    modulation = jnp.concatenate(sides, axis=1).reshape(slots, 6, dim)
    proj_bias = b_proj.astype(f32)[None]
    down_bias = b_down.astype(f32)[None]

    crossed = (wq[1], wp[1], qkv_bias[1], modulation)
    late_up, late_down, late_bias = lax.optimization_barrier((w_up, w_down, b_up, crossed))[:3]
    wu = [w_up, swap_cores(late_up)]
    wd = [w_down, swap_cores(late_down)]
    up_bias = [b_up[None], swap_cores(late_bias[None])]

    local = lambda i, s: (s[0] * images + i, 0, 0)
    mine = lambda i, s: (i, 0, 0)
    tok_spec = pl.BlockSpec((1, seq, dim), local)
    own_spec = pl.BlockSpec((1, seq, dim), mine)
    mod_spec = pl.BlockSpec((1, 6, dim), local)
    row_spec = pl.BlockSpec((1, 1, dim), mine)
    qkv_spec = pl.BlockSpec((1, 6 * cols, seq), mine)
    prob_spec = pl.BlockSpec((1, 2 * heads, seq, seq), lambda i, s: (i, 0, 0, 0))
    mixed_spec = pl.BlockSpec((1, 2 * cols, seq), mine)
    token_f = shape_of((images, seq, dim), f32)
    token_b = shape_of((images, seq, dim), bf16)
    attn_args = wq + wp + qkv_bias
    qkv, prob, mixed, attn_out, residual, normed_mlp, normed, grad_mlp, down_sums = run_kernel(
        functools.partial(attention_kernel, 2, images),
        order.sc,
        [tokens, cotangent, modulation, proj_bias] + attn_args,
        [tok_spec, tok_spec, mod_spec, whole_block(proj_bias)] + [whole_block(a) for a in attn_args],
        [qkv_spec, prob_spec, mixed_spec] + [own_spec] * 5 + [row_spec],
        [
            shape_of((images, 6 * cols, seq), bf16),
            shape_of((images, 2 * heads, seq, seq), bf16),
            shape_of((images, 2 * cols, seq), bf16),
            token_f,
            token_f,
            token_b,
            token_b,
            token_b,
            shape_of((images, 1, dim), f32),
        ],
        (images,),
        33,
    )
    order.after(down_sums)

    rows_flat = normed_mlp.reshape(count, dim)
    grad_flat = grad_mlp.reshape(count, dim)
    width = ff // CHUNKS
    per = width // 16
    steps = 2
    block = width // steps
    anywhere = pl.BlockSpec(memory_space=pl.ANY)
    act = back = jnp.zeros((8, 128), bf16)
    up_sums = {}

    def mlp_call(jobs, came, micros):
        nonlocal act, back
        first = act.shape[0] == 8
        kinds = tuple((None if job[0] < PLAIN else columns(MLP_WAYS), job in came) for job in jobs)

        def turn(k):
            return lambda p, s, c: jnp.clip((p - k) * steps + s, 0, steps - 1)

        def pick(values):
            return lambda p: sum(jnp.where(p == k, value, 0) for k, value in enumerate(values))

        parts = pick([part for _, part in jobs])
        starts = pick([chunk * steps for chunk, _ in jobs])
        spread = pl.BlockSpec((1, block, count), lambda p, s, c: (parts(p), starts(p) + s, 0))
        args, specs = [], []
        for k, (chunk, part) in enumerate(jobs):
            at = chunk * steps
            wide = lambda p, s, c, k=k, at=at: (0, at + turn(k)(p, s, c))
            tall = lambda p, s, c, k=k, at=at: (at + turn(k)(p, s, c), 0)
            args += [wu[part], wd[part], up_bias[part]]
            specs += [
                pl.BlockSpec((dim, block), wide),
                pl.BlockSpec((block, dim), tall),
                pl.BlockSpec((1, block), wide),
            ]
        grad_specs, grad_shapes, sizes = [], [], []
        for k, (split, _) in enumerate(kinds):
            own = lambda p, s, c, k=k: (turn(k)(p, s, c), 0, 0)
            fixed = lambda p, s, c: (0, 0, 0)
            wides = [dim] if split is None else [hi - lo for lo, hi in split]
            lead = (16 // steps, own) if split is None else (16, fixed)
            grad_specs.append([pl.BlockSpec((lead[0], 2 * per, wide), lead[1]) for wide in wides])
            grad_shapes += [shape_of((16, 2 * per, wide), bf16) for wide in wides]
            sizes.append(len(wides))
        for k, job in enumerate(jobs):
            if job in came:
                args.append(came[job])
                specs += grad_specs[k]
        args += [act, back]
        spot = len(args) + 1
        outs = run_kernel(
            functools.partial(mlp_kernel, per, kinds),
            order.sc,
            [rows_flat, grad_flat] + args,
            [whole_block(rows_flat), whole_block(grad_flat)] + specs + [anywhere, anywhere],
            [spread, spread]
            + [spec for specs in grad_specs for spec in specs]
            + [pl.BlockSpec((1, block), lambda p, s, c, k=k: (0, turn(k)(p, s, c))) for k in range(len(jobs))],
            [shape_of((2, ff, count), bf16)] * 2 + grad_shapes + [shape_of((1, width), f32)] * len(jobs),
            (len(jobs), steps),
            micros,
            alias=None if first else {spot: 0, spot + 1: 1},
        )
        act, back = outs[:2]
        grads, outs = list(outs[2 : 2 + sum(sizes)]), outs[2 + sum(sizes) :]
        up_sums.update(zip(jobs, outs))
        order.after(outs[-1])
        return [[grads.pop(0) for _ in range(size)] for size in sizes]

    summed = range(PLAIN)
    swaps = [swap_flow(grad) for (grad,) in mlp_call([(chunk, 1) for chunk in summed], {}, 26)]
    order.tick(*swaps)
    rest = range(PLAIN, CHUNKS)
    made_rest = []
    flows = [
        sum_flow(MLP_WAYS, lambda k=k: made_rest[k], others)
        for k, others in enumerate(mlp_call([(chunk, 1) for chunk in rest], {}, 13))
    ]
    wide_scaled = jnp.pad(scaled.reshape(-1), (0, 3 * own_cols - slots * dim)).reshape(3, own_cols)
    early = rows_flow(wide_scaled)
    order.tick(*swaps, *flows, early)
    came = {(chunk, 0): order.results[swap] for chunk, swap in zip(summed, swaps)}
    grads = mlp_call([(chunk, 0) for chunk in summed], came, 26)
    plain_sums = lax.psum([grad for (grad,) in grads], "dp")
    order.tick(early)
    made_rest += mlp_call([(chunk, 0) for chunk in rest], {}, 13)
    order.tick(*flows, early)

    reach = 768
    turns = ff // reach
    every = lambda s, c: (0, 0, 0)
    tail = lambda first: lambda s, c: (jnp.maximum(s - first, 0), 0, 0)
    tail_local = lambda first: lambda s, c: (c[0] * images + jnp.maximum(s - first, 0), 0, 0)

    def image_spec(first, where=tail):
        return pl.BlockSpec((1, seq, dim), where(first))

    def rows_of(part, size):
        if part == 0:
            return lambda s, c: jnp.minimum(s, size - 1)
        return lambda s, c: jnp.clip(s - size, 0, size - 1)

    span_spec = pl.BlockSpec(
        (1, reach, count),
        lambda s, c: (jnp.minimum(s // turns, 1), jnp.where(s < 2 * turns, s % turns, turns - 1), 0),
    )
    grad_residual, grad_attn, mid_sums = run_kernel(
        functools.partial(norm_back_kernel, turns, images),
        order.sc,
        [back] + wu + [residual, cotangent, modulation, attn_out],
        [
            span_spec,
            pl.BlockSpec((dim, reach), lambda s, c: (0, rows_of(0, turns)(s, c))),
            pl.BlockSpec((dim, reach), lambda s, c: (0, rows_of(1, turns)(s, c))),
            image_spec(2 * turns),
            image_spec(2 * turns, tail_local),
            pl.BlockSpec((1, 6, dim), tail_local(2 * turns)),
            image_spec(2 * turns),
        ],
        [image_spec(2 * turns)] * 2 + [pl.BlockSpec((1, 4, dim), tail(2 * turns))],
        [token_f, token_b, shape_of((images, 4, dim), f32)],
        (2 * turns + images,),
        60,
        scratch=[pltpu.VMEM((count, dim), f32)],
    )
    order.after(mid_sums)
    order.tick(*flows, early)
    pieces = 2
    each = images // pieces
    grad_qkv = []
    for piece in range(pieces):
        there = lambda i, s, piece=piece: (piece * each + i, 0, 0)
        (grad_piece,) = run_kernel(
            functools.partial(back_kernel, 2),
            order.sc,
            [grad_attn, qkv, prob] + wp,
            [
                pl.BlockSpec((1, seq, dim), there),
                pl.BlockSpec((1, 6 * cols, seq), there),
                pl.BlockSpec((1, 2 * heads, seq, seq), lambda i, s, piece=piece: (piece * each + i, 0, 0, 0)),
            ]
            + [whole_block(a) for a in wp],
            [qkv_spec],
            [shape_of((each, 6 * cols, seq), bf16)],
            (each,),
            60,
            scratch=[pltpu.VMEM((2 * cols, seq), bf16)],
            )
        grad_qkv.append(grad_piece)
        order.after(grad_piece)
        order.tick(*flows, early)

    attn_per = 4 * cols // 16
    qv_sums = [None, None]

    def attn_part(part):
        *grads, sums = run_kernel(
            functools.partial(attn_grad_kernel, pieces, attn_per, columns(ATTN_WAYS)),
            order.sc,
            grad_qkv + [mixed, normed, grad_attn],
            [
                pl.BlockSpec((each, cols, seq), lambda s, c: (0, 3 * part + jnp.minimum(s, 2), 0))
                for _ in range(pieces)
            ]
            + [pl.BlockSpec((images, cols, seq), lambda s, c: (0, part, 0))]
            + [whole_block(normed), whole_block(grad_attn)],
            [pl.BlockSpec((16, attn_per, hi - lo), every) for lo, hi in columns(ATTN_WAYS)]
            + [pl.BlockSpec((1, 1, cols), lambda s, c: (jnp.minimum(s, 2), 0, 0))],
            [shape_of((16, attn_per, hi - lo), bf16) for lo, hi in columns(ATTN_WAYS)]
            + [shape_of((3, 1, cols), f32)],
            (4,),
            60,
            )
        qv_sums[part] = sums
        order.after(sums)
        return grads

    grad_other = attn_part(1)
    made = []
    last = sum_flow(ATTN_WAYS, lambda: made[0], grad_other)
    order.tick(last, *flows)
    made.append(attn_part(0))
    order.tick(last, *flows)

    first_spec = lambda part: pl.BlockSpec((cols, dim), lambda s, c: (rows_of(part, 3)(s, c), 0))
    grad_tokens, grad_own_tokens, low_sums = run_kernel(
        functools.partial(first_back_kernel, pieces, images),
        order.sc,
        grad_qkv + wq + [tokens, modulation, grad_residual],
        [pl.BlockSpec((each, cols, seq), lambda s, c: (0, jnp.minimum(s, 5), 0)) for _ in range(pieces)]
        + [first_spec(0), first_spec(1)]
        + [image_spec(6, tail_local), pl.BlockSpec((1, 6, dim), tail_local(6)), image_spec(6)],
        [image_spec(6, tail_local), image_spec(6), pl.BlockSpec((1, 2, dim), tail(6))],
        [shape_of((slots, seq, dim), f32), token_f, shape_of((images, 2, dim), f32)],
        (6 + images,),
        60,
        scratch=[pltpu.VMEM((count, dim), f32)],
    )
    order.after(low_sums)
    order.tick(last, *flows)
    down_spec = lambda part: pl.BlockSpec((reach, dim), lambda s, c: (rows_of(part, turns)(s, c), 0))
    output, own_output, gate_sums = run_kernel(
        functools.partial(output_kernel, turns, images),
        order.sc,
        [act] + wd + [residual, cotangent, modulation, down_bias],
        [
            span_spec,
            down_spec(0),
            down_spec(1),
            image_spec(2 * turns),
            image_spec(2 * turns, tail_local),
            pl.BlockSpec((1, 6, dim), tail_local(2 * turns)),
            whole_block(down_bias),
        ],
        [image_spec(2 * turns, tail_local), image_spec(2 * turns), pl.BlockSpec((1, 1, dim), tail(2 * turns))],
        [shape_of((slots, seq, dim), bf16), token_b, shape_of((images, 1, dim), f32)],
        (2 * turns + images,),
        60,
        scratch=[pltpu.VMEM((count, dim), f32)],
    )
    order.after(gate_sums)
    order.tick(last, *flows)

    low_sums, mid_sums, gate_sums, down_sums, qv_sums, up_sums = order.fence(
        (low_sums, mid_sums, gate_sums, down_sums, qv_sums, up_sums)
    )
    grad_modulation = jnp.concatenate([low_sums, mid_sums[:, 2:3], mid_sums[:, 0:2], gate_sums], axis=1)
    grad_modulation = grad_modulation.reshape(images, 6 * dim).astype(bf16)
    bias_sums = [
        jnp.concatenate(
            [qv_sums[part][0], qv_sums[part][2]]
            + [up_sums[chunk, part] for chunk in range(CHUNKS)],
            axis=1,
        )
        for part in range(2)
    ]
    shared = jnp.concatenate(
        [
            jnp.sum(mid_sums[:, 3], axis=0, keepdims=True),
            jnp.sum(down_sums[:, 0], axis=0, keepdims=True),
            jnp.zeros((1, own_cols - 2 * dim), f32),
        ],
        axis=1,
    )
    halves = grad_modulation.reshape(images, 2, own_cols)
    kept = lax.dynamic_index_in_dim(halves, core, 1, keepdims=False)
    given = lax.dynamic_index_in_dim(halves, 1 - core, 1, keepdims=False)
    got = swap_cores(jnp.concatenate([given.astype(f32), bias_sums[1], shared]))
    came = got[:images].astype(bf16)
    group_mod = jnp.where(core == 0, jnp.concatenate([kept, came]), jnp.concatenate([came, kept]))
    own_bias_sum = bias_sums[0] + got[images : images + 1]
    shared_sum = shared + got[images + 1 :]
    packed_rows = jnp.concatenate(
        [group_mod, own_bias_sum.astype(bf16), shared_sum.astype(bf16)]
    )
    (packed_rows,) = order.fence([packed_rows])
    small = rows_flow(packed_rows)
    def cuts(ways):
        return tuple((way, lo, hi) for lo, hi, way in ways)

    grad_w_down = grad_w_up = jnp.zeros((8, 128), f32)

    def final_mlp(chunk, body, args):
        nonlocal grad_w_down, grad_w_up
        first = grad_w_down.shape[0] == 8
        spot = len(args) + 1
        grad_w_down, grad_w_up, _ = run_kernel(
            body,
            order.sc,
            list(args) + [grad_w_down, grad_w_up],
            [
                whole_block(a)
                if a.shape[0] == 8
                else pl.BlockSpec((16 // steps,) + a.shape[1:], lambda s, c: (s, 0, 0))
                for a in args
            ]
            + [anywhere, anywhere],
            [
                pl.BlockSpec((block, dim), lambda s, c: (chunk * steps + s, 0)),
                pl.BlockSpec((dim, block), lambda s, c: (0, chunk * steps + s)),
                pl.BlockSpec((8, 128), lambda s, c: (0, 0)),
            ],
            [shape_of((ff, dim), f32), shape_of((dim, ff), f32), shape_of((8, 128), f32)],
            (steps,),
            4,
            scratch=[pltpu.VMEM((block, dim), f32)],
            alias=None if first else {spot: 0, spot + 1: 1},
        )
        grad_w_down, grad_w_up = order.fence((grad_w_down, grad_w_up))

    order.tick(last, small, *flows)
    own_output, grad_own_tokens, group_mod = order.fence((own_output, grad_own_tokens, group_mod))
    other_output, other_tokens = swap_cores(own_output), swap_cores(grad_own_tokens)
    part_scaled = outer_cols(group_mod, w_mod).astype(bf16)
    part_scaled = order.fence(part_scaled)
    for chunk, flow in enumerate(flows):
        body = functools.partial(final_mlp_kernel, cuts(MLP_WAYS), per)
        final_mlp(PLAIN + chunk, body, order.finish(flow))
    order.tick(last, small)
    came_scaled = swap_cores(order.fence(part_scaled))
    other_output, other_tokens = order.fence((other_output, other_tokens))
    output = fill_other(output, other_output, core)
    grad_tokens = fill_other(grad_tokens, other_tokens, core)
    output, grad_tokens = order.fence((output, grad_tokens))
    order.tick(last, small)
    grad_scaled = part_scaled.astype(f32) + order.fence(came_scaled).astype(f32)
    _, silu_back = jax.vjp(jax.nn.silu, cond_f)
    grad_condition = silu_back(grad_scaled)[0]
    grad_condition = order.fence(grad_condition)
    plain_sums = order.fence(plain_sums)
    final_mlp(0, functools.partial(final_plain_kernel, per), [plain_sums[0]])
    order.tick(last, small)
    final_mlp(1, functools.partial(final_plain_kernel, per), [plain_sums[1]])
    order.tick(last)
    all_rows = order.fence(order.finish(small)).reshape(16, slots + 2, own_cols)
    all_mod = all_rows[:, :slots].reshape(-1, own_cols)
    all_scaled = order.finish(early).reshape(16, -1)[:, : slots * dim].reshape(-1, dim)
    grad_w_mod = inner_rows(all_scaled, all_mod)
    grad_b_mod = jnp.sum(all_mod.astype(f32), axis=0)
    bias_total = jnp.sum(all_rows[:, slots : slots + 2].astype(f32), axis=0)
    grad_b_qv = bias_total[0, : 2 * cols].reshape(2, cols)
    grad_b_up = bias_total[0, 2 * cols :]
    grad_b_proj = bias_total[1, :dim]
    grad_b_down = bias_total[1, dim : 2 * dim]
    grad_w_mod = order.fence(grad_w_mod)
    args = order.finish(last)
    grad_qkv_rows, grad_w_proj = run_kernel(
        functools.partial(final_attn_kernel, cuts(ATTN_WAYS), attn_per),
        order.sc,
        list(args),
        [whole_block(a) for a in args],
        [
            pl.BlockSpec((cols, dim), lambda s, c: (jnp.minimum(s, 2), 0)),
            pl.BlockSpec((cols, dim), lambda s, c: (0, 0)),
        ],
        [shape_of((3 * cols, dim), f32), shape_of((cols, dim), f32)],
        (4,),
        9,
    )
    grad_w_qkv = jnp.transpose(grad_qkv_rows.reshape(3, cols, dim), (2, 0, 1))
    return (
        output,
        grad_tokens,
        grad_condition,
        grad_w_qkv,
        grad_b_qv,
        grad_w_proj,
        grad_b_proj,
        grad_w_up,
        grad_b_up,
        grad_w_down,
        grad_b_down,
        grad_w_mod,
        grad_b_mod,
    )


def layer_norm(values):
    center = values - jnp.mean(values, axis=-1, keepdims=True)
    return center * lax.rsqrt(jnp.mean(center * center, axis=-1, keepdims=True) + epsilon)


def modulate(values, shift_part, scale_part):
    return layer_norm(values) * (1.0 + scale_part) + shift_part


def gelu_tanh(values):
    return (
        0.5
        * values
        * (1.0 + jnp.tanh(0.7978845608028654 * (values + 0.044715 * values * values * values)))
    )


def inner_rows(left, right):
    return lax.dot_general(
        left, right, (((0,), (0,)), ((), ())), preferred_element_type=jnp.float32
    )


def outer_cols(left, right):
    return lax.dot_general(
        left, right, (((1,), (1,)), ((), ())), preferred_element_type=jnp.float32
    )


def attention_forward(query_rows, key_rows, value_rows):
    factor = HEAD_DIM ** (-0.5)
    scores = (
        jnp.einsum("bqhd,bkhd->bhqk", query_rows, key_rows, preferred_element_type=jnp.float32)
        * factor
    )
    row_max = jnp.max(scores, axis=-1, keepdims=True)
    row_total = jnp.sum(jnp.exp(scores - row_max), axis=-1, keepdims=True)
    logsum = row_max + jnp.log(row_total)
    prob_b = jnp.exp(scores - logsum).astype(jnp.bfloat16)
    mixed_out = jnp.einsum(
        "bhqk,bkhd->bqhd", prob_b, value_rows, preferred_element_type=jnp.float32
    )
    return (mixed_out, logsum)


def attention_backward(query_rows, key_rows, value_rows, logsum, grad_mixed):
    factor = HEAD_DIM ** (-0.5)
    scores = (
        jnp.einsum("bqhd,bkhd->bhqk", query_rows, key_rows, preferred_element_type=jnp.float32)
        * factor
    )
    prob_f = jnp.exp(scores - logsum)
    prob_b = prob_f.astype(jnp.bfloat16)
    grad_prob = jnp.einsum(
        "bqhd,bkhd->bhqk", grad_mixed, value_rows, preferred_element_type=jnp.float32
    )
    row_delta = jnp.sum(prob_f * grad_prob, axis=-1, keepdims=True)
    grad_scores = (prob_f * (grad_prob - row_delta)).astype(jnp.bfloat16)
    grad_query = (
        jnp.einsum("bhqk,bkhd->bqhd", grad_scores, key_rows, preferred_element_type=jnp.float32)
        * factor
    )
    grad_key = (
        jnp.einsum("bhqk,bqhd->bkhd", grad_scores, query_rows, preferred_element_type=jnp.float32)
        * factor
    )
    grad_value = jnp.einsum(
        "bhqk,bqhd->bkhd", prob_b, grad_mixed, preferred_element_type=jnp.float32
    )
    return (
        grad_query.astype(jnp.bfloat16),
        grad_key.astype(jnp.bfloat16),
        grad_value.astype(jnp.bfloat16),
    )


def forward(tokens_f, spans, weights, repeat):
    w_qkv, b_qv, w_proj, b_proj, w_up, b_up, w_down, b_down = weights
    shift_attn, scale_attn, gate_attn, shift_mlp, scale_mlp, gate_mlp = spans
    slot_count, seq_len, model_dim = tokens_f.shape
    row_count = slot_count * seq_len
    head_cols = w_qkv.shape[2]
    head_count = head_cols // HEAD_DIM
    shape_four = (slot_count, seq_len, head_count, HEAD_DIM)
    normed = (
        modulate(tokens_f, shift_attn, scale_attn)
        .astype(jnp.bfloat16)
        .reshape(row_count, model_dim)
    )
    projected = jnp.dot(
        normed, w_qkv.reshape(model_dim, 3 * head_cols), preferred_element_type=jnp.float32
    )
    qkv_bias = jnp.stack([b_qv[0], jnp.zeros_like(b_qv[0]), b_qv[1]]).astype(jnp.float32)
    projected = (projected.reshape(row_count, 3, head_cols) + qkv_bias).astype(jnp.bfloat16)
    query_rows = projected[:, 0].reshape(shape_four)
    key_rows = projected[:, 1].reshape(shape_four)
    value_rows = projected[:, 2].reshape(shape_four)
    mixed_out, logsum = attention_forward(query_rows, key_rows, value_rows)
    mixed_b = mixed_out.astype(jnp.bfloat16).reshape(row_count, head_cols)
    partial_value = jnp.dot(mixed_b, w_proj, preferred_element_type=jnp.float32)
    if repeat:
        summed = lax.psum(partial_value.astype(jnp.bfloat16), "mp").astype(jnp.float32)
    else:
        summed = lax.psum(partial_value.astype(jnp.bfloat16), "mp").astype(jnp.float32)
    attn_out = (summed + b_proj.astype(jnp.float32)).reshape(slot_count, seq_len, model_dim)
    residual = tokens_f + gate_attn * attn_out
    normed_mlp = (
        modulate(residual, shift_mlp, scale_mlp).astype(jnp.bfloat16).reshape(row_count, model_dim)
    )
    hidden = jnp.dot(normed_mlp, w_up, preferred_element_type=jnp.float32) + b_up.astype(
        jnp.float32
    )
    act_bf = gelu_tanh(hidden).astype(jnp.bfloat16)
    partial_mlp = jnp.dot(act_bf, w_down, preferred_element_type=jnp.float32)
    if repeat:
        summed_mlp = lax.psum(partial_mlp.astype(jnp.bfloat16), "mp").astype(jnp.float32)
    else:
        summed_mlp = lax.psum(partial_mlp.astype(jnp.bfloat16), "mp").astype(jnp.float32)
    mlp_out = (summed_mlp + b_down.astype(jnp.float32)).reshape(slot_count, seq_len, model_dim)
    output = residual + gate_mlp * mlp_out
    return {
        "normed": normed,
        "query_rows": query_rows,
        "key_rows": key_rows,
        "value_rows": value_rows,
        "logsum": logsum,
        "mixed_b": mixed_b,
        "attn_out": attn_out,
        "residual": residual,
        "normed_mlp": normed_mlp,
        "hidden": hidden,
        "act_bf": act_bf,
        "mlp_out": mlp_out,
        "output": output,
    }


def image_pass(tokens_f, grad_out, spans, weights):
    w_qkv, b_qv, w_proj, b_proj, w_up, b_up, w_down, b_down = weights
    shift_attn, scale_attn, gate_attn, shift_mlp, scale_mlp, gate_mlp = spans
    slot_count, seq_len, model_dim = tokens_f.shape
    row_count = slot_count * seq_len
    head_cols = w_qkv.shape[2]
    head_count = head_cols // HEAD_DIM
    kept_fwd = forward(tokens_f, spans, weights, False)
    out_one = kept_fwd["output"]
    stored = forward(tokens_f, spans, weights, True)
    grad_gate_mlp = jnp.sum(grad_out * stored["mlp_out"], axis=1)
    grad_mlp = (gate_mlp * grad_out).astype(jnp.bfloat16).reshape(row_count, model_dim)
    grad_b_down = jnp.sum(grad_mlp.astype(jnp.float32), axis=0)
    grad_w_down = inner_rows(stored["act_bf"], grad_mlp)
    grad_act = outer_cols(grad_mlp, w_down)
    gelu_value, gelu_back = jax.vjp(gelu_tanh, stored["hidden"])
    grad_hidden = gelu_back(grad_act)[0].astype(jnp.bfloat16)
    grad_b_up = jnp.sum(grad_hidden.astype(jnp.float32), axis=0)
    grad_w_up = inner_rows(stored["normed_mlp"], grad_hidden)
    part_normed_mlp = outer_cols(grad_hidden, w_up)
    grad_normed_mlp = (
        lax.psum(part_normed_mlp.astype(jnp.bfloat16), "mp")
        .astype(jnp.float32)
        .reshape(slot_count, seq_len, model_dim)
    )
    norm_value, norm_back = jax.vjp(modulate, stored["residual"], shift_mlp, scale_mlp)
    grad_resid_norm, grad_shift_mlp, grad_scale_mlp = norm_back(grad_normed_mlp)
    grad_residual = grad_out + grad_resid_norm
    grad_gate_attn = jnp.sum(grad_residual * stored["attn_out"], axis=1)
    grad_attn = (gate_attn * grad_residual).astype(jnp.bfloat16).reshape(row_count, model_dim)
    grad_b_proj = jnp.sum(grad_attn.astype(jnp.float32), axis=0)
    grad_w_proj = inner_rows(stored["mixed_b"], grad_attn)
    grad_mixed = (
        outer_cols(grad_attn, w_proj)
        .astype(jnp.bfloat16)
        .reshape(slot_count, seq_len, head_count, HEAD_DIM)
    )
    grad_query, grad_key, grad_value = attention_backward(
        stored["query_rows"], stored["key_rows"], stored["value_rows"], stored["logsum"], grad_mixed
    )
    grad_qkv = jnp.stack(
        [
            grad_query.reshape(row_count, head_cols),
            grad_key.reshape(row_count, head_cols),
            grad_value.reshape(row_count, head_cols),
        ],
        axis=1,
    )
    grad_b_qv = jnp.stack(
        [
            jnp.sum(grad_qkv[:, 0].astype(jnp.float32), axis=0),
            jnp.sum(grad_qkv[:, 2].astype(jnp.float32), axis=0),
        ]
    )
    grad_w_qkv = inner_rows(stored["normed"], grad_qkv)
    part_normed = outer_cols(
        grad_qkv.reshape(row_count, 3 * head_cols), w_qkv.reshape(model_dim, 3 * head_cols)
    )
    grad_normed = (
        lax.psum(part_normed.astype(jnp.bfloat16), "mp")
        .astype(jnp.float32)
        .reshape(slot_count, seq_len, model_dim)
    )
    first_value, first_back = jax.vjp(modulate, tokens_f, shift_attn, scale_attn)
    grad_tok_norm, grad_shift_attn, grad_scale_attn = first_back(grad_normed)
    grad_tok_one = grad_residual + grad_tok_norm
    grad_mod_one = jnp.concatenate(
        [
            grad_shift_attn[:, 0],
            grad_scale_attn[:, 0],
            grad_gate_attn,
            grad_shift_mlp[:, 0],
            grad_scale_mlp[:, 0],
            grad_gate_mlp,
        ],
        axis=1,
    )
    grad_terms = (
        grad_w_qkv,
        grad_b_qv,
        grad_w_proj,
        grad_b_proj,
        grad_w_up,
        grad_b_up,
        grad_w_down,
        grad_b_down,
    )
    return (out_one, grad_tok_one, grad_mod_one, grad_terms)


def run_layer(tokens, condition, cotangent, live_count, turns, weights, w_mod, b_mod):
    slot_count, seq_len, model_dim = tokens.shape
    cond_f = condition.astype(jnp.float32)
    scaled = jax.nn.silu(cond_f).astype(jnp.bfloat16)
    own_mod = jnp.dot(scaled, w_mod, preferred_element_type=jnp.float32) + b_mod.astype(jnp.float32)
    modulation = lax.all_gather(own_mod, "mp", axis=1, tiled=True)
    tokens_f = tokens.astype(jnp.float32)
    cot_f = cotangent.astype(jnp.float32)

    def image_step(slot_idx, carry):
        out_buf, grad_buf, mod_buf, grad_sums = carry
        live_flag = (slot_idx < live_count).astype(jnp.float32)
        tok_one = lax.dynamic_slice_in_dim(tokens_f, slot_idx, 1, 0)
        cot_one = lax.dynamic_slice_in_dim(cot_f, slot_idx, 1, 0) * live_flag
        mod_row = lax.dynamic_slice_in_dim(modulation, slot_idx, 1, 0)
        spans = [
            mod_row[:, None, part_idx * model_dim : (part_idx + 1) * model_dim]
            for part_idx in range(6)
        ]
        out_one, grad_tok_one, grad_mod_one, grad_terms = image_pass(
            tok_one, cot_one, spans, weights
        )
        out_one = (out_one * live_flag).astype(jnp.bfloat16)
        out_buf = lax.dynamic_update_slice_in_dim(out_buf, out_one, slot_idx, 0)
        grad_buf = lax.dynamic_update_slice_in_dim(grad_buf, grad_tok_one, slot_idx, 0)
        mod_buf = lax.dynamic_update_slice_in_dim(mod_buf, grad_mod_one, slot_idx, 0)
        grad_sums = tuple((total_a + term_b for total_a, term_b in zip(grad_sums, grad_terms)))
        return (out_buf, grad_buf, mod_buf, grad_sums)

    start_sums = tuple((jnp.zeros(weight_in.shape, jnp.float32) for weight_in in weights))
    start_state = (
        jnp.zeros(tokens.shape, jnp.bfloat16),
        jnp.zeros(tokens.shape, jnp.float32),
        jnp.zeros((slot_count, 6 * model_dim), jnp.float32),
        start_sums,
    )
    out_buf, grad_buf, mod_buf, grad_sums = lax.fori_loop(0, turns, image_step, start_state)
    grad_modulation = mod_buf.astype(jnp.bfloat16)
    own_cols = w_mod.shape[1]
    grad_own = lax.dynamic_slice_in_dim(
        grad_modulation, lax.axis_index("mp") * own_cols, own_cols, 1
    )
    part_scaled = outer_cols(grad_own, w_mod)
    grad_scaled = lax.psum(part_scaled.astype(jnp.bfloat16), "mp").astype(jnp.float32)
    silu_value, silu_back = jax.vjp(jax.nn.silu, cond_f)
    grad_condition = silu_back(grad_scaled)[0]
    return (out_buf, grad_buf, grad_condition, grad_sums, scaled, grad_own)


def on_device(
    tokens,
    condition,
    counts,
    w_qkv,
    b_qv,
    w_proj,
    b_proj,
    w_up,
    b_up,
    w_down,
    b_down,
    w_mod,
    b_mod,
    cotangent,
):
    slot_count, seq_len, model_dim = tokens.shape
    weights = (w_qkv, b_qv, w_proj, b_proj, w_up, b_up, w_down, b_down)
    own_count = counts[0]
    output, grad_tokens, grad_condition, grad_sums, scaled, grad_own = run_layer(
        tokens, condition, cotangent, own_count, slot_count, weights, w_mod, b_mod
    )
    (
        grad_w_qkv,
        grad_b_qv,
        grad_w_proj,
        grad_b_proj,
        grad_w_up,
        grad_b_up,
        grad_w_down,
        grad_b_down,
    ) = grad_sums
    grad_w_mod = inner_rows(scaled, grad_own)
    grad_b_mod = jnp.sum(grad_own.astype(jnp.float32), axis=0)
    (
        grad_w_qkv,
        grad_b_qv,
        grad_w_proj,
        grad_b_proj,
        grad_w_up,
        grad_b_up,
        grad_w_down,
        grad_b_down,
        grad_w_mod,
        grad_b_mod,
    ) = (
        lax.psum(grad_w_qkv.astype(jnp.bfloat16), "dp").astype(jnp.float32),
        lax.psum(grad_b_qv.astype(jnp.bfloat16), "dp").astype(jnp.float32),
        lax.psum(grad_w_proj.astype(jnp.bfloat16), "dp").astype(jnp.float32),
        lax.psum(grad_b_proj.astype(jnp.bfloat16), "dp").astype(jnp.float32),
        lax.psum(grad_w_up.astype(jnp.bfloat16), "dp").astype(jnp.float32),
        lax.psum(grad_b_up.astype(jnp.bfloat16), "dp").astype(jnp.float32),
        lax.psum(grad_w_down.astype(jnp.bfloat16), "dp").astype(jnp.float32),
        lax.psum(grad_b_down.astype(jnp.bfloat16), "dp").astype(jnp.float32),
        lax.psum(grad_w_mod.astype(jnp.bfloat16), "dp").astype(jnp.float32),
        lax.psum(grad_b_mod.astype(jnp.bfloat16), "dp").astype(jnp.float32),
    )
    return (
        output,
        grad_tokens,
        grad_condition,
        grad_w_qkv,
        grad_b_qv,
        grad_w_proj,
        grad_b_proj,
        grad_w_up,
        grad_b_up,
        grad_w_down,
        grad_b_down,
        grad_w_mod,
        grad_b_mod,
    )


def solution(mesh):
    placed = (
        P("dp", None, None),
        P("dp", None),
        P("dp"),
        P(None, None, "mp"),
        P(None, "mp"),
        P("mp", None),
        P(),
        P(None, "mp"),
        P("mp"),
        P("mp", None),
        P(),
        P(None, "mp"),
        P("mp"),
        P("dp", None, None),
    )
    fast = mesh.shape["dp"] == 16 and mesh.shape["mp"] == 2
    return jax.shard_map(
        fast_device if fast else on_device,
        mesh=mesh,
        in_specs=placed,
        out_specs=(
            P("dp", None, None),
            P("dp", None, None),
            P("dp", None),
            P(None, None, "mp"),
            P(None, "mp"),
            P("mp", None),
            P(),
            P(None, "mp"),
            P("mp"),
            P("mp", None),
            P(),
            P(None, "mp"),
            P("mp"),
        ),
        check_vma=False,
    )
```
